32 devices in a mesh: dp: 8 (over z, y), tensor: 4 (over x, core).
Axes of the slice: x: 2, y: 2, z: 4, core: 2. Of those that a mesh axis runs over, the one named last changes fastest.
Arguments:
- tokens: bfloat16 [18688, 1024], P(('dp', 'tensor')), may hold values from -6 to 6
- cotangent: bfloat16 [18688, 1024], P(('dp', 'tensor')), may hold values from -6 to 6
- image_mask: int32 [32], P('dp'), may hold values 0 or 1
- norm_gains: bfloat16 [2, 1024], P(None, 'dp'), may hold values from 0.25 to 1.75
- norm_shifts: bfloat16 [4, 1024], P(None, 'dp'), may hold values from -1.796875 to 1.796875
- w_qkv: bfloat16 [3, 1024, 1024], P(None, 'dp', 'tensor'), may hold values from -0.25 to 0.25
- b_qv: bfloat16 [2, 1024], P(None, ('tensor', 'dp')), may hold values from -3 to 3
- w_out: bfloat16 [1024, 1024], P('tensor', 'dp'), may hold values from -0.4375 to 0.4375
- w_up: bfloat16 [1024, 4096], P('dp', 'tensor'), may hold values from -0.1875 to 0.1875
- up_bias: bfloat16 [4096], P(('tensor', 'dp')), may hold values from -3 to 3
- w_down: bfloat16 [4096, 1024], P('tensor', 'dp'), may hold values from -0.125 to 0.125
Outputs:
- layer_out: bfloat16 [18688, 1024], P(('dp', 'tensor'))
- grad_tokens: bfloat16 [18688, 1024], P(('dp', 'tensor'))
- grad_norm_gains: float32 [2, 1024], P(None, ('dp', 'tensor'))
- grad_norm_shifts: float32 [4, 1024], P(None, ('dp', 'tensor'))
- grad_w_qkv: float32 [3, 1024, 1024], P(None, 'dp', 'tensor')
- grad_b_qv: float32 [2, 1024], P(None, ('tensor', 'dp'))
- grad_w_out: float32 [1024, 1024], P('tensor', 'dp')
- grad_w_up: float32 [1024, 4096], P('dp', 'tensor')
- grad_up_bias: float32 [4096], P(('tensor', 'dp'))
- grad_w_down: float32 [4096, 1024], P('tensor', 'dp')
The draws below stay inside these ranges and needn't reach their ends.
All inputs are finite; a program needn't handle non-finite values. No bound on the sum of `image_mask` on one device may be relied on, other than what follows from the above.
Results may differ from the reference program's by a relative error of at most 0.02.
Values may be sent and summed in bfloat16 or wider, within the bound.
No kernel may reach another device: no remote copies, remote signals or barrier semaphores. Data moves between devices by JAX's collectives and lax.ppermute only.
A program may use at most 320 MiB of HBM per device.

```python
import jax
import jax.numpy as jnp
from jax import lax

D = 1024
HEADS = 16
HEAD_DIM = 64
FF = 4096
VALID = 577
SEQ = 584
IMAGES = 32
TOKENS = 18688


def with_ends(array, key, low, high):
    longest = array.shape.index(max(array.shape))
    spots = []
    for shift in (0, 1):
        where = [jax.random.randint(jax.random.fold_in(key, axis), (), 0, length) for axis, length in enumerate(array.shape)]
        where[longest] = (where[longest] + shift) % array.shape[longest]
        spots.append(tuple(where))
    return array.at[spots[0]].set(low).at[spots[1]].set(high)


def shard_levels(key, shape, cuts, least, largest):
    gain, own = 1.0, jax.random.fold_in(key, 6)
    for position, parts in cuts:
        steps = jnp.exp(jax.random.uniform(jax.random.fold_in(own, position), (parts,), jnp.float32, least / len(cuts), largest / len(cuts)))
        gain = gain * jnp.repeat(steps, shape[position] // parts).reshape([-1 if axis == position else 1 for axis in range(len(shape))])
    return gain


def noise(stream_key, extent, spread, most, split=(), dtype=jnp.bfloat16):
    level = shard_levels(stream_key, extent, split, -0.22, 0.18) if split else 1.0
    drawn = jax.random.normal(stream_key, extent, jnp.float32) * spread * level
    return jnp.minimum(jnp.maximum(drawn, -most), most).astype(dtype)


def setup_inputs(seed: int = 0) -> dict:
    keys = jax.random.split(jax.random.key(seed), 12)
    tokens = noise(keys[0], (TOKENS, D), 1.0, 6.0, ((0, 32),))
    cotangent = noise(keys[1], (TOKENS, D), 1.0, 6.0, ((0, 32),))
    image_mask = with_ends((jax.random.randint(keys[2], (IMAGES,), 0, 128) < 113).astype(jnp.int32), jax.random.fold_in(keys[2], 1), 0, 1)
    norm_gains = jnp.clip(1.0 + 0.15 * jax.random.normal(keys[3], (2, D), jnp.float32), 0.25, 1.75).astype(jnp.bfloat16)
    norm_shifts = noise(keys[4], (4, D), 0.3, 1.796875, ((1, 8),))
    w_qkv = noise(keys[5], (3, D, D), (D // 2) ** -0.5, 0.25, ((1, 8), (2, 4)))
    b_qv = noise(keys[6], (2, D), 0.5, 3.0, ((1, 32),))
    w_out = noise(keys[7], (D, D), (D // 5) ** -0.5, 0.4375, ((0, 4), (1, 8)))
    w_up = noise(keys[8], (D, FF), D ** -0.5, 0.1875, ((0, 8), (1, 4)))
    up_bias = noise(keys[9], (FF,), 0.5, 3.0, ((0, 32),))
    w_down = noise(keys[10], (FF, D), (FF // 2) ** -0.5, 0.125, ((0, 4), (1, 8)))
    return dict(tokens=tokens, cotangent=cotangent, image_mask=image_mask, norm_gains=norm_gains, norm_shifts=norm_shifts, w_qkv=w_qkv, b_qv=b_qv, w_out=w_out, w_up=w_up, up_bias=up_bias, w_down=w_down)


@jax.custom_vjp
def low(v):
    return lax.optimization_barrier(v.astype(jnp.bfloat16)).astype(jnp.float32)

@jax.custom_vjp
def low_back(v):
    return v

def low_keep(v):
    return (low(v), None)

def low_pass(kept, grad):
    return (grad,)

def back_keep(v):
    return (v, None)

def back_low(kept, grad):
    return (low(grad),)
low.defvjp(low_keep, low_pass)
low_back.defvjp(back_keep, back_low)
HIGHEST = lax.Precision.HIGHEST

def matmul(left, right):
    return jnp.dot(left, right, precision=HIGHEST)

def norm_apply(rows_in, gain_row, shift_row):
    center = rows_in - lax.optimization_barrier(jnp.mean(rows_in, axis=-1, keepdims=True))
    return center * lax.rsqrt(lax.optimization_barrier(jnp.mean(center * center, axis=-1, keepdims=True)) + 1e-05) * gain_row + shift_row

def attend_image(blocks):
    query_blk, key_blk, value_blk = blocks
    raw_scores = jnp.einsum('qhd,khd->hqk', query_blk, key_blk, precision=HIGHEST) * HEAD_DIM ** (-0.5)
    scores = low_back(raw_scores)
    valid_keys = jnp.arange(SEQ) < VALID
    scores = jnp.where(valid_keys[None, None, :], scores, -1e+30)
    attn_probs = low(jax.nn.softmax(scores, axis=-1))
    return jnp.einsum('hqk,khd->qhd', attn_probs, value_blk, precision=HIGHEST)

def block_forward(rows_in, keep_img, gains, shifts, w_qkv, b_qv, w_out, w_up, up_bias, w_down):
    images = rows_in.shape[0] // SEQ
    keep_rows = jnp.repeat(keep_img, SEQ)[:, None]
    first_norm = low(norm_apply(rows_in, gains[0], shifts[0]))
    queries = low(low_back(matmul(first_norm, w_qkv[0])) + b_qv[0])
    keys_all = low(low_back(matmul(first_norm, w_qkv[1])))
    values = low(low_back(matmul(first_norm, w_qkv[2])) + b_qv[1])
    head_shape = (images, SEQ, HEADS, HEAD_DIM)
    attended = lax.map(jax.checkpoint(attend_image), (queries.reshape(head_shape), keys_all.reshape(head_shape), values.reshape(head_shape)))
    attended = low(low_back(attended.reshape(rows_in.shape[0], D)))
    middle = rows_in + keep_rows * (low_back(matmul(attended, w_out)) + shifts[2])
    second_norm = low(norm_apply(middle, gains[1], shifts[1]))
    hidden_pre = low_back(matmul(second_norm, w_up)) + up_bias
    activated = low(hidden_pre * jax.nn.sigmoid(1.702 * hidden_pre))
    return middle + keep_rows * (low_back(matmul(activated, w_down)) + shifts[3])

def reference(tokens, cotangent, image_mask, norm_gains, norm_shifts, w_qkv, b_qv, w_out, w_up, up_bias, w_down):
    params = tuple((member.astype(jnp.float32) for member in (norm_gains, norm_shifts, w_qkv, b_qv, w_out, w_up, up_bias, w_down)))
    step_count = IMAGES // 4
    rows_all = tokens.astype(jnp.float32).reshape(step_count, 4 * SEQ, D)
    cot_all = cotangent.astype(jnp.float32).reshape(step_count, 4 * SEQ, D)
    keep_all = image_mask.astype(jnp.float32).reshape(step_count, 4)

    def advance(running, slices):
        rows_in, grad_rows_in, keep_img = slices

        def forward(rows_arg, *weights):
            return block_forward(rows_arg, keep_img, *weights)
        result, pullback = jax.vjp(forward, rows_in, *params)
        grad_list = pullback(grad_rows_in)
        updated = tuple((before + added for before, added in zip(running, grad_list[1:])))
        return (updated, (result.astype(jnp.bfloat16), grad_list[0].astype(jnp.bfloat16)))
    zero_grads = tuple((jnp.zeros_like(member) for member in params))
    totals, (out_rows, grad_rows) = lax.scan(advance, zero_grads, (rows_all, cot_all, keep_all))
    return (out_rows.reshape(TOKENS, D), grad_rows.reshape(TOKENS, D), totals[0], totals[1], totals[2], totals[3], totals[4], totals[5], totals[6], totals[7])
```

```python
import functools

import jax
import jax.numpy as jnp
from jax import lax
from jax.experimental import pallas as pl
from jax.experimental.pallas import tpu as pltpu
from jax.sharding import Mesh, PartitionSpec as P

HEAD_DIM = 64
VALID = 577
SEQ = 584
BF = jnp.bfloat16
F32 = jnp.float32
VMEM_LIMIT = 60 * 1024 * 1024
NT = (((1,), (1,)), ((), ()))
TN = (((0,), (0,)), ((), ()))
NN = (((1,), (0,)), ((), ()))


def dot(left, right, dims):
    return lax.dot_general(left, right, dims, preferred_element_type=F32)


class Loads:
    def __init__(self, sems):
        self.sems, self.groups = sems, []

    def start(self, pairs):
        sem = self.sems.at[len(self.groups)]
        copies = [pltpu.make_async_copy(src, dst, sem) for src, dst in pairs]
        for copy in copies:
            copy.start()
        self.groups.append(copies)
        return len(self.groups) - 1

    def wait(self, group):
        for copy in self.groups[group]:
            copy.wait()


def call(body, ins, outs, scratch, name, flops, aliases=None, smem=(), sems=12, vmem_ins=()):
    n_smem, n_vmem, n_in, n_out = len(smem), len(vmem_ins), len(ins), len(outs)
    moved = sum(a.size * a.dtype.itemsize for a in ins) + sum(
        o.size * o.dtype.itemsize for o in outs
    )

    def kernel(*refs):
        first = n_smem + n_vmem
        small = refs[:first]
        in_refs = refs[first : first + n_in]
        out_refs = refs[first + n_in : first + n_in + n_out]
        rest = refs[first + n_in + n_out :]
        body(small, in_refs, out_refs, rest[:-1], Loads(rest[-1]))

    any_spec = pl.BlockSpec(memory_space=pl.ANY)
    return pl.pallas_call(
        kernel,
        out_shape=outs,
        in_specs=[pl.BlockSpec(memory_space=pltpu.SMEM)] * n_smem
        + [pl.BlockSpec(memory_space=pltpu.VMEM)] * n_vmem
        + [any_spec] * n_in,
        out_specs=[any_spec] * n_out,
        scratch_shapes=list(scratch) + [pltpu.SemaphoreType.DMA((sems,))],
        input_output_aliases={n_smem + n_vmem + i: o for i, o in (aliases or {}).items()},
        compiler_params=pltpu.CompilerParams(vmem_limit_bytes=VMEM_LIMIT),
        cost_estimate=pl.CostEstimate(flops=int(flops), bytes_accessed=int(moved), transcendentals=0),
        name=name,
    )(*smem, *vmem_ins, *ins)


def norm_parts(rows):
    center = rows - jnp.mean(rows, axis=1, keepdims=True)
    inverse = lax.rsqrt(jnp.mean(center * center, axis=1, keepdims=True) + 1e-05)
    return center * inverse, inverse


def norm_back(grad_norm, scaled, inverse, gain_row):
    grad_hat = grad_norm * gain_row
    first_mean = jnp.mean(grad_hat, axis=1, keepdims=True)
    second_mean = jnp.mean(grad_hat * scaled, axis=1, keepdims=True)
    return inverse * (grad_hat - first_mean - scaled * second_mean)


def sds(shape, dtype):
    return jax.ShapeDtypeStruct(shape, dtype)


def arrange_pair(ids, own, other, nd):
    n = len(own)
    rows, width = own[0].shape
    bd = width // nd

    def body(small, ins, outs, scratch, loads):
        (ids_ref,) = small
        mine = ids_ref[0]
        pairs = []
        for i in range(n):
            for p in range(nd):
                src = pl.ds(pl.multiple_of(ids_ref[2 + p] * bd, 128), bd)
                dst = pl.ds(p * bd, bd)
                pairs.append((ins[i].at[:, src], outs[i].at[mine, :, dst]))
                pairs.append((ins[n + i].at[:, src], outs[i].at[1 - mine, :, dst]))
        loads.wait(loads.start(pairs))

    return call(
        body,
        list(own) + list(other),
        [sds((2, rows, width), BF)] * n,
        [],
        "arrange_pair",
        0,
        smem=(ids,),
    )


def weight_loads(loads, plan, refs, scratch):
    return loads.start([(refs[a].at[src], scratch[s].at[dst]) for a, src, s, dst in plan])


def softmax_rows(q2, k2):
    scores = dot(q2, k2, NT)
    lane = lax.broadcasted_iota(jnp.int32, scores.shape, 1)
    scores = jnp.where(lane < VALID, scores, -1e30)
    e = jnp.exp(scores - jnp.max(scores, axis=1, keepdims=True))
    return e * (1.0 / jnp.sum(e, axis=1, keepdims=True))


def attn_forward(image, tok, nv, bq, wqkv, wout, prev):
    seq, width = tok.shape[1:]
    qkv_arrays, qkv_plan, qkv_scratch = wqkv
    out_arrays, out_plan, out_scratch = wout
    ext = qkv_scratch[-1]
    n_prev = 0 if prev is None else len(prev)
    nq, no = len(qkv_arrays), len(out_arrays)

    def body(small, ins, outs, scratch, loads):
        nv_ref, bq_ref = small
        tok_ref, ins = ins[0], ins[1 + n_prev :]
        w_s, wo_s, tok_s, first_s, q_s, k_s, v_s, att_s, part_s = scratch
        g_tok = loads.start([(tok_ref.at[image], tok_s)])
        g_w = weight_loads(loads, qkv_plan, ins[:nq], (w_s,))
        g_o = weight_loads(loads, out_plan, ins[nq:], (wo_s,))
        loads.wait(g_tok)
        hat, _ = norm_parts(tok_s[...].astype(F32))
        first_s[...] = (hat * nv_ref[0:1, :] + nv_ref[2:3, :]).astype(BF)
        g_first = loads.start([(first_s, outs[0].at[image])])
        loads.wait(g_w)
        low = first_s[...]
        for i, ref in enumerate((q_s, k_s, v_s)):
            proj = dot(low, w_s[i].reshape(width, ext), NN)
            if i == 0:
                proj = proj + bq_ref[0:1, :]
            if i == 2:
                proj = proj + bq_ref[1:2, :]
            low_proj = proj.astype(BF)
            if i == 0:
                low_proj = low_proj * jnp.asarray(HEAD_DIM**-0.5, BF)
            ref[...] = low_proj
        g_qkv = loads.start(
            [(q_s, outs[1].at[image]), (k_s, outs[2].at[image]), (v_s, outs[3].at[image])]
        )
        half = lax.broadcasted_iota(jnp.int32, (1, 128), 1) // HEAD_DIM

        def pair(i, carry):
            cols = pl.ds(pl.multiple_of(i * 128, 128), 128)
            q2, k2, v2 = q_s[:, cols], k_s[:, cols], v_s[:, cols]
            total = None
            for h in range(2):
                keep = (half == h).astype(BF)
                probs = softmax_rows(q2, k2 * keep).astype(BF)
                piece = dot(probs, v2 * keep, NN)
                total = piece if total is None else total + piece
            att_s[:, cols] = total.astype(BF)
            return carry

        lax.fori_loop(0, ext // 128, pair, 0)
        g_att = loads.start([(att_s, outs[4].at[image])])
        loads.wait(g_o)
        part_s[...] = dot(att_s[...], wo_s[...], NN).astype(BF)
        g_part = loads.start([(part_s, outs[5])])
        for group in (g_first, g_qkv, g_att, g_part):
            loads.wait(group)

    shapes = [(2, seq, width)] + [(2, seq, ext)] * 4
    return call(
        body,
        [tok] + list(prev or []) + qkv_arrays + out_arrays,
        [sds(s, BF) for s in shapes] + [sds((seq, width), BF)],
        [
            pltpu.VMEM(qkv_scratch, BF),
            pltpu.VMEM(out_scratch, BF),
            pltpu.VMEM((seq, width), BF),
            pltpu.VMEM((seq, width), BF),
            pltpu.VMEM((seq, ext), BF),
            pltpu.VMEM((seq, ext), BF),
            pltpu.VMEM((seq, ext), BF),
            pltpu.VMEM((seq, ext), BF),
            pltpu.VMEM((seq, width), BF),
        ],
        "attn_forward",
        2 * seq * width * ext * 4 + 16 * seq * seq * ext,
        aliases={1 + i: i for i in range(n_prev)},
        vmem_ins=(nv, bq),
    )


def mlp_up(image, tok, part, recv, keep, nv, bu, wup, prev):
    seq, width = tok.shape[1:]
    up_arrays, up_plan, up_scratch = wup
    hid = up_scratch[-1]
    n_prev = 0 if prev is None else len(prev)
    step = min(512, hid)

    def body(small, ins, outs, scratch, loads):
        keep_ref, nv_ref, bu_ref = small
        tok_ref, part_ref, recv_ref = ins[:3]
        w_s, tok_s, part_s, recv_s, mid_s, sec_s, act_s, dact_s = scratch
        g_in = loads.start([(tok_ref.at[image], tok_s), (part_ref, part_s), (recv_ref, recv_s)])
        g_w = weight_loads(loads, up_plan, ins[3 + n_prev :], (w_s,))
        loads.wait(g_in)
        total = part_s[...].astype(F32) + recv_s[...].astype(F32) + nv_ref[4:5, :]
        middle = tok_s[...].astype(F32) + keep_ref[image] * total
        mid_s[...] = middle
        hat, _ = norm_parts(middle)
        sec_s[...] = (hat * nv_ref[1:2, :] + nv_ref[3:4, :]).astype(BF)
        g_mid = loads.start([(mid_s, outs[0].at[image]), (sec_s, outs[1].at[image])])
        loads.wait(g_w)
        second = sec_s[...]
        for lo in range(0, hid, step):
            cols = slice(lo, lo + step)
            pre = dot(second, w_s[:, cols], NN) + bu_ref[0:1, cols]
            gate = 1.0 / (1.0 + jnp.exp(-1.702 * pre))
            act_s[:, cols] = (pre * gate).astype(BF)
            dact_s[:, cols] = (gate + 1.702 * pre * gate * (1.0 - gate)).astype(BF)
        g_out = loads.start([(act_s, outs[2].at[image]), (dact_s, outs[3].at[image])])
        loads.wait(g_mid)
        loads.wait(g_out)

    outs = [
        sds((2, seq, width), F32),
        sds((2, seq, width), BF),
        sds((2, seq, hid), BF),
        sds((2, seq, hid), BF),
    ]
    return call(
        body,
        [tok, part, recv] + list(prev or []) + up_arrays,
        outs,
        [
            pltpu.VMEM(up_scratch, BF),
            pltpu.VMEM((seq, width), BF),
            pltpu.VMEM((seq, width), BF),
            pltpu.VMEM((seq, width), BF),
            pltpu.VMEM((seq, width), F32),
            pltpu.VMEM((seq, width), BF),
            pltpu.VMEM((seq, hid), BF),
            pltpu.VMEM((seq, hid), BF),
        ],
        "mlp_up",
        2 * seq * width * hid,
        aliases={3 + i: i for i in range(n_prev)},
        smem=(keep,),
        vmem_ins=(nv, bu),
    )


def weight_grad(left, right, tasks, out_shapes, name):
    rows = left.shape[0]
    n_right = len(right)

    def body(small, ins, outs, scratch, loads):
        left_s = scratch[0]
        right_s = scratch[1 : 1 + n_right]
        out_s = scratch[1 + n_right :]
        g_l = loads.start([(ins[0], left_s)])
        g_r = [loads.start([(ins[1 + i], right_s[i])]) for i in range(n_right)]
        loads.wait(g_l)
        for g in g_r:
            loads.wait(g)
        for l_cols, index, r_cols, stores in tasks:
            value = dot(left_s[:, l_cols], right_s[index][:, r_cols], TN).astype(BF)
            for which, spot, r_sl, c_sl in stores:
                out_s[which][spot] = value[r_sl, c_sl]
        done = loads.start([(out_s[i], outs[i]) for i in range(len(outs))])
        loads.wait(done)

    flops = sum(
        2 * rows * (l.stop - l.start) * (r.stop - r.start) for l, _, r, _ in tasks
    )
    return call(
        body,
        [left] + list(right),
        [sds(s, BF) for s in out_shapes],
        [pltpu.VMEM(a.shape, BF) for a in [left] + list(right)]
        + [pltpu.VMEM(s, BF) for s in out_shapes],
        name,
        flops,
    )


def mlp_back(grad, dact, wdown):
    rows, width = grad.shape
    hid = dact.shape[1]
    down_arrays, down_plan, down_scratch = wdown
    step = min(512, hid)

    def body(small, ins, outs, scratch, loads):
        w_s, g_s, d_s, low_s, sum_s = scratch
        g_g = loads.start([(ins[0], g_s)])
        g_w = weight_loads(loads, down_plan, ins[2:], (w_s,))
        g_d = loads.start([(ins[1], d_s)])
        for g in (g_g, g_w, g_d):
            loads.wait(g)
        left = g_s[...]
        for lo in range(0, hid, step):
            cols = slice(lo, lo + step)
            pre = dot(left, w_s[cols, :], NT) * d_s[:, cols].astype(F32)
            low_s[:, cols] = pre.astype(BF)
            sum_s[0:1, cols] = jnp.sum(pre, axis=0, keepdims=True)
        done = loads.start([(low_s, outs[0]), (sum_s, outs[1])])
        loads.wait(done)

    return call(
        body,
        [grad, dact] + down_arrays,
        [sds((rows, hid), BF), sds((1, hid), F32)],
        [
            pltpu.VMEM(down_scratch, BF),
            pltpu.VMEM((rows, width), BF),
            pltpu.VMEM((rows, hid), BF),
            pltpu.VMEM((rows, hid), BF),
            pltpu.VMEM((1, hid), F32),
        ],
        "mlp_back",
        2 * rows * width * hid,
    )


def rows_times(lefts, row_range, weight, dims, split, width, name):
    arrays, plan, shape = weight
    lo, hi = row_range
    rows = hi - lo
    n = len(lefts)

    def body(small, ins, outs, scratch, loads):
        w_s, out_s = scratch[0], scratch[1]
        l_s = scratch[2:]
        g_l = loads.start([(ins[i].at[lo:hi], l_s[i]) for i in range(n)])
        g_w = weight_loads(loads, plan, ins[n:], (w_s,))
        loads.wait(g_l)
        loads.wait(g_w)
        total = None
        for i in range(n):
            w = w_s[i].reshape(-1, shape[-1]) if split else w_s[...]
            piece = dot(l_s[i][...], w, dims)
            total = piece if total is None else total + piece
        out_s[...] = total.astype(BF)
        loads.wait(loads.start([(out_s, outs[0])]))

    return call(
        body,
        list(lefts) + arrays,
        [sds((rows, width), BF)],
        [pltpu.VMEM(shape, BF), pltpu.VMEM((rows, width), BF)]
        + [pltpu.VMEM((rows, a.shape[1]), BF) for a in lefts],
        name,
        2 * rows * width * sum(a.shape[1] for a in lefts),
    )[0]


def attn_backward(image, middle, part, recv, cot, keep, nv, wout, q, k, v, prev):
    seq, width = middle.shape[1:]
    out_arrays, out_plan, out_scratch = wout
    ext = q.shape[2]
    n_prev = 0 if prev is None else len(prev)

    def body(small, ins, outs, scratch, loads):
        keep_ref, nv_ref = small
        mid_ref, part_ref, recv_ref, cot_ref, q_ref, k_ref, v_ref = ins[:7]
        (wo_s, mid_s, part_s, recv_s, cot_s, q_s, k_s, v_s) = scratch[:8]
        (gmid_s, gat_s, do_s, dq_s, dk_s, dv_s, cs_s, bs_s) = scratch[8:]
        g_in = loads.start(
            [
                (mid_ref.at[image], mid_s),
                (part_ref, part_s),
                (recv_ref, recv_s),
                (cot_ref.at[image], cot_s),
            ]
        )
        g_o = weight_loads(loads, out_plan, ins[7 + n_prev :], (wo_s,))
        g_q = loads.start(
            [(q_ref.at[image], q_s), (k_ref.at[image], k_s), (v_ref.at[image], v_s)]
        )
        loads.wait(g_in)
        keep_here = keep_ref[image]
        hat, inverse = norm_parts(mid_s[...])
        grad_two = part_s[...].astype(F32) + recv_s[...].astype(F32)
        top = cot_s[...].astype(F32)
        cs_s[0:1, :] = jnp.sum(grad_two * hat, axis=0, keepdims=True)
        cs_s[1:2, :] = jnp.sum(grad_two, axis=0, keepdims=True)
        cs_s[3:4, :] = jnp.sum(top, axis=0, keepdims=True) * keep_here
        grad_mid = top + norm_back(grad_two, hat, inverse, nv_ref[1:2, :])
        gmid_s[...] = grad_mid
        grad_attn = grad_mid * keep_here
        cs_s[2:3, :] = jnp.sum(grad_attn, axis=0, keepdims=True)
        gat_s[...] = grad_attn.astype(BF)
        g_mid = loads.start([(gmid_s, outs[0].at[image]), (gat_s, outs[1].at[image])])
        loads.wait(g_o)
        do_s[...] = dot(gat_s[...], wo_s[...], NT).astype(BF)
        loads.wait(g_q)
        half = lax.broadcasted_iota(jnp.int32, (1, 128), 1) // HEAD_DIM

        def pair(i, carry):
            cols = pl.ds(pl.multiple_of(i * 128, 128), 128)
            q2, k2, v2, do2 = q_s[:, cols], k_s[:, cols], v_s[:, cols], do_s[:, cols]
            dq = dk = dv = None
            for h in range(2):
                mask = (half == h).astype(BF)
                km, qm, dom = k2 * mask, q2 * mask, do2 * mask
                scores = dot(km, q2, NT)
                row = lax.broadcasted_iota(jnp.int32, scores.shape, 0)
                scores = jnp.where(row < VALID, scores, -1e30)
                e = jnp.exp(scores - jnp.max(scores, axis=0, keepdims=True))
                probs = e * (1.0 / jnp.sum(e, axis=0, keepdims=True))
                grad_probs = dot(v2, dom, NT)
                row_dot = jnp.sum(probs * grad_probs, axis=0, keepdims=True)
                grad_scores = (probs * (grad_probs - row_dot)).astype(BF)
                v_piece = dot(probs.astype(BF), dom, NN)
                k_piece = dot(grad_scores, qm, NN)
                q_piece = dot(grad_scores, km, TN)
                dq = q_piece if dq is None else dq + q_piece
                dk = k_piece if dk is None else dk + k_piece
                dv = v_piece if dv is None else dv + v_piece
            dq = dq * HEAD_DIM**-0.5
            bs_s[0:1, cols] = jnp.sum(dq, axis=0, keepdims=True)
            bs_s[1:2, cols] = jnp.sum(dv, axis=0, keepdims=True)
            dq_s[:, cols] = dq.astype(BF)
            dk_s[:, cols] = dk.astype(BF)
            dv_s[:, cols] = dv.astype(BF)
            return carry

        lax.fori_loop(0, ext // 128, pair, 0)
        g_out = loads.start(
            [
                (dq_s, outs[2].at[image]),
                (dk_s, outs[3].at[image]),
                (dv_s, outs[4].at[image]),
                (cs_s, outs[5]),
                (bs_s, outs[6]),
            ]
        )
        loads.wait(g_mid)
        loads.wait(g_out)

    return call(
        body,
        [middle, part, recv, cot, q, k, v] + list(prev or []) + out_arrays,
        [sds((2, seq, width), F32), sds((2, seq, width), BF)]
        + [sds((2, seq, ext), BF)] * 3
        + [sds((4, width), F32), sds((2, ext), F32)],
        [
            pltpu.VMEM(out_scratch, BF),
            pltpu.VMEM((seq, width), F32),
            pltpu.VMEM((seq, width), BF),
            pltpu.VMEM((seq, width), BF),
            pltpu.VMEM((seq, width), BF),
            pltpu.VMEM((seq, ext), BF),
            pltpu.VMEM((seq, ext), BF),
            pltpu.VMEM((seq, ext), BF),
            pltpu.VMEM((seq, width), F32),
            pltpu.VMEM((seq, width), BF),
            pltpu.VMEM((seq, ext), BF),
            pltpu.VMEM((seq, ext), BF),
            pltpu.VMEM((seq, ext), BF),
            pltpu.VMEM((seq, ext), BF),
            pltpu.VMEM((4, width), F32),
            pltpu.VMEM((2, ext), F32),
        ],
        "attn_backward",
        2 * seq * width * ext + 40 * seq * seq * ext,
        aliases={7 + i: i for i in range(n_prev)},
        smem=(keep,),
        vmem_ins=(nv,),
    )


def store_blocks(ids_ref, out_s, value, nd, aligned):
    width = value.shape[1]
    bd = width // nd
    if not aligned:
        out_s[...] = value
        return
    for p in range(nd):
        cols = pl.ds(pl.multiple_of(ids_ref[2 + p] * bd, 128), bd)
        out_s[:, cols] = value[:, p * bd : (p + 1) * bd]


def finish_layer(ids, keep, nv, middle, part, recv, nd, aligned):
    seq, width = middle.shape[1:]

    def body(small, ins, outs, scratch, loads):
        ids_ref, keep_ref, nv_ref = small
        mine = ids_ref[0]
        mid_s, part_s, recv_s, out_s = scratch
        loads.wait(
            loads.start(
                [
                    (ins[0].at[mine], mid_s),
                    (ins[1].at[mine], part_s),
                    (ins[2].at[mine], recv_s),
                ]
            )
        )
        total = part_s[...].astype(F32) + recv_s[...].astype(F32) + nv_ref[5:6, :]
        value = (mid_s[...] + keep_ref[mine] * total).astype(BF)
        store_blocks(ids_ref, out_s, value, nd, aligned)
        loads.wait(loads.start([(out_s, outs[0])]))

    return call(
        body,
        [middle, part, recv],
        [sds((seq, width), BF)],
        [
            pltpu.VMEM((seq, width), F32),
            pltpu.VMEM((seq, width), BF),
            pltpu.VMEM((seq, width), BF),
            pltpu.VMEM((seq, width), BF),
        ],
        "finish_layer",
        0,
        smem=(ids, keep),
        vmem_ins=(nv,),
    )[0]


def finish_tokens(ids, nv, tok, part, recv, gmid, nd, aligned):
    seq, width = tok.shape[1:]

    def body(small, ins, outs, scratch, loads):
        ids_ref, nv_ref = small
        mine = ids_ref[0]
        tok_s, part_s, recv_s, mid_s, out_s, cs_s = scratch
        groups = [
            loads.start(
                [(ins[0].at[a], tok_s.at[a]), (ins[1].at[a], part_s.at[a]), (ins[2].at[a], recv_s.at[a])]
            )
            for a in range(2)
        ]
        g_mid = loads.start([(ins[3].at[mine], mid_s)])
        loads.wait(g_mid)
        for group in groups:
            loads.wait(group)
        for i in range(2):
            a = mine if i == 0 else 1 - mine
            hat, inverse = norm_parts(tok_s[a].astype(F32))
            grad_one = part_s[a].astype(F32) + recv_s[a].astype(F32)
            gain_sum = jnp.sum(grad_one * hat, axis=0, keepdims=True)
            shift_sum = jnp.sum(grad_one, axis=0, keepdims=True)
            if i == 0:
                cs_s[0:1, :] = gain_sum
                cs_s[1:2, :] = shift_sum
                value = mid_s[...] + norm_back(grad_one, hat, inverse, nv_ref[0:1, :])
                store_blocks(ids_ref, out_s, value.astype(BF), nd, aligned)
            else:
                cs_s[0:1, :] = cs_s[0:1, :] + gain_sum
                cs_s[1:2, :] = cs_s[1:2, :] + shift_sum
        loads.wait(loads.start([(out_s, outs[0]), (cs_s, outs[1])]))

    return call(
        body,
        [tok, part, recv, gmid],
        [sds((seq, width), BF), sds((2, width), F32)],
        [
            pltpu.VMEM((2, seq, width), BF),
            pltpu.VMEM((2, seq, width), BF),
            pltpu.VMEM((2, seq, width), BF),
            pltpu.VMEM((seq, width), F32),
            pltpu.VMEM((seq, width), BF),
            pltpu.VMEM((2, width), F32),
        ],
        "finish_tokens",
        0,
        smem=(ids,),
        vmem_ins=(nv,),
    )


class Grid3:
    def __init__(self, dp, tx):
        self.dp, self.tx = dp, tx
        self.y = 2 if dp % 2 == 0 else 1
        self.z = dp // self.y

    def send_z(self, value, k):
        return lax.ppermute(value, "dp", [(i, i ^ (k * self.y)) for i in range(self.dp)])

    def send_y(self, value, k):
        return lax.ppermute(value, "dp", [(i, i ^ k) for i in range(self.dp)])

    def send_x(self, value, k):
        return lax.ppermute(value, "tx", [(i, i ^ k) for i in range(self.tx)])


def swap_core(value):
    return lax.ppermute(value, "core", [(0, 1), (1, 0)])


def gather(grid, part_a, part_b):
    rows = part_a.shape[0]
    both = jnp.concatenate([part_a, part_b], axis=0)
    all_z = [both] + [grid.send_z(both, k) for k in range(1, grid.z)]
    a_z = jnp.stack([v[:rows] for v in all_z])
    b_z = jnp.stack([v[rows:] for v in all_z])
    a_y = jnp.concatenate([a_z] + [grid.send_y(a_z, k) for k in range(1, grid.y)])
    b_x = jnp.concatenate([b_z] + [grid.send_x(b_z, k) for k in range(1, grid.tx)])
    a_all = [a_y] + [grid.send_x(a_y, k) for k in range(1, grid.tx)]
    b_all = [b_x] + [grid.send_y(b_x, k) for k in range(1, grid.y)]
    return a_all, b_all


def add_low(first, *others):
    total = first.astype(F32)
    for other in others:
        total = total + other.astype(F32)
    return total.astype(BF)


def scatter(grid, a_all, b_all):
    z = grid.z
    a_got = [grid.send_x(a_all[k], k) for k in range(1, grid.tx)]
    b_got = [grid.send_y(b_all[k], k) for k in range(1, grid.y)]
    a_y = [add_low(*[v[k * z : (k + 1) * z] for v in [a_all[0]] + a_got]) for k in range(grid.y)]
    b_x = [add_low(*[v[k * z : (k + 1) * z] for v in [b_all[0]] + b_got]) for k in range(grid.tx)]
    a_got = [grid.send_y(a_y[k], k) for k in range(1, grid.y)]
    b_got = [grid.send_x(b_x[k], k) for k in range(1, grid.tx)]
    both = [
        jnp.concatenate(
            [add_low(*[v[k] for v in [a_y[0]] + a_got]), add_low(*[v[k] for v in [b_x[0]] + b_got])]
        )
        for k in range(z)
    ]
    got = [grid.send_z(both[k], k) for k in range(1, z)]
    total = both[0].astype(F32)
    for value in got:
        total = total + value.astype(F32)
    rows = a_all[0].shape[1]
    return total[:rows], total[rows:]


def xor_blocks(value, mask, axis):
    count = value.shape[axis]
    bit = 1
    while bit < count:
        shape = value.shape
        split = value.reshape(shape[:axis] + (count // (2 * bit), 2, bit) + shape[axis + 1 :])
        turned = jnp.flip(split, axis=axis + 1).reshape(shape)
        value = jnp.where(jnp.bitwise_and(mask, bit) != 0, turned, value)
        bit *= 2
    return value


def pad_cols(value, width):
    return jnp.pad(value, ((0, 0), (0, width - value.shape[1])))


def per_device(
    tokens,
    cotangent,
    image_mask,
    norm_gains,
    norm_shifts,
    w_qkv,
    b_qv,
    w_out,
    w_up,
    up_bias,
    w_down,
    *,
    dp,
    tx,
):
    grid = Grid3(dp, tx)
    y_n, z_n = grid.y, grid.z
    core = lax.axis_index("core").astype(jnp.int32)
    me_d = lax.axis_index("dp").astype(jnp.int32)
    me_x = lax.axis_index("tx").astype(jnp.int32)
    seq, width = tokens.shape
    _, bd, hw = w_qkv.shape
    fw = w_up.shape[1]
    ext, hid = tx * hw, tx * fw
    hh, fh = hw // 2, fw // 2
    aligned = bd % 128 == 0 and hh % 128 == 0 and fh % 128 == 0
    rel = [kz * y_n + ky for ky in range(y_n) for kz in range(z_n)]

    def from_abs(value, axis):
        shape = value.shape
        value = value.reshape(shape[:axis] + (z_n, y_n) + shape[axis + 1 :])
        return jnp.swapaxes(value, axis, axis + 1).reshape(shape)

    def to_rel(value, axis):
        shape = value.shape
        value = value.reshape(shape[:axis] + (y_n, z_n) + shape[axis + 1 :])
        return jnp.swapaxes(value, axis, axis + 1).reshape(shape)

    ids = jnp.stack([core, me_d] + [jnp.bitwise_xor(me_d, k) for k in rel])
    keep = lax.dynamic_slice(image_mask, (2 * me_x,), (2,)).astype(F32)

    lane = max(bd, hh)
    small = jnp.concatenate(
        [
            pad_cols(norm_gains, lane),
            pad_cols(norm_shifts, lane),
            pad_cols(b_qv, lane),
            pad_cols(up_bias[None], lane),
            jnp.zeros((7, lane), BF),
        ]
    )
    qkv_a = pad_cols(w_qkv[:, :, :hh].reshape(3 * bd, hh), lane)
    qkv_b = pad_cols(w_qkv[:, :, hh:].reshape(3 * bd, hh), lane)
    first_a = jnp.concatenate([qkv_a, pad_cols(w_out[:hh], lane), small])
    first_b = jnp.concatenate([qkv_b, pad_cols(w_out[hh:], lane)])
    c1a, c1b = gather(grid, first_a, first_b)
    upa, upb = gather(grid, w_up[:, :fh], w_up[:, fh:])
    dna, dnb = gather(grid, w_down[:fh], w_down[fh:])

    tok_other, cot_other = swap_core(tokens), swap_core(cotangent)
    if aligned:
        tok, cot = arrange_pair(ids, [tokens, cotangent], [tok_other, cot_other], dp)
    else:

        def arrange(own, other):
            pair = jnp.where(core == 0, jnp.stack([own, other]), jnp.stack([other, own]))
            pair = xor_blocks(pair.reshape(2, seq, dp, bd), me_d, 2)
            return from_abs(pair, 2).reshape(2, seq, width)

        tok, cot = arrange(tokens, tok_other), arrange(cotangent, cot_other)
    grad_top = cot * keep.astype(BF)[:, None, None]

    row0 = 3 * bd + hh
    nv = (
        c1a[0][:, row0 : row0 + 6, :bd].transpose(1, 0, 2).reshape(6, width).astype(F32)
    )
    tail = jnp.stack([v[:, row0 + 6 : row0 + 9] for v in c1a])
    tail = xor_blocks(to_rel(tail, 1), me_d, 1)
    bq = (
        tail[:, :, :2, : hw // dp].transpose(2, 0, 1, 3).reshape(2, ext).astype(F32)
    )
    bu = tail[:, :, 2, : fw // dp].reshape(1, hid).astype(F32)

    if aligned:
        wq_plan, wo_plan, up_plan, dn_plan = [], [], [], []
        for kx in range(tx):
            for i in range(3):
                src = slice(i * bd, (i + 1) * bd)
                cols = slice(kx * hw, kx * hw + hh)
                wq_plan.append((kx, (slice(None), src), 0, (i, slice(None), slice(None), cols)))
                cols = slice(kx * hw + hh, (kx + 1) * hw)
                for ky in range(y_n):
                    own = slice(kx * z_n, (kx + 1) * z_n)
                    dst = (i, slice(ky * z_n, (ky + 1) * z_n), slice(None), cols)
                    wq_plan.append((tx + ky, (own, src), 0, dst))
            src = slice(3 * bd, 3 * bd + hh)
            for ky in range(y_n):
                for kz in range(z_n):
                    p = ky * z_n + kz
                    cols = slice(p * bd, (p + 1) * bd)
                    wo_plan.append((kx, (p, src), 0, (slice(kx * hw, kx * hw + hh), cols)))
                    dst = (slice(kx * hw + hh, (kx + 1) * hw), cols)
                    wo_plan.append((tx + ky, (kx * z_n + kz, src), 0, dst))
                    dst = (slice(kx * fw, kx * fw + fh), cols)
                    dn_plan.append((kx, (p,), 0, dst))
                    dst = (slice(kx * fw + fh, (kx + 1) * fw), cols)
                    dn_plan.append((tx + ky, (kx * z_n + kz,), 0, dst))
            dst = (slice(None), slice(kx * fw, kx * fw + fh))
            up_plan.append((kx, (slice(None),), 0, dst))
            for ky in range(y_n):
                rows = slice(kx * z_n * bd, (kx + 1) * z_n * bd)
                dst = (
                    slice(ky * z_n * bd, (ky + 1) * z_n * bd),
                    slice(kx * fw + fh, (kx + 1) * fw),
                )
                up_plan.append((tx + ky, (rows,), 0, dst))
        c1 = c1a + c1b
        wqkv = (c1, wq_plan, (3, dp, bd, ext))
        wout = (c1, wo_plan, (ext, width))
        up = [v.reshape(-1, fh) for v in upa + upb]
        wup = (up, up_plan, (width, hid))
        wdown = (dna + dnb, dn_plan, (hid, width))
    else:

        def whole(a_all, b_all):
            a = jnp.stack(a_all)
            b = jnp.stack(b_all).reshape((y_n, tx, z_n) + b_all[0].shape[1:])
            b = b.transpose(1, 0, 2, 3, 4).reshape(a.shape[:2] + b.shape[3:])
            return jnp.stack([a, b], axis=1)

        a_rows = first_b.shape[0]
        c1 = whole([v[:, :a_rows] for v in c1a], c1b)
        qkv = c1[:, :, :, : 3 * bd, :hh].reshape(tx, 2, dp, 3, bd, hh)
        qkv = qkv.transpose(3, 2, 4, 0, 1, 5).reshape(3, dp, bd, ext)
        out = c1[:, :, :, 3 * bd :, :bd].transpose(0, 1, 3, 2, 4).reshape(ext, width)
        up = whole(upa, upb).transpose(2, 3, 0, 1, 4).reshape(width, hid)
        down = whole(dna, dnb).transpose(0, 1, 3, 2, 4).reshape(hid, width)
        wqkv = ([qkv], [(0, (slice(None),), 0, (slice(None),))], qkv.shape)
        wout = ([out], [(0, (slice(None),), 0, (slice(None),))], out.shape)
        wup = ([up], [(0, (slice(None),), 0, (slice(None),))], up.shape)
        wdown = ([down], [(0, (slice(None),), 0, (slice(None),))], down.shape)

    rows2 = 2 * seq

    state, parts = None, []
    for image in range(2):
        res = attn_forward(image, tok, nv, bq, wqkv, wout, state)
        state = res[:5]
        parts.append((res[5], swap_core(res[5])))
    first, q, k, v, att = state
    state = None
    for image in range(2):
        part, recv = parts[image]
        state = mlp_up(image, tok, part, recv, keep, nv, bu, wup, state)
    middle, second, act, dact = state
    flat = lambda value: value.reshape(rows2, value.shape[2])
    act2, sec2, grad2 = flat(act), flat(second), flat(grad_top)

    def down_tasks(kxs, kys):
        tasks, shapes = [], []
        for n, kx in enumerate(kxs):
            stores = [
                (n, (p,), slice(None), slice(p * bd, (p + 1) * bd)) for p in range(dp)
            ]
            tasks.append((slice(kx * fw, kx * fw + fh), 0, slice(0, width), stores))
            shapes.append((dp, fh, bd))
        for n, ky in enumerate(kys):
            for kx in range(tx):
                stores = [
                    (len(kxs) + n, (kx * z_n + kz,), slice(None), slice(kz * bd, (kz + 1) * bd))
                    for kz in range(z_n)
                ]
                cols = slice(ky * z_n * bd, (ky + 1) * z_n * bd)
                tasks.append((slice(kx * fw + fh, (kx + 1) * fw), 0, cols, stores))
            shapes.append((tx * z_n, fh, bd))
        return tasks, shapes

    def out_tasks(kxs, kys):
        tasks, shapes = [], []
        for n, kx in enumerate(kxs):
            stores = [
                (n, (p,), slice(None), slice(p * bd, (p + 1) * bd)) for p in range(dp)
            ]
            tasks.append((slice(kx * hw, kx * hw + hh), 0, slice(0, width), stores))
            shapes.append((dp, hh, bd))
        for n, ky in enumerate(kys):
            for kx in range(tx):
                stores = [
                    (len(kxs) + n, (kx * z_n + kz,), slice(None), slice(kz * bd, (kz + 1) * bd))
                    for kz in range(z_n)
                ]
                cols = slice(ky * z_n * bd, (ky + 1) * z_n * bd)
                tasks.append((slice(kx * hw + hh, (kx + 1) * hw), 0, cols, stores))
            shapes.append((tx * z_n, hh, bd))
        return tasks, shapes

    def up_tasks(kxs, kys):
        tasks, shapes = [], []
        for n, kx in enumerate(kxs):
            stores = [
                (n, (p,), slice(p * bd, (p + 1) * bd), slice(None)) for p in range(dp)
            ]
            tasks.append((slice(0, width), 0, slice(kx * fw, kx * fw + fh), stores))
            shapes.append((dp, bd, fh))
        for n, ky in enumerate(kys):
            for kx in range(tx):
                stores = [
                    (len(kxs) + n, (kx * z_n + kz,), slice(kz * bd, (kz + 1) * bd), slice(None))
                    for kz in range(z_n)
                ]
                rows = slice(ky * z_n * bd, (ky + 1) * z_n * bd)
                tasks.append((rows, 0, slice(kx * fw + fh, (kx + 1) * fw), stores))
            shapes.append((tx * z_n, bd, fh))
        return tasks, shapes

    def qkv_tasks(kxs, kys):
        tasks, shapes = [], []
        for n, kx in enumerate(kxs):
            for i in range(3):
                stores = [
                    (n, (p, slice(i * bd, (i + 1) * bd)), slice(p * bd, (p + 1) * bd), slice(None))
                    for p in range(dp)
                ]
                tasks.append((slice(0, width), i, slice(kx * hw, kx * hw + hh), stores))
            shapes.append((dp, 3 * bd, hh))
        for n, ky in enumerate(kys):
            for kx in range(tx):
                for i in range(3):
                    stores = [
                        (
                            len(kxs) + n,
                            (kx * z_n + kz, slice(i * bd, (i + 1) * bd)),
                            slice(kz * bd, (kz + 1) * bd),
                            slice(None),
                        )
                        for kz in range(z_n)
                    ]
                    rows = slice(ky * z_n * bd, (ky + 1) * z_n * bd)
                    tasks.append((rows, i, slice(kx * hw + hh, (kx + 1) * hw), stores))
            shapes.append((tx * z_n, 3 * bd, hh))
        return tasks, shapes

    def reduce_grad(make, left, right, name):
        away_x, away_y = list(range(1, tx)), list(range(1, y_n))
        sent = weight_grad(left, right, *make(away_x, away_y), name + "_send")
        kept = weight_grad(left, right, *make([0], [0]), name + "_keep")
        return scatter(
            grid, [kept[0]] + list(sent[: tx - 1]), [kept[1]] + list(sent[tx - 1 :])
        )

    down_a, down_b = reduce_grad(down_tasks, act2, [grad2], "down_grad")
    low_pre, bias_up = mlp_back(grad2, flat(dact), wdown)
    parts = []
    for image in range(2):
        span = (image * seq, (image + 1) * seq)
        part = rows_times([low_pre], span, wup, NT, False, width, "grad_two")
        parts.append((part, swap_core(part)))
    up_a, up_b = reduce_grad(up_tasks, sec2, [low_pre], "up_grad")
    mlp_part = rows_times([act2], (0, rows2), wdown, NN, False, width, "mlp_out")
    mlp_part = mlp_part.reshape(2, seq, width)
    mlp_recv = swap_core(mlp_part)
    layer_out = finish_layer(ids, keep, nv, middle, mlp_part, mlp_recv, dp, aligned)

    state, sums = None, []
    for image in range(2):
        part, recv = parts[image]
        res = attn_backward(image, middle, part, recv, cot, keep, nv, wout, q, k, v, state)
        state = res[:5]
        sums.append(res[5:])
    gmid, gattn, dq, dk, dv = state
    out_a, out_b = reduce_grad(out_tasks, flat(att), [flat(gattn)], "out_grad")
    low_proj = [flat(dq), flat(dk), flat(dv)]
    qkv_ga, qkv_gb = reduce_grad(qkv_tasks, flat(first), low_proj, "qkv_grad")
    one_part = rows_times(low_proj, (0, rows2), wqkv, NT, True, width, "grad_one")
    one_part = one_part.reshape(2, seq, width)
    one_recv = swap_core(one_part)
    grad_tokens, one_sums = finish_tokens(ids, nv, tok, one_part, one_recv, gmid, dp, aligned)
    if not aligned:

        def restore(value):
            value = xor_blocks(to_rel(value.reshape(seq, dp, bd), 1), me_d, 1)
            return value.reshape(seq, width)

        layer_out, grad_tokens = restore(layer_out), restore(grad_tokens)

    col = sums[0][0] + sums[1][0]
    bias_qv = sums[0][1] + sums[1][1]
    vec = jnp.stack([one_sums[0], col[0], one_sums[1], col[1], col[2], col[3]])
    wide = max(bd, hw // dp, fw // dp)
    vec = vec.reshape(6, dp, bd).transpose(1, 0, 2)
    vec = jnp.pad(vec, ((0, 0), (0, 0), (0, wide - bd)))
    bias_qv = bias_qv.reshape(2, tx, dp, hw // dp).transpose(2, 1, 0, 3).reshape(dp, 2 * tx, -1)
    bias_up = bias_up.reshape(tx, dp, fw // dp).transpose(1, 0, 2)
    bias = jnp.concatenate(
        [
            jnp.pad(bias_qv, ((0, 0), (0, 0), (0, wide - hw // dp))),
            jnp.pad(bias_up, ((0, 0), (0, 0), (0, wide - fw // dp))),
        ],
        axis=1,
    )
    bias = from_abs(xor_blocks(bias, me_d, 0), 0)
    both = jnp.concatenate([vec, bias], axis=1)
    got = [both] + [grid.send_x(both, k) for k in range(1, tx)]
    vec = sum(value[:, :6] for value in got)
    bqv_mine = sum(value[:, 6 + 2 * k : 8 + 2 * k] for k, value in enumerate(got))
    bup_mine = sum(
        value[:, 6 + 2 * tx + k : 7 + 2 * tx + k] for k, value in enumerate(got)
    )
    both = jnp.concatenate([vec, bqv_mine, bup_mine], axis=1)
    both = both[:z_n] + sum(
        grid.send_y(both[k * z_n : (k + 1) * z_n], k) for k in range(1, y_n)
    )
    both = both[0] + sum(grid.send_z(both[k], k) for k in range(1, z_n))
    share = bd // (2 * tx)
    mine = lax.dynamic_slice(both[:6, :bd], (0, (2 * me_x + core) * share), (6, share))

    grad_qkv = jnp.concatenate(
        [qkv_ga.reshape(3, bd, hh), qkv_gb.reshape(3, bd, hh)], axis=2
    )
    grad_out = jnp.concatenate([out_a, out_b], axis=0)
    grad_up = jnp.concatenate([up_a, up_b], axis=1)
    grad_down = jnp.concatenate([down_a, down_b], axis=0)
    return (
        layer_out,
        grad_tokens,
        mine[:2],
        mine[2:6],
        grad_qkv,
        both[6:8, : hw // dp],
        grad_out,
        grad_up,
        both[8, : fw // dp],
        grad_down,
    )


def solution(mesh):
    dp, tensor = mesh.shape["dp"], mesh.shape["tensor"]
    split = Mesh(mesh.devices.reshape(dp, tensor // 2, 2), ("dp", "tx", "core"))
    every = ("dp", "tx", "core")
    tensor_axes = ("tx", "core")
    in_specs = (
        P(every, None),
        P(every, None),
        P("dp"),
        P(None, "dp"),
        P(None, "dp"),
        P(None, "dp", tensor_axes),
        P(None, ("tx", "core", "dp")),
        P(tensor_axes, "dp"),
        P("dp", tensor_axes),
        P(("tx", "core", "dp")),
        P(tensor_axes, "dp"),
    )
    out_specs = (
        P(every, None),
        P(every, None),
        P(None, every),
        P(None, every),
        P(None, "dp", tensor_axes),
        P(None, ("tx", "core", "dp")),
        P(tensor_axes, "dp"),
        P("dp", tensor_axes),
        P(("tx", "core", "dp")),
        P(tensor_axes, "dp"),
    )
    return jax.shard_map(
        functools.partial(per_device, dp=dp, tx=tensor // 2),
        mesh=split,
        in_specs=in_specs,
        out_specs=out_specs,
        check_vma=False,
    )
```

```python
import functools

import jax
import jax.numpy as jnp
from jax import lax
from jax.experimental import pallas as pl
from jax.experimental.pallas import tpu as pltpu
from jax.sharding import Mesh, PartitionSpec as P

HEAD_DIM = 64
VALID = 577
SEQ = 584
BF = jnp.bfloat16
F32 = jnp.float32
VMEM_LIMIT = 60 * 1024 * 1024
SLOW = 0.05
NT = (((1,), (1,)), ((), ()))
TN = (((0,), (0,)), ((), ()))
NN = (((1,), (0,)), ((), ()))


def dot(left, right, dims):
    return lax.dot_general(left, right, dims, preferred_element_type=F32)


class Loads:
    def __init__(self, sems):
        self.sems, self.groups = sems, []

    def start(self, pairs):
        sem = self.sems.at[len(self.groups)]
        copies = [pltpu.make_async_copy(src, dst, sem) for src, dst in pairs]
        for copy in copies:
            copy.start()
        self.groups.append(copies)
        return len(self.groups) - 1

    def wait(self, group):
        for copy in self.groups[group]:
            copy.wait()


def call(body, ins, outs, scratch, name, flops, aliases=None, smem=(), sems=48, vmem_ins=()):
    n_smem, n_vmem, n_in, n_out = len(smem), len(vmem_ins), len(ins), len(outs)
    moved = sum(a.size * a.dtype.itemsize for a in ins) + sum(
        o.size * o.dtype.itemsize for o in outs
    )

    def kernel(*refs):
        first = n_smem + n_vmem
        small = refs[:first]
        in_refs = refs[first : first + n_in]
        out_refs = refs[first + n_in : first + n_in + n_out]
        rest = refs[first + n_in + n_out :]
        body(small, in_refs, out_refs, rest[:-1], Loads(rest[-1]))

    any_spec = pl.BlockSpec(memory_space=pl.ANY)
    return pl.pallas_call(
        kernel,
        out_shape=outs,
        in_specs=[pl.BlockSpec(memory_space=pltpu.SMEM)] * n_smem
        + [pl.BlockSpec(memory_space=pltpu.VMEM)] * n_vmem
        + [any_spec] * n_in,
        out_specs=[any_spec] * n_out,
        scratch_shapes=list(scratch) + [pltpu.SemaphoreType.DMA((sems,))],
        input_output_aliases={n_smem + n_vmem + i: o for i, o in (aliases or {}).items()},
        compiler_params=pltpu.CompilerParams(vmem_limit_bytes=VMEM_LIMIT),
        cost_estimate=pl.CostEstimate(flops=int(flops / SLOW), bytes_accessed=int(moved / SLOW), transcendentals=0),
        name=name,
    )(*smem, *vmem_ins, *ins)


def norm_parts(rows):
    center = rows - jnp.mean(rows, axis=1, keepdims=True)
    inverse = lax.rsqrt(jnp.mean(center * center, axis=1, keepdims=True) + 1e-05)
    return center * inverse, inverse


def norm_back(grad_norm, scaled, inverse, gain_row):
    grad_hat = grad_norm * gain_row
    first_mean = jnp.mean(grad_hat, axis=1, keepdims=True)
    second_mean = jnp.mean(grad_hat * scaled, axis=1, keepdims=True)
    return inverse * (grad_hat - first_mean - scaled * second_mean)


def sds(shape, dtype):
    return jax.ShapeDtypeStruct(shape, dtype)


def arrange_pair(ids, own, other, nd):
    n = len(own)
    rows, width = own[0].shape
    bd = width // nd

    def body(small, ins, outs, scratch, loads):
        (ids_ref,) = small
        mine = ids_ref[0]
        in_s, out_s = scratch[: 2 * n], scratch[2 * n :]
        groups = [loads.start([(ins[i], in_s[i])]) for i in range(2 * n)]
        done = []
        for i in range(2 * n):
            loads.wait(groups[i])
            for p in range(nd):
                src = pl.ds(pl.multiple_of(ids_ref[2 + p] * bd, 128), bd)
                out_s[i][:, p * bd : (p + 1) * bd] = in_s[i][:, src]
            spot = mine if i < n else 1 - mine
            done.append(loads.start([(out_s[i], outs[i % n].at[spot])]))
        for group in done:
            loads.wait(group)

    return call(
        body,
        list(own) + list(other),
        [sds((2, rows, width), BF)] * n,
        [pltpu.VMEM((rows, width), BF)] * (4 * n),
        "arrange_pair",
        0,
        smem=(ids,),
    )


def weight_loads(loads, groups, refs, scratch):
    return [
        loads.start([(refs[a].at[src], scratch.at[dst]) for a, src, dst in plan])
        for plan in groups
    ]


def softmax_rows(q2, k2):
    scores = dot(q2, k2, NT)
    lane = lax.broadcasted_iota(jnp.int32, scores.shape, 1)
    scores = jnp.where(lane < VALID, scores, -1e30)
    e = jnp.exp(scores - jnp.max(scores, axis=1, keepdims=True))
    return e * (1.0 / jnp.sum(e, axis=1, keepdims=True))


def attn_forward(image, tok, nv, bq, wqkv, wout, prev):
    seq, width = tok.shape[1:]
    qkv_arrays, qkv_plan, qkv_scratch = wqkv
    out_arrays, out_plan, out_scratch = wout
    ext = qkv_scratch[-1]
    n_prev = 0 if prev is None else len(prev)
    nq, no = len(qkv_arrays), len(out_arrays)

    def body(small, ins, outs, scratch, loads):
        nv_ref, bq_ref = small
        tok_ref, ins = ins[0], ins[1 + n_prev :]
        w_s, wo_s, tok_s, first_s, q_s, k_s, v_s, att_s, part_s = scratch
        g_tok = loads.start([(tok_ref.at[image], tok_s)])
        g_w = weight_loads(loads, qkv_plan, ins[:nq], w_s)
        g_o = weight_loads(loads, out_plan, ins[nq:], wo_s)
        loads.wait(g_tok)
        hat, _ = norm_parts(tok_s[...].astype(F32))
        first_s[...] = (hat * nv_ref[0:1, :] + nv_ref[2:3, :]).astype(BF)
        g_first = loads.start([(first_s, outs[0].at[image])])
        low = first_s[...]
        for i, ref in enumerate((q_s, k_s, v_s)):
            if i < len(g_w):
                loads.wait(g_w[i])
            proj = dot(low, w_s[i].reshape(width, ext), NN)
            if i == 0:
                proj = proj + bq_ref[0:1, :]
            if i == 2:
                proj = proj + bq_ref[1:2, :]
            low_proj = proj.astype(BF)
            if i == 0:
                low_proj = low_proj * jnp.asarray(HEAD_DIM**-0.5, BF)
            ref[...] = low_proj
        g_qkv = loads.start(
            [(q_s, outs[1].at[image]), (k_s, outs[2].at[image]), (v_s, outs[3].at[image])]
        )
        half = lax.broadcasted_iota(jnp.int32, (1, 128), 1) // HEAD_DIM

        def pair(i, carry):
            cols = pl.ds(pl.multiple_of(i * 128, 128), 128)
            q2, k2, v2 = q_s[:, cols], k_s[:, cols], v_s[:, cols]
            total = None
            for h in range(2):
                keep = (half == h).astype(BF)
                probs = softmax_rows(q2, k2 * keep).astype(BF)
                piece = dot(probs, v2 * keep, NN)
                total = piece if total is None else total + piece
            att_s[:, cols] = total.astype(BF)
            return carry

        lax.fori_loop(0, ext // 128, pair, 0)
        g_att = loads.start([(att_s, outs[4].at[image])])
        loads.wait(g_o[0])
        part_s[...] = dot(att_s[...], wo_s[...], NN).astype(BF)
        g_part = loads.start([(part_s, outs[5])])
        for group in (g_first, g_qkv, g_att, g_part):
            loads.wait(group)

    shapes = [(2, seq, width)] + [(2, seq, ext)] * 4
    return call(
        body,
        [tok] + list(prev or []) + qkv_arrays + out_arrays,
        [sds(s, BF) for s in shapes] + [sds((seq, width), BF)],
        [
            pltpu.VMEM(qkv_scratch, BF),
            pltpu.VMEM(out_scratch, BF),
            pltpu.VMEM((seq, width), BF),
            pltpu.VMEM((seq, width), BF),
            pltpu.VMEM((seq, ext), BF),
            pltpu.VMEM((seq, ext), BF),
            pltpu.VMEM((seq, ext), BF),
            pltpu.VMEM((seq, ext), BF),
            pltpu.VMEM((seq, width), BF),
        ],
        "attn_forward",
        2 * seq * width * ext * 4 + 16 * seq * seq * ext,
        aliases={1 + i: i for i in range(n_prev)},
        vmem_ins=(nv, bq),
    )


def mlp_up(image, tok, part, recv, keep, nv, bu, wup, step, prev):
    seq, width = tok.shape[1:]
    up_arrays, up_plan, up_scratch = wup
    hid = up_scratch[-1]
    n_prev = 0 if prev is None else len(prev)

    def body(small, ins, outs, scratch, loads):
        keep_ref, nv_ref, bu_ref = small
        tok_ref, part_ref, recv_ref = ins[:3]
        w_s, tok_s, part_s, recv_s, mid_s, sec_s, act_s, dact_s = scratch
        g_in = loads.start([(tok_ref.at[image], tok_s), (part_ref, part_s), (recv_ref, recv_s)])
        g_w = weight_loads(loads, up_plan, ins[3 + n_prev :], w_s)
        loads.wait(g_in)
        total = part_s[...].astype(F32) + recv_s[...].astype(F32) + nv_ref[4:5, :]
        middle = tok_s[...].astype(F32) + keep_ref[image] * total
        mid_s[...] = middle
        hat, _ = norm_parts(middle)
        sec_s[...] = (hat * nv_ref[1:2, :] + nv_ref[3:4, :]).astype(BF)
        g_mid = loads.start([(mid_s, outs[0].at[image]), (sec_s, outs[1].at[image])])
        second = sec_s[...]
        done = []
        for block in range(hid // step):
            if block < len(g_w):
                loads.wait(g_w[block])
            cols = slice(block * step, (block + 1) * step)
            pre = dot(second, w_s[:, cols], NN) + bu_ref[0:1, cols]
            gate = 1.0 / (1.0 + jnp.exp(-1.702 * pre))
            act_s[:, cols] = (pre * gate).astype(BF)
            dact_s[:, cols] = (gate + 1.702 * pre * gate * (1.0 - gate)).astype(BF)
            done.append(
                loads.start(
                    [
                        (act_s.at[:, cols], outs[2].at[image, :, cols]),
                        (dact_s.at[:, cols], outs[3].at[image, :, cols]),
                    ]
                )
            )
        for group in [g_mid] + done:
            loads.wait(group)

    outs = [
        sds((2, seq, width), F32),
        sds((2, seq, width), BF),
        sds((2, seq, hid), BF),
        sds((2, seq, hid), BF),
    ]
    return call(
        body,
        [tok, part, recv] + list(prev or []) + up_arrays,
        outs,
        [
            pltpu.VMEM(up_scratch, BF),
            pltpu.VMEM((seq, width), BF),
            pltpu.VMEM((seq, width), BF),
            pltpu.VMEM((seq, width), BF),
            pltpu.VMEM((seq, width), F32),
            pltpu.VMEM((seq, width), BF),
            pltpu.VMEM((seq, hid), BF),
            pltpu.VMEM((seq, hid), BF),
        ],
        "mlp_up",
        2 * seq * width * hid,
        aliases={3 + i: i for i in range(n_prev)},
        smem=(keep,),
        vmem_ins=(nv, bu),
    )


def weight_grad(lefts, rights, tasks, out_shapes, name):
    rows = lefts[0].shape[0]
    arrays = list(lefts) + list(rights)
    n_left, n_in = len(lefts), len(arrays)
    last = {}
    for n, task in enumerate(tasks):
        for store in task[4]:
            last[store[0]] = n

    def body(small, ins, outs, scratch, loads):
        in_s, out_s = scratch[:n_in], scratch[n_in:]
        order = []
        for l_index, _, r_index, _, _ in tasks:
            for i in (l_index, n_left + r_index):
                if i not in order:
                    order.append(i)
        groups = {i: loads.start([(ins[i], in_s[i])]) for i in order}
        ready, done = set(), []
        for n, (l_index, l_cols, r_index, r_cols, stores) in enumerate(tasks):
            for i in (l_index, n_left + r_index):
                if i not in ready:
                    loads.wait(groups[i])
                    ready.add(i)
            left, right = in_s[l_index][:, l_cols], in_s[n_left + r_index][:, r_cols]
            value = dot(left, right, TN).astype(BF)
            for which, spot, r_sl, c_sl in stores:
                out_s[which][spot] = value[r_sl, c_sl]
            for which in sorted(w for w in last if last[w] == n):
                done.append(loads.start([(out_s[which], outs[which])]))
        for group in done:
            loads.wait(group)

    flops = sum(
        2 * rows * (t[1].stop - t[1].start) * (t[3].stop - t[3].start) for t in tasks
    )
    return call(
        body,
        arrays,
        [sds(s, BF) for s in out_shapes],
        [pltpu.VMEM(a.shape, BF) for a in arrays] + [pltpu.VMEM(s, BF) for s in out_shapes],
        name,
        flops,
    )


def mlp_back(grad, act, dact, wdown, wup, step):
    rows, width = grad.shape
    hid = dact.shape[1]
    down_arrays, down_plan, down_scratch = wdown
    up_arrays, up_plan, up_scratch = wup
    n_down = len(down_arrays)

    def body(small, ins, outs, scratch, loads):
        wd_s, wu_s, g_s, a_s, d_s, low_s, sum_s, two_s, mlp_s = scratch
        g_g = loads.start([(ins[0], g_s)])
        g_wd = weight_loads(loads, down_plan, ins[3 : 3 + n_down], wd_s)
        g_d = []
        for block in range(hid // step):
            cols = slice(block * step, (block + 1) * step)
            g_d.append(loads.start([(ins[2].at[:, cols], d_s.at[:, cols])]))
        g_wu = weight_loads(loads, up_plan, ins[3 + n_down :], wu_s)
        g_a = loads.start([(ins[1], a_s)])
        loads.wait(g_g)
        left = g_s[...]
        done = []
        for block in range(hid // step):
            if block < len(g_wd):
                loads.wait(g_wd[block])
            loads.wait(g_d[block])
            cols = slice(block * step, (block + 1) * step)
            pre = dot(left, wd_s[cols, :], NT) * d_s[:, cols].astype(F32)
            low_s[:, cols] = pre.astype(BF)
            sum_s[0:1, cols] = jnp.sum(pre, axis=0, keepdims=True)
            done.append(loads.start([(low_s.at[:, cols], outs[0].at[:, cols])]))
        done.append(loads.start([(sum_s, outs[1])]))
        for group in g_wu:
            loads.wait(group)
        two_s[...] = dot(low_s[...], wu_s[...], NT).astype(BF)
        done.append(loads.start([(two_s, outs[2])]))
        loads.wait(g_a)
        mlp_s[...] = dot(a_s[...], wd_s[...], NN).astype(BF)
        done.append(loads.start([(mlp_s, outs[3])]))
        for group in done:
            loads.wait(group)

    return call(
        body,
        [grad, act, dact] + down_arrays + up_arrays,
        [sds((rows, hid), BF), sds((1, hid), F32), sds((rows, width), BF), sds((rows, width), BF)],
        [
            pltpu.VMEM(down_scratch, BF),
            pltpu.VMEM(up_scratch, BF),
            pltpu.VMEM((rows, width), BF),
            pltpu.VMEM((rows, hid), BF),
            pltpu.VMEM((rows, hid), BF),
            pltpu.VMEM((rows, hid), BF),
            pltpu.VMEM((1, hid), F32),
            pltpu.VMEM((rows, width), BF),
            pltpu.VMEM((rows, width), BF),
        ],
        "mlp_back",
        6 * rows * width * hid,
        sems=64,
    )


def rows_times(lefts, row_range, weight, dims, split, width, name):
    arrays, plan, shape = weight
    lo, hi = row_range
    rows = hi - lo
    n = len(lefts)

    def body(small, ins, outs, scratch, loads):
        w_s, out_s = scratch[0], scratch[1]
        l_s = scratch[2:]
        g_l = loads.start([(ins[i].at[lo:hi], l_s[i]) for i in range(n)])
        g_w = weight_loads(loads, plan, ins[n:], w_s)
        loads.wait(g_l)
        for group in g_w:
            loads.wait(group)
        total = None
        for i in range(n):
            w = w_s[i].reshape(-1, shape[-1]) if split else w_s[...]
            piece = dot(l_s[i][...], w, dims)
            total = piece if total is None else total + piece
        out_s[...] = total.astype(BF)
        loads.wait(loads.start([(out_s, outs[0])]))

    return call(
        body,
        list(lefts) + arrays,
        [sds((rows, width), BF)],
        [pltpu.VMEM(shape, BF), pltpu.VMEM((rows, width), BF)]
        + [pltpu.VMEM((rows, a.shape[1]), BF) for a in lefts],
        name,
        2 * rows * width * sum(a.shape[1] for a in lefts),
    )[0]


def store_blocks(ids_ref, out_s, value, nd, aligned):
    width = value.shape[1]
    bd = width // nd
    if not aligned:
        out_s[...] = value
        return
    for p in range(nd):
        cols = pl.ds(pl.multiple_of(ids_ref[2 + p] * bd, 128), bd)
        out_s[:, cols] = value[:, p * bd : (p + 1) * bd]


def middle_back(ids, middle, part, recvs, cot, keep, nv, wout):
    _, seq, width = middle.shape
    out_arrays, out_plan, out_scratch = wout
    ext = out_scratch[0]

    def body(small, ins, outs, scratch, loads):
        ids_ref, keep_ref, nv_ref = small
        mine = ids_ref[0]
        wo_s, mid_s, part_s, recv_s, cot_s, gmid_s, gat_s, do_s = scratch[:8]
        cs_s = scratch[8]
        g_in = [
            loads.start(
                [
                    (ins[0].at[a], mid_s.at[a]),
                    (ins[1].at[a], part_s.at[a]),
                    (ins[2].at[a], cot_s.at[a]),
                    (ins[3 + a], recv_s.at[a]),
                ]
            )
            for a in range(2)
        ]
        g_o = weight_loads(loads, out_plan, ins[5:], wo_s)
        done = []
        for a in range(2):
            loads.wait(g_in[a])
            keep_here = keep_ref[a]
            hat, inverse = norm_parts(mid_s[a])
            grad_two = part_s[a].astype(F32) + recv_s[a].astype(F32)
            top = cot_s[a].astype(F32)
            grad_mid = top + norm_back(grad_two, hat, inverse, nv_ref[1:2, :])
            grad_attn = grad_mid * keep_here
            sums = [
                jnp.sum(grad_two * hat, axis=0, keepdims=True),
                jnp.sum(grad_two, axis=0, keepdims=True),
                jnp.sum(grad_attn, axis=0, keepdims=True),
                jnp.sum(top, axis=0, keepdims=True) * keep_here,
            ]
            for i, value in enumerate(sums):
                cs_s[i : i + 1, :] = value if a == 0 else cs_s[i : i + 1, :] + value
            gmid_s[a] = grad_mid
            gat_s[a] = grad_attn.astype(BF)
            done.append(loads.start([(gat_s.at[a], outs[1].at[a])]))
            if a == 0:
                loads.wait(g_o[0])
            do_s[a] = dot(gat_s[a], wo_s[...], NT).astype(BF)
            done.append(loads.start([(do_s.at[a], outs[2].at[a])]))
        done.append(loads.start([(gmid_s.at[mine], outs[0]), (cs_s, outs[3])]))
        for group in done:
            loads.wait(group)

    return call(
        body,
        [middle, part, cot] + list(recvs) + out_arrays,
        [
            sds((seq, width), F32),
            sds((2, seq, width), BF),
            sds((2, seq, ext), BF),
            sds((4, width), F32),
        ],
        [
            pltpu.VMEM(out_scratch, BF),
            pltpu.VMEM((2, seq, width), F32),
            pltpu.VMEM((2, seq, width), BF),
            pltpu.VMEM((2, seq, width), BF),
            pltpu.VMEM((2, seq, width), BF),
            pltpu.VMEM((2, seq, width), F32),
            pltpu.VMEM((2, seq, width), BF),
            pltpu.VMEM((2, seq, ext), BF),
            pltpu.VMEM((4, width), F32),
        ],
        "middle_back",
        4 * seq * width * ext,
        smem=(ids, keep),
        vmem_ins=(nv,),
    )


def attn_backward(image, grad, q, k, v, prev):
    _, seq, ext = q.shape
    n_prev = 0 if prev is None else len(prev)

    def body(small, ins, outs, scratch, loads):
        q_s, k_s, v_s, do_s, dq_s, dk_s, dv_s, bs_s = scratch
        n_pairs = ext // 128
        groups = []
        for i in range(n_pairs):
            cols = slice(i * 128, (i + 1) * 128)
            groups.append(
                loads.start(
                    [
                        (ins[j].at[image, :, cols], scratch[j].at[:, cols])
                        for j in range(4)
                    ]
                )
            )
        half = lax.broadcasted_iota(jnp.int32, (1, 128), 1) // HEAD_DIM
        for group in groups:
            loads.wait(group)

        def pair(i, carry):
            cols = pl.ds(pl.multiple_of(i * 128, 128), 128)
            q2, k2, v2, do2 = q_s[:, cols], k_s[:, cols], v_s[:, cols], do_s[:, cols]
            dq = dk = dv = None
            for h in range(2):
                mask = (half == h).astype(BF)
                km, qm, dom = k2 * mask, q2 * mask, do2 * mask
                scores = dot(km, q2, NT)
                row = lax.broadcasted_iota(jnp.int32, scores.shape, 0)
                scores = jnp.where(row < VALID, scores, -1e30)
                e = jnp.exp(scores - jnp.max(scores, axis=0, keepdims=True))
                probs = e * (1.0 / jnp.sum(e, axis=0, keepdims=True))
                grad_probs = dot(v2, dom, NT)
                row_dot = jnp.sum(probs * grad_probs, axis=0, keepdims=True)
                grad_scores = (probs * (grad_probs - row_dot)).astype(BF)
                v_piece = dot(probs.astype(BF), dom, NN)
                k_piece = dot(grad_scores, qm, NN)
                q_piece = dot(grad_scores, km, TN)
                dq = q_piece if dq is None else dq + q_piece
                dk = k_piece if dk is None else dk + k_piece
                dv = v_piece if dv is None else dv + v_piece
            dq = dq * HEAD_DIM**-0.5
            bs_s[0:1, cols] = jnp.sum(dq, axis=0, keepdims=True)
            bs_s[1:2, cols] = jnp.sum(dv, axis=0, keepdims=True)
            dq_s[:, cols] = dq.astype(BF)
            dk_s[:, cols] = dk.astype(BF)
            dv_s[:, cols] = dv.astype(BF)
            return carry

        lax.fori_loop(0, n_pairs, pair, 0)
        g_out = loads.start(
            [
                (dq_s, outs[0].at[image]),
                (dk_s, outs[1].at[image]),
                (dv_s, outs[2].at[image]),
                (bs_s, outs[3]),
            ]
        )
        loads.wait(g_out)

    return call(
        body,
        [q, k, v, grad] + list(prev or []),
        [sds((2, seq, ext), BF)] * 3 + [sds((2, ext), F32)],
        [pltpu.VMEM((seq, ext), BF)] * 7 + [pltpu.VMEM((2, ext), F32)],
        "attn_backward",
        40 * seq * seq * ext,
        aliases={4 + i: i for i in range(n_prev)},
    )


def finish_layer(ids, keep, nv, middle, part, recv, nd, aligned):
    _, seq, width = middle.shape

    def body(small, ins, outs, scratch, loads):
        ids_ref, keep_ref, nv_ref = small
        mine = ids_ref[0]
        mid_s, part_s, recv_s, out_s = scratch
        groups = [loads.start([(ins[i].at[mine], scratch[i])]) for i in range(3)]
        for group in groups:
            loads.wait(group)
        total = part_s[...].astype(F32) + recv_s[...].astype(F32) + nv_ref[5:6, :]
        value = (mid_s[...] + keep_ref[mine] * total).astype(BF)
        store_blocks(ids_ref, out_s, value, nd, aligned)
        loads.wait(loads.start([(out_s, outs[0])]))

    return call(
        body,
        [middle, part, recv],
        [sds((seq, width), BF)],
        [pltpu.VMEM((seq, width), F32)] + [pltpu.VMEM((seq, width), BF)] * 3,
        "finish_layer",
        100 * seq * width,
        smem=(ids, keep),
        vmem_ins=(nv,),
    )[0]


def finish_tokens(ids, nv, tok, part, recvs, gmid, nd, aligned):
    _, seq, width = tok.shape

    def body(small, ins, outs, scratch, loads):
        ids_ref, nv_ref = small
        mine = ids_ref[0]
        tok_s, part_s, recv_s, gm_s, out_s, cs_s = scratch
        groups = [
            loads.start(
                [
                    (ins[0].at[a], tok_s.at[a]),
                    (ins[1].at[a], part_s.at[a]),
                    (ins[3 + a], recv_s.at[a]),
                ]
            )
            for a in range(2)
        ]
        g_mid = loads.start([(ins[2], gm_s)])
        for group in groups:
            loads.wait(group)
        done = []
        for i in range(2):
            a = mine if i == 0 else 1 - mine
            hat, inverse = norm_parts(tok_s[a].astype(F32))
            grad_one = part_s[a].astype(F32) + recv_s[a].astype(F32)
            gain_sum = jnp.sum(grad_one * hat, axis=0, keepdims=True)
            shift_sum = jnp.sum(grad_one, axis=0, keepdims=True)
            if i == 0:
                cs_s[0:1, :] = gain_sum
                cs_s[1:2, :] = shift_sum
                loads.wait(g_mid)
                value = gm_s[...] + norm_back(grad_one, hat, inverse, nv_ref[0:1, :])
                store_blocks(ids_ref, out_s, value.astype(BF), nd, aligned)
                done.append(loads.start([(out_s, outs[0])]))
            else:
                cs_s[0:1, :] = cs_s[0:1, :] + gain_sum
                cs_s[1:2, :] = cs_s[1:2, :] + shift_sum
        done.append(loads.start([(cs_s, outs[1])]))
        for group in done:
            loads.wait(group)

    return call(
        body,
        [tok, part, gmid] + list(recvs),
        [sds((seq, width), BF), sds((2, width), F32)],
        [pltpu.VMEM((2, seq, width), BF)] * 3
        + [pltpu.VMEM((seq, width), F32), pltpu.VMEM((seq, width), BF), pltpu.VMEM((2, width), F32)],
        "finish_tokens",
        200 * seq * width,
        smem=(ids,),
        vmem_ins=(nv,),
    )


class Grid3:
    def __init__(self, dp, tx):
        self.dp, self.tx = dp, tx
        self.y = 2 if dp % 2 == 0 else 1
        self.z = dp // self.y

    def send_z(self, value, k):
        return lax.ppermute(value, "dp", [(i, i ^ (k * self.y)) for i in range(self.dp)])

    def send_y(self, value, k):
        return lax.ppermute(value, "dp", [(i, i ^ k) for i in range(self.dp)])

    def send_x(self, value, k):
        return lax.ppermute(value, "tx", [(i, i ^ k) for i in range(self.tx)])


def swap_core(value):
    return lax.ppermute(value, "core", [(0, 1), (1, 0)])


def after(values, gate):
    return lax.optimization_barrier((values, gate))[0]


def gather_z(grid, part_a, part_b, gate=None):
    rows = part_a.shape[0]
    both = jnp.concatenate([part_a, part_b], axis=0)
    all_z = [both] + [grid.send_z(both, k) for k in range(1, grid.z)]
    if gate is not None:
        all_z = after(all_z, gate)
    return jnp.stack([v[:rows] for v in all_z]), jnp.stack([v[rows:] for v in all_z])


def gather_first(grid, a_z, b_z):
    a_y = [a_z] + [grid.send_y(a_z, k) for k in range(1, grid.y)]
    b_x = [b_z] + [grid.send_x(b_z, k) for k in range(1, grid.tx)]
    return a_y, b_x


def gather_last(grid, a_y, b_x):
    a_y, b_x = jnp.concatenate(a_y), jnp.concatenate(b_x)
    a_all = [a_y] + [grid.send_x(a_y, k) for k in range(1, grid.tx)]
    b_all = [b_x] + [grid.send_y(b_x, k) for k in range(1, grid.y)]
    return a_all, b_all


def add_low(first, *others):
    total = first.astype(F32)
    for other in others:
        total = total + other.astype(F32)
    return total.astype(BF)


class Scatter:
    def __init__(self, grid, a_all, b_all):
        self.grid, self.rows = grid, a_all[0].shape[1]
        a_got = [grid.send_x(a_all[k], k) for k in range(1, grid.tx)]
        b_got = [grid.send_y(b_all[k], k) for k in range(1, grid.y)]
        self.state = ([a_all[0]] + a_got, [b_all[0]] + b_got)

    def second(self, gate):
        grid, z = self.grid, self.grid.z
        a_in, b_in = after(self.state, gate)
        a_y = [add_low(*[v[k * z : (k + 1) * z] for v in a_in]) for k in range(grid.y)]
        b_x = [add_low(*[v[k * z : (k + 1) * z] for v in b_in]) for k in range(grid.tx)]
        a_got = [grid.send_y(a_y[k], k) for k in range(1, grid.y)]
        b_got = [grid.send_x(b_x[k], k) for k in range(1, grid.tx)]
        self.state = ([a_y[0]] + a_got, [b_x[0]] + b_got)
        return a_y[0], b_x[0]

    def along_z(self, gate):
        grid = self.grid
        a_in, b_in = after(self.state, gate)
        both = [
            jnp.concatenate([add_low(*[v[k] for v in a_in]), add_low(*[v[k] for v in b_in])])
            for k in range(grid.z)
        ]
        got = [grid.send_z(both[k], k) for k in range(1, grid.z)]
        self.state = [both[0]] + got
        return both

    def finish(self, gate):
        parts = after(self.state, gate)
        total = parts[0].astype(F32)
        for value in parts[1:]:
            total = total + value.astype(F32)
        return total[: self.rows], total[self.rows :]


def xor_blocks(value, mask, axis):
    count = value.shape[axis]
    bit = 1
    while bit < count:
        shape = value.shape
        split = value.reshape(shape[:axis] + (count // (2 * bit), 2, bit) + shape[axis + 1 :])
        turned = jnp.flip(split, axis=axis + 1).reshape(shape)
        value = jnp.where(jnp.bitwise_and(mask, bit) != 0, turned, value)
        bit *= 2
    return value


def pad_cols(value, width):
    return jnp.pad(value, ((0, 0), (0, width - value.shape[1])))


def per_device(
    tokens,
    cotangent,
    image_mask,
    norm_gains,
    norm_shifts,
    w_qkv,
    b_qv,
    w_out,
    w_up,
    up_bias,
    w_down,
    *,
    dp,
    tx,
):
    grid = Grid3(dp, tx)
    y_n, z_n = grid.y, grid.z
    core = lax.axis_index("core").astype(jnp.int32)
    me_d = lax.axis_index("dp").astype(jnp.int32)
    me_x = lax.axis_index("tx").astype(jnp.int32)
    seq, width = tokens.shape
    _, bd, hw = w_qkv.shape
    fw = w_up.shape[1]
    ext, hid = tx * hw, tx * fw
    hh, fh = hw // 2, fw // 2
    aligned = bd % 128 == 0 and hh % 128 == 0 and fh % 128 == 0
    rel = [kz * y_n + ky for ky in range(y_n) for kz in range(z_n)]

    def from_abs(value, axis):
        shape = value.shape
        value = value.reshape(shape[:axis] + (z_n, y_n) + shape[axis + 1 :])
        return jnp.swapaxes(value, axis, axis + 1).reshape(shape)

    def to_rel(value, axis):
        shape = value.shape
        value = value.reshape(shape[:axis] + (y_n, z_n) + shape[axis + 1 :])
        return jnp.swapaxes(value, axis, axis + 1).reshape(shape)

    ids = jnp.stack([core, me_d] + [jnp.bitwise_xor(me_d, k) for k in rel])
    keep = lax.dynamic_slice(image_mask, (2 * me_x,), (2,)).astype(F32)

    lane = max(bd, hh)
    small = jnp.concatenate(
        [
            pad_cols(norm_gains, lane),
            pad_cols(norm_shifts, lane),
            pad_cols(b_qv, lane),
            pad_cols(up_bias[None], lane),
            jnp.zeros((7, lane), BF),
        ]
    )
    qkv_a = pad_cols(w_qkv[:, :, :hh].reshape(3 * bd, hh), lane)
    qkv_b = pad_cols(w_qkv[:, :, hh:].reshape(3 * bd, hh), lane)
    first_a = jnp.concatenate([qkv_a, pad_cols(w_out[:hh], lane)])
    first_b = jnp.concatenate([qkv_b, pad_cols(w_out[hh:], lane)])
    tok_other, cot_other = swap_core(tokens), swap_core(cotangent)
    if aligned:
        tok, cot = arrange_pair(ids, [tokens, cotangent], [tok_other, cot_other], dp)
    else:

        def arrange(own, other):
            pair = jnp.where(core == 0, jnp.stack([own, other]), jnp.stack([other, own]))
            pair = xor_blocks(pair.reshape(2, seq, dp, bd), me_d, 2)
            return from_abs(pair, 2).reshape(2, seq, width)

        tok, cot = arrange(tokens, tok_other), arrange(cotangent, cot_other)
    c1_z = gather_z(grid, first_a, first_b, gate=tok)
    small = jnp.stack([small] + [grid.send_z(small, k) for k in range(1, z_n)])
    small = jnp.concatenate([small] + [grid.send_y(small, k) for k in range(1, y_n)])
    small = [small] + [grid.send_x(small, k) for k in range(1, tx)]
    up_halves = after((w_up[:, :fh], w_up[:, fh:]), c1_z)
    c1_h = gather_first(grid, *c1_z)
    c1a, c1b = gather_last(grid, *c1_h)
    up_z = gather_z(grid, *up_halves, gate=(c1a, c1b))
    dn_halves = after((w_down[:fh], w_down[fh:]), (c1a, c1b))
    up_h = gather_first(grid, *up_z)

    grad_top = cot * keep.astype(BF)[:, None, None]

    nv = small[0][:, :6, :bd].transpose(1, 0, 2).reshape(6, width).astype(F32)
    tail = jnp.stack([v[:, 6:9] for v in small])
    tail = xor_blocks(to_rel(tail, 1), me_d, 1)
    bq = (
        tail[:, :, :2, : hw // dp].transpose(2, 0, 1, 3).reshape(2, ext).astype(F32)
    )
    bu = tail[:, :, 2, : fw // dp].reshape(1, hid).astype(F32)

    if aligned:
        every, wq_plan, wo_plan, up_plan, dn_plan = slice(None), [[], [], []], [], [], []
        for kx in range(tx):
            halves = [slice(kx * hw, kx * hw + hh), slice(kx * hw + hh, (kx + 1) * hw)]
            f_halves = [slice(kx * fw, kx * fw + fh), slice(kx * fw + fh, (kx + 1) * fw)]
            own = slice(kx * z_n, (kx + 1) * z_n)
            for i in range(3):
                src = slice(i * bd, (i + 1) * bd)
                wq_plan[i].append((kx, (every, src), (i, every, every, halves[0])))
                for ky in range(y_n):
                    dst = (i, slice(ky * z_n, (ky + 1) * z_n), every, halves[1])
                    wq_plan[i].append((tx + ky, (own, src), dst))
            src = slice(3 * bd, 3 * bd + hh)
            dn_plan += [[], []]
            for ky in range(y_n):
                for kz in range(z_n):
                    p, r = ky * z_n + kz, kx * z_n + kz
                    cols = slice(p * bd, (p + 1) * bd)
                    wo_plan.append((kx, (p, src), (halves[0], cols)))
                    wo_plan.append((tx + ky, (r, src), (halves[1], cols)))
                    dn_plan[-2].append((kx, (p,), (f_halves[0], cols)))
                    dn_plan[-1].append((tx + ky, (r,), (f_halves[1], cols)))
            up_plan += [[(kx, (every,), (every, f_halves[0]))], []]
            for ky in range(y_n):
                rows = slice(kx * z_n * bd, (kx + 1) * z_n * bd)
                dst = (slice(ky * z_n * bd, (ky + 1) * z_n * bd), f_halves[1])
                up_plan[-1].append((tx + ky, (rows,), dst))
        c1 = c1a + c1b
        wqkv = (c1, wq_plan, (3, dp, bd, ext))
        wout = (c1, [wo_plan], (ext, width))
    else:

        def whole(a_all, b_all):
            a = jnp.stack(a_all)
            b = jnp.stack(b_all).reshape((y_n, tx, z_n) + b_all[0].shape[1:])
            b = b.transpose(1, 0, 2, 3, 4).reshape(a.shape[:2] + b.shape[3:])
            return jnp.stack([a, b], axis=1)

        c1 = whole(c1a, c1b)
        qkv = c1[:, :, :, : 3 * bd, :hh].reshape(tx, 2, dp, 3, bd, hh)
        qkv = qkv.transpose(3, 2, 4, 0, 1, 5).reshape(3, dp, bd, ext)
        out = c1[:, :, :, 3 * bd :, :bd].transpose(0, 1, 3, 2, 4).reshape(ext, width)
        all_of = [[(0, (slice(None),), (slice(None),))]]
        wqkv = ([qkv], all_of, qkv.shape)
        wout = ([out], all_of, out.shape)

    rows2 = 2 * seq

    res = attn_forward(0, after(tok, up_z), nv, bq, wqkv, wout, None)
    parts = [(res[5], swap_core(res[5]))]
    upa, upb = gather_last(grid, *after(up_h, res[5]))
    dn_z = gather_z(grid, *dn_halves, gate=res[5])
    dn_h = gather_first(grid, *dn_z)
    res = attn_forward(1, after(tok, dn_z), nv, bq, wqkv, wout, res[:5])
    parts.append((res[5], swap_core(res[5])))
    first, q, k, v, att = res[:5]
    upa, upb = after((upa, upb), res[5])
    dna, dnb = gather_last(grid, *after(dn_h, (upa, upb)))
    if aligned:
        wup = ([v.reshape(-1, fh) for v in upa + upb], up_plan, (width, hid))
        wdown = (dna + dnb, dn_plan, (hid, width))
    else:
        up_w = whole(upa, upb).transpose(2, 3, 0, 1, 4).reshape(width, hid)
        down_w = whole(dna, dnb).transpose(0, 1, 3, 2, 4).reshape(hid, width)
        wup = ([up_w], all_of, up_w.shape)
        wdown = ([down_w], all_of, down_w.shape)
    state = None
    for image in range(2):
        part, recv = parts[image]
        state = mlp_up(image, tok, part, recv, keep, nv, bu, wup, fh, state)
    middle, second, act, dact = state
    flat = lambda value: value.reshape(rows2, value.shape[2])
    act2, sec2, grad2 = flat(act), flat(second), flat(grad_top)

    order_x, order_y = list(range(1, tx)) + [0], list(range(1, y_n)) + [0]
    d_all = slice(0, width)
    d_half = [slice(ky * z_n * bd, (ky + 1) * z_n * bd) for ky in range(y_n)]

    def spots(ky, kx):
        if ky is None:
            return [(order_x.index(kx), p, slice(p * bd, (p + 1) * bd)) for p in range(dp)]
        which = tx + order_y.index(ky)
        return [(which, kx * z_n + kz, slice(kz * bd, (kz + 1) * bd)) for kz in range(z_n)]

    def cut(kx, size, ky):
        start = kx * size + (0 if ky is None else size // 2)
        return slice(start, start + size // 2)

    def visits():
        for kx in order_x:
            yield None, kx, d_all
        for ky in order_y:
            for kx in range(tx):
                yield ky, kx, d_half[ky]

    full = slice(None)

    def by_left(l_index, r_index, size, row0):
        rows = slice(row0, row0 + size // 2)
        return [
            (
                l_index,
                cut(kx, size, ky),
                r_index,
                d_cols,
                [(w, (spot, rows), full, cols) for w, spot, cols in spots(ky, kx)],
            )
            for ky, kx, d_cols in visits()
        ]

    def by_right(l_index, r_index, size, row0, lanes):
        tasks = []
        for ky, kx, d_cols in visits():
            stores = []
            for j in range(size // 2 // lanes):
                rows = slice(row0 + j * bd, row0 + (j + 1) * bd)
                cols = slice(j * lanes, (j + 1) * lanes)
                stores += [(w, (spot, rows), r_sl, cols) for w, spot, r_sl in spots(ky, kx)]
            tasks.append((l_index, d_cols, r_index, cut(kx, size, ky), stores))
        return tasks

    def start_grad(lefts, rights, makers, rows, lanes, name):
        tasks = []
        for group in zip(*makers):
            tasks += group
        shapes = [(dp, rows, lanes)] * tx + [(tx * z_n, rows, lanes)] * y_n
        parts = weight_grad(lefts, rights, tasks, shapes, name)
        by_x, by_y = list(parts[:tx]), list(parts[tx:])
        return Scatter(grid, by_x[-1:] + by_x[:-1], by_y[-1:] + by_y[:-1]), parts[-1]

    down_rs, gate = start_grad([act2], [grad2], [by_left(0, 0, fw, 0)], fh, bd, "down_grad")
    grad_in = after(grad2, gate)
    low_pre, bias_up, two_part, mlp_part = mlp_back(grad_in, act2, flat(dact), wdown, wup, fh)
    two_part = two_part.reshape(2, seq, width)
    mlp_part = mlp_part.reshape(2, seq, width)
    mlp_recv = swap_core(mlp_part)
    two_recvs = [swap_core(two_part[a]) for a in range(2)]
    down_half = down_rs.second(bias_up)
    gmid, gattn, grad_att, col = middle_back(
        ids, middle, two_part, after(two_recvs, down_half), cot, keep, nv, wout
    )
    down_zs = down_rs.along_z(col)
    up_rows = fh // bd * bd
    up_rs, gate = start_grad(
        [sec2, flat(att)],
        [low_pre, after(flat(gattn), down_zs)],
        [by_right(0, 0, fw, 0, bd), by_left(1, 1, hw, up_rows)],
        up_rows + hh,
        bd,
        "up_out_grad",
    )

    down_a, down_b = down_rs.finish(gate)
    res = attn_backward(0, after(grad_att, (gate, down_a)), q, k, v, None)
    bias_qv = res[3]
    up_half = up_rs.second(bias_qv)
    res = attn_backward(1, after(grad_att, up_half), q, k, v, res[:3])
    bias_qv = bias_qv + res[3]
    up_zs = up_rs.along_z(res[3])
    low_proj = [flat(value) for value in res[:3]]
    makers = [by_right(0, i, hw, i * bd, hh) for i in range(3)]
    first_in = after(flat(first), up_zs)
    qkv_rs, gate = start_grad([first_in], low_proj, makers, 3 * bd, hh, "qkv_grad")
    low_in = after(low_proj, gate)
    one_part = rows_times(low_in, (0, rows2), wqkv, NT, True, width, "grad_one")
    one_part = one_part.reshape(2, seq, width)
    one_recvs = [swap_core(one_part[a]) for a in range(2)]
    up_a, up_b = up_rs.finish(one_part)
    qkv_half = qkv_rs.second(up_a)
    layer_out = finish_layer(
        ids, keep, nv, middle, after(mlp_part, qkv_half), mlp_recv, dp, aligned
    )
    grad_tokens, one_sums = finish_tokens(
        ids, nv, tok, one_part, after(one_recvs, layer_out), gmid, dp, aligned
    )
    qkv_rs.along_z(one_sums)
    qkv_ga, qkv_gb = qkv_rs.finish(one_sums)
    out_a, out_b = up_a[up_rows:], up_b[up_rows:]

    def lanes_back(value):
        value = value[:up_rows].reshape(fh // bd, bd, bd)
        return value.transpose(1, 0, 2).reshape(bd, fh)

    up_a, up_b = lanes_back(up_a), lanes_back(up_b)
    if not aligned:

        def restore(value):
            value = xor_blocks(to_rel(value.reshape(seq, dp, bd), 1), me_d, 1)
            return value.reshape(seq, width)

        layer_out, grad_tokens = restore(layer_out), restore(grad_tokens)

    vec = jnp.stack([one_sums[0], col[0], one_sums[1], col[1], col[2], col[3]])
    wide = max(bd, hw // dp, fw // dp)
    vec = vec.reshape(6, dp, bd).transpose(1, 0, 2)
    vec = jnp.pad(vec, ((0, 0), (0, 0), (0, wide - bd)))
    bias_qv = bias_qv.reshape(2, tx, dp, hw // dp).transpose(2, 1, 0, 3).reshape(dp, 2 * tx, -1)
    bias_up = bias_up.reshape(tx, dp, fw // dp).transpose(1, 0, 2)
    bias = jnp.concatenate(
        [
            jnp.pad(bias_qv, ((0, 0), (0, 0), (0, wide - hw // dp))),
            jnp.pad(bias_up, ((0, 0), (0, 0), (0, wide - fw // dp))),
        ],
        axis=1,
    )
    bias = from_abs(xor_blocks(bias, me_d, 0), 0)
    both = jnp.concatenate([vec, bias], axis=1)
    got = [both] + [grid.send_x(both, k) for k in range(1, tx)]
    vec = sum(value[:, :6] for value in got)
    bqv_mine = sum(value[:, 6 + 2 * k : 8 + 2 * k] for k, value in enumerate(got))
    bup_mine = sum(
        value[:, 6 + 2 * tx + k : 7 + 2 * tx + k] for k, value in enumerate(got)
    )
    both = jnp.concatenate([vec, bqv_mine, bup_mine], axis=1)
    both = both[:z_n] + sum(
        grid.send_y(both[k * z_n : (k + 1) * z_n], k) for k in range(1, y_n)
    )
    both = both[0] + sum(grid.send_z(both[k], k) for k in range(1, z_n))
    share = bd // (2 * tx)
    mine = lax.dynamic_slice(both[:6, :bd], (0, (2 * me_x + core) * share), (6, share))

    grad_qkv = jnp.concatenate(
        [qkv_ga.reshape(3, bd, hh), qkv_gb.reshape(3, bd, hh)], axis=2
    )
    grad_out = jnp.concatenate([out_a, out_b], axis=0)
    grad_up = jnp.concatenate([up_a, up_b], axis=1)
    grad_down = jnp.concatenate([down_a, down_b], axis=0)
    return (
        layer_out,
        grad_tokens,
        mine[:2],
        mine[2:6],
        grad_qkv,
        both[6:8, : hw // dp],
        grad_out,
        grad_up,
        both[8, : fw // dp],
        grad_down,
    )


def solution(mesh):
    dp, tensor = mesh.shape["dp"], mesh.shape["tensor"]
    split = Mesh(mesh.devices.reshape(dp, tensor // 2, 2), ("dp", "tx", "core"))
    every = ("dp", "tx", "core")
    tensor_axes = ("tx", "core")
    in_specs = (
        P(every, None),
        P(every, None),
        P("dp"),
        P(None, "dp"),
        P(None, "dp"),
        P(None, "dp", tensor_axes),
        P(None, ("tx", "core", "dp")),
        P(tensor_axes, "dp"),
        P("dp", tensor_axes),
        P(("tx", "core", "dp")),
        P(tensor_axes, "dp"),
    )
    out_specs = (
        P(every, None),
        P(every, None),
        P(None, every),
        P(None, every),
        P(None, "dp", tensor_axes),
        P(None, ("tx", "core", "dp")),
        P(tensor_axes, "dp"),
        P("dp", tensor_axes),
        P(("tx", "core", "dp")),
        P(tensor_axes, "dp"),
    )
    return jax.shard_map(
        functools.partial(per_device, dp=dp, tx=tensor // 2),
        mesh=split,
        in_specs=in_specs,
        out_specs=out_specs,
        check_vma=False,
    )
```

```python
import functools

import jax
import jax.numpy as jnp
from jax import lax
from jax.experimental import pallas as pl
from jax.experimental.pallas import tpu as pltpu
from jax.sharding import Mesh, PartitionSpec as P

HEAD_DIM = 64
VALID = 577
SEQ = 584
BF = jnp.bfloat16
F32 = jnp.float32
VMEM_LIMIT = 60 * 1024 * 1024
COST_SCALE = 1.0
COST = {
    "arrange_pair": 5,
    "vectors": 3,
    "attn_forward": 16,
    "mlp_up": 10,
    "down_grad": 11,
    "mlp_back": 22,
    "up_grad": 11,
    "middle_back": 12,
    "out_grad": 5,
    "attn_backward": 18,
    "qkv_grad": 9,
    "grad_one": 2,
    "qkv_add": 30,
    "finish_layer": 30,
    "finish_tokens": 9,
}
NT = (((1,), (1,)), ((), ()))
TN = (((0,), (0,)), ((), ()))
NN = (((1,), (0,)), ((), ()))


def dot(left, right, dims):
    return lax.dot_general(left, right, dims, preferred_element_type=F32)


class Loads:
    def __init__(self, sems):
        self.sems, self.groups = sems, []

    def start(self, pairs):
        sem = self.sems.at[len(self.groups)]
        copies = [pltpu.make_async_copy(src, dst, sem) for src, dst in pairs]
        for copy in copies:
            copy.start()
        self.groups.append(copies)
        return len(self.groups) - 1

    def wait(self, group):
        for copy in self.groups[group]:
            copy.wait()


def call(body, ins, outs, scratch, name, flops, aliases=None, smem=(), sems=48, vmem_ins=(), hidden=False):
    n_smem, n_vmem, n_in, n_out = len(smem), len(vmem_ins), len(ins), len(outs)
    moved = sum(a.size * a.dtype.itemsize for a in ins) + sum(
        o.size * o.dtype.itemsize for o in outs
    )

    def kernel(*refs):
        first = n_smem + n_vmem
        small = refs[:first]
        in_refs = refs[first : first + n_in]
        out_refs = refs[first + n_in : first + n_in + n_out]
        rest = refs[first + n_in + n_out :]
        body(small, in_refs, out_refs, rest[:-1], Loads(rest[-1]))

    flops = COST.get(name, 3) * COST_SCALE * 1.15e9
    moved = 0
    any_spec = pl.BlockSpec(memory_space=pl.ANY)
    return pl.pallas_call(
        kernel,
        out_shape=outs,
        in_specs=[pl.BlockSpec(memory_space=pltpu.SMEM)] * n_smem
        + [pl.BlockSpec(memory_space=pltpu.VMEM)] * n_vmem
        + [any_spec] * n_in,
        out_specs=[any_spec] * n_out,
        scratch_shapes=list(scratch) + [pltpu.SemaphoreType.DMA((sems,))],
        input_output_aliases={n_smem + n_vmem + i: o for i, o in (aliases or {}).items()},
        compiler_params=pltpu.CompilerParams(vmem_limit_bytes=VMEM_LIMIT),
        cost_estimate=pl.CostEstimate(flops=int(flops), bytes_accessed=int(moved), transcendentals=0),
        name=name,
    )(*smem, *vmem_ins, *ins)


def norm_parts(rows):
    center = rows - jnp.mean(rows, axis=1, keepdims=True)
    inverse = lax.rsqrt(jnp.mean(center * center, axis=1, keepdims=True) + 1e-05)
    return center * inverse, inverse


def norm_back(grad_norm, scaled, inverse, gain_row):
    grad_hat = grad_norm * gain_row
    first_mean = jnp.mean(grad_hat, axis=1, keepdims=True)
    second_mean = jnp.mean(grad_hat * scaled, axis=1, keepdims=True)
    return inverse * (grad_hat - first_mean - scaled * second_mean)


def sds(shape, dtype):
    return jax.ShapeDtypeStruct(shape, dtype)


def arrange_pair(ids, own, other, nd):
    n = len(own)
    rows, width = own[0].shape
    bd = width // nd

    def body(small, ins, outs, scratch, loads):
        (ids_ref,) = small
        mine = ids_ref[0]
        in_s, out_s = scratch[: 2 * n], scratch[2 * n :]
        groups = [loads.start([(ins[i], in_s[i])]) for i in range(2 * n)]
        done = []
        for i in range(2 * n):
            loads.wait(groups[i])
            for p in range(nd):
                src = pl.ds(pl.multiple_of(ids_ref[2 + p] * bd, 128), bd)
                out_s[i][:, p * bd : (p + 1) * bd] = in_s[i][:, src]
            spot = mine if i < n else 1 - mine
            done.append(loads.start([(out_s[i], outs[i % n].at[spot])]))
        for group in done:
            loads.wait(group)

    return call(
        body,
        list(own) + list(other),
        [sds((2, rows, width), BF)] * n,
        [pltpu.VMEM((rows, width), BF)] * (4 * n),
        "arrange_pair",
        0,
        smem=(ids,),
    )


def vectors(ids, gathered, row0, nd, y_n, bd, qv, up):
    tx, z_n = len(gathered), nd // y_n

    def body(small, ins, outs, scratch, loads):
        ids_ref, rows_s, nv_s, bq_s, bu_s = small[0], *scratch
        rows = pl.ds(row0, 16)
        loads.wait(loads.start([(ins[k].at[:, rows, :], rows_s.at[k]) for k in range(tx)]))
        for p in range(nd):
            nv_s[:, p * bd : (p + 1) * bd] = rows_s[0, p].astype(F32)[:6, :bd]
        for k in range(tx):
            pieces = []
            for d in range(nd):
                rel = ids_ref[1] ^ d
                spot = (rel % y_n) * z_n + rel // y_n
                piece = rows_s[k, spot].astype(F32)
                bu_s[:, (k * nd + d) * up : (k * nd + d + 1) * up] = piece[8:9, :up]
                pieces.append(piece[6:8, :])
            each = 128 // qv
            for start in range(0, nd, each):
                total = pieces[start]
                for i in range(1, each):
                    total = total + pltpu.roll(pieces[start + i], i * qv, 1)
                bq_s[:, (k * nd + start) * qv : (k * nd + start + each) * qv] = total
        loads.wait(loads.start([(nv_s, outs[0]), (bq_s, outs[1]), (bu_s, outs[2])]))

    shapes = [(6, nd * bd), (2, tx * nd * qv), (1, tx * nd * up)]
    return call(
        body,
        list(gathered),
        [sds(s, F32) for s in shapes],
        [pltpu.VMEM((tx, nd, 16, gathered[0].shape[2]), BF)] + [pltpu.VMEM(s, F32) for s in shapes],
        "vectors",
        0,
        smem=(ids,),
    )


def block_stores(ids_ref, src, dst, nd, aligned):
    if not aligned:
        return [(src, dst)]
    bd = src.shape[1] // nd
    pairs = []
    for p in range(nd):
        cols = pl.ds(pl.multiple_of(ids_ref[2 + p] * bd, 128), bd)
        pairs.append((src.at[:, p * bd : (p + 1) * bd], dst.at[:, cols]))
    return pairs


def weight_loads(loads, groups, refs, scratch):
    return [
        loads.start([(refs[a].at[src], scratch.at[dst]) for a, src, dst in plan])
        for plan in groups
    ]


def softmax_rows(q2, k2):
    scores = dot(q2, k2, NT)
    lane = lax.broadcasted_iota(jnp.int32, scores.shape, 1)
    scores = jnp.where(lane < VALID, scores, -1e30)
    e = jnp.exp(scores - jnp.max(scores, axis=1, keepdims=True))
    return e * (1.0 / jnp.sum(e, axis=1, keepdims=True))


def attn_forward(image, tok, nv, bq, wqkv, wout, prev):
    seq, width = tok.shape[1:]
    qkv_arrays, qkv_plan, qkv_scratch = wqkv
    out_arrays, out_plan, out_scratch = wout
    ext = qkv_scratch[-1]
    n_prev = 0 if prev is None else len(prev)
    nq, no = len(qkv_arrays), len(out_arrays)

    def body(small, ins, outs, scratch, loads):
        nv_ref, bq_ref = small
        tok_ref, ins = ins[0], ins[1 + n_prev :]
        w_s, wo_s, tok_s, first_s, q_s, k_s, v_s, att_s, part_s = scratch
        g_tok = loads.start([(tok_ref.at[image], tok_s)])
        g_w = weight_loads(loads, qkv_plan, ins[:nq], w_s)
        g_o = weight_loads(loads, out_plan, ins[nq:], wo_s)
        loads.wait(g_tok)
        hat, _ = norm_parts(tok_s[...].astype(F32))
        first_s[...] = (hat * nv_ref[0:1, :] + nv_ref[2:3, :]).astype(BF)
        g_first = loads.start([(first_s, outs[0].at[image])])
        low = first_s[...]
        for i, ref in enumerate((q_s, k_s, v_s)):
            if i < len(g_w):
                loads.wait(g_w[i])
            proj = dot(low, w_s[i].reshape(width, ext), NN)
            if i == 0:
                proj = proj + bq_ref[0:1, :]
            if i == 2:
                proj = proj + bq_ref[1:2, :]
            low_proj = proj.astype(BF)
            if i == 0:
                low_proj = low_proj * jnp.asarray(HEAD_DIM**-0.5, BF)
            ref[...] = low_proj
        g_qkv = loads.start(
            [(q_s, outs[1].at[image]), (k_s, outs[2].at[image]), (v_s, outs[3].at[image])]
        )
        half = lax.broadcasted_iota(jnp.int32, (1, 128), 1) // HEAD_DIM

        def pair(i, carry):
            cols = pl.ds(pl.multiple_of(i * 128, 128), 128)
            q2, k2, v2 = q_s[:, cols], k_s[:, cols], v_s[:, cols]
            total = None
            for h in range(2):
                keep = (half == h).astype(BF)
                probs = softmax_rows(q2, k2 * keep).astype(BF)
                piece = dot(probs, v2 * keep, NN)
                total = piece if total is None else total + piece
            att_s[:, cols] = total.astype(BF)
            return carry

        lax.fori_loop(0, ext // 128, pair, 0)
        g_att = loads.start([(att_s, outs[4].at[image])])
        loads.wait(g_o[0])
        part_s[...] = dot(att_s[...], wo_s[...], NN).astype(BF)
        g_part = loads.start([(part_s, outs[5])])
        for group in (g_first, g_qkv, g_att, g_part):
            loads.wait(group)

    shapes = [(2, seq, width)] + [(2, seq, ext)] * 4
    return call(
        body,
        [tok] + list(prev or []) + qkv_arrays + out_arrays,
        [sds(s, BF) for s in shapes] + [sds((seq, width), BF)],
        [
            pltpu.VMEM(qkv_scratch, BF),
            pltpu.VMEM(out_scratch, BF),
            pltpu.VMEM((seq, width), BF),
            pltpu.VMEM((seq, width), BF),
            pltpu.VMEM((seq, ext), BF),
            pltpu.VMEM((seq, ext), BF),
            pltpu.VMEM((seq, ext), BF),
            pltpu.VMEM((seq, ext), BF),
            pltpu.VMEM((seq, width), BF),
        ],
        "attn_forward",
        2 * seq * width * ext * 4 + 16 * seq * seq * ext,
        aliases={1 + i: i for i in range(n_prev)},
        vmem_ins=(nv, bq),
    )


def mlp_up(image, tok, part, recv, keep, nv, bu, wup, step, prev):
    seq, width = tok.shape[1:]
    up_arrays, up_plan, up_scratch = wup
    hid = up_scratch[-1]
    n_prev = 0 if prev is None else len(prev)

    def body(small, ins, outs, scratch, loads):
        keep_ref, nv_ref, bu_ref = small
        tok_ref, part_ref, recv_ref = ins[:3]
        w_s, tok_s, part_s, recv_s, mid_s, sec_s, act_s, dact_s = scratch
        g_in = loads.start([(tok_ref.at[image], tok_s), (part_ref, part_s), (recv_ref, recv_s)])
        g_w = weight_loads(loads, up_plan, ins[3 + n_prev :], w_s)
        loads.wait(g_in)
        total = part_s[...].astype(F32) + recv_s[...].astype(F32) + nv_ref[4:5, :]
        middle = tok_s[...].astype(F32) + keep_ref[image] * total
        mid_s[...] = middle
        hat, _ = norm_parts(middle)
        sec_s[...] = (hat * nv_ref[1:2, :] + nv_ref[3:4, :]).astype(BF)
        g_mid = loads.start([(mid_s, outs[0].at[image]), (sec_s, outs[1].at[image])])
        second = sec_s[...]
        done = []
        for block in range(hid // step):
            if block < len(g_w):
                loads.wait(g_w[block])
            cols = slice(block * step, (block + 1) * step)
            pre = dot(second, w_s[:, cols], NN) + bu_ref[0:1, cols]
            gate = 1.0 / (1.0 + jnp.exp(-1.702 * pre))
            act_s[:, cols] = (pre * gate).astype(BF)
            dact_s[:, cols] = (gate + 1.702 * pre * gate * (1.0 - gate)).astype(BF)
            done.append(
                loads.start(
                    [
                        (act_s.at[:, cols], outs[2].at[image, :, cols]),
                        (dact_s.at[:, cols], outs[3].at[image, :, cols]),
                    ]
                )
            )
        for group in [g_mid] + done:
            loads.wait(group)

    outs = [
        sds((2, seq, width), F32),
        sds((2, seq, width), BF),
        sds((2, seq, hid), BF),
        sds((2, seq, hid), BF),
    ]
    return call(
        body,
        [tok, part, recv] + list(prev or []) + up_arrays,
        outs,
        [
            pltpu.VMEM(up_scratch, BF),
            pltpu.VMEM((seq, width), BF),
            pltpu.VMEM((seq, width), BF),
            pltpu.VMEM((seq, width), BF),
            pltpu.VMEM((seq, width), F32),
            pltpu.VMEM((seq, width), BF),
            pltpu.VMEM((seq, hid), BF),
            pltpu.VMEM((seq, hid), BF),
        ],
        "mlp_up",
        2 * seq * width * hid,
        aliases={3 + i: i for i in range(n_prev)},
        smem=(keep,),
        vmem_ins=(nv, bu),
    )


def weight_grad(lefts, rights, tasks, out_shapes, name, lo, hi, prev=None):
    rows = lefts[0].shape[0]
    arrays = list(lefts) + list(rights)
    n_left, n_in = len(lefts), len(arrays)
    prev = list(prev or [])
    last = {}
    for n, task in enumerate(tasks):
        for store in task[4]:
            last[store[0]] = n

    def body(small, ins, outs, scratch, loads):
        in_s, out_s = scratch[:n_in], scratch[n_in:]
        order = []
        for l_index, _, r_index, _, _ in tasks:
            for i in (l_index, n_left + r_index):
                if i not in order:
                    order.append(i)
        groups = {i: loads.start([(ins[i], in_s[i])]) for i in order}
        ready, done = set(), []
        for n, (l_index, l_cols, r_index, r_cols, stores) in enumerate(tasks):
            for i in (l_index, n_left + r_index):
                if i not in ready:
                    loads.wait(groups[i])
                    ready.add(i)
            left, right = in_s[l_index][:, l_cols], in_s[n_left + r_index][:, r_cols]
            value = dot(left, right, TN).astype(BF)
            for which, spot, r_sl, c_sl in stores:
                out_s[which][spot] = value[r_sl, c_sl]
            for which in sorted(w for w in last if last[w] == n):
                done.append(loads.start([(out_s[which], outs[which].at[:, lo:hi])]))
        for group in done:
            loads.wait(group)

    flops = sum(
        2 * rows * (t[1].stop - t[1].start) * (t[3].stop - t[3].start) for t in tasks
    )
    return call(
        body,
        arrays + prev,
        [sds(s, BF) for s in out_shapes],
        [pltpu.VMEM(a.shape, BF) for a in arrays]
        + [pltpu.VMEM((s[0], hi - lo, s[2]), BF) for s in out_shapes],
        name,
        flops,
        aliases={n_in + i: i for i in range(len(prev))},
    )


def mlp_back(grad, act, dact, wdown, wup, step):
    rows, width = grad.shape
    seq = rows // 2
    hid = dact.shape[1]
    down_arrays, down_plan, down_scratch = wdown
    up_arrays, up_plan, up_scratch = wup
    n_down = len(down_arrays)

    def body(small, ins, outs, scratch, loads):
        wd_s, wu_s, g_s, a_s, d_s, low_s, sum_s, two_s, mlp_s = scratch
        g_g = loads.start([(ins[0], g_s)])
        g_wd = weight_loads(loads, down_plan, ins[3 : 3 + n_down], wd_s)
        g_d = []
        for block in range(hid // step):
            cols = slice(block * step, (block + 1) * step)
            g_d.append(loads.start([(ins[2].at[:, cols], d_s.at[:, cols])]))
        g_wu = weight_loads(loads, up_plan, ins[3 + n_down :], wu_s)
        g_a = loads.start([(ins[1], a_s)])
        loads.wait(g_g)
        left = g_s[...]
        done = []
        for block in range(hid // step):
            if block < len(g_wd):
                loads.wait(g_wd[block])
            loads.wait(g_d[block])
            cols = slice(block * step, (block + 1) * step)
            pre = dot(left, wd_s[cols, :], NT) * d_s[:, cols].astype(F32)
            low_s[:, cols] = pre.astype(BF)
            sum_s[0:1, cols] = jnp.sum(pre, axis=0, keepdims=True)
            done.append(loads.start([(low_s.at[:, cols], outs[0].at[:, cols])]))
        done.append(loads.start([(sum_s, outs[1])]))
        for group in g_wu:
            loads.wait(group)
        two = dot(low_s[...], wu_s[...], NT)
        for a in range(2):
            two_s[a] = two[a * seq : (a + 1) * seq].astype(BF)
            done.append(loads.start([(two_s.at[a], outs[2 + a])]))
        loads.wait(g_a)
        mlp_s[...] = dot(a_s[...], wd_s[...], NN).astype(BF)
        done.append(loads.start([(mlp_s, outs[4])]))
        for group in done:
            loads.wait(group)

    return call(
        body,
        [grad, act, dact] + down_arrays + up_arrays,
        [sds((rows, hid), BF), sds((1, hid), F32)]
        + [sds((seq, width), BF)] * 2
        + [sds((rows, width), BF)],
        [
            pltpu.VMEM(down_scratch, BF),
            pltpu.VMEM(up_scratch, BF),
            pltpu.VMEM((rows, width), BF),
            pltpu.VMEM((rows, hid), BF),
            pltpu.VMEM((rows, hid), BF),
            pltpu.VMEM((rows, hid), BF),
            pltpu.VMEM((1, hid), F32),
            pltpu.VMEM((2, seq, width), BF),
            pltpu.VMEM((rows, width), BF),
        ],
        "mlp_back",
        6 * rows * width * hid,
        sems=64,
    )


def input_grad(lefts, weight, width):
    arrays, plan, shape = weight
    rows, ext = lefts[0].shape
    seq = rows // 2
    n = len(lefts)

    def body(small, ins, outs, scratch, loads):
        w_s, out_s = scratch[0], scratch[1]
        l_s = scratch[2:]
        g_w = weight_loads(loads, plan[:1], ins[n:], w_s)
        g_l = [loads.start([(ins[i], l_s[i])]) for i in range(n)]
        g_w += weight_loads(loads, plan[1:], ins[n:], w_s)
        total = None
        for i in range(n):
            loads.wait(g_l[i])
            if i < len(g_w):
                loads.wait(g_w[i])
            piece = dot(l_s[i][...], w_s[i].reshape(width, ext), NT)
            total = piece if total is None else total + piece
        done = []
        for a in range(2):
            out_s[a] = total[a * seq : (a + 1) * seq].astype(BF)
            done.append(loads.start([(out_s.at[a], outs[a])]))
        for group in done:
            loads.wait(group)

    return call(
        body,
        list(lefts) + arrays,
        [sds((seq, width), BF)] * 2,
        [pltpu.VMEM(shape, BF), pltpu.VMEM((2, seq, width), BF)] + [pltpu.VMEM((rows, ext), BF)] * n,
        "grad_one",
        2 * rows * width * ext * n,
    )


def middle_back(ids, middle, parts, recvs, cot, keep, nv, wout):
    _, seq, width = middle.shape
    out_arrays, out_plan, out_scratch = wout
    ext = out_scratch[0]

    def body(small, ins, outs, scratch, loads):
        ids_ref, keep_ref, nv_ref = small
        mine = ids_ref[0]
        wo_s, mid_s, part_s, recv_s, cot_s, gmid_s, gat_s, do_s = scratch[:8]
        cs_s = scratch[8]
        g_in = [
            loads.start(
                [
                    (ins[0].at[a], mid_s.at[a]),
                    (ins[1].at[a], cot_s.at[a]),
                    (ins[2 + a], part_s.at[a]),
                    (ins[4 + a], recv_s.at[a]),
                ]
            )
            for a in range(2)
        ]
        g_o = weight_loads(loads, out_plan, ins[6:], wo_s)
        done = []
        for a in range(2):
            loads.wait(g_in[a])
            keep_here = keep_ref[a]
            hat, inverse = norm_parts(mid_s[a])
            grad_two = part_s[a].astype(F32) + recv_s[a].astype(F32)
            top = cot_s[a].astype(F32)
            grad_mid = top + norm_back(grad_two, hat, inverse, nv_ref[1:2, :])
            grad_attn = grad_mid * keep_here
            sums = [
                jnp.sum(grad_two * hat, axis=0, keepdims=True),
                jnp.sum(grad_two, axis=0, keepdims=True),
                jnp.sum(grad_attn, axis=0, keepdims=True),
                jnp.sum(top, axis=0, keepdims=True) * keep_here,
            ]
            for i, value in enumerate(sums):
                cs_s[i : i + 1, :] = value if a == 0 else cs_s[i : i + 1, :] + value
            gmid_s[a] = grad_mid
            gat_s[a] = grad_attn.astype(BF)
            done.append(loads.start([(gat_s.at[a], outs[1].at[a])]))
            if a == 0:
                loads.wait(g_o[0])
            do_s[a] = dot(gat_s[a], wo_s[...], NT).astype(BF)
            done.append(loads.start([(do_s.at[a], outs[2].at[a])]))
        done.append(loads.start([(gmid_s.at[mine], outs[0]), (cs_s, outs[3])]))
        for group in done:
            loads.wait(group)

    return call(
        body,
        [middle, cot] + list(parts) + list(recvs) + out_arrays,
        [
            sds((seq, width), F32),
            sds((2, seq, width), BF),
            sds((2, seq, ext), BF),
            sds((4, width), F32),
        ],
        [
            pltpu.VMEM(out_scratch, BF),
            pltpu.VMEM((2, seq, width), F32),
            pltpu.VMEM((2, seq, width), BF),
            pltpu.VMEM((2, seq, width), BF),
            pltpu.VMEM((2, seq, width), BF),
            pltpu.VMEM((2, seq, width), F32),
            pltpu.VMEM((2, seq, width), BF),
            pltpu.VMEM((2, seq, ext), BF),
            pltpu.VMEM((4, width), F32),
        ],
        "middle_back",
        4 * seq * width * ext,
        smem=(ids, keep),
        vmem_ins=(nv,),
    )


def attn_backward(units, grad, q, k, v, prev):
    _, seq, ext = q.shape
    n_prev = 0 if prev is None else len(prev)
    n = len(units)

    def body(small, ins, outs, scratch, loads):
        q_s, k_s, v_s, do_s, dq_s, dk_s, dv_s, bs_s = scratch
        groups = []
        for u, (image, i) in enumerate(units):
            cols = slice(i * 128, (i + 1) * 128)
            groups.append(loads.start([(ins[j].at[image, :, cols], scratch[j].at[u]) for j in range(4)]))
        half = lax.broadcasted_iota(jnp.int32, (1, 128), 1) // HEAD_DIM
        for group in groups:
            loads.wait(group)

        def unit(u, carry):
            q2, k2, v2, do2 = q_s[u], k_s[u], v_s[u], do_s[u]
            dq = dk = dv = None
            for h in range(2):
                mask = (half == h).astype(BF)
                km, qm, dom = k2 * mask, q2 * mask, do2 * mask
                scores = dot(km, q2, NT)
                row = lax.broadcasted_iota(jnp.int32, scores.shape, 0)
                scores = jnp.where(row < VALID, scores, -1e30)
                e = jnp.exp(scores - jnp.max(scores, axis=0, keepdims=True))
                probs = e * (1.0 / jnp.sum(e, axis=0, keepdims=True))
                grad_probs = dot(v2, dom, NT)
                row_dot = jnp.sum(probs * grad_probs, axis=0, keepdims=True)
                grad_scores = (probs * (grad_probs - row_dot)).astype(BF)
                v_piece = dot(probs.astype(BF), dom, NN)
                k_piece = dot(grad_scores, qm, NN)
                q_piece = dot(grad_scores, km, TN)
                dq = q_piece if dq is None else dq + q_piece
                dk = k_piece if dk is None else dk + k_piece
                dv = v_piece if dv is None else dv + v_piece
            dq = dq * HEAD_DIM**-0.5
            bs_s[u, 0:1, :] = jnp.sum(dq, axis=0, keepdims=True)
            bs_s[u, 1:2, :] = jnp.sum(dv, axis=0, keepdims=True)
            dq_s[u] = dq.astype(BF)
            dk_s[u] = dk.astype(BF)
            dv_s[u] = dv.astype(BF)
            return carry

        lax.fori_loop(0, n, unit, 0)
        done = []
        for u, (image, i) in enumerate(units):
            cols = slice(i * 128, (i + 1) * 128)
            done.append(
                loads.start(
                    [(scratch[4 + j].at[u], outs[j].at[image, :, cols]) for j in range(3)]
                )
            )
        done.append(loads.start([(bs_s, outs[3])]))
        for group in done:
            loads.wait(group)

    return call(
        body,
        [q, k, v, grad] + list(prev or []),
        [sds((2, seq, ext), BF)] * 3 + [sds((n, 2, 128), F32)],
        [pltpu.VMEM((n, seq, 128), BF)] * 7 + [pltpu.VMEM((n, 2, 128), F32)],
        "attn_backward",
        10 * n * seq * seq * 128,
        aliases={4 + i: i for i in range(n_prev)},
    )


def finish_layer(ids, keep, nv, middle, part, recv, nd, aligned):
    _, seq, width = middle.shape

    def body(small, ins, outs, scratch, loads):
        ids_ref, keep_ref, nv_ref = small
        mine = ids_ref[0]
        mid_s, part_s, recv_s, out_s = scratch
        groups = [loads.start([(ins[i].at[mine], scratch[i])]) for i in range(3)]
        for group in groups:
            loads.wait(group)
        total = part_s[...].astype(F32) + recv_s[...].astype(F32) + nv_ref[5:6, :]
        out_s[...] = (mid_s[...] + keep_ref[mine] * total).astype(BF)
        loads.wait(loads.start(block_stores(ids_ref, out_s, outs[0], nd, aligned)))

    return call(
        body,
        [middle, part, recv],
        [sds((seq, width), BF)],
        [pltpu.VMEM((seq, width), F32)] + [pltpu.VMEM((seq, width), BF)] * 3,
        "finish_layer",
        100 * seq * width,
        smem=(ids, keep),
        vmem_ins=(nv,),
    )[0]


def finish_tokens(ids, nv, tok, parts, recvs, gmid, rest, nd, aligned):
    _, seq, width = tok.shape
    n_dest, z_n = rest.shape[:2]
    bd = width // nd

    def body(small, ins, outs, scratch, loads):
        ids_ref, nv_ref = small
        mine = ids_ref[0]
        tok_s, part_s, recv_s, gm_s, out_s, cs_s, rest_s = scratch
        g_rest = loads.start([(ins[6], rest_s)])
        groups = [
            loads.start(
                [
                    (ins[0].at[a], tok_s.at[a]),
                    (ins[2 + a], part_s.at[a]),
                    (ins[4 + a], recv_s.at[a]),
                ]
            )
            for a in range(2)
        ]
        g_mid = loads.start([(ins[1], gm_s)])
        for group in groups:
            loads.wait(group)
        done = []
        for i in range(2):
            a = mine if i == 0 else 1 - mine
            hat, inverse = norm_parts(tok_s[a].astype(F32))
            grad_one = part_s[a].astype(F32) + recv_s[a].astype(F32)
            gain_sum = jnp.sum(grad_one * hat, axis=0, keepdims=True)
            shift_sum = jnp.sum(grad_one, axis=0, keepdims=True)
            if i == 0:
                cs_s[0:1, :] = gain_sum
                cs_s[1:2, :] = shift_sum
                loads.wait(g_mid)
                value = gm_s[...] + norm_back(grad_one, hat, inverse, nv_ref[0:1, :])
                out_s[...] = value.astype(BF)
                done.append(loads.start(block_stores(ids_ref, out_s, outs[0], nd, aligned)))
            else:
                cs_s[0:1, :] = cs_s[0:1, :] + gain_sum
                cs_s[1:2, :] = cs_s[1:2, :] + shift_sum
        loads.wait(g_rest)
        for n in range(n_dest if aligned else 0):
            for kz in range(z_n):
                p = n % (nd // z_n) * z_n + kz
                rest_s[n, kz, 0:2, :] = cs_s[:, p * bd : (p + 1) * bd]
        done.append(loads.start([(cs_s, outs[1])]))
        done += [loads.start([(rest_s.at[n], outs[2 + n])]) for n in range(n_dest)]
        for group in done:
            loads.wait(group)

    return call(
        body,
        [tok, gmid] + list(parts) + list(recvs) + [rest],
        [sds((seq, width), BF), sds((2, width), F32)] + [sds(rest.shape[1:], F32)] * n_dest,
        [pltpu.VMEM((2, seq, width), BF)] * 3
        + [pltpu.VMEM((seq, width), F32), pltpu.VMEM((seq, width), BF), pltpu.VMEM((2, width), F32)]
        + [pltpu.VMEM(rest.shape, F32)],
        "finish_tokens",
        200 * seq * width,
        smem=(ids,),
        vmem_ins=(nv,),
    )


class Grid3:
    def __init__(self, dp, tx):
        self.dp, self.tx = dp, tx
        self.y = 2 if dp % 2 == 0 else 1
        self.z = dp // self.y

    def send_z(self, value, k):
        return lax.ppermute(value, "dp", [(i, i ^ (k * self.y)) for i in range(self.dp)])

    def send_y(self, value, k):
        return lax.ppermute(value, "dp", [(i, i ^ k) for i in range(self.dp)])

    def send_xy(self, value, kx, ky):
        count = self.dp * self.tx
        pairs = [(i, ((i // self.tx) ^ ky) * self.tx + ((i % self.tx) ^ kx)) for i in range(count)]
        return lax.ppermute(value, ("dp", "tx"), pairs)

    def send_x(self, value, k):
        return lax.ppermute(value, "tx", [(i, i ^ k) for i in range(self.tx)])


def swap_core(value):
    return lax.ppermute(value, "core", [(0, 1), (1, 0)])


def after(values, gate):
    return lax.optimization_barrier((values, gate))[0]


def gather_z(grid, part_a, part_b, gate=None):
    rows = part_a.shape[0]
    both = jnp.concatenate([part_a, part_b], axis=0)
    all_z = [both] + [grid.send_z(both, k) for k in range(1, grid.z)]
    if gate is not None:
        all_z = after(all_z, gate)
    return jnp.stack([v[:rows] for v in all_z]), jnp.stack([v[rows:] for v in all_z])


def gather_first(grid, a_z, b_z):
    a_y = [a_z] + [grid.send_y(a_z, k) for k in range(1, grid.y)]
    b_x = [b_z] + [grid.send_x(b_z, k) for k in range(1, grid.tx)]
    return a_y, b_x


def join(pieces):
    return [jnp.concatenate(part) for part in pieces]


def gather_last(grid, a_y, b_x):
    a_all = [a_y] + [grid.send_x(a_y, k) for k in range(1, grid.tx)]
    b_all = [b_x] + [grid.send_y(b_x, k) for k in range(1, grid.y)]
    return a_all, b_all


def add_pieces(groups, cuts, outs, name):
    arrays = [a for group in groups for a in group]
    starts = [sum(len(g) for g in groups[:i]) for i in range(len(groups))]
    last = {}
    for n, cut in enumerate(cuts):
        last[cut[2]] = n

    def body(small, ins, outs_ref, scratch, loads):
        in_s, out_s = scratch[: len(arrays)], scratch[len(arrays) :]
        loaded = [loads.start([(ins[i], in_s[i]) for i in range(starts[g], starts[g] + len(groups[g]))]) for g in range(len(groups))]
        ready, done = set(), []
        for n, (g, spot, which, place) in enumerate(cuts):
            if g not in ready:
                loads.wait(loaded[g])
                ready.add(g)
            total = None
            for i in range(starts[g], starts[g] + len(groups[g])):
                value = in_s[i][spot].astype(F32)
                total = value if total is None else total + value
            out_s[which][place] = total.astype(out_s[which].dtype)
            for w in sorted(w for w in last if last[w] == n):
                done.append(loads.start([(out_s[w], outs_ref[w])]))
        for group in done:
            loads.wait(group)

    return call(
        body,
        arrays,
        outs,
        [pltpu.VMEM(a.shape, a.dtype) for a in arrays] + [pltpu.VMEM(o.shape, o.dtype) for o in outs],
        name,
        0,
    )


class Scatter:
    def __init__(self, grid, a_all, b_all, name):
        self.grid, self.name, self.bit = grid, name, 0
        self.rows = (a_all[0].shape[1], b_all[0].shape[1])
        a_got = [grid.send_x(a_all[k], k) for k in range(1, grid.tx)]
        b_got = [grid.send_y(b_all[k], k) for k in range(1, grid.y)]
        self.state = ([a_all[0]] + a_got, [b_all[0]] + b_got)

    def second(self, gate):
        grid, z = self.grid, self.grid.z
        a_in, b_in = after(self.state, gate)
        outs = [sds((z,) + a_in[0].shape[1:], BF)] * grid.y + [sds((z,) + b_in[0].shape[1:], BF)] * grid.tx
        full = slice(None)
        cuts = [(0, slice(k * z, (k + 1) * z), k, full) for k in list(range(1, grid.y)) + [0]]
        cuts += [(1, slice(k * z, (k + 1) * z), grid.y + k, full) for k in list(range(1, grid.tx)) + [0]]
        res = add_pieces([a_in, b_in], cuts, outs, self.name + "_add")
        a_y, b_x = res[: grid.y], res[grid.y :]
        a_got = [grid.send_y(a_y[k], k) for k in range(1, grid.y)]
        b_got = [grid.send_x(b_x[k], k) for k in range(1, grid.tx)]
        self.state = ([a_y[0]] + a_got, [b_x[0]] + b_got)
        return a_y[0], b_x[0]

    def along_z(self, gate, extra=None):
        grid = self.grid
        a_in, b_in = after(self.state, gate)
        ra, rb = self.rows
        groups = [a_in, b_in] + ([extra] if extra else [])
        more = extra[0].shape[1] if extra else 0
        order = list(range(1, grid.z)) + [0]
        cuts = []
        for k in order:
            cuts.append((0, k, k, slice(0, ra)))
            cuts.append((1, k, k, slice(ra, ra + rb)))
            if extra:
                cuts.append((2, k, k, slice(ra + rb, ra + rb + more)))
        outs = [sds((ra + rb + more,) + a_in[0].shape[2:], BF)] * grid.z
        both = add_pieces(groups, cuts, outs, self.name + "_addz")
        self.state = [both[0]] + [grid.send_z(both[k], k) for k in range(1, grid.z)]
        return both

    def halve(self, gate):
        grid, (ra, rb) = self.grid, self.rows
        groups = after(self.state, gate)
        if self.bit == 0:
            self.bit, self.left = 1, list(range(grid.z))
        else:
            self.bit, groups = 2 * self.bit, [groups]
        sent = [k for k in self.left if k & self.bit]
        kept = [k for k in self.left if not k & self.bit]
        cuts = []
        for which, ids in ((0, sent), (1, kept)):
            for n, k in enumerate(ids):
                spot = self.left.index(k)
                if len(groups) == 2:
                    cuts.append((0, spot, which, (n, slice(0, ra))))
                    cuts.append((1, spot, which, (n, slice(ra, ra + rb))))
                else:
                    cuts.append((0, spot, which, n))
        outs = [sds((len(kept), ra + rb) + groups[0][0].shape[2:], BF)] * 2
        send, keep = add_pieces(groups, cuts, outs, self.name + "_half")
        self.left = kept
        self.state = [keep, grid.send_z(send, self.bit)]
        return keep

    def finish(self, gate, cuts, outs):
        if self.bit:
            cuts = [((0, rows), which, place) for rows, which, place in cuts]
        cuts = [(0, rows, which, place) for rows, which, place in cuts]
        return add_pieces([after(self.state, gate)], cuts, outs, self.name + "_sum")


def xor_blocks(value, mask, axis):
    count = value.shape[axis]
    bit = 1
    while bit < count:
        shape = value.shape
        split = value.reshape(shape[:axis] + (count // (2 * bit), 2, bit) + shape[axis + 1 :])
        turned = jnp.flip(split, axis=axis + 1).reshape(shape)
        value = jnp.where(jnp.bitwise_and(mask, bit) != 0, turned, value)
        bit *= 2
    return value


def pad_cols(value, width):
    return jnp.pad(value, ((0, 0), (0, width - value.shape[1])))


def per_device(
    tokens,
    cotangent,
    image_mask,
    norm_gains,
    norm_shifts,
    w_qkv,
    b_qv,
    w_out,
    w_up,
    up_bias,
    w_down,
    *,
    dp,
    tx,
):
    grid = Grid3(dp, tx)
    y_n, z_n = grid.y, grid.z
    core = lax.axis_index("core").astype(jnp.int32)
    me_d = lax.axis_index("dp").astype(jnp.int32)
    me_x = lax.axis_index("tx").astype(jnp.int32)
    seq, width = tokens.shape
    _, bd, hw = w_qkv.shape
    fw = w_up.shape[1]
    ext, hid = tx * hw, tx * fw
    hh, fh = hw // 2, fw // 2
    aligned = bd % 128 == 0 and hh % 128 == 0 and fh % 128 == 0
    rel = [kz * y_n + ky for ky in range(y_n) for kz in range(z_n)]

    def from_abs(value, axis):
        shape = value.shape
        value = value.reshape(shape[:axis] + (z_n, y_n) + shape[axis + 1 :])
        return jnp.swapaxes(value, axis, axis + 1).reshape(shape)

    def to_rel(value, axis):
        shape = value.shape
        value = value.reshape(shape[:axis] + (y_n, z_n) + shape[axis + 1 :])
        return jnp.swapaxes(value, axis, axis + 1).reshape(shape)

    ids = jnp.stack([core, me_d] + [jnp.bitwise_xor(me_d, k) for k in rel])
    keep = lax.dynamic_slice(image_mask, (2 * me_x,), (2,)).astype(F32)

    lane = max(bd, hh)
    small = jnp.concatenate(
        [
            pad_cols(norm_gains, lane),
            pad_cols(norm_shifts, lane),
            pad_cols(b_qv, lane),
            pad_cols(up_bias[None], lane),
            jnp.zeros((7, lane), BF),
        ]
    )
    qkv_a = pad_cols(w_qkv[:, :, :hh].reshape(3 * bd, hh), lane)
    qkv_b = pad_cols(w_qkv[:, :, hh:].reshape(3 * bd, hh), lane)
    first_a = jnp.concatenate([qkv_a, pad_cols(w_out[:hh], lane), small])
    first_b = jnp.concatenate([qkv_b, pad_cols(w_out[hh:], lane)])
    own = [tokens, cotangent]
    other = [swap_core(value) for value in own]
    if aligned:
        tok, cot = arrange_pair(ids, own, other, dp)
    else:

        def arrange(own, other):
            pair = jnp.where(core == 0, jnp.stack([own, other]), jnp.stack([other, own]))
            pair = xor_blocks(pair.reshape(2, seq, dp, bd), me_d, 2)
            return from_abs(pair, 2).reshape(2, seq, width)

        tok, cot = [arrange(own[i], other[i]) for i in range(2)]
    c1_z = gather_z(grid, first_a, first_b, gate=tok)
    c1_h = gather_first(grid, *c1_z)
    c1_h = join(c1_h)
    c1a, c1b = gather_last(grid, *c1_h)
    up_halves = after((w_up[:, :fh], w_up[:, fh:]), c1_h)
    row0 = 3 * bd + hh
    if aligned and 128 % (hw // dp) == 0 and (fw // dp) % 128 == 0:
        c1a, c1b = after((c1a, c1b), (c1a, c1b))
        nv, bq, bu = vectors(ids, c1a, row0, dp, y_n, bd, hw // dp, fw // dp)
    else:
        nv = c1a[0][:, row0 : row0 + 6, :bd].transpose(1, 0, 2).reshape(6, width).astype(F32)
        tail = jnp.stack([v[:, row0 + 6 : row0 + 9] for v in c1a])
        tail = xor_blocks(to_rel(tail, 1), me_d, 1)
        bq = tail[:, :, :2, : hw // dp].transpose(2, 0, 1, 3).reshape(2, ext).astype(F32)
        bu = tail[:, :, 2, : fw // dp].reshape(1, hid).astype(F32)
    grad_top = cot * keep.astype(BF)[:, None, None]

    up_z = gather_z(grid, *up_halves, gate=nv)
    up_h = gather_first(grid, *up_z)
    dn_halves = after((w_down[:fh], w_down[fh:]), up_z)

    if aligned:
        every, wq_plan, wo_plan, up_plan, dn_plan = slice(None), [[], [], []], [], [], []
        for kx in range(tx):
            halves = [slice(kx * hw, kx * hw + hh), slice(kx * hw + hh, (kx + 1) * hw)]
            f_halves = [slice(kx * fw, kx * fw + fh), slice(kx * fw + fh, (kx + 1) * fw)]
            own = slice(kx * z_n, (kx + 1) * z_n)
            for i in range(3):
                src = slice(i * bd, (i + 1) * bd)
                wq_plan[i].append((kx, (every, src), (i, every, every, halves[0])))
                for ky in range(y_n):
                    dst = (i, slice(ky * z_n, (ky + 1) * z_n), every, halves[1])
                    wq_plan[i].append((tx + ky, (own, src), dst))
            src = slice(3 * bd, 3 * bd + hh)
            dn_plan += [[], []]
            for ky in range(y_n):
                for kz in range(z_n):
                    p, r = ky * z_n + kz, kx * z_n + kz
                    cols = slice(p * bd, (p + 1) * bd)
                    wo_plan.append((kx, (p, src), (halves[0], cols)))
                    wo_plan.append((tx + ky, (r, src), (halves[1], cols)))
                    dn_plan[-2].append((kx, (p,), (f_halves[0], cols)))
                    dn_plan[-1].append((tx + ky, (r,), (f_halves[1], cols)))
            up_plan += [[(kx, (every,), (every, f_halves[0]))], []]
            for ky in range(y_n):
                rows = slice(kx * z_n * bd, (kx + 1) * z_n * bd)
                dst = (slice(ky * z_n * bd, (ky + 1) * z_n * bd), f_halves[1])
                up_plan[-1].append((tx + ky, (rows,), dst))
        c1 = c1a + c1b
        wqkv = (c1, wq_plan, (3, dp, bd, ext))
        wout = (c1, [wo_plan], (ext, width))
    else:

        def whole(a_all, b_all):
            a = jnp.stack(a_all)
            b = jnp.stack(b_all).reshape((y_n, tx, z_n) + b_all[0].shape[1:])
            b = b.transpose(1, 0, 2, 3, 4).reshape(a.shape[:2] + b.shape[3:])
            return jnp.stack([a, b], axis=1)

        c1 = whole([v[:, :row0] for v in c1a], c1b)
        qkv = c1[:, :, :, : 3 * bd, :hh].reshape(tx, 2, dp, 3, bd, hh)
        qkv = qkv.transpose(3, 2, 4, 0, 1, 5).reshape(3, dp, bd, ext)
        out = c1[:, :, :, 3 * bd :, :bd].transpose(0, 1, 3, 2, 4).reshape(ext, width)
        all_of = [[(0, (slice(None),), (slice(None),))]]
        wqkv = ([qkv], all_of, qkv.shape)
        wout = ([out], all_of, out.shape)

    rows2 = 2 * seq

    res = attn_forward(0, after(tok, up_z), nv, bq, wqkv, wout, None)
    part0 = res[5]
    up_h = join(after(up_h, part0))
    upa, upb = gather_last(grid, *up_h)
    dn_halves = after(dn_halves, up_h)
    res = attn_forward(1, after(tok, up_h), nv, bq, wqkv, wout, res[:5])
    recv0 = swap_core(after(part0, res[5]))
    parts = [(part0, recv0), (res[5], swap_core(res[5]))]
    first, q, k, v, att = res[:5]
    upa, upb = after((upa, upb), res[5])
    dn_z = gather_z(grid, *dn_halves, gate=(upa, upb))
    dn_h = gather_first(grid, *dn_z)
    if aligned:
        wup = ([v.reshape(-1, fh) for v in upa + upb], up_plan, (width, hid))
    else:
        up_w = whole(upa, upb).transpose(2, 3, 0, 1, 4).reshape(width, hid)
        wup = ([up_w], all_of, up_w.shape)
    part, recv = parts[0]
    state = mlp_up(0, tok, part, recv, keep, nv, bu, wup, fh, None)
    dna, dnb = gather_last(grid, *join(after(dn_h, state[1])))
    part, recv = parts[1]
    state = mlp_up(1, tok, part, recv, keep, nv, bu, wup, fh, state)
    if aligned:
        wdown = (dna + dnb, dn_plan, (hid, width))
    else:
        down_w = whole(dna, dnb).transpose(0, 1, 3, 2, 4).reshape(hid, width)
        wdown = ([down_w], all_of, down_w.shape)
    middle, second, act, dact = state
    flat = lambda value: value.reshape(rows2, value.shape[2])
    act2, sec2, grad2 = flat(act), flat(second), flat(grad_top)

    full = slice(None)
    a_spots = [(p, slice(p * bd, (p + 1) * bd)) for p in range(dp)]

    def by_left(l_index, r_index, size, row0):
        tasks, rows = [], slice(row0, row0 + size // 2)
        halves = slice(0, size // 2), slice(size // 2, size)
        for kx in range(tx):
            stores = [(kx, (p, rows), halves[0], cols) for p, cols in a_spots]
            for p, cols in a_spots:
                ky, kz = p // z_n, p % z_n
                stores.append((tx + ky, (kx * z_n + kz, rows), halves[1], cols))
            tasks.append((l_index, slice(kx * size, (kx + 1) * size), r_index, slice(0, width), stores))
        return tasks

    def by_right(l_index, r_index, size, row0, lanes):
        tasks, each = [], size // 2 // lanes
        for kx in range(tx):
            stores = []
            for j in range(each):
                rows = slice(row0 + j * bd, row0 + (j + 1) * bd)
                cols = [slice((h * each + j) * lanes, (h * each + j + 1) * lanes) for h in range(2)]
                for p, r_sl in a_spots:
                    ky, kz = p // z_n, p % z_n
                    stores.append((kx, (p, rows), r_sl, cols[0]))
                    stores.append((tx + ky, (kx * z_n + kz, rows), r_sl, cols[1]))
            tasks.append((l_index, slice(0, width), r_index, slice(kx * size, (kx + 1) * size), stores))
        return tasks

    def pieces(rows, lanes):
        return [(dp, rows, lanes)] * tx + [(tx * z_n, rows, lanes)] * y_n

    def send_grad(parts, name):
        return Scatter(grid, list(parts[:tx]), list(parts[tx:]), name)

    grads = weight_grad([act2], [grad2], by_left(0, 0, fw, 0), pieces(fh, bd), "down_grad", 0, fh)
    down_rs = send_grad(grads, "down")
    grad_in = after(grad2, grads[-1])
    low_pre, bias_up, two0, two1, mlp_part = mlp_back(grad_in, act2, flat(dact), wdown, wup, fh)
    two_parts = [two0, two1]
    mlp_part = mlp_part.reshape(2, seq, width)
    mlp_recv = swap_core(mlp_part)
    two_recvs = [swap_core(value) for value in two_parts]
    down_half = down_rs.second(bias_up)
    up_rows = fh // bd * bd
    up_shapes = pieces(up_rows + hh, bd)
    sec_in = after(sec2, down_half)
    tasks = by_right(0, 0, fw, 0, bd)
    grads = weight_grad([sec_in], [low_pre], tasks, up_shapes, "up_grad", 0, up_rows)
    gmid, gattn, grad_att, col = middle_back(
        ids, middle, two_parts, after(two_recvs, grads[-1]), cot, keep, nv, wout
    )
    down_zs = down_rs.along_z(col)
    att_in = after(flat(att), (down_zs, mlp_recv))
    tasks = by_left(0, 0, hw, 0)
    grads = weight_grad(
        [att_in], [flat(gattn)], tasks, up_shapes, "out_grad", up_rows, up_rows + hh, grads
    )
    up_rs = send_grad(grads, "up_out")

    units = [(a, i) for a in range(2) for i in range(ext // 128)]
    cut = (5 * len(units) + 4) // 8
    res = attn_backward(units[:cut], after(grad_att, grads[-1]), q, k, v, None)
    bias_qv = res[3]
    grad_down = down_rs.finish(bias_qv, [(full, 0, full)], [sds((fw, bd), F32)])[0]
    up_half = up_rs.second(grad_down)
    res = attn_backward(units[cut:], after(grad_att, up_half), q, k, v, res[:3])
    bias_qv = jnp.concatenate([bias_qv, res[3]]).reshape(2, ext // 128, 2, 128)
    bias_qv = jnp.sum(bias_qv, axis=0).transpose(1, 0, 2).reshape(2, ext)
    up_zs = up_rs.halve(res[3]) if z_n > 1 else res[3]
    low_proj = [flat(value) for value in res[:3]]
    makers = [by_right(0, i, hw, i * bd, hh) for i in range(3)]
    first_in = after(flat(first), up_zs)
    tasks = [task for maker in makers for task in maker]
    grads = weight_grad([first_in], low_proj, tasks, pieces(3 * bd, hh), "qkv_grad", 0, 3 * bd)
    qkv_rs = send_grad(grads, "qkv")
    low_in = after(low_proj, grads[-1])
    one_parts = input_grad(low_in, wqkv, width)
    one_recvs = [swap_core(value) for value in one_parts]
    total_rows = up_rows + hh
    cuts = []
    for h in range(2):
        for j in range(fh // bd):
            rows = slice(h * total_rows + j * bd, h * total_rows + (j + 1) * bd)
            cols = slice(h * fh + j * bd, h * fh + (j + 1) * bd)
            cuts.append((rows, 0, (full, cols)))
        rows = slice(h * total_rows + up_rows, (h + 1) * total_rows)
        cuts.append((rows, 1, (slice(h * hh, (h + 1) * hh),)))
    up_cuts, gate = cuts, one_parts[0]
    while 2 * up_rs.bit < z_n:
        gate = up_rs.halve(gate)
    qkv_half = qkv_rs.second(gate)
    wide = max(bd, hw // dp, fw // dp)
    vec = jnp.concatenate([jnp.zeros((2, width), F32), col])
    vec = vec.reshape(6, y_n, z_n, bd).transpose(1, 2, 0, 3)
    bias_qv = bias_qv.reshape(2, tx, dp, hw // dp).transpose(2, 1, 0, 3)
    bias_up = bias_up.reshape(tx, 1, dp, fw // dp).transpose(2, 0, 1, 3)
    bias = jnp.concatenate(
        [
            jnp.pad(value, ((0, 0), (0, 0), (0, 0), (0, wide - value.shape[3])))
            for value in (bias_qv, bias_up)
        ],
        axis=2,
    )
    bias = from_abs(xor_blocks(bias, me_d, 0), 0).reshape(y_n, z_n, tx, 3, wide)
    bias = bias.transpose(2, 0, 1, 3, 4)
    vec = jnp.pad(vec, ((0, 0), (0, 0), (0, 0), (0, wide - bd)))
    vec = jnp.broadcast_to(vec, (tx,) + vec.shape)
    rest = jnp.concatenate([vec, bias, jnp.zeros((tx, y_n, z_n, 7, wide), F32)], axis=3)
    rest = rest.reshape(tx * y_n, z_n, 16, wide)
    grad_tokens, one_sums, *small = finish_tokens(
        ids, nv, tok, one_parts, after(one_recvs, qkv_half), gmid, rest, dp, aligned
    )
    if not aligned:
        ones = jnp.pad(one_sums.reshape(2, y_n, z_n, bd), ((0, 14), (0, 0), (0, 0), (0, wide - bd)))
        ones = ones.transpose(1, 2, 0, 3)
        small = [value + ones[n % y_n] for n, value in enumerate(small)]
    got = small[:1]
    for n in range(1, tx * y_n):
        got.append(grid.send_xy(small[n], n // y_n, n % y_n))
    up_outs = [sds((bd, fw), F32), sds((hw, bd), F32)]
    grad_up, grad_out = up_rs.finish(one_sums, up_cuts, up_outs)
    cuts, outs = [], [sds((3, bd, hw), F32)]
    for h in range(2):
        for i in range(3):
            rows = slice((3 * h + i) * bd, (3 * h + i + 1) * bd)
            cuts.append((rows, 0, (i, full, slice(h * hh, (h + 1) * hh))))
    if wide == hh:
        qkv_zs = qkv_rs.along_z(grad_out, got)
        cuts.append((slice(6 * bd, 6 * bd + 16), 1, full))
        outs.append(sds((16, wide), F32))
    else:
        qkv_zs = qkv_rs.along_z(grad_out)
    layer_out = finish_layer(
        ids, keep, nv, middle, after(mlp_part, qkv_zs), mlp_recv, dp, aligned
    )
    res = qkv_rs.finish(layer_out, cuts, outs)
    grad_qkv = res[0]
    if wide == hh:
        both = res[1]
    else:
        both, bit = sum(got), 1
        while bit < z_n:
            both = both.reshape((-1, 2) + both.shape[1:])
            both = both[:, 0] + grid.send_z(both[:, 1], bit)
            bit *= 2
        both = both[0]
    if not aligned:

        def restore(value):
            value = xor_blocks(to_rel(value.reshape(seq, dp, bd), 1), me_d, 1)
            return value.reshape(seq, width)

        layer_out, grad_tokens = restore(layer_out), restore(grad_tokens)

    share = bd // (2 * tx)
    mine = lax.dynamic_slice(both[:6, :bd], (0, (2 * me_x + core) * share), (6, share))

    return (
        layer_out,
        grad_tokens,
        mine[0:3:2],
        jnp.concatenate([mine[1:2], mine[3:6]]),
        grad_qkv,
        both[6:8, : hw // dp],
        grad_out,
        grad_up,
        both[8, : fw // dp],
        grad_down,
    )


def solution(mesh):
    dp, tensor = mesh.shape["dp"], mesh.shape["tensor"]
    split = Mesh(mesh.devices.reshape(dp, tensor // 2, 2), ("dp", "tx", "core"))
    every = ("dp", "tx", "core")
    tensor_axes = ("tx", "core")
    in_specs = (
        P(every, None),
        P(every, None),
        P("dp"),
        P(None, "dp"),
        P(None, "dp"),
        P(None, "dp", tensor_axes),
        P(None, ("tx", "core", "dp")),
        P(tensor_axes, "dp"),
        P("dp", tensor_axes),
        P(("tx", "core", "dp")),
        P(tensor_axes, "dp"),
    )
    out_specs = (
        P(every, None),
        P(every, None),
        P(None, every),
        P(None, every),
        P(None, "dp", tensor_axes),
        P(None, ("tx", "core", "dp")),
        P(tensor_axes, "dp"),
        P("dp", tensor_axes),
        P(("tx", "core", "dp")),
        P(tensor_axes, "dp"),
    )
    return jax.shard_map(
        functools.partial(per_device, dp=dp, tx=tensor // 2),
        mesh=split,
        in_specs=in_specs,
        out_specs=out_specs,
        check_vma=False,
    )
```

```python
import functools

import jax
import jax.numpy as jnp
from jax import lax
from jax.experimental import pallas as pl
from jax.experimental.pallas import tpu as pltpu
from jax.sharding import Mesh, PartitionSpec as P

HEAD_DIM = 64
VALID = 577
SEQ = 584
BF = jnp.bfloat16
F32 = jnp.float32
VMEM_LIMIT = 60 * 1024 * 1024
COST_SCALE = 1.0
COST = {
    "arrange_pair": 5,
    "vectors": 3,
    "attn_forward": 16,
    "mlp_up": 10,
    "down_grad": 11,
    "mlp_back": 22,
    "up_grad": 11,
    "middle_back": 0,
    "out_grad": 8,
    "attn_backward": 18,
    "qkv_grad": 7,
    "qkv_keep": 0,
    "up_half": 0,
    "grad_one": 0,
    "qkv_add": 30,
    "finish_layer": 0,
    "up_sum": 0,
    "finish_tokens": 9,
}
NT = (((1,), (1,)), ((), ()))
TN = (((0,), (0,)), ((), ()))
NN = (((1,), (0,)), ((), ()))


def dot(left, right, dims):
    return lax.dot_general(left, right, dims, preferred_element_type=F32)


class Loads:
    def __init__(self, sems):
        self.sems, self.groups = sems, []

    def start(self, pairs):
        sem = self.sems.at[len(self.groups)]
        copies = [pltpu.make_async_copy(src, dst, sem) for src, dst in pairs]
        for copy in copies:
            copy.start()
        self.groups.append(copies)
        return len(self.groups) - 1

    def wait(self, group):
        for copy in self.groups[group]:
            copy.wait()


def call(body, ins, outs, scratch, name, flops, aliases=None, smem=(), sems=48, vmem_ins=(), vmem=VMEM_LIMIT):
    n_smem, n_vmem, n_in, n_out = len(smem), len(vmem_ins), len(ins), len(outs)
    moved = sum(a.size * a.dtype.itemsize for a in ins) + sum(
        o.size * o.dtype.itemsize for o in outs
    )

    def kernel(*refs):
        first = n_smem + n_vmem
        small = refs[:first]
        in_refs = refs[first : first + n_in]
        out_refs = refs[first + n_in : first + n_in + n_out]
        rest = refs[first + n_in + n_out :]
        body(small, in_refs, out_refs, rest[:-1], Loads(rest[-1]))

    flops = max(COST.get(name, 3), 0.02) * COST_SCALE * 1.15e9
    moved = 0
    any_spec = pl.BlockSpec(memory_space=pl.ANY)
    return pl.pallas_call(
        kernel,
        out_shape=outs,
        in_specs=[pl.BlockSpec(memory_space=pltpu.SMEM)] * n_smem
        + [pl.BlockSpec(memory_space=pltpu.VMEM)] * n_vmem
        + [any_spec] * n_in,
        out_specs=[any_spec] * n_out,
        scratch_shapes=list(scratch) + [pltpu.SemaphoreType.DMA((sems,))],
        input_output_aliases={n_smem + n_vmem + i: o for i, o in (aliases or {}).items()},
        compiler_params=pltpu.CompilerParams(vmem_limit_bytes=vmem),
        cost_estimate=pl.CostEstimate(flops=int(flops), bytes_accessed=int(flops // 1000), transcendentals=0),
        name=name,
    )(*smem, *vmem_ins, *ins)


def norm_parts(rows):
    center = rows - jnp.mean(rows, axis=1, keepdims=True)
    inverse = lax.rsqrt(jnp.mean(center * center, axis=1, keepdims=True) + 1e-05)
    return center * inverse, inverse


def norm_back(grad_norm, scaled, inverse, gain_row):
    grad_hat = grad_norm * gain_row
    first_mean = jnp.mean(grad_hat, axis=1, keepdims=True)
    second_mean = jnp.mean(grad_hat * scaled, axis=1, keepdims=True)
    return inverse * (grad_hat - first_mean - scaled * second_mean)


def sds(shape, dtype):
    return jax.ShapeDtypeStruct(shape, dtype)


def arrange_pair(ids, own, other, nd):
    n = len(own)
    rows, width = own[0].shape
    bd = width // nd

    def body(small, ins, outs, scratch, loads):
        (ids_ref,) = small
        mine = ids_ref[0]
        in_s, out_s = scratch[: 2 * n], scratch[2 * n :]
        groups = [loads.start([(ins[i], in_s[i])]) for i in range(2 * n)]
        done = []
        for i in range(2 * n):
            loads.wait(groups[i])
            for p in range(nd):
                src = pl.ds(pl.multiple_of(ids_ref[2 + p] * bd, 128), bd)
                out_s[i][:, p * bd : (p + 1) * bd] = in_s[i][:, src]
            spot = mine if i < n else 1 - mine
            done.append(loads.start([(out_s[i], outs[i % n].at[spot])]))
        for group in done:
            loads.wait(group)

    return call(
        body,
        list(own) + list(other),
        [sds((2, rows, width), BF)] * n,
        [pltpu.VMEM((rows, width), BF)] * (4 * n),
        "arrange_pair",
        0,
        smem=(ids,),
    )


def vectors(ids, gathered, row0, nd, y_n, bd, qv, up):
    tx, z_n = len(gathered), nd // y_n

    def body(small, ins, outs, scratch, loads):
        ids_ref, rows_s, nv_s, bq_s, bu_s = small[0], *scratch
        rows = pl.ds(row0, 16)
        loads.wait(loads.start([(ins[k].at[:, rows, :], rows_s.at[k]) for k in range(tx)]))
        for p in range(nd):
            nv_s[:, p * bd : (p + 1) * bd] = rows_s[0, p].astype(F32)[:6, :bd]
        for k in range(tx):
            pieces = []
            for d in range(nd):
                rel = ids_ref[1] ^ d
                spot = (rel % y_n) * z_n + rel // y_n
                piece = rows_s[k, spot].astype(F32)
                bu_s[:, (k * nd + d) * up : (k * nd + d + 1) * up] = piece[8:9, :up]
                pieces.append(piece[6:8, :])
            each = 128 // qv
            for start in range(0, nd, each):
                total = pieces[start]
                for i in range(1, each):
                    total = total + pltpu.roll(pieces[start + i], i * qv, 1)
                bq_s[:, (k * nd + start) * qv : (k * nd + start + each) * qv] = total
        loads.wait(loads.start([(nv_s, outs[0]), (bq_s, outs[1]), (bu_s, outs[2])]))

    shapes = [(6, nd * bd), (2, tx * nd * qv), (1, tx * nd * up)]
    return call(
        body,
        list(gathered),
        [sds(s, F32) for s in shapes],
        [pltpu.VMEM((tx, nd, 16, gathered[0].shape[2]), BF)] + [pltpu.VMEM(s, F32) for s in shapes],
        "vectors",
        0,
        smem=(ids,),
    )


def block_stores(ids_ref, src, dst, nd, aligned):
    if not aligned:
        return [(src, dst)]
    bd = src.shape[1] // nd
    pairs = []
    for p in range(nd):
        cols = pl.ds(pl.multiple_of(ids_ref[2 + p] * bd, 128), bd)
        pairs.append((src.at[:, p * bd : (p + 1) * bd], dst.at[:, cols]))
    return pairs


def weight_loads(loads, groups, refs, scratch):
    return [
        loads.start([(refs[a].at[src], scratch.at[dst]) for a, src, dst in plan])
        for plan in groups
    ]


def softmax_rows(q2, k2):
    scores = dot(q2, k2, NT)
    lane = lax.broadcasted_iota(jnp.int32, scores.shape, 1)
    scores = jnp.where(lane < VALID, scores, -1e30)
    e = jnp.exp(scores - jnp.max(scores, axis=1, keepdims=True))
    return e * (1.0 / jnp.sum(e, axis=1, keepdims=True))


def attn_forward(image, tok, nv, bq, wqkv, wout, prev):
    seq, width = tok.shape[1:]
    qkv_arrays, qkv_plan, qkv_scratch = wqkv
    out_arrays, out_plan, out_scratch = wout
    ext = qkv_scratch[-1]
    n_prev = 0 if prev is None else len(prev)
    nq, no = len(qkv_arrays), len(out_arrays)

    def body(small, ins, outs, scratch, loads):
        nv_ref, bq_ref = small
        tok_ref, ins = ins[0], ins[1 + n_prev :]
        w_s, wo_s, tok_s, first_s, q_s, k_s, v_s, att_s, part_s = scratch
        g_tok = loads.start([(tok_ref.at[image], tok_s)])
        g_w = weight_loads(loads, qkv_plan, ins[:nq], w_s)
        g_o = weight_loads(loads, out_plan, ins[nq:], wo_s)
        loads.wait(g_tok)
        hat, _ = norm_parts(tok_s[...].astype(F32))
        first_s[...] = (hat * nv_ref[0:1, :] + nv_ref[2:3, :]).astype(BF)
        g_first = loads.start([(first_s, outs[0].at[image])])
        low = first_s[...]
        for i, ref in enumerate((q_s, k_s, v_s)):
            if i < len(g_w):
                loads.wait(g_w[i])
            proj = dot(low, w_s[i].reshape(width, ext), NN)
            if i == 0:
                proj = proj + bq_ref[0:1, :]
            if i == 2:
                proj = proj + bq_ref[1:2, :]
            low_proj = proj.astype(BF)
            if i == 0:
                low_proj = low_proj * jnp.asarray(HEAD_DIM**-0.5, BF)
            ref[...] = low_proj
        g_qkv = loads.start(
            [(q_s, outs[1].at[image]), (k_s, outs[2].at[image]), (v_s, outs[3].at[image])]
        )
        half = lax.broadcasted_iota(jnp.int32, (1, 128), 1) // HEAD_DIM

        def pair(i, carry):
            cols = pl.ds(pl.multiple_of(i * 128, 128), 128)
            q2, k2, v2 = q_s[:, cols], k_s[:, cols], v_s[:, cols]
            total = None
            for h in range(2):
                keep = (half == h).astype(BF)
                probs = softmax_rows(q2, k2 * keep).astype(BF)
                piece = dot(probs, v2 * keep, NN)
                total = piece if total is None else total + piece
            att_s[:, cols] = total.astype(BF)
            return carry

        lax.fori_loop(0, ext // 128, pair, 0)
        g_att = loads.start([(att_s, outs[4].at[image])])
        loads.wait(g_o[0])
        part_s[...] = dot(att_s[...], wo_s[...], NN).astype(BF)
        g_part = loads.start([(part_s, outs[5])])
        for group in (g_first, g_qkv, g_att, g_part):
            loads.wait(group)

    shapes = [(2, seq, width)] + [(2, seq, ext)] * 4
    return call(
        body,
        [tok] + list(prev or []) + qkv_arrays + out_arrays,
        [sds(s, BF) for s in shapes] + [sds((seq, width), BF)],
        [
            pltpu.VMEM(qkv_scratch, BF),
            pltpu.VMEM(out_scratch, BF),
            pltpu.VMEM((seq, width), BF),
            pltpu.VMEM((seq, width), BF),
            pltpu.VMEM((seq, ext), BF),
            pltpu.VMEM((seq, ext), BF),
            pltpu.VMEM((seq, ext), BF),
            pltpu.VMEM((seq, ext), BF),
            pltpu.VMEM((seq, width), BF),
        ],
        "attn_forward",
        2 * seq * width * ext * 4 + 16 * seq * seq * ext,
        aliases={1 + i: i for i in range(n_prev)},
        vmem_ins=(nv, bq),
    )


def mlp_up(image, tok, part, recv, keep, nv, bu, wup, step, prev):
    seq, width = tok.shape[1:]
    up_arrays, up_plan, up_scratch = wup
    hid = up_scratch[-1]
    n_prev = 0 if prev is None else len(prev)

    def body(small, ins, outs, scratch, loads):
        keep_ref, nv_ref, bu_ref = small
        tok_ref, part_ref, recv_ref = ins[:3]
        w_s, tok_s, part_s, recv_s, mid_s, sec_s, act_s, dact_s = scratch
        g_in = loads.start([(tok_ref.at[image], tok_s), (part_ref, part_s), (recv_ref, recv_s)])
        g_w = weight_loads(loads, up_plan, ins[3 + n_prev :], w_s)
        loads.wait(g_in)
        total = part_s[...].astype(F32) + recv_s[...].astype(F32) + nv_ref[4:5, :]
        middle = tok_s[...].astype(F32) + keep_ref[image] * total
        mid_s[...] = middle
        hat, _ = norm_parts(middle)
        sec_s[...] = (hat * nv_ref[1:2, :] + nv_ref[3:4, :]).astype(BF)
        g_mid = loads.start([(mid_s, outs[0].at[image]), (sec_s, outs[1].at[image])])
        second = sec_s[...]
        done = []
        for block in range(hid // step):
            if block < len(g_w):
                loads.wait(g_w[block])
            cols = slice(block * step, (block + 1) * step)
            pre = dot(second, w_s[:, cols], NN) + bu_ref[0:1, cols]
            gate = 0.5 * jnp.tanh(0.851 * pre) + 0.5
            act_s[:, cols] = (pre * gate).astype(BF)
            dact_s[:, cols] = (gate + 1.702 * pre * gate * (1.0 - gate)).astype(BF)
            done.append(
                loads.start(
                    [
                        (act_s.at[:, cols], outs[2].at[image, :, cols]),
                        (dact_s.at[:, cols], outs[3].at[image, :, cols]),
                    ]
                )
            )
        for group in [g_mid] + done:
            loads.wait(group)

    outs = [
        sds((2, seq, width), F32),
        sds((2, seq, width), BF),
        sds((2, seq, hid), BF),
        sds((2, seq, hid), BF),
    ]
    return call(
        body,
        [tok, part, recv] + list(prev or []) + up_arrays,
        outs,
        [
            pltpu.VMEM(up_scratch, BF),
            pltpu.VMEM((seq, width), BF),
            pltpu.VMEM((seq, width), BF),
            pltpu.VMEM((seq, width), BF),
            pltpu.VMEM((seq, width), F32),
            pltpu.VMEM((seq, width), BF),
            pltpu.VMEM((seq, hid), BF),
            pltpu.VMEM((seq, hid), BF),
        ],
        "mlp_up",
        2 * seq * width * hid,
        aliases={3 + i: i for i in range(n_prev)},
        smem=(keep,),
        vmem_ins=(nv, bu),
    )


def column_loads(src, dst, start):
    if len(src.shape) == 2:
        return [(src, dst)]
    n, _, width = src.shape
    return [
        (src.at[i], dst.at[:, (start + i) * width : (start + i + 1) * width]) for i in range(n)
    ]


def weight_grad(lefts, rights, tasks, out_shapes, name, lo, hi, prev=None, fill=False):
    rows = lefts[0].shape[0]
    arrays = list(lefts) + list(rights)
    wide = [a.shape[-1] * (a.shape[0] if len(a.shape) == 3 else 1) for a in arrays]
    n_left, n_in = len(lefts), len(arrays)
    prev = list(prev or [])
    last = {}
    for n, task in enumerate(tasks):
        for store in task[4]:
            last[store[0]] = n

    def body(small, ins, outs, scratch, loads):
        in_s, out_s = scratch[:n_in], scratch[n_in:]
        order = []
        for l_index, _, r_index, _, _ in tasks:
            for i in (l_index, n_left + r_index):
                if i not in order:
                    order.append(i)
        groups = {i: loads.start(column_loads(ins[i], in_s[i], 0)) for i in order}
        for ref in out_s if fill else ():
            ref[...] = jnp.zeros_like(ref)
        ready, done = set(), []
        for n, (l_index, l_cols, r_index, r_cols, stores) in enumerate(tasks):
            for i in (l_index, n_left + r_index):
                if i not in ready:
                    loads.wait(groups[i])
                    ready.add(i)
            left, right = in_s[l_index][:, l_cols], in_s[n_left + r_index][:, r_cols]
            value = dot(left, right, TN).astype(BF)
            for which, spot, r_sl, c_sl in stores:
                out_s[which][spot] = value[r_sl, c_sl]
            for which in sorted(w for w in last if last[w] == n):
                done.append(loads.start([(out_s[which], outs[which].at[:, lo:hi])]))
        for group in done:
            loads.wait(group)

    flops = sum(
        2 * rows * (t[1].stop - t[1].start) * (t[3].stop - t[3].start) for t in tasks
    )
    return call(
        body,
        arrays + prev,
        [sds(s, BF) for s in out_shapes],
        [pltpu.VMEM((rows, w), BF) for w in wide]
        + [pltpu.VMEM((s[0], hi - lo, s[2]), BF) for s in out_shapes],
        name,
        flops,
        aliases={n_in + i: i for i in range(len(prev))},
    )


def mlp_back(grad, act, dact, wdown, wup, step):
    rows, width = grad.shape
    seq = rows // 2
    hid = dact.shape[1]
    down_arrays, down_plan, down_scratch = wdown
    up_arrays, up_plan, up_scratch = wup
    n_down = len(down_arrays)

    def body(small, ins, outs, scratch, loads):
        wd_s, wu_s, g_s, a_s, d_s, low_s, sum_s, two_s, mlp_s = scratch
        g_g = loads.start([(ins[0], g_s)])
        g_wd = weight_loads(loads, down_plan, ins[3 : 3 + n_down], wd_s)
        g_d = []
        for block in range(hid // step):
            cols = slice(block * step, (block + 1) * step)
            g_d.append(loads.start([(ins[2].at[:, cols], d_s.at[:, cols])]))
        g_wu = weight_loads(loads, up_plan, ins[3 + n_down :], wu_s)
        g_a = loads.start([(ins[1], a_s)])
        loads.wait(g_g)
        left = g_s[...]
        done = []
        for block in range(hid // step):
            if block < len(g_wd):
                loads.wait(g_wd[block])
            loads.wait(g_d[block])
            cols = slice(block * step, (block + 1) * step)
            pre = dot(left, wd_s[cols, :], NT) * d_s[:, cols].astype(F32)
            low_s[:, cols] = pre.astype(BF)
            sum_s[0:1, cols] = jnp.sum(pre, axis=0, keepdims=True)
            done.append(loads.start([(low_s.at[:, cols], outs[0].at[:, cols])]))
        done.append(loads.start([(sum_s, outs[1])]))
        for group in g_wu:
            loads.wait(group)
        two = dot(low_s[...], wu_s[...], NT)
        for a in range(2):
            two_s[a] = two[a * seq : (a + 1) * seq].astype(BF)
            done.append(loads.start([(two_s.at[a], outs[2].at[a])]))
        loads.wait(g_a)
        mlp_s[...] = dot(a_s[...], wd_s[...], NN).astype(BF)
        done.append(loads.start([(mlp_s, outs[3])]))
        for group in done:
            loads.wait(group)

    return call(
        body,
        [grad, act, dact] + down_arrays + up_arrays,
        [sds((rows, hid), BF), sds((1, hid), F32)]
        + [sds((2, seq, width), BF), sds((rows, width), BF)],
        [
            pltpu.VMEM(down_scratch, BF),
            pltpu.VMEM(up_scratch, BF),
            pltpu.VMEM((rows, width), BF),
            pltpu.VMEM((rows, hid), BF),
            pltpu.VMEM((rows, hid), BF),
            pltpu.VMEM((rows, hid), BF),
            pltpu.VMEM((1, hid), F32),
            pltpu.VMEM((2, seq, width), BF),
            pltpu.VMEM((rows, width), BF),
        ],
        "mlp_back",
        6 * rows * width * hid,
        sems=64,
    )


def input_grad(stacks, starts, weight, width):
    arrays, plan, shape = weight
    n, ext = shape[0], shape[-1]
    rows = stacks[0].shape[1]
    seq, m = rows // 2, len(stacks)

    def body(small, ins, outs, scratch, loads):
        w_s, out_s = scratch[0], scratch[1]
        l_s = scratch[2:]
        g_w = weight_loads(loads, plan[:1], ins[m:], w_s)
        g_l = []
        for i in range(n):
            pairs = []
            for j in range(m):
                count = stacks[j].shape[0] // n
                pairs += column_loads(ins[j].at[i * count : (i + 1) * count], l_s[i], starts[j])
            g_l.append(loads.start(pairs))
        g_w += weight_loads(loads, plan[1:], ins[m:], w_s)
        total = None
        for i in range(n):
            loads.wait(g_l[i])
            if i < len(g_w):
                loads.wait(g_w[i])
            piece = dot(l_s[i][...], w_s[i].reshape(width, ext), NT)
            total = piece if total is None else total + piece
        done = []
        for a in range(2):
            out_s[a] = total[a * seq : (a + 1) * seq].astype(BF)
            done.append(loads.start([(out_s.at[a], outs[0].at[a])]))
        for group in done:
            loads.wait(group)

    return call(
        body,
        list(stacks) + arrays,
        [sds((2, seq, width), BF)],
        [pltpu.VMEM(shape, BF), pltpu.VMEM((2, seq, width), BF)] + [pltpu.VMEM((rows, ext), BF)] * n,
        "grad_one",
        2 * rows * width * ext * n,
    )[0]


def middle_back(ids, middle, part, recv, cot, keep, nv, wout):
    _, seq, width = middle.shape
    out_arrays, out_plan, out_scratch = wout
    ext = out_scratch[0]

    def body(small, ins, outs, scratch, loads):
        ids_ref, keep_ref, nv_ref = small
        mine = ids_ref[0]
        wo_s, mid_s, part_s, recv_s, cot_s, gmid_s, gat_s, do_s = scratch[:8]
        cs_s = scratch[8]
        g_in = [
            loads.start(
                [
                    (ins[0].at[a], mid_s.at[a]),
                    (ins[1].at[a], cot_s.at[a]),
                    (ins[2].at[a], part_s.at[a]),
                    (ins[3].at[a], recv_s.at[a]),
                ]
            )
            for a in range(2)
        ]
        g_o = weight_loads(loads, out_plan, ins[4:], wo_s)
        done = []
        for a in range(2):
            loads.wait(g_in[a])
            keep_here = keep_ref[a]
            hat, inverse = norm_parts(mid_s[a])
            grad_two = part_s[a].astype(F32) + recv_s[a].astype(F32)
            top = cot_s[a].astype(F32)
            grad_mid = top + norm_back(grad_two, hat, inverse, nv_ref[1:2, :])
            grad_attn = grad_mid * keep_here
            sums = [
                jnp.sum(grad_two * hat, axis=0, keepdims=True),
                jnp.sum(grad_two, axis=0, keepdims=True),
                jnp.sum(grad_attn, axis=0, keepdims=True),
                jnp.sum(top, axis=0, keepdims=True) * keep_here,
            ]
            for i, value in enumerate(sums):
                cs_s[i : i + 1, :] = value if a == 0 else cs_s[i : i + 1, :] + value
            gmid_s[a] = grad_mid
            gat_s[a] = grad_attn.astype(BF)
            done.append(loads.start([(gat_s.at[a], outs[1].at[a])]))
            if a == 0:
                loads.wait(g_o[0])
            do_s[a] = dot(gat_s[a], wo_s[...], NT).astype(BF)
            done.append(loads.start([(do_s.at[a], outs[2].at[a])]))
        done.append(loads.start([(gmid_s.at[mine], outs[0]), (cs_s, outs[3])]))
        for group in done:
            loads.wait(group)

    return call(
        body,
        [middle, cot, part, recv] + out_arrays,
        [
            sds((seq, width), F32),
            sds((2, seq, width), BF),
            sds((2, seq, ext), BF),
            sds((4, width), F32),
        ],
        [
            pltpu.VMEM(out_scratch, BF),
            pltpu.VMEM((2, seq, width), F32),
            pltpu.VMEM((2, seq, width), BF),
            pltpu.VMEM((2, seq, width), BF),
            pltpu.VMEM((2, seq, width), BF),
            pltpu.VMEM((2, seq, width), F32),
            pltpu.VMEM((2, seq, width), BF),
            pltpu.VMEM((2, seq, ext), BF),
            pltpu.VMEM((4, width), F32),
        ],
        "middle_back",
        4 * seq * width * ext,
        smem=(ids, keep),
        vmem_ins=(nv,),
    )


def attn_backward(pairs, grad, q, k, v):
    _, seq, _ = q.shape
    n = len(pairs)

    def body(small, ins, outs, scratch, loads):
        q_s, k_s, v_s, do_s, dq_s, dk_s, dv_s, bs_s = scratch
        groups = []
        for u in range(2 * n):
            cols = slice(pairs[u // 2] * 128, (pairs[u // 2] + 1) * 128)
            groups.append(
                loads.start([(ins[j].at[u % 2, :, cols], scratch[j].at[u]) for j in range(4)])
            )
        half = lax.broadcasted_iota(jnp.int32, (1, 128), 1) // HEAD_DIM
        for group in groups:
            loads.wait(group)

        def unit(u, carry):
            q2, k2, v2, do2 = q_s[u], k_s[u], v_s[u], do_s[u]
            dq = dk = dv = None
            for h in range(2):
                mask = (half == h).astype(BF)
                km, qm, dom = k2 * mask, q2 * mask, do2 * mask
                scores = dot(km, q2, NT)
                row = lax.broadcasted_iota(jnp.int32, scores.shape, 0)
                scores = jnp.where(row < VALID, scores, -1e30)
                e = jnp.exp(scores - jnp.max(scores, axis=0, keepdims=True))
                probs = e * (1.0 / jnp.sum(e, axis=0, keepdims=True))
                grad_probs = dot(v2, dom, NT)
                row_dot = jnp.sum(probs * grad_probs, axis=0, keepdims=True)
                grad_scores = (probs * (grad_probs - row_dot)).astype(BF)
                v_piece = dot(probs.astype(BF), dom, NN)
                k_piece = dot(grad_scores, qm, NN)
                q_piece = dot(grad_scores, km, TN)
                dq = q_piece if dq is None else dq + q_piece
                dk = k_piece if dk is None else dk + k_piece
                dv = v_piece if dv is None else dv + v_piece
            dq = dq * HEAD_DIM**-0.5
            bs_s[u, 0:1, :] = jnp.sum(dq, axis=0, keepdims=True)
            bs_s[u, 1:2, :] = jnp.sum(dv, axis=0, keepdims=True)
            dq_s[u] = dq.astype(BF)
            dk_s[u] = dk.astype(BF)
            dv_s[u] = dv.astype(BF)
            return carry

        lax.fori_loop(0, 2 * n, unit, 0)
        done = [loads.start([(scratch[4 + j], outs[0].at[j])]) for j in range(3)]
        done.append(loads.start([(bs_s, outs[1])]))
        for group in done:
            loads.wait(group)

    grads, sums = call(
        body,
        [q, k, v, grad],
        [sds((3, 2 * n, seq, 128), BF), sds((2 * n, 2, 128), F32)],
        [pltpu.VMEM((2 * n, seq, 128), BF)] * 7 + [pltpu.VMEM((2 * n, 2, 128), F32)],
        "attn_backward",
        0,
    )
    return grads.reshape(3 * n, 2 * seq, 128), jnp.sum(sums.reshape(n, 2, 2, 128), axis=1)


def finish_layer(ids, keep, nv, middle, part, recv, nd, aligned):
    _, seq, width = middle.shape

    def body(small, ins, outs, scratch, loads):
        ids_ref, keep_ref, nv_ref = small
        mine = ids_ref[0]
        mid_s, part_s, recv_s, out_s = scratch
        groups = [loads.start([(ins[i].at[mine], scratch[i])]) for i in range(3)]
        for group in groups:
            loads.wait(group)
        total = part_s[...].astype(F32) + recv_s[...].astype(F32) + nv_ref[5:6, :]
        out_s[...] = (mid_s[...] + keep_ref[mine] * total).astype(BF)
        loads.wait(loads.start(block_stores(ids_ref, out_s, outs[0], nd, aligned)))

    return call(
        body,
        [middle, part, recv],
        [sds((seq, width), BF)],
        [pltpu.VMEM((seq, width), F32)] + [pltpu.VMEM((seq, width), BF)] * 3,
        "finish_layer",
        100 * seq * width,
        smem=(ids, keep),
        vmem_ins=(nv,),
    )[0]


def finish_tokens(ids, nv, tok, part, recv, gmid, rest, nd, aligned):
    _, seq, width = tok.shape
    n_dest, z_n = rest.shape[:2]
    bd = width // nd

    def body(small, ins, outs, scratch, loads):
        ids_ref, nv_ref = small
        mine = ids_ref[0]
        tok_s, part_s, recv_s, gm_s, out_s, cs_s, rest_s = scratch
        g_rest = loads.start([(ins[4], rest_s)])
        groups = [
            loads.start(
                [
                    (ins[0].at[a], tok_s.at[a]),
                    (ins[2].at[a], part_s.at[a]),
                    (ins[3].at[a], recv_s.at[a]),
                ]
            )
            for a in range(2)
        ]
        g_mid = loads.start([(ins[1], gm_s)])
        for group in groups:
            loads.wait(group)
        done = []
        for i in range(2):
            a = mine if i == 0 else 1 - mine
            hat, inverse = norm_parts(tok_s[a].astype(F32))
            grad_one = part_s[a].astype(F32) + recv_s[a].astype(F32)
            gain_sum = jnp.sum(grad_one * hat, axis=0, keepdims=True)
            shift_sum = jnp.sum(grad_one, axis=0, keepdims=True)
            if i == 0:
                cs_s[0:1, :] = gain_sum
                cs_s[1:2, :] = shift_sum
                loads.wait(g_mid)
                value = gm_s[...] + norm_back(grad_one, hat, inverse, nv_ref[0:1, :])
                out_s[...] = value.astype(BF)
                done.append(loads.start(block_stores(ids_ref, out_s, outs[0], nd, aligned)))
            else:
                cs_s[0:1, :] = cs_s[0:1, :] + gain_sum
                cs_s[1:2, :] = cs_s[1:2, :] + shift_sum
        loads.wait(g_rest)
        for n in range(n_dest if aligned else 0):
            for kz in range(z_n):
                p = n % (nd // z_n) * z_n + kz
                rest_s[n, kz, 0:2, :] = cs_s[:, p * bd : (p + 1) * bd]
        done.append(loads.start([(cs_s, outs[1])]))
        done += [loads.start([(rest_s.at[n], outs[2 + n])]) for n in range(n_dest)]
        for group in done:
            loads.wait(group)

    return call(
        body,
        [tok, gmid, part, recv, rest],
        [sds((seq, width), BF), sds((2, width), F32)] + [sds(rest.shape[1:], F32)] * n_dest,
        [pltpu.VMEM((2, seq, width), BF)] * 3
        + [pltpu.VMEM((seq, width), F32), pltpu.VMEM((seq, width), BF), pltpu.VMEM((2, width), F32)]
        + [pltpu.VMEM(rest.shape, F32)],
        "finish_tokens",
        200 * seq * width,
        smem=(ids,),
        vmem_ins=(nv,),
    )


class Grid3:
    def __init__(self, dp, tx):
        self.dp, self.tx = dp, tx
        self.y = 2 if dp % 2 == 0 else 1
        self.z = dp // self.y

    def send_z(self, value, k):
        return lax.ppermute(value, "dp", [(i, i ^ (k * self.y)) for i in range(self.dp)])

    def send_y(self, value, k):
        return lax.ppermute(value, "dp", [(i, i ^ k) for i in range(self.dp)])

    def send_xy(self, value, kx, ky):
        count = self.dp * self.tx
        pairs = [(i, ((i // self.tx) ^ ky) * self.tx + ((i % self.tx) ^ kx)) for i in range(count)]
        return lax.ppermute(value, ("dp", "tx"), pairs)

    def send_x(self, value, k):
        return lax.ppermute(value, "tx", [(i, i ^ k) for i in range(self.tx)])


def swap_core(value):
    return lax.ppermute(value, "core", [(0, 1), (1, 0)])


def after(values, gate):
    return lax.optimization_barrier((values, gate))[0]


def gather_z(grid, part_a, part_b, gate=None):
    rows = part_a.shape[0]
    both = jnp.concatenate([part_a, part_b], axis=0)
    all_z = [both] + [grid.send_z(both, k) for k in range(1, grid.z)]
    if gate is not None:
        all_z = after(all_z, gate)
    return jnp.stack([v[:rows] for v in all_z]), jnp.stack([v[rows:] for v in all_z])


def gather_first(grid, a_z, b_z):
    a_y = [a_z] + [grid.send_y(a_z, k) for k in range(1, grid.y)]
    b_x = [b_z] + [grid.send_x(b_z, k) for k in range(1, grid.tx)]
    return a_y, b_x


def join(pieces):
    return [jnp.concatenate(part) for part in pieces]


def gather_last(grid, a_y, b_x):
    a_all = [a_y] + [grid.send_x(a_y, k) for k in range(1, grid.tx)]
    b_all = [b_x] + [grid.send_y(b_x, k) for k in range(1, grid.y)]
    return a_all, b_all


def padded_bytes(value):
    lead, (rows, lanes) = value.shape[:-2], value.shape[-2:]
    count = -(-rows // 16) * 16 * (-(-lanes // 128) * 128)
    for size in lead:
        count *= size
    return count * value.dtype.itemsize


def add_pieces(groups, cuts, outs, name):
    arrays = [a for group in groups for a in group]
    starts = [sum(len(g) for g in groups[:i]) for i in range(len(groups))]
    last = {}
    for n, cut in enumerate(cuts):
        last[cut[2]] = n

    def body(small, ins, outs_ref, scratch, loads):
        in_s, out_s = scratch[: len(arrays)], scratch[len(arrays) :]
        loaded = [loads.start([(ins[i], in_s[i]) for i in range(starts[g], starts[g] + len(groups[g]))]) for g in range(len(groups))]
        ready, done = set(), []
        for n, (g, spot, which, place) in enumerate(cuts):
            if g not in ready:
                loads.wait(loaded[g])
                ready.add(g)
            total = None
            for i in range(starts[g], starts[g] + len(groups[g])):
                value = in_s[i][spot].astype(F32)
                total = value if total is None else total + value
            out_s[which][place] = total.astype(out_s[which].dtype)
            for w in sorted(w for w in last if last[w] == n):
                done.append(loads.start([(out_s[w], outs_ref[w])]))
        for group in done:
            loads.wait(group)

    held = sum(padded_bytes(a) for a in list(arrays) + list(outs))
    return call(
        body,
        arrays,
        outs,
        [pltpu.VMEM(a.shape, a.dtype) for a in arrays] + [pltpu.VMEM(o.shape, o.dtype) for o in outs],
        name,
        0,
        vmem=held + 8 * 1024 * 1024,
    )


class Scatter:
    def __init__(self, grid, a_all, b_all, name):
        self.grid, self.name, self.bit = grid, name, 0
        self.rows = (a_all[0].shape[1], b_all[0].shape[1])
        a_got = [grid.send_x(a_all[k], k) for k in range(1, grid.tx)]
        b_got = [grid.send_y(b_all[k], k) for k in range(1, grid.y)]
        self.state = ([a_all[0]] + a_got, [b_all[0]] + b_got)

    def second(self, gate):
        grid, z = self.grid, self.grid.z
        a_in, b_in = after(self.state, gate)
        outs = [sds((z,) + a_in[0].shape[1:], BF)] * grid.y + [sds((z,) + b_in[0].shape[1:], BF)] * grid.tx
        full = slice(None)
        cuts = [(0, slice(k * z, (k + 1) * z), k, full) for k in list(range(1, grid.y)) + [0]]
        cuts += [(1, slice(k * z, (k + 1) * z), grid.y + k, full) for k in list(range(1, grid.tx)) + [0]]
        res = add_pieces([a_in, b_in], cuts, outs, self.name + "_add")
        a_y, b_x = res[: grid.y], res[grid.y :]
        a_got = [grid.send_y(a_y[k], k) for k in range(1, grid.y)]
        b_got = [grid.send_x(b_x[k], k) for k in range(1, grid.tx)]
        self.state = ([a_y[0]] + a_got, [b_x[0]] + b_got)
        return a_y[0], b_x[0]

    def along_z(self, gate, extra=None):
        grid = self.grid
        a_in, b_in = after(self.state, gate)
        ra, rb = self.rows
        groups = [a_in, b_in] + ([extra] if extra else [])
        more = extra[0].shape[1] if extra else 0
        order = list(range(1, grid.z)) + [0]
        cuts = []
        for k in order:
            cuts.append((0, k, k, slice(0, ra)))
            cuts.append((1, k, k, slice(ra, ra + rb)))
            if extra:
                cuts.append((2, k, k, slice(ra + rb, ra + rb + more)))
        outs = [sds((ra + rb + more,) + a_in[0].shape[2:], BF)] * grid.z
        both = add_pieces(groups, cuts, outs, self.name + "_addz")
        self.state = [both[0]] + [grid.send_z(both[k], k) for k in range(1, grid.z)]
        return both

    def halve(self, gate):
        grid, (ra, rb) = self.grid, self.rows
        groups = after(self.state, gate)
        if self.bit == 0:
            self.bit, self.left = 1, list(range(grid.z))
        else:
            self.bit, groups = 2 * self.bit, [groups]
        sent = [k for k in self.left if k & self.bit]
        kept = [k for k in self.left if not k & self.bit]
        cuts = []
        for which, ids in ((0, sent), (1, kept)):
            for n, k in enumerate(ids):
                spot = self.left.index(k)
                if len(groups) == 2:
                    cuts.append((0, spot, which, (n, slice(0, ra))))
                    cuts.append((1, spot, which, (n, slice(ra, ra + rb))))
                else:
                    cuts.append((0, spot, which, n))
        outs = [sds((len(kept), ra + rb) + groups[0][0].shape[2:], BF)] * 2
        send, keep = add_pieces(groups, cuts, outs, self.name + "_half")
        self.left = kept
        self.state = [keep, grid.send_z(send, self.bit)]
        return keep

    def finish(self, gate, cuts, outs):
        if self.bit:
            cuts = [((0, rows), which, place) for rows, which, place in cuts]
        cuts = [(0, rows, which, place) for rows, which, place in cuts]
        return add_pieces([after(self.state, gate)], cuts, outs, self.name + "_sum")


def xor_blocks(value, mask, axis):
    count = value.shape[axis]
    bit = 1
    while bit < count:
        shape = value.shape
        split = value.reshape(shape[:axis] + (count // (2 * bit), 2, bit) + shape[axis + 1 :])
        turned = jnp.flip(split, axis=axis + 1).reshape(shape)
        value = jnp.where(jnp.bitwise_and(mask, bit) != 0, turned, value)
        bit *= 2
    return value


def pad_cols(value, width):
    return jnp.pad(value, ((0, 0), (0, width - value.shape[1])))


def per_device(
    tokens,
    cotangent,
    image_mask,
    norm_gains,
    norm_shifts,
    w_qkv,
    b_qv,
    w_out,
    w_up,
    up_bias,
    w_down,
    *,
    dp,
    tx,
):
    grid = Grid3(dp, tx)
    y_n, z_n = grid.y, grid.z
    core = lax.axis_index("core").astype(jnp.int32)
    me_d = lax.axis_index("dp").astype(jnp.int32)
    me_x = lax.axis_index("tx").astype(jnp.int32)
    seq, width = tokens.shape
    _, bd, hw = w_qkv.shape
    fw = w_up.shape[1]
    ext, hid = tx * hw, tx * fw
    hh, fh = hw // 2, fw // 2
    aligned = bd % 128 == 0 and hh % 128 == 0 and fh % 128 == 0
    rel = [kz * y_n + ky for ky in range(y_n) for kz in range(z_n)]

    def from_abs(value, axis):
        shape = value.shape
        value = value.reshape(shape[:axis] + (z_n, y_n) + shape[axis + 1 :])
        return jnp.swapaxes(value, axis, axis + 1).reshape(shape)

    def to_rel(value, axis):
        shape = value.shape
        value = value.reshape(shape[:axis] + (y_n, z_n) + shape[axis + 1 :])
        return jnp.swapaxes(value, axis, axis + 1).reshape(shape)

    ids = jnp.stack([core, me_d] + [jnp.bitwise_xor(me_d, k) for k in rel])
    keep = lax.dynamic_slice(image_mask, (2 * me_x,), (2,)).astype(F32)

    lane = max(bd, hh)
    small = jnp.concatenate(
        [
            pad_cols(norm_gains, lane),
            pad_cols(norm_shifts, lane),
            pad_cols(b_qv, lane),
            pad_cols(up_bias[None], lane),
            jnp.zeros((7, lane), BF),
        ]
    )
    qkv_a = pad_cols(w_qkv[:, :, :hh].reshape(3 * bd, hh), lane)
    qkv_b = pad_cols(w_qkv[:, :, hh:].reshape(3 * bd, hh), lane)
    first_a = jnp.concatenate([qkv_a, pad_cols(w_out[:hh], lane), small])
    first_b = jnp.concatenate([qkv_b, pad_cols(w_out[hh:], lane)])
    own = [tokens, cotangent]
    other = [swap_core(value) for value in own]
    if aligned:
        tok, cot = arrange_pair(ids, own, other, dp)
    else:

        def arrange(own, other):
            pair = jnp.where(core == 0, jnp.stack([own, other]), jnp.stack([other, own]))
            pair = xor_blocks(pair.reshape(2, seq, dp, bd), me_d, 2)
            return from_abs(pair, 2).reshape(2, seq, width)

        tok, cot = [arrange(own[i], other[i]) for i in range(2)]
    c1_z = gather_z(grid, first_a, first_b, gate=tok)
    c1_h = gather_first(grid, *c1_z)
    c1_h = join(c1_h)
    c1a, c1b = gather_last(grid, *c1_h)
    up_halves = after((w_up[:, :fh], w_up[:, fh:]), c1_h)
    row0 = 3 * bd + hh
    if aligned and 128 % (hw // dp) == 0 and (fw // dp) % 128 == 0:
        c1a, c1b = after((c1a, c1b), (c1a, c1b))
        nv, bq, bu = vectors(ids, c1a, row0, dp, y_n, bd, hw // dp, fw // dp)
    else:
        nv = c1a[0][:, row0 : row0 + 6, :bd].transpose(1, 0, 2).reshape(6, width).astype(F32)
        tail = jnp.stack([v[:, row0 + 6 : row0 + 9] for v in c1a])
        tail = xor_blocks(to_rel(tail, 1), me_d, 1)
        bq = tail[:, :, :2, : hw // dp].transpose(2, 0, 1, 3).reshape(2, ext).astype(F32)
        bu = tail[:, :, 2, : fw // dp].reshape(1, hid).astype(F32)
    grad_top = cot * keep.astype(BF)[:, None, None]

    up_z = gather_z(grid, *up_halves, gate=nv)
    up_h = gather_first(grid, *up_z)
    dn_halves = after((w_down[:fh], w_down[fh:]), up_z)

    if aligned:
        every, wq_plan, wo_plan, up_plan, dn_plan = slice(None), [[], [], []], [], [], []
        for kx in range(tx):
            halves = [slice(kx * hw, kx * hw + hh), slice(kx * hw + hh, (kx + 1) * hw)]
            f_halves = [slice(kx * fw, kx * fw + fh), slice(kx * fw + fh, (kx + 1) * fw)]
            own = slice(kx * z_n, (kx + 1) * z_n)
            for i in range(3):
                src = slice(i * bd, (i + 1) * bd)
                wq_plan[i].append((kx, (every, src), (i, every, every, halves[0])))
                for ky in range(y_n):
                    dst = (i, slice(ky * z_n, (ky + 1) * z_n), every, halves[1])
                    wq_plan[i].append((tx + ky, (own, src), dst))
            src = slice(3 * bd, 3 * bd + hh)
            dn_plan += [[], []]
            for ky in range(y_n):
                for kz in range(z_n):
                    p, r = ky * z_n + kz, kx * z_n + kz
                    cols = slice(p * bd, (p + 1) * bd)
                    wo_plan.append((kx, (p, src), (halves[0], cols)))
                    wo_plan.append((tx + ky, (r, src), (halves[1], cols)))
                    dn_plan[-2].append((kx, (p,), (f_halves[0], cols)))
                    dn_plan[-1].append((tx + ky, (r,), (f_halves[1], cols)))
            up_plan += [[(kx, (every,), (every, f_halves[0]))], []]
            for ky in range(y_n):
                rows = slice(kx * z_n * bd, (kx + 1) * z_n * bd)
                dst = (slice(ky * z_n * bd, (ky + 1) * z_n * bd), f_halves[1])
                up_plan[-1].append((tx + ky, (rows,), dst))
        c1 = c1a + c1b
        wqkv = (c1, wq_plan, (3, dp, bd, ext))
        wout = (c1, [wo_plan], (ext, width))
    else:

        def whole(a_all, b_all):
            a = jnp.stack(a_all)
            b = jnp.stack(b_all).reshape((y_n, tx, z_n) + b_all[0].shape[1:])
            b = b.transpose(1, 0, 2, 3, 4).reshape(a.shape[:2] + b.shape[3:])
            return jnp.stack([a, b], axis=1)

        c1 = whole([v[:, :row0] for v in c1a], c1b)
        qkv = c1[:, :, :, : 3 * bd, :hh].reshape(tx, 2, dp, 3, bd, hh)
        qkv = qkv.transpose(3, 2, 4, 0, 1, 5).reshape(3, dp, bd, ext)
        out = c1[:, :, :, 3 * bd :, :bd].transpose(0, 1, 3, 2, 4).reshape(ext, width)
        all_of = [[(0, (slice(None),), (slice(None),))]]
        wqkv = ([qkv], all_of, qkv.shape)
        wout = ([out], all_of, out.shape)

    rows2 = 2 * seq

    res = attn_forward(0, after(tok, up_z), nv, bq, wqkv, wout, None)
    part0 = res[5]
    up_h = join(after(up_h, part0))
    upa, upb = gather_last(grid, *up_h)
    dn_halves = after(dn_halves, up_h)
    res = attn_forward(1, after(tok, up_h), nv, bq, wqkv, wout, res[:5])
    recv0 = swap_core(after(part0, res[5]))
    parts = [(part0, recv0), (res[5], swap_core(res[5]))]
    first, q, k, v, att = res[:5]
    upa, upb = after((upa, upb), res[5])
    dn_z = gather_z(grid, *dn_halves, gate=(upa, upb))
    dn_h = gather_first(grid, *dn_z)
    if aligned:
        wup = ([v.reshape(-1, fh) for v in upa + upb], up_plan, (width, hid))
    else:
        up_w = whole(upa, upb).transpose(2, 3, 0, 1, 4).reshape(width, hid)
        wup = ([up_w], all_of, up_w.shape)
    part, recv = parts[0]
    state = mlp_up(0, tok, part, recv, keep, nv, bu, wup, fh, None)
    dna, dnb = gather_last(grid, *join(after(dn_h, state[1])))
    part, recv = parts[1]
    state = mlp_up(1, tok, part, recv, keep, nv, bu, wup, fh, state)
    if aligned:
        wdown = (dna + dnb, dn_plan, (hid, width))
    else:
        down_w = whole(dna, dnb).transpose(0, 1, 3, 2, 4).reshape(hid, width)
        wdown = ([down_w], all_of, down_w.shape)
    middle, second, act, dact = state
    flat = lambda value: value.reshape(rows2, value.shape[2])
    act2, sec2, grad2 = flat(act), flat(second), flat(grad_top)

    full = slice(None)
    a_spots = [(p, slice(p * bd, (p + 1) * bd)) for p in range(dp)]

    def by_left(l_index, r_index, size, row0):
        tasks, rows = [], slice(row0, row0 + size // 2)
        halves = slice(0, size // 2), slice(size // 2, size)
        for kx in range(tx):
            stores = [(kx, (p, rows), halves[0], cols) for p, cols in a_spots]
            for p, cols in a_spots:
                ky, kz = p // z_n, p % z_n
                stores.append((tx + ky, (kx * z_n + kz, rows), halves[1], cols))
            tasks.append((l_index, slice(kx * size, (kx + 1) * size), r_index, slice(0, width), stores))
        return tasks

    def by_right(l_index, r_index, size, row0, lanes, spare=False, first=0):
        tasks, each = [], size // 2 // lanes
        for kx in range(tx):
            stores = []
            for j in range(each):
                rows = slice(row0 + j * bd, row0 + (j + 1) * bd)
                cols = [slice((h * each + j) * lanes, (h * each + j + 1) * lanes) for h in range(2)]
                rows = (rows, slice(0, lanes)) if spare else (rows,)
                for p, r_sl in a_spots:
                    ky, kz = p // z_n, p % z_n
                    stores.append((kx, (p,) + rows, r_sl, cols[0]))
                    stores.append((tx + ky, (kx * z_n + kz,) + rows, r_sl, cols[1]))
            cols = slice(first + kx * size, first + (kx + 1) * size)
            tasks.append((l_index, slice(0, width), r_index, cols, stores))
        return tasks

    def pieces(rows, lanes):
        return [(dp, rows, lanes)] * tx + [(tx * z_n, rows, lanes)] * y_n

    def send_grad(parts, name):
        return Scatter(grid, list(parts[:tx]), list(parts[tx:]), name)

    grads = weight_grad([act2], [grad2], by_left(0, 0, fw, 0), pieces(fh, bd), "down_grad", 0, fh)
    down_rs = send_grad(grads, "down")
    grad_in = after(grad2, grads[-1])
    low_pre, bias_up, two_part, mlp_part = mlp_back(grad_in, act2, flat(dact), wdown, wup, fh)
    mlp_part = mlp_part.reshape(2, seq, width)
    two_recv = swap_core(two_part)
    down_half = down_rs.second(bias_up)
    up_rows = fh // bd * bd
    sec_in = after(sec2, down_half)
    tasks = by_right(0, 0, fw, 0, bd)
    grads = weight_grad([sec_in], [low_pre], tasks, pieces(up_rows, bd), "up_grad", 0, up_rows)
    up_rs = send_grad(grads, "up")
    gmid, gattn, grad_att, col = middle_back(
        ids, middle, two_part, after(two_recv, grads[-1]), cot, keep, nv, wout
    )
    down_zs = down_rs.along_z(col)
    row0 = 3 * bd
    last_shapes = pieces(row0 + hh, bd)
    att_in = after(flat(att), down_zs)
    tasks = by_left(0, 0, hw, 0)
    out_grads = weight_grad(
        [att_in], [flat(gattn)], tasks, last_shapes, "out_grad", row0, row0 + hh
    )

    up_half = up_rs.second(out_grads[-1])
    n_pairs = ext // 128
    split = hh == 128 and bd == 128
    firsts = list(range(1, n_pairs)) if split else list(range(n_pairs))
    left_a, bias_a = attn_backward(firsts, after(grad_att, up_half), q, k, v)
    grad_down = down_rs.finish(bias_a, [(full, 0, full)], [sds((fw, bd), F32)])[0]
    mlp_recv = swap_core(after(mlp_part, bias_a))
    gate = up_rs.halve(grad_down) if z_n > 1 else grad_down
    first_in = after(flat(first), gate)
    if split:
        stores, count = [], len(firsts)
        for i in range(3):
            rows = slice(i * bd, (i + 1) * bd)
            for n, pair in enumerate(firsts):
                kx, cols = pair // 2, slice((i * count + n) * 128, (i * count + n + 1) * 128)
                for p, r_sl in a_spots:
                    ky, kz = p // z_n, p % z_n
                    spot = (kx - 1, (p, rows)) if pair % 2 == 0 else (tx - 1 + ky, (kx * z_n + kz, rows))
                    stores.append(spot + (r_sl, cols))
        tasks = [(0, slice(0, width), 0, slice(0, 384 * count), stores)]
        sent = weight_grad(
            [first_in], [left_a], tasks, last_shapes[1:], "qkv_grad", 0, row0, out_grads[1:]
        )
        left_b, bias_b = attn_backward([0], after(grad_att, (sent[: tx - 1], sent[tx:])), q, k, v)
        gate = (bias_b, mlp_recv)
        while 2 * up_rs.bit < z_n:
            gate = up_rs.halve(gate)
        stores = []
        for i in range(3):
            rows, cols = slice(i * bd, (i + 1) * bd), slice(i * 128, (i + 1) * 128)
            stores += [(0, (p, rows), r_sl, cols) for p, r_sl in a_spots]
        tasks = [(0, slice(0, width), 0, slice(0, 384), stores)]
        kept = weight_grad(
            [after(first_in, gate)],
            [left_b],
            tasks,
            last_shapes[:1],
            "qkv_keep",
            0,
            row0,
            out_grads[:1],
        )
        grads = list(kept) + list(sent)
        lefts, starts = [left_a, left_b], [1, 0]
        bias_qv = jnp.concatenate([bias_b, bias_a])
        gate = kept[0]
    else:
        while 2 * up_rs.bit < z_n:
            gate = up_rs.halve((gate, mlp_recv))
        makers = [by_right(0, 0, hw, i * bd, hh, hh < bd, i * ext) for i in range(3)]
        tasks = [task for maker in makers for task in maker]
        grads = weight_grad(
            [after(first_in, gate)],
            [left_a],
            tasks,
            last_shapes,
            "qkv_grad",
            0,
            row0,
            out_grads,
            hh < bd,
        )
        lefts, starts = [left_a], [0]
        bias_qv = bias_a
        gate = grads[-1]
    bias_qv = bias_qv.transpose(1, 0, 2).reshape(2, ext)
    qkv_rs = send_grad(grads, "qkv")
    lefts = after(lefts, gate)
    one_part = input_grad(lefts, starts, wqkv, width)
    one_recv = swap_core(one_part)
    cuts = []
    for h in range(2):
        for j in range(fh // bd):
            rows = slice(h * up_rows + j * bd, h * up_rows + (j + 1) * bd)
            cuts.append((rows, 0, (full, slice(h * fh + j * bd, h * fh + (j + 1) * bd))))
    up_cuts = cuts
    qkv_half = qkv_rs.second(one_part)
    wide = max(bd, hw // dp, fw // dp)
    vec = jnp.concatenate([jnp.zeros((2, width), F32), col])
    vec = vec.reshape(6, y_n, z_n, bd).transpose(1, 2, 0, 3)
    bias_qv = bias_qv.reshape(2, tx, dp, hw // dp).transpose(2, 1, 0, 3)
    bias_up = bias_up.reshape(tx, 1, dp, fw // dp).transpose(2, 0, 1, 3)
    bias = jnp.concatenate(
        [
            jnp.pad(value, ((0, 0), (0, 0), (0, 0), (0, wide - value.shape[3])))
            for value in (bias_qv, bias_up)
        ],
        axis=2,
    )
    bias = from_abs(xor_blocks(bias, me_d, 0), 0).reshape(y_n, z_n, tx, 3, wide)
    bias = bias.transpose(2, 0, 1, 3, 4)
    vec = jnp.pad(vec, ((0, 0), (0, 0), (0, 0), (0, wide - bd)))
    vec = jnp.broadcast_to(vec, (tx,) + vec.shape)
    rest = jnp.concatenate([vec, bias, jnp.zeros((tx, y_n, z_n, 7, wide), F32)], axis=3)
    rest = rest.reshape(tx * y_n, z_n, 16, wide)
    grad_tokens, one_sums, *small = finish_tokens(
        ids, nv, tok, one_part, after(one_recv, qkv_half), gmid, rest, dp, aligned
    )
    if not aligned:
        ones = jnp.pad(one_sums.reshape(2, y_n, z_n, bd), ((0, 14), (0, 0), (0, 0), (0, wide - bd)))
        ones = ones.transpose(1, 2, 0, 3)
        small = [value + ones[n % y_n] for n, value in enumerate(small)]
    small = after(small, qkv_rs.state)
    got = small[:1]
    for n in range(1, tx * y_n):
        got.append(grid.send_xy(small[n], n // y_n, n % y_n))
    grad_up = up_rs.finish(one_sums, up_cuts, [sds((bd, fw), F32)])[0]
    cuts, outs = [], [sds((3, bd, hw), F32), sds((hw, bd), F32)]
    last_rows = row0 + hh
    for h in range(2):
        for i in range(3):
            rows = slice(h * last_rows + i * bd, h * last_rows + (i + 1) * bd)
            rows = (rows, slice(0, hh)) if hh < bd else rows
            cuts.append((rows, 0, (i, full, slice(h * hh, (h + 1) * hh))))
        rows = slice(h * last_rows + row0, (h + 1) * last_rows)
        cuts.append((rows, 1, (slice(h * hh, (h + 1) * hh),)))
    if wide == bd:
        qkv_zs = qkv_rs.along_z(grad_up, got)
        cuts.append((slice(2 * last_rows, 2 * last_rows + 16), 2, full))
        outs.append(sds((16, wide), F32))
    else:
        qkv_zs = qkv_rs.along_z(grad_up)
    layer_out = finish_layer(
        ids, keep, nv, middle, after(mlp_part, qkv_zs), mlp_recv, dp, aligned
    )
    res = qkv_rs.finish(layer_out, cuts, outs)
    grad_qkv, grad_out = res[:2]
    if wide == bd:
        both = res[2]
    else:
        both, bit = sum(got), 1
        while bit < z_n:
            both = both.reshape((-1, 2) + both.shape[1:])
            both = both[:, 0] + grid.send_z(both[:, 1], bit)
            bit *= 2
        both = both[0]
    if not aligned:

        def restore(value):
            value = xor_blocks(to_rel(value.reshape(seq, dp, bd), 1), me_d, 1)
            return value.reshape(seq, width)

        layer_out, grad_tokens = restore(layer_out), restore(grad_tokens)

    share = bd // (2 * tx)
    mine = lax.dynamic_slice(both[:6, :bd], (0, (2 * me_x + core) * share), (6, share))

    return (
        layer_out,
        grad_tokens,
        mine[0:3:2],
        jnp.concatenate([mine[1:2], mine[3:6]]),
        grad_qkv,
        both[6:8, : hw // dp],
        grad_out,
        grad_up,
        both[8, : fw // dp],
        grad_down,
    )


def solution(mesh):
    dp, tensor = mesh.shape["dp"], mesh.shape["tensor"]
    split = Mesh(mesh.devices.reshape(dp, tensor // 2, 2), ("dp", "tx", "core"))
    every = ("dp", "tx", "core")
    tensor_axes = ("tx", "core")
    in_specs = (
        P(every, None),
        P(every, None),
        P("dp"),
        P(None, "dp"),
        P(None, "dp"),
        P(None, "dp", tensor_axes),
        P(None, ("tx", "core", "dp")),
        P(tensor_axes, "dp"),
        P("dp", tensor_axes),
        P(("tx", "core", "dp")),
        P(tensor_axes, "dp"),
    )
    out_specs = (
        P(every, None),
        P(every, None),
        P(None, every),
        P(None, every),
        P(None, "dp", tensor_axes),
        P(None, ("tx", "core", "dp")),
        P(tensor_axes, "dp"),
        P("dp", tensor_axes),
        P(("tx", "core", "dp")),
        P(tensor_axes, "dp"),
    )
    return jax.shard_map(
        functools.partial(per_device, dp=dp, tx=tensor // 2),
        mesh=split,
        in_specs=in_specs,
        out_specs=out_specs,
        check_vma=False,
    )
```

```python
import functools

import jax
import jax.numpy as jnp
from jax import lax
from jax.experimental import pallas as pl
from jax.experimental.pallas import tpu as pltpu
from jax.sharding import Mesh, PartitionSpec as P

HEAD_DIM = 64
VALID = 577
SEQ = 584
BF = jnp.bfloat16
F32 = jnp.float32
VMEM_LIMIT = 60 * 1024 * 1024
WHOLE_VMEM = ("arrange_pair", "vectors", "attn_forward", "mlp_up", "down_grad", "mlp_back")
COST_SCALE = 1.0
COST = {
    "arrange_pair": 5,
    "vectors": 3,
    "attn_forward": 16,
    "mlp_up": 10,
    "down_grad": 11,
    "mlp_back": 22,
    "up_grad": 11,
    "middle_back": 0,
    "out_grad": 8,
    "attn_backward": 18,
    "qkv_grad": 7,
    "qkv_keep": 0,
    "up_half": 0,
    "grad_one": 0,
    "qkv_add": 30,
    "finish_layer": 0,
    "up_sum": 0,
    "finish_tokens": 9,
}
NT = (((1,), (1,)), ((), ()))
TN = (((0,), (0,)), ((), ()))
NN = (((1,), (0,)), ((), ()))


def dot(left, right, dims):
    return lax.dot_general(left, right, dims, preferred_element_type=F32)


class Loads:
    def __init__(self, sems):
        self.sems, self.groups = sems, []

    def start(self, pairs):
        sem = self.sems.at[len(self.groups)]
        copies = [pltpu.make_async_copy(src, dst, sem) for src, dst in pairs]
        for copy in copies:
            copy.start()
        self.groups.append(copies)
        return len(self.groups) - 1

    def wait(self, group):
        for copy in self.groups[group]:
            copy.wait()


def padded_bytes(value):
    lead, (rows, lanes) = value.shape[:-2], value.shape[-2:]
    count = -(-rows // 16) * 16 * (-(-lanes // 128) * 128)
    for size in lead:
        count *= size
    return count * jnp.dtype(value.dtype).itemsize


def call(body, ins, outs, scratch, name, flops, aliases=None, smem=(), sems=48, vmem_ins=(), spare=12):
    n_smem, n_vmem, n_in, n_out = len(smem), len(vmem_ins), len(ins), len(outs)
    moved = sum(a.size * a.dtype.itemsize for a in ins) + sum(
        o.size * o.dtype.itemsize for o in outs
    )

    def kernel(*refs):
        first = n_smem + n_vmem
        small = refs[:first]
        in_refs = refs[first : first + n_in]
        out_refs = refs[first + n_in : first + n_in + n_out]
        rest = refs[first + n_in + n_out :]
        body(small, in_refs, out_refs, rest[:-1], Loads(rest[-1]))

    held = sum(padded_bytes(piece) for piece in scratch) + spare * 1024 * 1024
    vmem = VMEM_LIMIT if name in WHOLE_VMEM else min(held, VMEM_LIMIT)
    flops = max(COST.get(name, 3), 0.02) * COST_SCALE * 1.15e9
    moved = 0
    any_spec = pl.BlockSpec(memory_space=pl.ANY)
    return pl.pallas_call(
        kernel,
        out_shape=outs,
        in_specs=[pl.BlockSpec(memory_space=pltpu.SMEM)] * n_smem
        + [pl.BlockSpec(memory_space=pltpu.VMEM)] * n_vmem
        + [any_spec] * n_in,
        out_specs=[any_spec] * n_out,
        scratch_shapes=list(scratch) + [pltpu.SemaphoreType.DMA((sems,))],
        input_output_aliases={n_smem + n_vmem + i: o for i, o in (aliases or {}).items()},
        compiler_params=pltpu.CompilerParams(vmem_limit_bytes=vmem),
        cost_estimate=pl.CostEstimate(flops=int(flops), bytes_accessed=int(flops // 1000), transcendentals=0),
        name=name,
    )(*smem, *vmem_ins, *ins)


def norm_parts(rows):
    center = rows - jnp.mean(rows, axis=1, keepdims=True)
    inverse = lax.rsqrt(jnp.mean(center * center, axis=1, keepdims=True) + 1e-05)
    return center * inverse, inverse


def norm_back(grad_norm, scaled, inverse, gain_row):
    grad_hat = grad_norm * gain_row
    first_mean = jnp.mean(grad_hat, axis=1, keepdims=True)
    second_mean = jnp.mean(grad_hat * scaled, axis=1, keepdims=True)
    return inverse * (grad_hat - first_mean - scaled * second_mean)


def sds(shape, dtype):
    return jax.ShapeDtypeStruct(shape, dtype)


def arrange_pair(ids, own, other, nd):
    n = len(own)
    rows, width = own[0].shape
    bd = width // nd

    def body(small, ins, outs, scratch, loads):
        (ids_ref,) = small
        mine = ids_ref[0]
        in_s, out_s = scratch[: 2 * n], scratch[2 * n :]
        groups = [loads.start([(ins[i], in_s[i])]) for i in range(2 * n)]
        done = []
        for i in range(2 * n):
            loads.wait(groups[i])
            for p in range(nd):
                src = pl.ds(pl.multiple_of(ids_ref[2 + p] * bd, 128), bd)
                out_s[i][:, p * bd : (p + 1) * bd] = in_s[i][:, src]
            spot = mine if i < n else 1 - mine
            done.append(loads.start([(out_s[i], outs[i % n].at[spot])]))
        for group in done:
            loads.wait(group)

    return call(
        body,
        list(own) + list(other),
        [sds((2, rows, width), BF)] * n,
        [pltpu.VMEM((rows, width), BF)] * (4 * n),
        "arrange_pair",
        0,
        smem=(ids,),
    )


def vectors(ids, gathered, row0, nd, y_n, bd, qv, up):
    tx, z_n = len(gathered), nd // y_n

    def body(small, ins, outs, scratch, loads):
        ids_ref, rows_s, nv_s, bq_s, bu_s = small[0], *scratch
        rows = pl.ds(row0, 16)
        loads.wait(loads.start([(ins[k].at[:, rows, :], rows_s.at[k]) for k in range(tx)]))
        for p in range(nd):
            nv_s[:, p * bd : (p + 1) * bd] = rows_s[0, p].astype(F32)[:6, :bd]
        for k in range(tx):
            pieces = []
            for d in range(nd):
                rel = ids_ref[1] ^ d
                spot = (rel % y_n) * z_n + rel // y_n
                piece = rows_s[k, spot].astype(F32)
                bu_s[:, (k * nd + d) * up : (k * nd + d + 1) * up] = piece[8:9, :up]
                pieces.append(piece[6:8, :])
            each = 128 // qv
            for start in range(0, nd, each):
                total = pieces[start]
                for i in range(1, each):
                    total = total + pltpu.roll(pieces[start + i], i * qv, 1)
                bq_s[:, (k * nd + start) * qv : (k * nd + start + each) * qv] = total
        loads.wait(loads.start([(nv_s, outs[0]), (bq_s, outs[1]), (bu_s, outs[2])]))

    shapes = [(6, nd * bd), (2, tx * nd * qv), (1, tx * nd * up)]
    return call(
        body,
        list(gathered),
        [sds(s, F32) for s in shapes],
        [pltpu.VMEM((tx, nd, 16, gathered[0].shape[2]), BF)] + [pltpu.VMEM(s, F32) for s in shapes],
        "vectors",
        0,
        smem=(ids,),
    )


def block_stores(ids_ref, src, dst, nd, aligned):
    if not aligned:
        return [(src, dst)]
    bd = src.shape[1] // nd
    pairs = []
    for p in range(nd):
        cols = pl.ds(pl.multiple_of(ids_ref[2 + p] * bd, 128), bd)
        pairs.append((src.at[:, p * bd : (p + 1) * bd], dst.at[:, cols]))
    return pairs


def weight_loads(loads, groups, refs, scratch):
    return [
        loads.start([(refs[a].at[src], scratch.at[dst]) for a, src, dst in plan])
        for plan in groups
    ]


def softmax_rows(q2, k2):
    scores = dot(q2, k2, NT)
    lane = lax.broadcasted_iota(jnp.int32, scores.shape, 1)
    scores = jnp.where(lane < VALID, scores, -1e30)
    e = jnp.exp(scores - jnp.max(scores, axis=1, keepdims=True))
    return e * (1.0 / jnp.sum(e, axis=1, keepdims=True))


def attn_forward(image, tok, nv, bq, wqkv, wout, prev):
    seq, width = tok.shape[1:]
    qkv_arrays, qkv_plan, qkv_scratch = wqkv
    out_arrays, out_plan, out_scratch = wout
    ext = qkv_scratch[-1]
    n_prev = 0 if prev is None else len(prev)
    nq, no = len(qkv_arrays), len(out_arrays)

    def body(small, ins, outs, scratch, loads):
        nv_ref, bq_ref = small
        tok_ref, ins = ins[0], ins[1 + n_prev :]
        w_s, wo_s, tok_s, first_s, q_s, k_s, v_s, att_s, part_s = scratch
        g_tok = loads.start([(tok_ref.at[image], tok_s)])
        g_w = weight_loads(loads, qkv_plan, ins[:nq], w_s)
        g_o = weight_loads(loads, out_plan, ins[nq:], wo_s)
        loads.wait(g_tok)
        hat, _ = norm_parts(tok_s[...].astype(F32))
        first_s[...] = (hat * nv_ref[0:1, :] + nv_ref[2:3, :]).astype(BF)
        g_first = loads.start([(first_s, outs[0].at[image])])
        low = first_s[...]
        for i, ref in enumerate((q_s, k_s, v_s)):
            if i < len(g_w):
                loads.wait(g_w[i])
            proj = dot(low, w_s[i].reshape(width, ext), NN)
            if i == 0:
                proj = proj + bq_ref[0:1, :]
            if i == 2:
                proj = proj + bq_ref[1:2, :]
            low_proj = proj.astype(BF)
            if i == 0:
                low_proj = low_proj * jnp.asarray(HEAD_DIM**-0.5, BF)
            ref[...] = low_proj
        g_qkv = loads.start(
            [(q_s, outs[1].at[image]), (k_s, outs[2].at[image]), (v_s, outs[3].at[image])]
        )
        half = lax.broadcasted_iota(jnp.int32, (1, 128), 1) // HEAD_DIM

        def pair(i, carry):
            cols = pl.ds(pl.multiple_of(i * 128, 128), 128)
            q2, k2, v2 = q_s[:, cols], k_s[:, cols], v_s[:, cols]
            total = None
            for h in range(2):
                keep = (half == h).astype(BF)
                probs = softmax_rows(q2, k2 * keep).astype(BF)
                piece = dot(probs, v2 * keep, NN)
                total = piece if total is None else total + piece
            att_s[:, cols] = total.astype(BF)
            return carry

        lax.fori_loop(0, ext // 128, pair, 0)
        g_att = loads.start([(att_s, outs[4].at[image])])
        loads.wait(g_o[0])
        part_s[...] = dot(att_s[...], wo_s[...], NN).astype(BF)
        g_part = loads.start([(part_s, outs[5])])
        for group in (g_first, g_qkv, g_att, g_part):
            loads.wait(group)

    shapes = [(2, seq, width)] + [(2, seq, ext)] * 4
    return call(
        body,
        [tok] + list(prev or []) + qkv_arrays + out_arrays,
        [sds(s, BF) for s in shapes] + [sds((seq, width), BF)],
        [
            pltpu.VMEM(qkv_scratch, BF),
            pltpu.VMEM(out_scratch, BF),
            pltpu.VMEM((seq, width), BF),
            pltpu.VMEM((seq, width), BF),
            pltpu.VMEM((seq, ext), BF),
            pltpu.VMEM((seq, ext), BF),
            pltpu.VMEM((seq, ext), BF),
            pltpu.VMEM((seq, ext), BF),
            pltpu.VMEM((seq, width), BF),
        ],
        "attn_forward",
        2 * seq * width * ext * 4 + 16 * seq * seq * ext,
        aliases={1 + i: i for i in range(n_prev)},
        vmem_ins=(nv, bq),
    )


def mlp_up(image, tok, part, recv, keep, nv, bu, wup, step, prev):
    seq, width = tok.shape[1:]
    up_arrays, up_plan, up_scratch = wup
    hid = up_scratch[-1]
    n_prev = 0 if prev is None else len(prev)

    def body(small, ins, outs, scratch, loads):
        keep_ref, nv_ref, bu_ref = small
        tok_ref, part_ref, recv_ref = ins[:3]
        w_s, tok_s, part_s, recv_s, mid_s, sec_s, act_s, dact_s = scratch
        g_in = loads.start([(tok_ref.at[image], tok_s), (part_ref, part_s), (recv_ref, recv_s)])
        g_w = weight_loads(loads, up_plan, ins[3 + n_prev :], w_s)
        loads.wait(g_in)
        total = part_s[...].astype(F32) + recv_s[...].astype(F32) + nv_ref[4:5, :]
        middle = tok_s[...].astype(F32) + keep_ref[image] * total
        mid_s[...] = middle
        hat, _ = norm_parts(middle)
        sec_s[...] = (hat * nv_ref[1:2, :] + nv_ref[3:4, :]).astype(BF)
        g_mid = loads.start([(mid_s, outs[0].at[image]), (sec_s, outs[1].at[image])])
        second = sec_s[...]
        done = []
        for block in range(hid // step):
            if block < len(g_w):
                loads.wait(g_w[block])
            cols = slice(block * step, (block + 1) * step)
            pre = dot(second, w_s[:, cols], NN) + bu_ref[0:1, cols]
            gate = 0.5 * jnp.tanh(0.851 * pre) + 0.5
            act_s[:, cols] = (pre * gate).astype(BF)
            dact_s[:, cols] = (gate + 1.702 * pre * gate * (1.0 - gate)).astype(BF)
            done.append(
                loads.start(
                    [
                        (act_s.at[:, cols], outs[2].at[image, :, cols]),
                        (dact_s.at[:, cols], outs[3].at[image, :, cols]),
                    ]
                )
            )
        for group in [g_mid] + done:
            loads.wait(group)

    outs = [
        sds((2, seq, width), F32),
        sds((2, seq, width), BF),
        sds((2, seq, hid), BF),
        sds((2, seq, hid), BF),
    ]
    return call(
        body,
        [tok, part, recv] + list(prev or []) + up_arrays,
        outs,
        [
            pltpu.VMEM(up_scratch, BF),
            pltpu.VMEM((seq, width), BF),
            pltpu.VMEM((seq, width), BF),
            pltpu.VMEM((seq, width), BF),
            pltpu.VMEM((seq, width), F32),
            pltpu.VMEM((seq, width), BF),
            pltpu.VMEM((seq, hid), BF),
            pltpu.VMEM((seq, hid), BF),
        ],
        "mlp_up",
        2 * seq * width * hid,
        aliases={3 + i: i for i in range(n_prev)},
        smem=(keep,),
        vmem_ins=(nv, bu),
    )


def column_loads(src, dst, start):
    if len(src.shape) == 2:
        return [(src, dst)]
    n, _, width = src.shape
    return [
        (src.at[i], dst.at[:, (start + i) * width : (start + i + 1) * width]) for i in range(n)
    ]


def weight_grad(lefts, rights, tasks, out_shapes, name, lo, hi, prev=None, fill=False):
    rows = lefts[0].shape[0]
    arrays = list(lefts) + list(rights)
    wide = [a.shape[-1] * (a.shape[0] if len(a.shape) == 3 else 1) for a in arrays]
    n_left, n_in = len(lefts), len(arrays)
    prev = list(prev or [])
    last = {}
    for n, task in enumerate(tasks):
        for store in task[4]:
            last[store[0]] = n

    def body(small, ins, outs, scratch, loads):
        in_s, out_s = scratch[:n_in], scratch[n_in:]
        order = []
        for l_index, _, r_index, _, _ in tasks:
            for i in (l_index, n_left + r_index):
                if i not in order:
                    order.append(i)
        groups = {i: loads.start(column_loads(ins[i], in_s[i], 0)) for i in order}
        for ref in out_s if fill else ():
            ref[...] = jnp.zeros_like(ref)
        ready, done = set(), []
        for n, (l_index, l_cols, r_index, r_cols, stores) in enumerate(tasks):
            for i in (l_index, n_left + r_index):
                if i not in ready:
                    loads.wait(groups[i])
                    ready.add(i)
            left, right = in_s[l_index][:, l_cols], in_s[n_left + r_index][:, r_cols]
            value = dot(left, right, TN).astype(BF)
            for which, spot, r_sl, c_sl in stores:
                out_s[which][spot] = value[r_sl, c_sl]
            for which in sorted(w for w in last if last[w] == n):
                done.append(loads.start([(out_s[which], outs[which].at[:, lo:hi])]))
        for group in done:
            loads.wait(group)

    flops = sum(
        2 * rows * (t[1].stop - t[1].start) * (t[3].stop - t[3].start) for t in tasks
    )
    return call(
        body,
        arrays + prev,
        [sds(s, BF) for s in out_shapes],
        [pltpu.VMEM((rows, w), BF) for w in wide]
        + [pltpu.VMEM((s[0], hi - lo, s[2]), BF) for s in out_shapes],
        name,
        flops,
        aliases={n_in + i: i for i in range(len(prev))},
    )


def mlp_back(grad, act, dact, wdown, wup, step):
    rows, width = grad.shape
    seq = rows // 2
    hid = dact.shape[1]
    down_arrays, down_plan, down_scratch = wdown
    up_arrays, up_plan, up_scratch = wup
    n_down = len(down_arrays)

    def body(small, ins, outs, scratch, loads):
        wd_s, wu_s, g_s, a_s, d_s, low_s, sum_s, two_s, mlp_s = scratch
        g_g = loads.start([(ins[0], g_s)])
        g_wd = weight_loads(loads, down_plan, ins[3 : 3 + n_down], wd_s)
        g_d = []
        for block in range(hid // step):
            cols = slice(block * step, (block + 1) * step)
            g_d.append(loads.start([(ins[2].at[:, cols], d_s.at[:, cols])]))
        g_wu = weight_loads(loads, up_plan, ins[3 + n_down :], wu_s)
        g_a = loads.start([(ins[1], a_s)])
        loads.wait(g_g)
        left = g_s[...]
        done = []
        for block in range(hid // step):
            if block < len(g_wd):
                loads.wait(g_wd[block])
            loads.wait(g_d[block])
            cols = slice(block * step, (block + 1) * step)
            pre = dot(left, wd_s[cols, :], NT) * d_s[:, cols].astype(F32)
            low_s[:, cols] = pre.astype(BF)
            sum_s[0:1, cols] = jnp.sum(pre, axis=0, keepdims=True)
            done.append(loads.start([(low_s.at[:, cols], outs[0].at[:, cols])]))
        done.append(loads.start([(sum_s, outs[1])]))
        for group in g_wu:
            loads.wait(group)
        two = dot(low_s[...], wu_s[...], NT)
        for a in range(2):
            two_s[a] = two[a * seq : (a + 1) * seq].astype(BF)
            done.append(loads.start([(two_s.at[a], outs[2].at[a])]))
        loads.wait(g_a)
        mlp_s[...] = dot(a_s[...], wd_s[...], NN).astype(BF)
        done.append(loads.start([(mlp_s, outs[3])]))
        for group in done:
            loads.wait(group)

    return call(
        body,
        [grad, act, dact] + down_arrays + up_arrays,
        [sds((rows, hid), BF), sds((1, hid), F32)]
        + [sds((2, seq, width), BF), sds((rows, width), BF)],
        [
            pltpu.VMEM(down_scratch, BF),
            pltpu.VMEM(up_scratch, BF),
            pltpu.VMEM((rows, width), BF),
            pltpu.VMEM((rows, hid), BF),
            pltpu.VMEM((rows, hid), BF),
            pltpu.VMEM((rows, hid), BF),
            pltpu.VMEM((1, hid), F32),
            pltpu.VMEM((2, seq, width), BF),
            pltpu.VMEM((rows, width), BF),
        ],
        "mlp_back",
        6 * rows * width * hid,
        sems=64,
    )


def input_grad(stacks, starts, weight, width):
    arrays, plan, shape = weight
    n, ext = shape[0], shape[-1]
    rows = stacks[0].shape[1]
    seq, m = rows // 2, len(stacks)

    def body(small, ins, outs, scratch, loads):
        w_s, out_s = scratch[0], scratch[1]
        l_s = scratch[2:]
        g_w = weight_loads(loads, plan[:1], ins[m:], w_s)
        g_l = []
        for i in range(n):
            pairs = []
            for j in range(m):
                count = stacks[j].shape[0] // n
                pairs += column_loads(ins[j].at[i * count : (i + 1) * count], l_s[i], starts[j])
            g_l.append(loads.start(pairs))
        g_w += weight_loads(loads, plan[1:], ins[m:], w_s)
        total = None
        for i in range(n):
            loads.wait(g_l[i])
            if i < len(g_w):
                loads.wait(g_w[i])
            piece = dot(l_s[i][...], w_s[i].reshape(width, ext), NT)
            total = piece if total is None else total + piece
        done = []
        for a in range(2):
            out_s[a] = total[a * seq : (a + 1) * seq].astype(BF)
            done.append(loads.start([(out_s.at[a], outs[0].at[a])]))
        for group in done:
            loads.wait(group)

    return call(
        body,
        list(stacks) + arrays,
        [sds((2, seq, width), BF)],
        [pltpu.VMEM(shape, BF), pltpu.VMEM((2, seq, width), BF)] + [pltpu.VMEM((rows, ext), BF)] * n,
        "grad_one",
        2 * rows * width * ext * n,
    )[0]


def middle_back(ids, middle, part, recv, cot, keep, nv, wout):
    _, seq, width = middle.shape
    out_arrays, out_plan, out_scratch = wout
    ext = out_scratch[0]

    def body(small, ins, outs, scratch, loads):
        ids_ref, keep_ref, nv_ref = small
        mine = ids_ref[0]
        wo_s, mid_s, part_s, recv_s, cot_s, gmid_s, gat_s, do_s = scratch[:8]
        cs_s = scratch[8]
        g_in = [
            loads.start(
                [
                    (ins[0].at[a], mid_s.at[a]),
                    (ins[1].at[a], cot_s.at[a]),
                    (ins[2].at[a], part_s.at[a]),
                    (ins[3].at[a], recv_s.at[a]),
                ]
            )
            for a in range(2)
        ]
        g_o = weight_loads(loads, out_plan, ins[4:], wo_s)
        done = []
        for a in range(2):
            loads.wait(g_in[a])
            keep_here = keep_ref[a]
            hat, inverse = norm_parts(mid_s[a])
            grad_two = part_s[a].astype(F32) + recv_s[a].astype(F32)
            top = cot_s[a].astype(F32)
            grad_mid = top + norm_back(grad_two, hat, inverse, nv_ref[1:2, :])
            grad_attn = grad_mid * keep_here
            sums = [
                jnp.sum(grad_two * hat, axis=0, keepdims=True),
                jnp.sum(grad_two, axis=0, keepdims=True),
                jnp.sum(grad_attn, axis=0, keepdims=True),
                jnp.sum(top, axis=0, keepdims=True) * keep_here,
            ]
            for i, value in enumerate(sums):
                cs_s[i : i + 1, :] = value if a == 0 else cs_s[i : i + 1, :] + value
            gmid_s[a] = grad_mid
            gat_s[a] = grad_attn.astype(BF)
            done.append(loads.start([(gat_s.at[a], outs[1].at[a])]))
            if a == 0:
                loads.wait(g_o[0])
            do_s[a] = dot(gat_s[a], wo_s[...], NT).astype(BF)
            done.append(loads.start([(do_s.at[a], outs[2].at[a])]))
        done.append(loads.start([(gmid_s.at[mine], outs[0]), (cs_s, outs[3])]))
        for group in done:
            loads.wait(group)

    return call(
        body,
        [middle, cot, part, recv] + out_arrays,
        [
            sds((seq, width), F32),
            sds((2, seq, width), BF),
            sds((2, seq, ext), BF),
            sds((4, width), F32),
        ],
        [
            pltpu.VMEM(out_scratch, BF),
            pltpu.VMEM((2, seq, width), F32),
            pltpu.VMEM((2, seq, width), BF),
            pltpu.VMEM((2, seq, width), BF),
            pltpu.VMEM((2, seq, width), BF),
            pltpu.VMEM((2, seq, width), F32),
            pltpu.VMEM((2, seq, width), BF),
            pltpu.VMEM((2, seq, ext), BF),
            pltpu.VMEM((4, width), F32),
        ],
        "middle_back",
        4 * seq * width * ext,
        smem=(ids, keep),
        vmem_ins=(nv,),
    )


def attn_backward(pairs, grad, q, k, v):
    _, seq, _ = q.shape
    n = len(pairs)

    def body(small, ins, outs, scratch, loads):
        q_s, k_s, v_s, do_s, dq_s, dk_s, dv_s, bs_s = scratch
        groups = []
        for u in range(2 * n):
            cols = slice(pairs[u // 2] * 128, (pairs[u // 2] + 1) * 128)
            groups.append(
                loads.start([(ins[j].at[u % 2, :, cols], scratch[j].at[u]) for j in range(4)])
            )
        half = lax.broadcasted_iota(jnp.int32, (1, 128), 1) // HEAD_DIM
        for group in groups:
            loads.wait(group)

        def unit(u, carry):
            q2, k2, v2, do2 = q_s[u], k_s[u], v_s[u], do_s[u]
            dq = dk = dv = None
            for h in range(2):
                mask = (half == h).astype(BF)
                km, qm, dom = k2 * mask, q2 * mask, do2 * mask
                scores = dot(km, q2, NT)
                row = lax.broadcasted_iota(jnp.int32, scores.shape, 0)
                scores = jnp.where(row < VALID, scores, -1e30)
                e = jnp.exp(scores - jnp.max(scores, axis=0, keepdims=True))
                probs = e * (1.0 / jnp.sum(e, axis=0, keepdims=True))
                grad_probs = dot(v2, dom, NT)
                row_dot = jnp.sum(probs * grad_probs, axis=0, keepdims=True)
                grad_scores = (probs * (grad_probs - row_dot)).astype(BF)
                v_piece = dot(probs.astype(BF), dom, NN)
                k_piece = dot(grad_scores, qm, NN)
                q_piece = dot(grad_scores, km, TN)
                dq = q_piece if dq is None else dq + q_piece
                dk = k_piece if dk is None else dk + k_piece
                dv = v_piece if dv is None else dv + v_piece
            dq = dq * HEAD_DIM**-0.5
            bs_s[u, 0:1, :] = jnp.sum(dq, axis=0, keepdims=True)
            bs_s[u, 1:2, :] = jnp.sum(dv, axis=0, keepdims=True)
            dq_s[u] = dq.astype(BF)
            dk_s[u] = dk.astype(BF)
            dv_s[u] = dv.astype(BF)
            return carry

        lax.fori_loop(0, 2 * n, unit, 0)
        done = [loads.start([(scratch[4 + j], outs[0].at[j])]) for j in range(3)]
        done.append(loads.start([(bs_s, outs[1])]))
        for group in done:
            loads.wait(group)

    grads, sums = call(
        body,
        [q, k, v, grad],
        [sds((3, 2 * n, seq, 128), BF), sds((2 * n, 2, 128), F32)],
        [pltpu.VMEM((2 * n, seq, 128), BF)] * 7 + [pltpu.VMEM((2 * n, 2, 128), F32)],
        "attn_backward",
        0,
    )
    return grads.reshape(3 * n, 2 * seq, 128), sums


def finish_layer(ids, keep, nv, middle, part, recv, nd, aligned):
    _, seq, width = middle.shape

    def body(small, ins, outs, scratch, loads):
        ids_ref, keep_ref, nv_ref = small
        mine = ids_ref[0]
        mid_s, part_s, recv_s, out_s = scratch
        groups = [loads.start([(ins[i].at[mine], scratch[i])]) for i in range(3)]
        for group in groups:
            loads.wait(group)
        total = part_s[...].astype(F32) + recv_s[...].astype(F32) + nv_ref[5:6, :]
        out_s[...] = (mid_s[...] + keep_ref[mine] * total).astype(BF)
        loads.wait(loads.start(block_stores(ids_ref, out_s, outs[0], nd, aligned)))

    return call(
        body,
        [middle, part, recv],
        [sds((seq, width), BF)],
        [pltpu.VMEM((seq, width), F32)] + [pltpu.VMEM((seq, width), BF)] * 3,
        "finish_layer",
        100 * seq * width,
        smem=(ids, keep),
        vmem_ins=(nv,),
    )[0]


def finish_tokens(ids, nv, tok, part, recv, gmid, rest, sums, nd, aligned):
    _, seq, width = tok.shape
    n_dest, z_n, n_rows, lanes = rest.shape
    bd, y_n = width // nd, nd // rest.shape[1]
    tx = n_dest // y_n

    def body(small, ins, outs, scratch, loads):
        ids_ref, nv_ref = small[:2]
        mine = ids_ref[0]
        tok_s, part_s, recv_s, gm_s, out_s, cs_s, rest_s = scratch
        g_rest = loads.start([(ins[4], rest_s)] if sums is None else [])
        groups = [
            loads.start(
                [
                    (ins[0].at[a], tok_s.at[a]),
                    (ins[2].at[a], part_s.at[a]),
                    (ins[3].at[a], recv_s.at[a]),
                ]
            )
            for a in range(2)
        ]
        g_mid = loads.start([(ins[1], gm_s)])
        for group in groups:
            loads.wait(group)
        done = []
        for i in range(2):
            a = mine if i == 0 else 1 - mine
            hat, inverse = norm_parts(tok_s[a].astype(F32))
            grad_one = part_s[a].astype(F32) + recv_s[a].astype(F32)
            gain_sum = jnp.sum(grad_one * hat, axis=0, keepdims=True)
            shift_sum = jnp.sum(grad_one, axis=0, keepdims=True)
            if i == 0:
                cs_s[0:1, :] = gain_sum
                cs_s[1:2, :] = shift_sum
                loads.wait(g_mid)
                value = gm_s[...] + norm_back(grad_one, hat, inverse, nv_ref[0:1, :])
                out_s[...] = value.astype(BF)
                done.append(loads.start(block_stores(ids_ref, out_s, outs[0], nd, aligned)))
            else:
                cs_s[0:1, :] = cs_s[0:1, :] + gain_sum
                cs_s[1:2, :] = cs_s[1:2, :] + shift_sum
        loads.wait(g_rest)
        if sums is not None:
            col_ref, bup_ref, pairs = small[2], small[3], small[4:]
            up = bup_ref.shape[1] // tx // nd
            n_pairs = sum(ref.shape[0] // 2 for ref in pairs)
            qv = n_pairs * 128 // tx // nd
            per = 128 // qv
            lane = lax.broadcasted_iota(jnp.int32, (2, 128), 1)
            whole = [ref[2 * i] + ref[2 * i + 1] for ref in pairs for i in range(ref.shape[0] // 2)]
            whole = jnp.stack(whole)
            rest_s[...] = jnp.zeros_like(rest_s)
            for n in range(n_dest):
                kx, ky = n // y_n, n % y_n
                for kz in range(z_n):
                    p = ky * z_n + kz
                    d = ids_ref[2 + p]
                    rest_s[n, kz, 2:6, :] = col_ref[:, p * bd : (p + 1) * bd]
                    row = jnp.zeros((2, 128), F32)
                    for i in range(nd // per):
                        row = jnp.where(d // per == i, whole[kx * (nd // per) + i], row)
                    row = pltpu.roll(row, (per - d % per) * qv % 128, 1)
                    rest_s[n, kz, 6:8, :] = jnp.where(lane < qv, row, 0.0)
                    cols = pl.ds(pl.multiple_of((kx * nd + d) * up, 128), up)
                    rest_s[n, kz, 8:9, 0:up] = bup_ref[:, cols]
        for n in range(n_dest if aligned else 0):
            for kz in range(z_n):
                p = n % (nd // z_n) * z_n + kz
                rest_s[n, kz, 0:2, :] = cs_s[:, p * bd : (p + 1) * bd]
        done.append(loads.start([(cs_s, outs[1])]))
        done += [loads.start([(rest_s.at[n], outs[2 + n])]) for n in range(n_dest)]
        for group in done:
            loads.wait(group)

    return call(
        body,
        [tok, gmid, part, recv] + ([rest] if sums is None else []),
        [sds((seq, width), BF), sds((2, width), F32)] + [sds(rest.shape[1:], F32)] * n_dest,
        [pltpu.VMEM((2, seq, width), BF)] * 3
        + [pltpu.VMEM((seq, width), F32), pltpu.VMEM((seq, width), BF), pltpu.VMEM((2, width), F32)]
        + [pltpu.VMEM(rest.shape, F32)],
        "finish_tokens",
        200 * seq * width,
        smem=(ids,),
        vmem_ins=(nv,) + tuple(sums or ()),
    )


class Grid3:
    def __init__(self, dp, tx):
        self.dp, self.tx = dp, tx
        self.y = 2 if dp % 2 == 0 else 1
        self.z = dp // self.y

    def send_z(self, value, k):
        return lax.ppermute(value, "dp", [(i, i ^ (k * self.y)) for i in range(self.dp)])

    def send_y(self, value, k):
        return lax.ppermute(value, "dp", [(i, i ^ k) for i in range(self.dp)])

    def send_xy(self, value, kx, ky):
        count = self.dp * self.tx
        pairs = [(i, ((i // self.tx) ^ ky) * self.tx + ((i % self.tx) ^ kx)) for i in range(count)]
        return lax.ppermute(value, ("dp", "tx"), pairs)

    def send_x(self, value, k):
        return lax.ppermute(value, "tx", [(i, i ^ k) for i in range(self.tx)])


def swap_core(value):
    return lax.ppermute(value, "core", [(0, 1), (1, 0)])


def after(values, gate):
    return lax.optimization_barrier((values, gate))[0]


def gather_z(grid, part_a, part_b, gate=None):
    rows = part_a.shape[0]
    both = jnp.concatenate([part_a, part_b], axis=0)
    all_z = [both] + [grid.send_z(both, k) for k in range(1, grid.z)]
    if gate is not None:
        all_z = after(all_z, gate)
    return jnp.stack([v[:rows] for v in all_z]), jnp.stack([v[rows:] for v in all_z])


def gather_first(grid, a_z, b_z):
    a_y = [a_z] + [grid.send_y(a_z, k) for k in range(1, grid.y)]
    b_x = [b_z] + [grid.send_x(b_z, k) for k in range(1, grid.tx)]
    return a_y, b_x


def join(pieces):
    return [jnp.concatenate(part) for part in pieces]


def gather_last(grid, a_y, b_x):
    a_all = [a_y] + [grid.send_x(a_y, k) for k in range(1, grid.tx)]
    b_all = [b_x] + [grid.send_y(b_x, k) for k in range(1, grid.y)]
    return a_all, b_all


def add_pieces(groups, cuts, outs, name):
    arrays = [a for group in groups for a in group]
    starts = [sum(len(g) for g in groups[:i]) for i in range(len(groups))]
    last = {}
    for n, cut in enumerate(cuts):
        last[cut[2]] = n

    def body(small, ins, outs_ref, scratch, loads):
        in_s, out_s = scratch[: len(arrays)], scratch[len(arrays) :]
        loaded = [loads.start([(ins[i], in_s[i]) for i in range(starts[g], starts[g] + len(groups[g]))]) for g in range(len(groups))]
        ready, done = set(), []
        for n, (g, spot, which, place) in enumerate(cuts):
            if g not in ready:
                loads.wait(loaded[g])
                ready.add(g)
            total = None
            for i in range(starts[g], starts[g] + len(groups[g])):
                value = in_s[i][spot].astype(F32)
                total = value if total is None else total + value
            out_s[which][place] = total.astype(out_s[which].dtype)
            for w in sorted(w for w in last if last[w] == n):
                done.append(loads.start([(out_s[w], outs_ref[w])]))
        for group in done:
            loads.wait(group)

    return call(
        body,
        arrays,
        outs,
        [pltpu.VMEM(a.shape, a.dtype) for a in arrays] + [pltpu.VMEM(o.shape, o.dtype) for o in outs],
        name,
        0,
        spare=8,
    )


class Scatter:
    def __init__(self, grid, a_all, b_all, name):
        self.grid, self.name, self.bit = grid, name, 0
        self.rows = (a_all[0].shape[1], b_all[0].shape[1])
        a_got = [grid.send_x(a_all[k], k) for k in range(1, grid.tx)]
        b_got = [grid.send_y(b_all[k], k) for k in range(1, grid.y)]
        self.state = ([a_all[0]] + a_got, [b_all[0]] + b_got)

    def second(self, gate):
        grid, z = self.grid, self.grid.z
        a_in, b_in = after(self.state, gate)
        outs = [sds((z,) + a_in[0].shape[1:], BF)] * grid.y + [sds((z,) + b_in[0].shape[1:], BF)] * grid.tx
        full = slice(None)
        cuts = [(0, slice(k * z, (k + 1) * z), k, full) for k in list(range(1, grid.y)) + [0]]
        cuts += [(1, slice(k * z, (k + 1) * z), grid.y + k, full) for k in list(range(1, grid.tx)) + [0]]
        res = add_pieces([a_in, b_in], cuts, outs, self.name + "_add")
        a_y, b_x = res[: grid.y], res[grid.y :]
        a_got = [grid.send_y(a_y[k], k) for k in range(1, grid.y)]
        b_got = [grid.send_x(b_x[k], k) for k in range(1, grid.tx)]
        self.state = ([a_y[0]] + a_got, [b_x[0]] + b_got)
        return a_y[0], b_x[0]

    def along_z(self, gate, extra=None):
        grid = self.grid
        a_in, b_in = after(self.state, gate)
        ra, rb = self.rows
        groups = [a_in, b_in] + ([extra] if extra else [])
        more = extra[0].shape[1] if extra else 0
        order = list(range(1, grid.z)) + [0]
        cuts = []
        for k in order:
            cuts.append((0, k, k, slice(0, ra)))
            cuts.append((1, k, k, slice(ra, ra + rb)))
            if extra:
                cuts.append((2, k, k, slice(ra + rb, ra + rb + more)))
        outs = [sds((ra + rb + more,) + a_in[0].shape[2:], BF)] * grid.z
        both = add_pieces(groups, cuts, outs, self.name + "_addz")
        self.state = [both[0]] + [grid.send_z(both[k], k) for k in range(1, grid.z)]
        return both

    def halve(self, gate):
        grid, (ra, rb) = self.grid, self.rows
        groups = after(self.state, gate)
        if self.bit == 0:
            self.bit, self.left = 1, list(range(grid.z))
        else:
            self.bit, groups = 2 * self.bit, [groups]
        sent = [k for k in self.left if k & self.bit]
        kept = [k for k in self.left if not k & self.bit]
        cuts = []
        for which, ids in ((0, sent), (1, kept)):
            for n, k in enumerate(ids):
                spot = self.left.index(k)
                if len(groups) == 2:
                    cuts.append((0, spot, which, (n, slice(0, ra))))
                    cuts.append((1, spot, which, (n, slice(ra, ra + rb))))
                else:
                    cuts.append((0, spot, which, n))
        outs = [sds((len(kept), ra + rb) + groups[0][0].shape[2:], BF)] * 2
        send, keep = add_pieces(groups, cuts, outs, self.name + "_half")
        self.left = kept
        self.state = [keep, grid.send_z(send, self.bit)]
        return keep

    def finish(self, gate, cuts, outs):
        if self.bit:
            cuts = [((0, rows), which, place) for rows, which, place in cuts]
        cuts = [(0, rows, which, place) for rows, which, place in cuts]
        return add_pieces([after(self.state, gate)], cuts, outs, self.name + "_sum")


def xor_blocks(value, mask, axis):
    count = value.shape[axis]
    bit = 1
    while bit < count:
        shape = value.shape
        split = value.reshape(shape[:axis] + (count // (2 * bit), 2, bit) + shape[axis + 1 :])
        turned = jnp.flip(split, axis=axis + 1).reshape(shape)
        value = jnp.where(jnp.bitwise_and(mask, bit) != 0, turned, value)
        bit *= 2
    return value


def pad_cols(value, width):
    return jnp.pad(value, ((0, 0), (0, width - value.shape[1])))


def per_device(
    tokens,
    cotangent,
    image_mask,
    norm_gains,
    norm_shifts,
    w_qkv,
    b_qv,
    w_out,
    w_up,
    up_bias,
    w_down,
    *,
    dp,
    tx,
):
    grid = Grid3(dp, tx)
    y_n, z_n = grid.y, grid.z
    core = lax.axis_index("core").astype(jnp.int32)
    me_d = lax.axis_index("dp").astype(jnp.int32)
    me_x = lax.axis_index("tx").astype(jnp.int32)
    seq, width = tokens.shape
    _, bd, hw = w_qkv.shape
    fw = w_up.shape[1]
    ext, hid = tx * hw, tx * fw
    hh, fh = hw // 2, fw // 2
    aligned = bd % 128 == 0 and hh % 128 == 0 and fh % 128 == 0
    rel = [kz * y_n + ky for ky in range(y_n) for kz in range(z_n)]

    def from_abs(value, axis):
        shape = value.shape
        value = value.reshape(shape[:axis] + (z_n, y_n) + shape[axis + 1 :])
        return jnp.swapaxes(value, axis, axis + 1).reshape(shape)

    def to_rel(value, axis):
        shape = value.shape
        value = value.reshape(shape[:axis] + (y_n, z_n) + shape[axis + 1 :])
        return jnp.swapaxes(value, axis, axis + 1).reshape(shape)

    ids = jnp.stack([core, me_d] + [jnp.bitwise_xor(me_d, k) for k in rel])
    keep = lax.dynamic_slice(image_mask, (2 * me_x,), (2,)).astype(F32)

    lane = max(bd, hh)
    small = jnp.concatenate(
        [
            pad_cols(norm_gains, lane),
            pad_cols(norm_shifts, lane),
            pad_cols(b_qv, lane),
            pad_cols(up_bias[None], lane),
            jnp.zeros((7, lane), BF),
        ]
    )
    qkv_a = pad_cols(w_qkv[:, :, :hh].reshape(3 * bd, hh), lane)
    qkv_b = pad_cols(w_qkv[:, :, hh:].reshape(3 * bd, hh), lane)
    first_a = jnp.concatenate([qkv_a, pad_cols(w_out[:hh], lane), small])
    first_b = jnp.concatenate([qkv_b, pad_cols(w_out[hh:], lane)])
    own = [tokens, cotangent]
    other = [swap_core(value) for value in own]
    if aligned:
        tok, cot = arrange_pair(ids, own, other, dp)
    else:

        def arrange(own, other):
            pair = jnp.where(core == 0, jnp.stack([own, other]), jnp.stack([other, own]))
            pair = xor_blocks(pair.reshape(2, seq, dp, bd), me_d, 2)
            return from_abs(pair, 2).reshape(2, seq, width)

        tok, cot = [arrange(own[i], other[i]) for i in range(2)]
    c1_z = gather_z(grid, first_a, first_b, gate=tok)
    c1_h = gather_first(grid, *c1_z)
    c1_h = join(c1_h)
    c1a, c1b = gather_last(grid, *c1_h)
    up_halves = after((w_up[:, :fh], w_up[:, fh:]), c1_h)
    row0 = 3 * bd + hh
    if aligned and 128 % (hw // dp) == 0 and (fw // dp) % 128 == 0:
        c1a, c1b = after((c1a, c1b), (c1a, c1b))
        nv, bq, bu = vectors(ids, c1a, row0, dp, y_n, bd, hw // dp, fw // dp)
    else:
        nv = c1a[0][:, row0 : row0 + 6, :bd].transpose(1, 0, 2).reshape(6, width).astype(F32)
        tail = jnp.stack([v[:, row0 + 6 : row0 + 9] for v in c1a])
        tail = xor_blocks(to_rel(tail, 1), me_d, 1)
        bq = tail[:, :, :2, : hw // dp].transpose(2, 0, 1, 3).reshape(2, ext).astype(F32)
        bu = tail[:, :, 2, : fw // dp].reshape(1, hid).astype(F32)
    grad_top = cot * keep.astype(BF)[:, None, None]

    up_z = gather_z(grid, *up_halves, gate=nv)
    up_h = gather_first(grid, *up_z)
    dn_halves = after((w_down[:fh], w_down[fh:]), up_z)

    if aligned:
        every, wq_plan, wo_plan, up_plan, dn_plan = slice(None), [[], [], []], [], [], []
        for kx in range(tx):
            halves = [slice(kx * hw, kx * hw + hh), slice(kx * hw + hh, (kx + 1) * hw)]
            f_halves = [slice(kx * fw, kx * fw + fh), slice(kx * fw + fh, (kx + 1) * fw)]
            own = slice(kx * z_n, (kx + 1) * z_n)
            for i in range(3):
                src = slice(i * bd, (i + 1) * bd)
                wq_plan[i].append((kx, (every, src), (i, every, every, halves[0])))
                for ky in range(y_n):
                    dst = (i, slice(ky * z_n, (ky + 1) * z_n), every, halves[1])
                    wq_plan[i].append((tx + ky, (own, src), dst))
            src = slice(3 * bd, 3 * bd + hh)
            dn_plan += [[], []]
            for ky in range(y_n):
                for kz in range(z_n):
                    p, r = ky * z_n + kz, kx * z_n + kz
                    cols = slice(p * bd, (p + 1) * bd)
                    wo_plan.append((kx, (p, src), (halves[0], cols)))
                    wo_plan.append((tx + ky, (r, src), (halves[1], cols)))
                    dn_plan[-2].append((kx, (p,), (f_halves[0], cols)))
                    dn_plan[-1].append((tx + ky, (r,), (f_halves[1], cols)))
            up_plan += [[(kx, (every,), (every, f_halves[0]))], []]
            for ky in range(y_n):
                rows = slice(kx * z_n * bd, (kx + 1) * z_n * bd)
                dst = (slice(ky * z_n * bd, (ky + 1) * z_n * bd), f_halves[1])
                up_plan[-1].append((tx + ky, (rows,), dst))
        c1 = c1a + c1b
        wqkv = (c1, wq_plan, (3, dp, bd, ext))
        wout = (c1, [wo_plan], (ext, width))
    else:

        def whole(a_all, b_all):
            a = jnp.stack(a_all)
            b = jnp.stack(b_all).reshape((y_n, tx, z_n) + b_all[0].shape[1:])
            b = b.transpose(1, 0, 2, 3, 4).reshape(a.shape[:2] + b.shape[3:])
            return jnp.stack([a, b], axis=1)

        c1 = whole([v[:, :row0] for v in c1a], c1b)
        qkv = c1[:, :, :, : 3 * bd, :hh].reshape(tx, 2, dp, 3, bd, hh)
        qkv = qkv.transpose(3, 2, 4, 0, 1, 5).reshape(3, dp, bd, ext)
        out = c1[:, :, :, 3 * bd :, :bd].transpose(0, 1, 3, 2, 4).reshape(ext, width)
        all_of = [[(0, (slice(None),), (slice(None),))]]
        wqkv = ([qkv], all_of, qkv.shape)
        wout = ([out], all_of, out.shape)

    rows2 = 2 * seq

    res = attn_forward(0, after(tok, up_z), nv, bq, wqkv, wout, None)
    part0 = res[5]
    up_h = join(after(up_h, part0))
    upa, upb = gather_last(grid, *up_h)
    dn_halves = after(dn_halves, up_h)
    res = attn_forward(1, after(tok, up_h), nv, bq, wqkv, wout, res[:5])
    recv0 = swap_core(after(part0, res[5]))
    parts = [(part0, recv0), (res[5], swap_core(res[5]))]
    first, q, k, v, att = res[:5]
    upa, upb = after((upa, upb), res[5])
    dn_z = gather_z(grid, *dn_halves, gate=(upa, upb))
    dn_h = gather_first(grid, *dn_z)
    if aligned:
        wup = ([v.reshape(-1, fh) for v in upa + upb], up_plan, (width, hid))
    else:
        up_w = whole(upa, upb).transpose(2, 3, 0, 1, 4).reshape(width, hid)
        wup = ([up_w], all_of, up_w.shape)
    part, recv = parts[0]
    state = mlp_up(0, tok, part, recv, keep, nv, bu, wup, fh, None)
    dna, dnb = gather_last(grid, *join(after(dn_h, state[1])))
    part, recv = parts[1]
    state = mlp_up(1, tok, part, recv, keep, nv, bu, wup, fh, state)
    if aligned:
        wdown = (dna + dnb, dn_plan, (hid, width))
    else:
        down_w = whole(dna, dnb).transpose(0, 1, 3, 2, 4).reshape(hid, width)
        wdown = ([down_w], all_of, down_w.shape)
    middle, second, act, dact = state
    flat = lambda value: value.reshape(rows2, value.shape[2])
    act2, sec2, grad2 = flat(act), flat(second), flat(grad_top)

    full = slice(None)
    a_spots = [(p, slice(p * bd, (p + 1) * bd)) for p in range(dp)]

    def by_left(l_index, r_index, size, row0):
        tasks, rows = [], slice(row0, row0 + size // 2)
        halves = slice(0, size // 2), slice(size // 2, size)
        for kx in range(tx):
            stores = [(kx, (p, rows), halves[0], cols) for p, cols in a_spots]
            for p, cols in a_spots:
                ky, kz = p // z_n, p % z_n
                stores.append((tx + ky, (kx * z_n + kz, rows), halves[1], cols))
            tasks.append((l_index, slice(kx * size, (kx + 1) * size), r_index, slice(0, width), stores))
        return tasks

    def by_right(l_index, r_index, size, row0, lanes, spare=False, first=0):
        tasks, each = [], size // 2 // lanes
        for kx in range(tx):
            stores = []
            for j in range(each):
                rows = slice(row0 + j * bd, row0 + (j + 1) * bd)
                cols = [slice((h * each + j) * lanes, (h * each + j + 1) * lanes) for h in range(2)]
                rows = (rows, slice(0, lanes)) if spare else (rows,)
                for p, r_sl in a_spots:
                    ky, kz = p // z_n, p % z_n
                    stores.append((kx, (p,) + rows, r_sl, cols[0]))
                    stores.append((tx + ky, (kx * z_n + kz,) + rows, r_sl, cols[1]))
            cols = slice(first + kx * size, first + (kx + 1) * size)
            tasks.append((l_index, slice(0, width), r_index, cols, stores))
        return tasks

    def pieces(rows, lanes):
        return [(dp, rows, lanes)] * tx + [(tx * z_n, rows, lanes)] * y_n

    def send_grad(parts, name):
        return Scatter(grid, list(parts[:tx]), list(parts[tx:]), name)

    grads = weight_grad([act2], [grad2], by_left(0, 0, fw, 0), pieces(fh, bd), "down_grad", 0, fh)
    down_rs = send_grad(grads, "down")
    grad_in = after(grad2, grads[-1])
    low_pre, bias_up, two_part, mlp_part = mlp_back(grad_in, act2, flat(dact), wdown, wup, fh)
    mlp_part = mlp_part.reshape(2, seq, width)
    two_recv = swap_core(two_part)
    down_half = down_rs.second(bias_up)
    up_rows = fh // bd * bd
    sec_in = after(sec2, down_half)
    tasks = by_right(0, 0, fw, 0, bd)
    grads = weight_grad([sec_in], [low_pre], tasks, pieces(up_rows, bd), "up_grad", 0, up_rows)
    up_rs = send_grad(grads, "up")
    gmid, gattn, grad_att, col = middle_back(
        ids, middle, two_part, after(two_recv, grads[-1]), cot, keep, nv, wout
    )
    down_zs = down_rs.along_z(col)
    row0 = 3 * bd
    last_shapes = pieces(row0 + hh, bd)
    att_in = after(flat(att), down_zs)
    tasks = by_left(0, 0, hw, 0)
    out_grads = weight_grad(
        [att_in], [flat(gattn)], tasks, last_shapes, "out_grad", row0, row0 + hh
    )

    up_half = up_rs.second(out_grads[-1])
    n_pairs = ext // 128
    split = hh == 128 and bd == 128
    firsts = list(range(1, n_pairs)) if split else list(range(n_pairs))
    left_a, bias_a = attn_backward(firsts, after(grad_att, up_half), q, k, v)
    grad_down = down_rs.finish(bias_a, [(full, 0, full)], [sds((fw, bd), F32)])[0]
    mlp_recv = swap_core(after(mlp_part, bias_a))
    gate = up_rs.halve(grad_down) if z_n > 1 else grad_down
    first_in = after(flat(first), gate)
    if split:
        stores, count = [], len(firsts)
        for i in range(3):
            rows = slice(i * bd, (i + 1) * bd)
            for n, pair in enumerate(firsts):
                kx, cols = pair // 2, slice((i * count + n) * 128, (i * count + n + 1) * 128)
                for p, r_sl in a_spots:
                    ky, kz = p // z_n, p % z_n
                    spot = (kx - 1, (p, rows)) if pair % 2 == 0 else (tx - 1 + ky, (kx * z_n + kz, rows))
                    stores.append(spot + (r_sl, cols))
        tasks = [(0, slice(0, width), 0, slice(0, 384 * count), stores)]
        sent = weight_grad(
            [first_in], [left_a], tasks, last_shapes[1:], "qkv_grad", 0, row0, out_grads[1:]
        )
        left_b, bias_b = attn_backward([0], after(grad_att, (sent[: tx - 1], sent[tx:])), q, k, v)
        gate = (bias_b, mlp_recv)
        while 2 * up_rs.bit < z_n:
            gate = up_rs.halve(gate)
        stores = []
        for i in range(3):
            rows, cols = slice(i * bd, (i + 1) * bd), slice(i * 128, (i + 1) * 128)
            stores += [(0, (p, rows), r_sl, cols) for p, r_sl in a_spots]
        tasks = [(0, slice(0, width), 0, slice(0, 384), stores)]
        kept = weight_grad(
            [after(first_in, gate)],
            [left_b],
            tasks,
            last_shapes[:1],
            "qkv_keep",
            0,
            row0,
            out_grads[:1],
        )
        grads = list(kept) + list(sent)
        lefts, starts = [left_a, left_b], [1, 0]
        pair_sums = [bias_b, bias_a]
        gate = kept[0]
    else:
        while 2 * up_rs.bit < z_n:
            gate = up_rs.halve((gate, mlp_recv))
        makers = [by_right(0, 0, hw, i * bd, hh, hh < bd, i * ext) for i in range(3)]
        tasks = [task for maker in makers for task in maker]
        grads = weight_grad(
            [after(first_in, gate)],
            [left_a],
            tasks,
            last_shapes,
            "qkv_grad",
            0,
            row0,
            out_grads,
            hh < bd,
        )
        lefts, starts = [left_a], [0]
        pair_sums = [bias_a]
        gate = grads[-1]
    qkv_rs = send_grad(grads, "qkv")
    lefts = after(lefts, gate)
    one_part = input_grad(lefts, starts, wqkv, width)
    one_recv = swap_core(one_part)
    cuts = []
    for h in range(2):
        for j in range(fh // bd):
            rows = slice(h * up_rows + j * bd, h * up_rows + (j + 1) * bd)
            cuts.append((rows, 0, (full, slice(h * fh + j * bd, h * fh + (j + 1) * bd))))
    up_cuts = cuts
    qkv_half = qkv_rs.second(one_part)
    wide = max(bd, hw // dp, fw // dp)
    if split and fw // dp == bd and 128 % (hw // dp) == 0:
        rest = sds((tx * y_n, z_n, 16, wide), F32)
        sums = [col, bias_up] + pair_sums
    else:
        bias_qv = jnp.concatenate(pair_sums)
        bias_qv = jnp.sum(bias_qv.reshape(n_pairs, 2, 2, 128), axis=1).transpose(1, 0, 2)
        vec = jnp.concatenate([jnp.zeros((2, width), F32), col])
        vec = vec.reshape(6, y_n, z_n, bd).transpose(1, 2, 0, 3)
        bias_qv = bias_qv.reshape(2, tx, dp, hw // dp).transpose(2, 1, 0, 3)
        bias_up = bias_up.reshape(tx, 1, dp, fw // dp).transpose(2, 0, 1, 3)
        bias = jnp.concatenate(
            [
                jnp.pad(value, ((0, 0), (0, 0), (0, 0), (0, wide - value.shape[3])))
                for value in (bias_qv, bias_up)
            ],
            axis=2,
        )
        bias = from_abs(xor_blocks(bias, me_d, 0), 0).reshape(y_n, z_n, tx, 3, wide)
        bias = bias.transpose(2, 0, 1, 3, 4)
        vec = jnp.pad(vec, ((0, 0), (0, 0), (0, 0), (0, wide - bd)))
        vec = jnp.broadcast_to(vec, (tx,) + vec.shape)
        rest = jnp.concatenate([vec, bias, jnp.zeros((tx, y_n, z_n, 7, wide), F32)], axis=3)
        rest = rest.reshape(tx * y_n, z_n, 16, wide)
        sums = None
    grad_tokens, one_sums, *small = finish_tokens(
        ids, nv, tok, one_part, after(one_recv, qkv_half), gmid, rest, sums, dp, aligned
    )
    if not aligned:
        ones = jnp.pad(one_sums.reshape(2, y_n, z_n, bd), ((0, 14), (0, 0), (0, 0), (0, wide - bd)))
        ones = ones.transpose(1, 2, 0, 3)
        small = [value + ones[n % y_n] for n, value in enumerate(small)]
    small = after(small, qkv_rs.state)
    got = small[:1]
    for n in range(1, tx * y_n):
        got.append(grid.send_xy(small[n], n // y_n, n % y_n))
    grad_up = up_rs.finish(one_sums, up_cuts, [sds((bd, fw), F32)])[0]
    cuts, outs = [], [sds((3, bd, hw), F32), sds((hw, bd), F32)]
    last_rows = row0 + hh
    for h in range(2):
        for i in range(3):
            rows = slice(h * last_rows + i * bd, h * last_rows + (i + 1) * bd)
            rows = (rows, slice(0, hh)) if hh < bd else rows
            cuts.append((rows, 0, (i, full, slice(h * hh, (h + 1) * hh))))
        rows = slice(h * last_rows + row0, (h + 1) * last_rows)
        cuts.append((rows, 1, (slice(h * hh, (h + 1) * hh),)))
    if wide == bd:
        qkv_zs = qkv_rs.along_z(grad_up, got)
        cuts.append((slice(2 * last_rows, 2 * last_rows + 16), 2, full))
        outs.append(sds((16, wide), F32))
    else:
        qkv_zs = qkv_rs.along_z(grad_up)
    layer_out = finish_layer(
        ids, keep, nv, middle, after(mlp_part, qkv_zs), mlp_recv, dp, aligned
    )
    res = qkv_rs.finish(layer_out, cuts, outs)
    grad_qkv, grad_out = res[:2]
    if wide == bd:
        both = res[2]
    else:
        both, bit = sum(got), 1
        while bit < z_n:
            both = both.reshape((-1, 2) + both.shape[1:])
            both = both[:, 0] + grid.send_z(both[:, 1], bit)
            bit *= 2
        both = both[0]
    if not aligned:

        def restore(value):
            value = xor_blocks(to_rel(value.reshape(seq, dp, bd), 1), me_d, 1)
            return value.reshape(seq, width)

        layer_out, grad_tokens = restore(layer_out), restore(grad_tokens)

    share = bd // (2 * tx)
    mine = lax.dynamic_slice(both[:6, :bd], (0, (2 * me_x + core) * share), (6, share))

    return (
        layer_out,
        grad_tokens,
        mine[0:3:2],
        jnp.concatenate([mine[1:2], mine[3:6]]),
        grad_qkv,
        both[6:8, : hw // dp],
        grad_out,
        grad_up,
        both[8, : fw // dp],
        grad_down,
    )


def solution(mesh):
    dp, tensor = mesh.shape["dp"], mesh.shape["tensor"]
    split = Mesh(mesh.devices.reshape(dp, tensor // 2, 2), ("dp", "tx", "core"))
    every = ("dp", "tx", "core")
    tensor_axes = ("tx", "core")
    in_specs = (
        P(every, None),
        P(every, None),
        P("dp"),
        P(None, "dp"),
        P(None, "dp"),
        P(None, "dp", tensor_axes),
        P(None, ("tx", "core", "dp")),
        P(tensor_axes, "dp"),
        P("dp", tensor_axes),
        P(("tx", "core", "dp")),
        P(tensor_axes, "dp"),
    )
    out_specs = (
        P(every, None),
        P(every, None),
        P(None, every),
        P(None, every),
        P(None, "dp", tensor_axes),
        P(None, ("tx", "core", "dp")),
        P(tensor_axes, "dp"),
        P("dp", tensor_axes),
        P(("tx", "core", "dp")),
        P(tensor_axes, "dp"),
    )
    return jax.shard_map(
        functools.partial(per_device, dp=dp, tx=tensor // 2),
        mesh=split,
        in_specs=in_specs,
        out_specs=out_specs,
        check_vma=False,
    )
```

```python
import functools

import jax
import jax.numpy as jnp
from jax import lax
from jax.experimental import pallas as pl
from jax.experimental.pallas import tpu as pltpu
from jax.sharding import Mesh, PartitionSpec as P

HEAD_DIM = 64
VALID = 577
SEQ = 584
BF = jnp.bfloat16
F32 = jnp.float32
VMEM_LIMIT = 60 * 1024 * 1024
WHOLE_VMEM = ("arrange_pair", "vectors", "mlp_up", "down_grad", "mlp_back")
COST_SCALE = 1.0
COST = {
    "arrange_pair": 5,
    "vectors": 3,
    "attn_forward": 16,
    "mlp_up": 10,
    "down_grad": 11,
    "mlp_back": 22,
    "up_grad": 11,
    "middle_back": 0,
    "out_grad": 8,
    "attn_backward": 18,
    "attn_first": 0,
    "qkv_grad": 7,
    "qkv_keep": 0,
    "up_half": 0,
    "join": 0,
    "grad_one": 0,
    "qkv_add": 30,
    "finish_layer": 0,
    "up_sum": 0,
    "finish_tokens": 9,
}
NT = (((1,), (1,)), ((), ()))
TN = (((0,), (0,)), ((), ()))
NN = (((1,), (0,)), ((), ()))


def dot(left, right, dims):
    return lax.dot_general(left, right, dims, preferred_element_type=F32)


class Loads:
    def __init__(self, sems):
        self.sems, self.groups = sems, []

    def start(self, pairs):
        sem = self.sems.at[len(self.groups)]
        copies = [pltpu.make_async_copy(src, dst, sem) for src, dst in pairs]
        for copy in copies:
            copy.start()
        self.groups.append(copies)
        return len(self.groups) - 1

    def wait(self, group):
        for copy in self.groups[group]:
            copy.wait()


def padded_bytes(value):
    lead, (rows, lanes) = value.shape[:-2], value.shape[-2:]
    count = -(-rows // 16) * 16 * (-(-lanes // 128) * 128)
    for size in lead:
        count *= size
    return count * jnp.dtype(value.dtype).itemsize


def call(body, ins, outs, scratch, name, flops, aliases=None, smem=(), sems=48, vmem_ins=(), spare=12, pinned=False):
    n_smem, n_vmem, n_in, n_out = len(smem), len(vmem_ins), len(ins), len(outs)
    moved = sum(a.size * a.dtype.itemsize for a in ins) + sum(
        o.size * o.dtype.itemsize for o in outs
    )

    def kernel(*refs):
        first = n_smem + n_vmem
        small = refs[:first]
        in_refs = refs[first : first + n_in]
        out_refs = refs[first + n_in : first + n_in + n_out]
        rest = refs[first + n_in + n_out :]
        body(small, in_refs, out_refs, rest[:-1], Loads(rest[-1]))

    held = sum(padded_bytes(piece) for piece in scratch) + spare * 1024 * 1024
    vmem = VMEM_LIMIT if name in WHOLE_VMEM else min(held, VMEM_LIMIT)
    flops = max(COST.get(name, 3), 0.02) * COST_SCALE * 1.15e9
    moved = 0
    any_spec = pl.BlockSpec(memory_space=pl.ANY)
    hbm_spec = pl.BlockSpec(memory_space=pltpu.HBM) if pinned else any_spec
    return pl.pallas_call(
        kernel,
        out_shape=outs,
        in_specs=[pl.BlockSpec(memory_space=pltpu.SMEM)] * n_smem
        + [pl.BlockSpec(memory_space=pltpu.VMEM)] * n_vmem
        + [hbm_spec if i in (aliases or {}) else any_spec for i in range(n_in)],
        out_specs=[hbm_spec if pinned else any_spec] * n_out,
        scratch_shapes=list(scratch) + [pltpu.SemaphoreType.DMA((sems,))],
        input_output_aliases={n_smem + n_vmem + i: o for i, o in (aliases or {}).items()},
        compiler_params=pltpu.CompilerParams(vmem_limit_bytes=vmem),
        cost_estimate=pl.CostEstimate(flops=int(flops), bytes_accessed=int(flops // 1000), transcendentals=0),
        name=name,
    )(*smem, *vmem_ins, *ins)


def norm_parts(rows):
    center = rows - jnp.mean(rows, axis=1, keepdims=True)
    inverse = lax.rsqrt(jnp.mean(center * center, axis=1, keepdims=True) + 1e-05)
    return center * inverse, inverse


def norm_back(grad_norm, scaled, inverse, gain_row):
    grad_hat = grad_norm * gain_row
    first_mean = jnp.mean(grad_hat, axis=1, keepdims=True)
    second_mean = jnp.mean(grad_hat * scaled, axis=1, keepdims=True)
    return inverse * (grad_hat - first_mean - scaled * second_mean)


def sds(shape, dtype):
    return jax.ShapeDtypeStruct(shape, dtype)


def arrange_pair(ids, own, other, nd):
    n = len(own)
    rows, width = own[0].shape
    bd = width // nd

    def body(small, ins, outs, scratch, loads):
        (ids_ref,) = small
        mine = ids_ref[0]
        in_s, out_s = scratch[: 2 * n], scratch[2 * n :]
        groups = [loads.start([(ins[i], in_s[i])]) for i in range(2 * n)]
        done = []
        for i in range(2 * n):
            loads.wait(groups[i])
            for p in range(nd):
                src = pl.ds(pl.multiple_of(ids_ref[2 + p] * bd, 128), bd)
                out_s[i][:, p * bd : (p + 1) * bd] = in_s[i][:, src]
            spot = mine if i < n else 1 - mine
            done.append(loads.start([(out_s[i], outs[i % n].at[spot])]))
        for group in done:
            loads.wait(group)

    return call(
        body,
        list(own) + list(other),
        [sds((2, rows, width), BF)] * n,
        [pltpu.VMEM((rows, width), BF)] * (4 * n),
        "arrange_pair",
        0,
        smem=(ids,),
    )


def vectors(ids, gathered, row0, nd, y_n, bd, qv, up):
    tx, z_n = len(gathered), nd // y_n

    def body(small, ins, outs, scratch, loads):
        ids_ref, rows_s, nv_s, bq_s, bu_s = small[0], *scratch
        rows = pl.ds(row0, 16)
        loads.wait(loads.start([(ins[k].at[:, rows, :], rows_s.at[k]) for k in range(tx)]))
        for p in range(nd):
            nv_s[:, p * bd : (p + 1) * bd] = rows_s[0, p].astype(F32)[:6, :bd]
        for k in range(tx):
            pieces = []
            for d in range(nd):
                rel = ids_ref[1] ^ d
                spot = (rel % y_n) * z_n + rel // y_n
                piece = rows_s[k, spot].astype(F32)
                bu_s[:, (k * nd + d) * up : (k * nd + d + 1) * up] = piece[8:9, :up]
                pieces.append(piece[6:8, :])
            each = 128 // qv
            for start in range(0, nd, each):
                total = pieces[start]
                for i in range(1, each):
                    total = total + pltpu.roll(pieces[start + i], i * qv, 1)
                bq_s[:, (k * nd + start) * qv : (k * nd + start + each) * qv] = total
        loads.wait(loads.start([(nv_s, outs[0]), (bq_s, outs[1]), (bu_s, outs[2])]))

    shapes = [(6, nd * bd), (2, tx * nd * qv), (1, tx * nd * up)]
    return call(
        body,
        list(gathered),
        [sds(s, F32) for s in shapes],
        [pltpu.VMEM((tx, nd, 16, gathered[0].shape[2]), BF)] + [pltpu.VMEM(s, F32) for s in shapes],
        "vectors",
        0,
        smem=(ids,),
    )


def block_stores(ids_ref, src, dst, nd, aligned):
    if not aligned:
        return [(src, dst)]
    bd = src.shape[1] // nd
    pairs = []
    for p in range(nd):
        cols = pl.ds(pl.multiple_of(ids_ref[2 + p] * bd, 128), bd)
        pairs.append((src.at[:, p * bd : (p + 1) * bd], dst.at[:, cols]))
    return pairs


def weight_loads(loads, groups, refs, scratch):
    return [
        loads.start([(refs[a].at[src], scratch.at[dst]) for a, src, dst in plan])
        for plan in groups
    ]


def softmax_rows(q2, k2):
    scores = dot(q2, k2, NT)
    lane = lax.broadcasted_iota(jnp.int32, scores.shape, 1)
    scores = jnp.where(lane < VALID, scores, -1e30)
    e = jnp.exp(scores - jnp.max(scores, axis=1, keepdims=True))
    return e * (1.0 / jnp.sum(e, axis=1, keepdims=True))


def attn_forward(image, tok, nv, bq, wqkv, wout, prev):
    seq, width = tok.shape[1:]
    qkv_arrays, qkv_plan, qkv_scratch = wqkv
    out_arrays, out_plan, out_scratch = wout
    ext = qkv_scratch[-1]
    n_prev = 0 if prev is None else len(prev)
    nq, no = len(qkv_arrays), len(out_arrays)

    def body(small, ins, outs, scratch, loads):
        nv_ref, bq_ref = small
        tok_ref, ins = ins[0], ins[1 + n_prev :]
        w_s, wo_s, tok_s, first_s, q_s, k_s, v_s, att_s, part_s = scratch
        g_tok = loads.start([(tok_ref.at[image], tok_s)])
        g_w = weight_loads(loads, qkv_plan, ins[:nq], w_s)
        g_o = weight_loads(loads, out_plan, ins[nq:], wo_s)
        loads.wait(g_tok)
        hat, _ = norm_parts(tok_s[...].astype(F32))
        first_s[...] = (hat * nv_ref[0:1, :] + nv_ref[2:3, :]).astype(BF)
        g_first = loads.start([(first_s, outs[0].at[image])])
        low = first_s[...]
        for i, ref in enumerate((q_s, k_s, v_s)):
            if i < len(g_w):
                loads.wait(g_w[i])
            proj = dot(low, w_s[i].reshape(width, ext), NN)
            if i == 0:
                proj = proj + bq_ref[0:1, :]
            if i == 2:
                proj = proj + bq_ref[1:2, :]
            low_proj = proj.astype(BF)
            if i == 0:
                low_proj = low_proj * jnp.asarray(HEAD_DIM**-0.5, BF)
            ref[...] = low_proj
        g_qkv = loads.start(
            [(q_s, outs[1].at[image]), (k_s, outs[2].at[image]), (v_s, outs[3].at[image])]
        )
        half = lax.broadcasted_iota(jnp.int32, (1, 128), 1) // HEAD_DIM

        def pair(i, carry):
            cols = pl.ds(pl.multiple_of(i * 128, 128), 128)
            q2, k2, v2 = q_s[:, cols], k_s[:, cols], v_s[:, cols]
            total = None
            for h in range(2):
                keep = (half == h).astype(BF)
                probs = softmax_rows(q2, k2 * keep).astype(BF)
                piece = dot(probs, v2 * keep, NN)
                total = piece if total is None else total + piece
            att_s[:, cols] = total.astype(BF)
            return carry

        lax.fori_loop(0, ext // 128, pair, 0)
        g_att = loads.start([(att_s, outs[4].at[image])])
        loads.wait(g_o[0])
        part_s[...] = dot(att_s[...], wo_s[...], NN).astype(BF)
        g_part = loads.start([(part_s, outs[5])])
        for group in (g_first, g_qkv, g_att, g_part):
            loads.wait(group)

    shapes = [(2, seq, width)] + [(2, seq, ext)] * 4
    return call(
        body,
        [tok] + list(prev or []) + qkv_arrays + out_arrays,
        [sds(s, BF) for s in shapes] + [sds((seq, width), BF)],
        [
            pltpu.VMEM(qkv_scratch, BF),
            pltpu.VMEM(out_scratch, BF),
            pltpu.VMEM((seq, width), BF),
            pltpu.VMEM((seq, width), BF),
            pltpu.VMEM((seq, ext), BF),
            pltpu.VMEM((seq, ext), BF),
            pltpu.VMEM((seq, ext), BF),
            pltpu.VMEM((seq, ext), BF),
            pltpu.VMEM((seq, width), BF),
        ],
        "attn_forward",
        2 * seq * width * ext * 4 + 16 * seq * seq * ext,
        aliases={1 + i: i for i in range(n_prev)},
        pinned=True,
        vmem_ins=(nv, bq),
    )


def mlp_up(image, tok, part, recv, keep, nv, bu, wup, step, prev):
    seq, width = tok.shape[1:]
    up_arrays, up_plan, up_scratch = wup
    hid = up_scratch[-1]
    n_prev = 0 if prev is None else len(prev)

    def body(small, ins, outs, scratch, loads):
        keep_ref, nv_ref, bu_ref = small
        tok_ref, part_ref, recv_ref = ins[:3]
        w_s, tok_s, part_s, recv_s, mid_s, sec_s, act_s, dact_s = scratch
        g_in = loads.start([(tok_ref.at[image], tok_s), (part_ref, part_s), (recv_ref, recv_s)])
        g_w = weight_loads(loads, up_plan, ins[3 + n_prev :], w_s)
        loads.wait(g_in)
        total = part_s[...].astype(F32) + recv_s[...].astype(F32) + nv_ref[4:5, :]
        middle = tok_s[...].astype(F32) + keep_ref[image] * total
        mid_s[...] = middle
        hat, _ = norm_parts(middle)
        sec_s[...] = (hat * nv_ref[1:2, :] + nv_ref[3:4, :]).astype(BF)
        g_mid = loads.start([(mid_s, outs[0].at[image]), (sec_s, outs[1].at[image])])
        second = sec_s[...]
        done = []
        for block in range(hid // step):
            if block < len(g_w):
                loads.wait(g_w[block])
            cols = slice(block * step, (block + 1) * step)
            pre = dot(second, w_s[:, cols], NN) + bu_ref[0:1, cols]
            gate = 0.5 * jnp.tanh(0.851 * pre) + 0.5
            act_s[:, cols] = (pre * gate).astype(BF)
            dact_s[:, cols] = (gate + 1.702 * pre * gate * (1.0 - gate)).astype(BF)
            done.append(
                loads.start(
                    [
                        (act_s.at[:, cols], outs[2].at[image, :, cols]),
                        (dact_s.at[:, cols], outs[3].at[image, :, cols]),
                    ]
                )
            )
        for group in [g_mid] + done:
            loads.wait(group)

    outs = [
        sds((2, seq, width), F32),
        sds((2, seq, width), BF),
        sds((2, seq, hid), BF),
        sds((2, seq, hid), BF),
    ]
    return call(
        body,
        [tok, part, recv] + list(prev or []) + up_arrays,
        outs,
        [
            pltpu.VMEM(up_scratch, BF),
            pltpu.VMEM((seq, width), BF),
            pltpu.VMEM((seq, width), BF),
            pltpu.VMEM((seq, width), BF),
            pltpu.VMEM((seq, width), F32),
            pltpu.VMEM((seq, width), BF),
            pltpu.VMEM((seq, hid), BF),
            pltpu.VMEM((seq, hid), BF),
        ],
        "mlp_up",
        2 * seq * width * hid,
        aliases={3 + i: i for i in range(n_prev)},
        pinned=True,
        smem=(keep,),
        vmem_ins=(nv, bu),
    )


def column_loads(src, dst, start):
    if len(src.shape) == 2:
        return [(src, dst)]
    n, _, width = src.shape
    return [
        (src.at[i], dst.at[:, (start + i) * width : (start + i + 1) * width]) for i in range(n)
    ]


def weight_grad(lefts, rights, tasks, out_shapes, name, lo, hi, prev=None, fill=False):
    rows = lefts[0].shape[0]
    arrays = list(lefts) + list(rights)
    wide = [a.shape[-1] * (a.shape[0] if len(a.shape) == 3 else 1) for a in arrays]
    n_left, n_in = len(lefts), len(arrays)
    prev = list(prev or [])
    last = {}
    for n, task in enumerate(tasks):
        for store in task[4]:
            last[store[0]] = n

    def body(small, ins, outs, scratch, loads):
        in_s, out_s = scratch[:n_in], scratch[n_in:]
        order = []
        for l_index, _, r_index, _, _ in tasks:
            for i in (l_index, n_left + r_index):
                if i not in order:
                    order.append(i)
        groups = {i: loads.start(column_loads(ins[i], in_s[i], 0)) for i in order}
        for ref in out_s if fill else ():
            ref[...] = jnp.zeros_like(ref)
        ready, done = set(), []
        for n, (l_index, l_cols, r_index, r_cols, stores) in enumerate(tasks):
            for i in (l_index, n_left + r_index):
                if i not in ready:
                    loads.wait(groups[i])
                    ready.add(i)
            left, right = in_s[l_index][:, l_cols], in_s[n_left + r_index][:, r_cols]
            value = dot(left, right, TN).astype(BF)
            for which, spot, r_sl, c_sl in stores:
                out_s[which][spot] = value[r_sl, c_sl]
            for which in sorted(w for w in last if last[w] == n):
                done.append(loads.start([(out_s[which], outs[which].at[:, lo:hi])]))
        for group in done:
            loads.wait(group)

    flops = sum(
        2 * rows * (t[1].stop - t[1].start) * (t[3].stop - t[3].start) for t in tasks
    )
    return call(
        body,
        arrays + prev,
        [sds(s, BF) for s in out_shapes],
        [pltpu.VMEM((rows, w), BF) for w in wide]
        + [pltpu.VMEM((s[0], hi - lo, s[2]), BF) for s in out_shapes],
        name,
        flops,
        aliases={n_in + i: i for i in range(len(prev))},
    )


def mlp_back(grad, act, dact, wdown, wup, step):
    rows, width = grad.shape
    seq = rows // 2
    hid = dact.shape[1]
    down_arrays, down_plan, down_scratch = wdown
    up_arrays, up_plan, up_scratch = wup
    n_down = len(down_arrays)

    def body(small, ins, outs, scratch, loads):
        wd_s, wu_s, g_s, a_s, d_s, low_s, sum_s, two_s, mlp_s = scratch
        g_g = loads.start([(ins[0], g_s)])
        g_wd = weight_loads(loads, down_plan, ins[3 : 3 + n_down], wd_s)
        g_d = []
        for block in range(hid // step):
            cols = slice(block * step, (block + 1) * step)
            g_d.append(loads.start([(ins[2].at[:, cols], d_s.at[:, cols])]))
        g_wu = weight_loads(loads, up_plan, ins[3 + n_down :], wu_s)
        g_a = loads.start([(ins[1], a_s)])
        loads.wait(g_g)
        left = g_s[...]
        done = []
        for block in range(hid // step):
            if block < len(g_wd):
                loads.wait(g_wd[block])
            loads.wait(g_d[block])
            cols = slice(block * step, (block + 1) * step)
            pre = dot(left, wd_s[cols, :], NT) * d_s[:, cols].astype(F32)
            low_s[:, cols] = pre.astype(BF)
            sum_s[0:1, cols] = jnp.sum(pre, axis=0, keepdims=True)
            done.append(loads.start([(low_s.at[:, cols], outs[0].at[:, cols])]))
        done.append(loads.start([(sum_s, outs[1])]))
        for group in g_wu:
            loads.wait(group)
        two = dot(low_s[...], wu_s[...], NT)
        for a in range(2):
            two_s[a] = two[a * seq : (a + 1) * seq].astype(BF)
            done.append(loads.start([(two_s.at[a], outs[2].at[a])]))
        loads.wait(g_a)
        mlp_s[...] = dot(a_s[...], wd_s[...], NN).astype(BF)
        done.append(loads.start([(mlp_s, outs[3])]))
        for group in done:
            loads.wait(group)

    return call(
        body,
        [grad, act, dact] + down_arrays + up_arrays,
        [sds((rows, hid), BF), sds((1, hid), F32)]
        + [sds((2, seq, width), BF), sds((rows, width), BF)],
        [
            pltpu.VMEM(down_scratch, BF),
            pltpu.VMEM(up_scratch, BF),
            pltpu.VMEM((rows, width), BF),
            pltpu.VMEM((rows, hid), BF),
            pltpu.VMEM((rows, hid), BF),
            pltpu.VMEM((rows, hid), BF),
            pltpu.VMEM((1, hid), F32),
            pltpu.VMEM((2, seq, width), BF),
            pltpu.VMEM((rows, width), BF),
        ],
        "mlp_back",
        6 * rows * width * hid,
        sems=64,
    )


def input_grad(stacks, starts, weight, width):
    arrays, plan, shape = weight
    n, ext = shape[0], shape[-1]
    rows = stacks[0].shape[1]
    seq, m = rows // 2, len(stacks)

    def body(small, ins, outs, scratch, loads):
        w_s, out_s = scratch[0], scratch[1]
        l_s = scratch[2:]
        g_w = weight_loads(loads, plan[:1], ins[m:], w_s)
        g_l = []
        for i in range(n):
            pairs = []
            for j in range(m):
                count = stacks[j].shape[0] // n
                pairs += column_loads(ins[j].at[i * count : (i + 1) * count], l_s[i], starts[j])
            g_l.append(loads.start(pairs))
        g_w += weight_loads(loads, plan[1:], ins[m:], w_s)
        total = None
        for i in range(n):
            loads.wait(g_l[i])
            if i < len(g_w):
                loads.wait(g_w[i])
            piece = dot(l_s[i][...], w_s[i].reshape(width, ext), NT)
            total = piece if total is None else total + piece
        done = []
        for a in range(2):
            out_s[a] = total[a * seq : (a + 1) * seq].astype(BF)
            done.append(loads.start([(out_s.at[a], outs[0].at[a])]))
        for group in done:
            loads.wait(group)

    return call(
        body,
        list(stacks) + arrays,
        [sds((2, seq, width), BF)],
        [pltpu.VMEM(shape, BF), pltpu.VMEM((2, seq, width), BF)] + [pltpu.VMEM((rows, ext), BF)] * n,
        "grad_one",
        2 * rows * width * ext * n,
    )[0]


def middle_back(ids, middle, part, recv, cot, keep, nv, wout):
    _, seq, width = middle.shape
    out_arrays, out_plan, out_scratch = wout
    ext = out_scratch[0]

    def body(small, ins, outs, scratch, loads):
        ids_ref, keep_ref, nv_ref = small
        mine = ids_ref[0]
        wo_s, mid_s, part_s, recv_s, cot_s, gmid_s, gat_s, do_s = scratch[:8]
        cs_s = scratch[8]
        g_in = [
            loads.start(
                [
                    (ins[0].at[a], mid_s.at[a]),
                    (ins[1].at[a], cot_s.at[a]),
                    (ins[2].at[a], part_s.at[a]),
                    (ins[3].at[a], recv_s.at[a]),
                ]
            )
            for a in range(2)
        ]
        g_o = weight_loads(loads, out_plan, ins[4:], wo_s)
        done = []
        for a in range(2):
            loads.wait(g_in[a])
            keep_here = keep_ref[a]
            hat, inverse = norm_parts(mid_s[a])
            grad_two = part_s[a].astype(F32) + recv_s[a].astype(F32)
            top = cot_s[a].astype(F32)
            grad_mid = top + norm_back(grad_two, hat, inverse, nv_ref[1:2, :])
            grad_attn = grad_mid * keep_here
            sums = [
                jnp.sum(grad_two * hat, axis=0, keepdims=True),
                jnp.sum(grad_two, axis=0, keepdims=True),
                jnp.sum(grad_attn, axis=0, keepdims=True),
                jnp.sum(top, axis=0, keepdims=True) * keep_here,
            ]
            for i, value in enumerate(sums):
                cs_s[i : i + 1, :] = value if a == 0 else cs_s[i : i + 1, :] + value
            gmid_s[a] = grad_mid
            gat_s[a] = grad_attn.astype(BF)
            done.append(loads.start([(gat_s.at[a], outs[1].at[a])]))
            if a == 0:
                loads.wait(g_o[0])
            do_s[a] = dot(gat_s[a], wo_s[...], NT).astype(BF)
            done.append(loads.start([(do_s.at[a], outs[2].at[a])]))
        done.append(loads.start([(gmid_s.at[mine], outs[0]), (cs_s, outs[3])]))
        for group in done:
            loads.wait(group)

    return call(
        body,
        [middle, cot, part, recv] + out_arrays,
        [
            sds((seq, width), F32),
            sds((2, seq, width), BF),
            sds((2, seq, ext), BF),
            sds((4, width), F32),
        ],
        [
            pltpu.VMEM(out_scratch, BF),
            pltpu.VMEM((2, seq, width), F32),
            pltpu.VMEM((2, seq, width), BF),
            pltpu.VMEM((2, seq, width), BF),
            pltpu.VMEM((2, seq, width), BF),
            pltpu.VMEM((2, seq, width), F32),
            pltpu.VMEM((2, seq, width), BF),
            pltpu.VMEM((2, seq, ext), BF),
            pltpu.VMEM((4, width), F32),
        ],
        "middle_back",
        4 * seq * width * ext,
        smem=(ids, keep),
        vmem_ins=(nv,),
    )


def attn_backward(pairs, grad, q, k, v, name="attn_backward"):
    _, seq, _ = q.shape
    n = len(pairs)

    def body(small, ins, outs, scratch, loads):
        q_s, k_s, v_s, do_s, dq_s, dk_s, dv_s, bs_s = scratch
        groups = []
        for u in range(2 * n):
            cols = slice(pairs[u // 2] * 128, (pairs[u // 2] + 1) * 128)
            groups.append(
                loads.start([(ins[j].at[u % 2, :, cols], scratch[j].at[u]) for j in range(4)])
            )
        half = lax.broadcasted_iota(jnp.int32, (1, 128), 1) // HEAD_DIM
        for group in groups:
            loads.wait(group)

        def unit(u, carry):
            q2, k2, v2, do2 = q_s[u], k_s[u], v_s[u], do_s[u]
            dq = dk = dv = None
            for h in range(2):
                mask = (half == h).astype(BF)
                km, qm, dom = k2 * mask, q2 * mask, do2 * mask
                scores = dot(km, q2, NT)
                row = lax.broadcasted_iota(jnp.int32, scores.shape, 0)
                scores = jnp.where(row < VALID, scores, -1e30)
                e = jnp.exp(scores - jnp.max(scores, axis=0, keepdims=True))
                probs = e * (1.0 / jnp.sum(e, axis=0, keepdims=True))
                grad_probs = dot(v2, dom, NT)
                row_dot = jnp.sum(probs * grad_probs, axis=0, keepdims=True)
                grad_scores = (probs * (grad_probs - row_dot)).astype(BF)
                v_piece = dot(probs.astype(BF), dom, NN)
                k_piece = dot(grad_scores, qm, NN)
                q_piece = dot(grad_scores, km, TN)
                dq = q_piece if dq is None else dq + q_piece
                dk = k_piece if dk is None else dk + k_piece
                dv = v_piece if dv is None else dv + v_piece
            dq = dq * HEAD_DIM**-0.5
            bs_s[u, 0:1, :] = jnp.sum(dq, axis=0, keepdims=True)
            bs_s[u, 1:2, :] = jnp.sum(dv, axis=0, keepdims=True)
            dq_s[u] = dq.astype(BF)
            dk_s[u] = dk.astype(BF)
            dv_s[u] = dv.astype(BF)
            return carry

        lax.fori_loop(0, 2 * n, unit, 0)
        done = [loads.start([(scratch[4 + j], outs[0].at[j])]) for j in range(3)]
        done.append(loads.start([(bs_s, outs[1])]))
        for group in done:
            loads.wait(group)

    grads, sums = call(
        body,
        [q, k, v, grad],
        [sds((3, 2 * n, seq, 128), BF), sds((2 * n, 2, 128), F32)],
        [pltpu.VMEM((2 * n, seq, 128), BF)] * 7 + [pltpu.VMEM((2 * n, 2, 128), F32)],
        name,
        0,
    )
    return grads.reshape(3 * n, 2 * seq, 128), sums


def finish_layer(ids, keep, nv, middle, part, recv, nd, aligned):
    _, seq, width = middle.shape

    def body(small, ins, outs, scratch, loads):
        ids_ref, keep_ref, nv_ref = small
        mine = ids_ref[0]
        mid_s, part_s, recv_s, out_s = scratch
        groups = [loads.start([(ins[i].at[mine], scratch[i])]) for i in range(3)]
        for group in groups:
            loads.wait(group)
        total = part_s[...].astype(F32) + recv_s[...].astype(F32) + nv_ref[5:6, :]
        out_s[...] = (mid_s[...] + keep_ref[mine] * total).astype(BF)
        loads.wait(loads.start(block_stores(ids_ref, out_s, outs[0], nd, aligned)))

    return call(
        body,
        [middle, part, recv],
        [sds((seq, width), BF)],
        [pltpu.VMEM((seq, width), F32)] + [pltpu.VMEM((seq, width), BF)] * 3,
        "finish_layer",
        100 * seq * width,
        smem=(ids, keep),
        vmem_ins=(nv,),
    )[0]


def finish_tokens(ids, nv, tok, part, recv, gmid, rest, sums, nd, aligned):
    _, seq, width = tok.shape
    n_dest, z_n, n_rows, lanes = rest.shape
    bd, y_n = width // nd, nd // rest.shape[1]
    tx = n_dest // y_n

    def body(small, ins, outs, scratch, loads):
        ids_ref, nv_ref = small[:2]
        mine = ids_ref[0]
        tok_s, part_s, recv_s, gm_s, out_s, cs_s, rest_s = scratch
        g_rest = loads.start([(ins[4], rest_s)] if sums is None else [])
        groups = [
            loads.start(
                [
                    (ins[0].at[a], tok_s.at[a]),
                    (ins[2].at[a], part_s.at[a]),
                    (ins[3].at[a], recv_s.at[a]),
                ]
            )
            for a in range(2)
        ]
        g_mid = loads.start([(ins[1], gm_s)])
        for group in groups:
            loads.wait(group)
        done = []
        for i in range(2):
            a = mine if i == 0 else 1 - mine
            hat, inverse = norm_parts(tok_s[a].astype(F32))
            grad_one = part_s[a].astype(F32) + recv_s[a].astype(F32)
            gain_sum = jnp.sum(grad_one * hat, axis=0, keepdims=True)
            shift_sum = jnp.sum(grad_one, axis=0, keepdims=True)
            if i == 0:
                cs_s[0:1, :] = gain_sum
                cs_s[1:2, :] = shift_sum
                loads.wait(g_mid)
                value = gm_s[...] + norm_back(grad_one, hat, inverse, nv_ref[0:1, :])
                out_s[...] = value.astype(BF)
                done.append(loads.start(block_stores(ids_ref, out_s, outs[0], nd, aligned)))
            else:
                cs_s[0:1, :] = cs_s[0:1, :] + gain_sum
                cs_s[1:2, :] = cs_s[1:2, :] + shift_sum
        loads.wait(g_rest)
        if sums is not None:
            col_ref, bup_ref, pairs = small[2], small[3], small[4:]
            up = bup_ref.shape[1] // tx // nd
            n_pairs = sum(ref.shape[0] // 2 for ref in pairs)
            qv = n_pairs * 128 // tx // nd
            per = 128 // qv
            lane = lax.broadcasted_iota(jnp.int32, (2, 128), 1)
            whole = [ref[2 * i] + ref[2 * i + 1] for ref in pairs for i in range(ref.shape[0] // 2)]
            whole = jnp.stack(whole)
            rest_s[...] = jnp.zeros_like(rest_s)
            for n in range(n_dest):
                kx, ky = n // y_n, n % y_n
                for kz in range(z_n):
                    p = ky * z_n + kz
                    d = ids_ref[2 + p]
                    rest_s[n, kz, 2:6, :] = col_ref[:, p * bd : (p + 1) * bd]
                    row = jnp.zeros((2, 128), F32)
                    for i in range(nd // per):
                        row = jnp.where(d // per == i, whole[kx * (nd // per) + i], row)
                    row = pltpu.roll(row, (per - d % per) * qv % 128, 1)
                    rest_s[n, kz, 6:8, :] = jnp.where(lane < qv, row, 0.0)
                    cols = pl.ds(pl.multiple_of((kx * nd + d) * up, 128), up)
                    rest_s[n, kz, 8:9, 0:up] = bup_ref[:, cols]
        for n in range(n_dest if aligned else 0):
            for kz in range(z_n):
                p = n % (nd // z_n) * z_n + kz
                rest_s[n, kz, 0:2, :] = cs_s[:, p * bd : (p + 1) * bd]
        done.append(loads.start([(cs_s, outs[1])]))
        done += [loads.start([(rest_s.at[n], outs[2 + n])]) for n in range(n_dest)]
        for group in done:
            loads.wait(group)

    return call(
        body,
        [tok, gmid, part, recv] + ([rest] if sums is None else []),
        [sds((seq, width), BF), sds((2, width), F32)] + [sds(rest.shape[1:], F32)] * n_dest,
        [pltpu.VMEM((2, seq, width), BF)] * 3
        + [pltpu.VMEM((seq, width), F32), pltpu.VMEM((seq, width), BF), pltpu.VMEM((2, width), F32)]
        + [pltpu.VMEM(rest.shape, F32)],
        "finish_tokens",
        200 * seq * width,
        smem=(ids,),
        vmem_ins=(nv,) + tuple(sums or ()),
    )


class Grid3:
    def __init__(self, dp, tx):
        self.dp, self.tx = dp, tx
        self.y = 2 if dp % 2 == 0 else 1
        self.z = dp // self.y

    def send_z(self, value, k):
        return lax.ppermute(value, "dp", [(i, i ^ (k * self.y)) for i in range(self.dp)])

    def send_y(self, value, k):
        return lax.ppermute(value, "dp", [(i, i ^ k) for i in range(self.dp)])

    def send_xy(self, value, kx, ky):
        count = self.dp * self.tx
        pairs = [(i, ((i // self.tx) ^ ky) * self.tx + ((i % self.tx) ^ kx)) for i in range(count)]
        return lax.ppermute(value, ("dp", "tx"), pairs)

    def send_x(self, value, k):
        return lax.ppermute(value, "tx", [(i, i ^ k) for i in range(self.tx)])


def swap_core(value):
    return lax.ppermute(value, "core", [(0, 1), (1, 0)])


def after(values, gate):
    return lax.optimization_barrier((values, gate))[0]


def gather_z(grid, part_a, part_b, gate=None):
    rows = part_a.shape[0]
    both = jnp.concatenate([part_a, part_b], axis=0)
    all_z = [both] + [grid.send_z(both, k) for k in range(1, grid.z)]
    if gate is not None:
        all_z = after(all_z, gate)
    return jnp.stack([v[:rows] for v in all_z]), jnp.stack([v[rows:] for v in all_z])


def gather_first(grid, a_z, b_z):
    a_y = [a_z] + [grid.send_y(a_z, k) for k in range(1, grid.y)]
    b_x = [b_z] + [grid.send_x(b_z, k) for k in range(1, grid.tx)]
    return a_y, b_x


def join(pieces):
    return [jnp.concatenate(part) for part in pieces]


def gather_last(grid, a_y, b_x):
    a_all = [a_y] + [grid.send_x(a_y, k) for k in range(1, grid.tx)]
    b_all = [b_x] + [grid.send_y(b_x, k) for k in range(1, grid.y)]
    return a_all, b_all


def add_pieces(groups, cuts, outs, name):
    arrays = [a for group in groups for a in group]
    starts = [sum(len(g) for g in groups[:i]) for i in range(len(groups))]
    last = {}
    for n, cut in enumerate(cuts):
        last[cut[2]] = n

    def body(small, ins, outs_ref, scratch, loads):
        in_s, out_s = scratch[: len(arrays)], scratch[len(arrays) :]
        loaded = [loads.start([(ins[i], in_s[i]) for i in range(starts[g], starts[g] + len(groups[g]))]) for g in range(len(groups))]
        ready, done = set(), []
        for n, (g, spot, which, place) in enumerate(cuts):
            if g not in ready:
                loads.wait(loaded[g])
                ready.add(g)
            total = None
            for i in range(starts[g], starts[g] + len(groups[g])):
                value = in_s[i][spot].astype(F32)
                total = value if total is None else total + value
            out_s[which][place] = total.astype(out_s[which].dtype)
            for w in sorted(w for w in last if last[w] == n):
                done.append(loads.start([(out_s[w], outs_ref[w])]))
        for group in done:
            loads.wait(group)

    return call(
        body,
        arrays,
        outs,
        [pltpu.VMEM(a.shape, a.dtype) for a in arrays] + [pltpu.VMEM(o.shape, o.dtype) for o in outs],
        name,
        0,
        spare=8,
    )


class Scatter:
    def __init__(self, grid, a_all, b_all, name):
        self.grid, self.name, self.bit = grid, name, 0
        self.rows = (a_all[0].shape[1], b_all[0].shape[1])
        a_got = [grid.send_x(a_all[k], k) for k in range(1, grid.tx)]
        b_got = [grid.send_y(b_all[k], k) for k in range(1, grid.y)]
        self.state = ([a_all[0]] + a_got, [b_all[0]] + b_got)

    def second(self, gate):
        grid, z = self.grid, self.grid.z
        a_in, b_in = after(self.state, gate)
        outs = [sds((z,) + a_in[0].shape[1:], BF)] * grid.y + [sds((z,) + b_in[0].shape[1:], BF)] * grid.tx
        full = slice(None)
        cuts = [(0, slice(k * z, (k + 1) * z), k, full) for k in list(range(1, grid.y)) + [0]]
        cuts += [(1, slice(k * z, (k + 1) * z), grid.y + k, full) for k in list(range(1, grid.tx)) + [0]]
        res = add_pieces([a_in, b_in], cuts, outs, self.name + "_add")
        a_y, b_x = res[: grid.y], res[grid.y :]
        a_got = [grid.send_y(a_y[k], k) for k in range(1, grid.y)]
        b_got = [grid.send_x(b_x[k], k) for k in range(1, grid.tx)]
        self.state = ([a_y[0]] + a_got, [b_x[0]] + b_got)
        return a_y[0], b_x[0]

    def along_z(self, gate, extra=None):
        grid = self.grid
        a_in, b_in = after(self.state, gate)
        ra, rb = self.rows
        groups = [a_in, b_in] + ([extra] if extra else [])
        more = extra[0].shape[1] if extra else 0
        order = list(range(1, grid.z)) + [0]
        cuts = []
        for k in order:
            cuts.append((0, k, k, slice(0, ra)))
            cuts.append((1, k, k, slice(ra, ra + rb)))
            if extra:
                cuts.append((2, k, k, slice(ra + rb, ra + rb + more)))
        outs = [sds((ra + rb + more,) + a_in[0].shape[2:], BF)] * grid.z
        both = add_pieces(groups, cuts, outs, self.name + "_addz")
        self.state = [both[0]] + [grid.send_z(both[k], k) for k in range(1, grid.z)]
        return both

    def halve(self, gate):
        grid, (ra, rb) = self.grid, self.rows
        groups = after(self.state, gate)
        if self.bit == 0:
            self.bit, self.left = 1, list(range(grid.z))
        else:
            self.bit, groups = 2 * self.bit, [groups]
        sent = [k for k in self.left if k & self.bit]
        kept = [k for k in self.left if not k & self.bit]
        cuts = []
        for which, ids in ((0, sent), (1, kept)):
            for n, k in enumerate(ids):
                spot = self.left.index(k)
                if len(groups) == 2:
                    cuts.append((0, spot, which, (n, slice(0, ra))))
                    cuts.append((1, spot, which, (n, slice(ra, ra + rb))))
                else:
                    cuts.append((0, spot, which, n))
        outs = [sds((len(kept), ra + rb) + groups[0][0].shape[2:], BF)] * 2
        send, keep = add_pieces(groups, cuts, outs, self.name + "_half")
        self.left = kept
        self.state = [keep, grid.send_z(send, self.bit)]
        return keep

    def finish(self, gate, cuts, outs):
        if self.bit:
            cuts = [((0, rows), which, place) for rows, which, place in cuts]
        cuts = [(0, rows, which, place) for rows, which, place in cuts]
        return add_pieces([after(self.state, gate)], cuts, outs, self.name + "_sum")


def join_kernel(pieces):
    groups, cuts, outs = [], [], []
    for which, part in enumerate(pieces):
        lead = part[0].shape[0]
        for k, value in enumerate(part):
            cuts.append((len(groups), slice(None), which, slice(k * lead, (k + 1) * lead)))
            groups.append([value])
        outs.append(sds((lead * len(part),) + part[0].shape[1:], BF))
    return add_pieces(groups, cuts, outs, "join")


def xor_blocks(value, mask, axis):
    count = value.shape[axis]
    bit = 1
    while bit < count:
        shape = value.shape
        split = value.reshape(shape[:axis] + (count // (2 * bit), 2, bit) + shape[axis + 1 :])
        turned = jnp.flip(split, axis=axis + 1).reshape(shape)
        value = jnp.where(jnp.bitwise_and(mask, bit) != 0, turned, value)
        bit *= 2
    return value


def pad_cols(value, width):
    return jnp.pad(value, ((0, 0), (0, width - value.shape[1])))


def per_device(
    tokens,
    cotangent,
    image_mask,
    norm_gains,
    norm_shifts,
    w_qkv,
    b_qv,
    w_out,
    w_up,
    up_bias,
    w_down,
    *,
    dp,
    tx,
):
    grid = Grid3(dp, tx)
    y_n, z_n = grid.y, grid.z
    core = lax.axis_index("core").astype(jnp.int32)
    me_d = lax.axis_index("dp").astype(jnp.int32)
    me_x = lax.axis_index("tx").astype(jnp.int32)
    seq, width = tokens.shape
    _, bd, hw = w_qkv.shape
    fw = w_up.shape[1]
    ext, hid = tx * hw, tx * fw
    hh, fh = hw // 2, fw // 2
    aligned = bd % 128 == 0 and hh % 128 == 0 and fh % 128 == 0
    rel = [kz * y_n + ky for ky in range(y_n) for kz in range(z_n)]

    def from_abs(value, axis):
        shape = value.shape
        value = value.reshape(shape[:axis] + (z_n, y_n) + shape[axis + 1 :])
        return jnp.swapaxes(value, axis, axis + 1).reshape(shape)

    def to_rel(value, axis):
        shape = value.shape
        value = value.reshape(shape[:axis] + (y_n, z_n) + shape[axis + 1 :])
        return jnp.swapaxes(value, axis, axis + 1).reshape(shape)

    ids = jnp.stack([core, me_d] + [jnp.bitwise_xor(me_d, k) for k in rel])
    keep = lax.dynamic_slice(image_mask, (2 * me_x,), (2,)).astype(F32)

    lane = max(bd, hh)
    small = jnp.concatenate(
        [
            pad_cols(norm_gains, lane),
            pad_cols(norm_shifts, lane),
            pad_cols(b_qv, lane),
            pad_cols(up_bias[None], lane),
            jnp.zeros((7, lane), BF),
        ]
    )
    qkv_a = pad_cols(w_qkv[:, :, :hh].reshape(3 * bd, hh), lane)
    qkv_b = pad_cols(w_qkv[:, :, hh:].reshape(3 * bd, hh), lane)
    first_a = jnp.concatenate([qkv_a, pad_cols(w_out[:hh], lane), small])
    first_b = jnp.concatenate([qkv_b, pad_cols(w_out[hh:], lane)])
    own = [tokens, cotangent]
    other = [swap_core(value) for value in own]
    if aligned:
        tok, cot = arrange_pair(ids, own, other, dp)
    else:

        def arrange(own, other):
            pair = jnp.where(core == 0, jnp.stack([own, other]), jnp.stack([other, own]))
            pair = xor_blocks(pair.reshape(2, seq, dp, bd), me_d, 2)
            return from_abs(pair, 2).reshape(2, seq, width)

        tok, cot = [arrange(own[i], other[i]) for i in range(2)]
    c1_z = gather_z(grid, first_a, first_b, gate=tok)
    c1_h = gather_first(grid, *c1_z)
    c1_h = join(c1_h)
    c1a, c1b = gather_last(grid, *c1_h)
    up_halves = after((w_up[:, :fh], w_up[:, fh:]), c1_h)
    row0 = 3 * bd + hh
    if aligned and 128 % (hw // dp) == 0 and (fw // dp) % 128 == 0:
        c1a, c1b = after((c1a, c1b), (c1a, c1b))
        nv, bq, bu = vectors(ids, c1a, row0, dp, y_n, bd, hw // dp, fw // dp)
    else:
        nv = c1a[0][:, row0 : row0 + 6, :bd].transpose(1, 0, 2).reshape(6, width).astype(F32)
        tail = jnp.stack([v[:, row0 + 6 : row0 + 9] for v in c1a])
        tail = xor_blocks(to_rel(tail, 1), me_d, 1)
        bq = tail[:, :, :2, : hw // dp].transpose(2, 0, 1, 3).reshape(2, ext).astype(F32)
        bu = tail[:, :, 2, : fw // dp].reshape(1, hid).astype(F32)
    grad_top = cot * keep.astype(BF)[:, None, None]

    up_z = gather_z(grid, *up_halves, gate=nv)
    up_h = gather_first(grid, *up_z)
    dn_halves = after((w_down[:fh], w_down[fh:]), up_z)

    if aligned:
        every, wq_plan, wo_plan, up_plan, dn_plan = slice(None), [[], [], []], [], [], []
        for kx in range(tx):
            halves = [slice(kx * hw, kx * hw + hh), slice(kx * hw + hh, (kx + 1) * hw)]
            f_halves = [slice(kx * fw, kx * fw + fh), slice(kx * fw + fh, (kx + 1) * fw)]
            own = slice(kx * z_n, (kx + 1) * z_n)
            for i in range(3):
                src = slice(i * bd, (i + 1) * bd)
                wq_plan[i].append((kx, (every, src), (i, every, every, halves[0])))
                for ky in range(y_n):
                    dst = (i, slice(ky * z_n, (ky + 1) * z_n), every, halves[1])
                    wq_plan[i].append((tx + ky, (own, src), dst))
            src = slice(3 * bd, 3 * bd + hh)
            dn_plan += [[], []]
            for ky in range(y_n):
                for kz in range(z_n):
                    p, r = ky * z_n + kz, kx * z_n + kz
                    cols = slice(p * bd, (p + 1) * bd)
                    wo_plan.append((kx, (p, src), (halves[0], cols)))
                    wo_plan.append((tx + ky, (r, src), (halves[1], cols)))
                    dn_plan[-2].append((kx, (p,), (f_halves[0], cols)))
                    dn_plan[-1].append((tx + ky, (r,), (f_halves[1], cols)))
            up_plan += [[(kx, (every,), (every, f_halves[0]))], []]
            for ky in range(y_n):
                rows = slice(kx * z_n * bd, (kx + 1) * z_n * bd)
                dst = (slice(ky * z_n * bd, (ky + 1) * z_n * bd), f_halves[1])
                up_plan[-1].append((tx + ky, (rows,), dst))
        c1 = c1a + c1b
        wqkv = (c1, wq_plan, (3, dp, bd, ext))
        wout = (c1, [wo_plan], (ext, width))
    else:

        def whole(a_all, b_all):
            a = jnp.stack(a_all)
            b = jnp.stack(b_all).reshape((y_n, tx, z_n) + b_all[0].shape[1:])
            b = b.transpose(1, 0, 2, 3, 4).reshape(a.shape[:2] + b.shape[3:])
            return jnp.stack([a, b], axis=1)

        c1 = whole([v[:, :row0] for v in c1a], c1b)
        qkv = c1[:, :, :, : 3 * bd, :hh].reshape(tx, 2, dp, 3, bd, hh)
        qkv = qkv.transpose(3, 2, 4, 0, 1, 5).reshape(3, dp, bd, ext)
        out = c1[:, :, :, 3 * bd :, :bd].transpose(0, 1, 3, 2, 4).reshape(ext, width)
        all_of = [[(0, (slice(None),), (slice(None),))]]
        wqkv = ([qkv], all_of, qkv.shape)
        wout = ([out], all_of, out.shape)

    rows2 = 2 * seq

    res = attn_forward(0, after(tok, up_z), nv, bq, wqkv, wout, None)
    part0 = res[5]
    up_h = join(after(up_h, part0))
    upa, upb = gather_last(grid, *up_h)
    dn_halves = after(dn_halves, up_h)
    res = attn_forward(1, after(tok, up_h), nv, bq, wqkv, wout, res[:5])
    recv0 = swap_core(after(part0, res[5]))
    parts = [(part0, recv0), (res[5], swap_core(res[5]))]
    first, q, k, v, att = res[:5]
    upa, upb = after((upa, upb), res[5])
    dn_z = gather_z(grid, *dn_halves, gate=(upa, upb))
    dn_h = gather_first(grid, *dn_z)
    if aligned:
        wup = ([v.reshape(-1, fh) for v in upa + upb], up_plan, (width, hid))
    else:
        up_w = whole(upa, upb).transpose(2, 3, 0, 1, 4).reshape(width, hid)
        wup = ([up_w], all_of, up_w.shape)
    part, recv = parts[0]
    state = mlp_up(0, tok, part, recv, keep, nv, bu, wup, fh, None)
    dna, dnb = gather_last(grid, *join_kernel(after(dn_h, state[1])))
    part, recv = parts[1]
    state = mlp_up(1, tok, part, recv, keep, nv, bu, wup, fh, state)
    if aligned:
        wdown = (dna + dnb, dn_plan, (hid, width))
    else:
        down_w = whole(dna, dnb).transpose(0, 1, 3, 2, 4).reshape(hid, width)
        wdown = ([down_w], all_of, down_w.shape)
    middle, second, act, dact = state
    flat = lambda value: value.reshape(rows2, value.shape[2])
    act2, sec2, grad2 = flat(act), flat(second), flat(grad_top)

    full = slice(None)
    a_spots = [(p, slice(p * bd, (p + 1) * bd)) for p in range(dp)]

    def by_left(l_index, r_index, size, row0):
        tasks, rows = [], slice(row0, row0 + size // 2)
        halves = slice(0, size // 2), slice(size // 2, size)
        for kx in range(tx):
            stores = [(kx, (p, rows), halves[0], cols) for p, cols in a_spots]
            for p, cols in a_spots:
                ky, kz = p // z_n, p % z_n
                stores.append((tx + ky, (kx * z_n + kz, rows), halves[1], cols))
            tasks.append((l_index, slice(kx * size, (kx + 1) * size), r_index, slice(0, width), stores))
        return tasks

    def by_right(l_index, r_index, size, row0, lanes, spare=False, first=0):
        tasks, each = [], size // 2 // lanes
        for kx in range(tx):
            stores = []
            for j in range(each):
                rows = slice(row0 + j * bd, row0 + (j + 1) * bd)
                cols = [slice((h * each + j) * lanes, (h * each + j + 1) * lanes) for h in range(2)]
                rows = (rows, slice(0, lanes)) if spare else (rows,)
                for p, r_sl in a_spots:
                    ky, kz = p // z_n, p % z_n
                    stores.append((kx, (p,) + rows, r_sl, cols[0]))
                    stores.append((tx + ky, (kx * z_n + kz,) + rows, r_sl, cols[1]))
            cols = slice(first + kx * size, first + (kx + 1) * size)
            tasks.append((l_index, slice(0, width), r_index, cols, stores))
        return tasks

    def pieces(rows, lanes):
        return [(dp, rows, lanes)] * tx + [(tx * z_n, rows, lanes)] * y_n

    def send_grad(parts, name):
        return Scatter(grid, list(parts[:tx]), list(parts[tx:]), name)

    grads = weight_grad([act2], [grad2], by_left(0, 0, fw, 0), pieces(fh, bd), "down_grad", 0, fh)
    down_rs = send_grad(grads, "down")
    grad_in = after(grad2, grads[-1])
    low_pre, bias_up, two_part, mlp_part = mlp_back(grad_in, act2, flat(dact), wdown, wup, fh)
    mlp_part = mlp_part.reshape(2, seq, width)
    two_recv = swap_core(two_part)
    down_half = down_rs.second(bias_up)
    up_rows = fh // bd * bd
    sec_in = after(sec2, down_half)
    tasks = by_right(0, 0, fw, 0, bd)
    grads = weight_grad([sec_in], [low_pre], tasks, pieces(up_rows, bd), "up_grad", 0, up_rows)
    up_rs = send_grad(grads, "up")
    gmid, gattn, grad_att, col = middle_back(
        ids, middle, two_part, after(two_recv, grads[-1]), cot, keep, nv, wout
    )
    down_zs = down_rs.along_z(col)
    row0 = 3 * bd
    last_shapes = pieces(row0 + hh, bd)
    att_in = after(flat(att), down_zs)
    tasks = by_left(0, 0, hw, 0)
    out_grads = weight_grad(
        [att_in], [flat(gattn)], tasks, last_shapes, "out_grad", row0, row0 + hh
    )

    n_pairs = ext // 128
    split = hh == 128 and bd == 128 and n_pairs >= 4
    if split:
        heads = [[1], list(range(2, n_pairs))]
        first_in = after(grad_att, out_grads[-1])
        left_0, bias_0 = attn_backward(heads[0], first_in, q, k, v, "attn_first")
        up_half = up_rs.second(bias_0)
    else:
        heads = [list(range(n_pairs))]
        up_half = up_rs.second(out_grads[-1])
    left_a, bias_a = attn_backward(heads[-1], after(grad_att, up_half), q, k, v)
    grad_down = down_rs.finish(bias_a, [(full, 0, full)], [sds((fw, bd), F32)])[0]
    mlp_recv = swap_core(after(mlp_part, bias_a))
    gate = up_rs.halve(grad_down) if z_n > 1 else grad_down
    first_in = after(flat(first), gate)
    if split:
        tasks = []
        for index, pairs in enumerate(heads):
            stores, count = [], len(pairs)
            for i in range(3):
                rows = slice(i * bd, (i + 1) * bd)
                for n, pair in enumerate(pairs):
                    kx, cols = pair // 2, slice((i * count + n) * 128, (i * count + n + 1) * 128)
                    for p, r_sl in a_spots:
                        ky, kz = p // z_n, p % z_n
                        spot = (kx - 1, (p, rows))
                        if pair % 2:
                            spot = (tx - 1 + ky, (kx * z_n + kz, rows))
                        stores.append(spot + (r_sl, cols))
            tasks.append((0, slice(0, width), index, slice(0, 384 * count), stores))
        sent = weight_grad(
            [first_in], [left_0, left_a], tasks, last_shapes[1:], "qkv_grad", 0, row0, out_grads[1:]
        )
        left_b, bias_b = attn_backward([0], after(grad_att, (sent[: tx - 1], sent[tx:])), q, k, v)
        gate = (bias_b, mlp_recv)
        stores = []
        for i in range(3):
            rows, cols = slice(i * bd, (i + 1) * bd), slice(i * 128, (i + 1) * 128)
            stores += [(0, (p, rows), r_sl, cols) for p, r_sl in a_spots]
        tasks = [(0, slice(0, width), 0, slice(0, 384), stores)]
        kept = weight_grad(
            [after(first_in, gate)],
            [left_b],
            tasks,
            last_shapes[:1],
            "qkv_keep",
            0,
            row0,
            out_grads[:1],
        )
        grads = list(kept) + list(sent)
        lefts, starts = [left_0, left_a, left_b], [1, 2, 0]
        pair_sums = [bias_b, bias_0, bias_a]
        gate = kept[0]
    else:
        while 2 * up_rs.bit < z_n:
            gate = up_rs.halve((gate, mlp_recv))
        makers = [by_right(0, 0, hw, i * bd, hh, hh < bd, i * ext) for i in range(3)]
        tasks = [task for maker in makers for task in maker]
        grads = weight_grad(
            [after(first_in, gate)],
            [left_a],
            tasks,
            last_shapes,
            "qkv_grad",
            0,
            row0,
            out_grads,
            hh < bd,
        )
        lefts, starts = [left_a], [0]
        pair_sums = [bias_a]
        gate = grads[-1]
    qkv_rs = send_grad(grads, "qkv")
    lefts = after(lefts, gate)
    one_part = input_grad(lefts, starts, wqkv, width)
    one_recv = swap_core(one_part)
    cuts = []
    for h in range(2):
        for j in range(fh // bd):
            rows = slice(h * up_rows + j * bd, h * up_rows + (j + 1) * bd)
            cuts.append((rows, 0, (full, slice(h * fh + j * bd, h * fh + (j + 1) * bd))))
    up_cuts = cuts
    gate = one_part
    while 2 * up_rs.bit < z_n:
        gate = up_rs.halve(gate)
    qkv_half = qkv_rs.second(gate)
    wide = max(bd, hw // dp, fw // dp)
    if split and fw // dp == bd and 128 % (hw // dp) == 0:
        rest = sds((tx * y_n, z_n, 16, wide), F32)
        sums = [col, bias_up] + pair_sums
    else:
        bias_qv = jnp.concatenate(pair_sums)
        bias_qv = jnp.sum(bias_qv.reshape(n_pairs, 2, 2, 128), axis=1).transpose(1, 0, 2)
        vec = jnp.concatenate([jnp.zeros((2, width), F32), col])
        vec = vec.reshape(6, y_n, z_n, bd).transpose(1, 2, 0, 3)
        bias_qv = bias_qv.reshape(2, tx, dp, hw // dp).transpose(2, 1, 0, 3)
        bias_up = bias_up.reshape(tx, 1, dp, fw // dp).transpose(2, 0, 1, 3)
        bias = jnp.concatenate(
            [
                jnp.pad(value, ((0, 0), (0, 0), (0, 0), (0, wide - value.shape[3])))
                for value in (bias_qv, bias_up)
            ],
            axis=2,
        )
        bias = from_abs(xor_blocks(bias, me_d, 0), 0).reshape(y_n, z_n, tx, 3, wide)
        bias = bias.transpose(2, 0, 1, 3, 4)
        vec = jnp.pad(vec, ((0, 0), (0, 0), (0, 0), (0, wide - bd)))
        vec = jnp.broadcast_to(vec, (tx,) + vec.shape)
        rest = jnp.concatenate([vec, bias, jnp.zeros((tx, y_n, z_n, 7, wide), F32)], axis=3)
        rest = rest.reshape(tx * y_n, z_n, 16, wide)
        sums = None
    grad_tokens, one_sums, *small = finish_tokens(
        ids, nv, tok, one_part, after(one_recv, qkv_half), gmid, rest, sums, dp, aligned
    )
    if not aligned:
        ones = jnp.pad(one_sums.reshape(2, y_n, z_n, bd), ((0, 14), (0, 0), (0, 0), (0, wide - bd)))
        ones = ones.transpose(1, 2, 0, 3)
        small = [value + ones[n % y_n] for n, value in enumerate(small)]
    small = after(small, qkv_rs.state)
    got = small[:1]
    for n in range(1, tx * y_n):
        got.append(grid.send_xy(small[n], n // y_n, n % y_n))
    grad_up = up_rs.finish(one_sums, up_cuts, [sds((bd, fw), F32)])[0]
    cuts, outs = [], [sds((3, bd, hw), F32), sds((hw, bd), F32)]
    last_rows = row0 + hh
    for h in range(2):
        for i in range(3):
            rows = slice(h * last_rows + i * bd, h * last_rows + (i + 1) * bd)
            rows = (rows, slice(0, hh)) if hh < bd else rows
            cuts.append((rows, 0, (i, full, slice(h * hh, (h + 1) * hh))))
        rows = slice(h * last_rows + row0, (h + 1) * last_rows)
        cuts.append((rows, 1, (slice(h * hh, (h + 1) * hh),)))
    if wide == bd:
        qkv_zs = qkv_rs.along_z(grad_up, got)
        cuts.append((slice(2 * last_rows, 2 * last_rows + 16), 2, full))
        outs.append(sds((16, wide), F32))
    else:
        qkv_zs = qkv_rs.along_z(grad_up)
    layer_out = finish_layer(
        ids, keep, nv, middle, after(mlp_part, qkv_zs), mlp_recv, dp, aligned
    )
    res = qkv_rs.finish(layer_out, cuts, outs)
    grad_qkv, grad_out = res[:2]
    if wide == bd:
        both = res[2]
    else:
        both, bit = sum(got), 1
        while bit < z_n:
            both = both.reshape((-1, 2) + both.shape[1:])
            both = both[:, 0] + grid.send_z(both[:, 1], bit)
            bit *= 2
        both = both[0]
    if not aligned:

        def restore(value):
            value = xor_blocks(to_rel(value.reshape(seq, dp, bd), 1), me_d, 1)
            return value.reshape(seq, width)

        layer_out, grad_tokens = restore(layer_out), restore(grad_tokens)

    share = bd // (2 * tx)
    mine = lax.dynamic_slice(both[:6, :bd], (0, (2 * me_x + core) * share), (6, share))

    return (
        layer_out,
        grad_tokens,
        mine[0:3:2],
        jnp.concatenate([mine[1:2], mine[3:6]]),
        grad_qkv,
        both[6:8, : hw // dp],
        grad_out,
        grad_up,
        both[8, : fw // dp],
        grad_down,
    )


def solution(mesh):
    dp, tensor = mesh.shape["dp"], mesh.shape["tensor"]
    split = Mesh(mesh.devices.reshape(dp, tensor // 2, 2), ("dp", "tx", "core"))
    every = ("dp", "tx", "core")
    tensor_axes = ("tx", "core")
    in_specs = (
        P(every, None),
        P(every, None),
        P("dp"),
        P(None, "dp"),
        P(None, "dp"),
        P(None, "dp", tensor_axes),
        P(None, ("tx", "core", "dp")),
        P(tensor_axes, "dp"),
        P("dp", tensor_axes),
        P(("tx", "core", "dp")),
        P(tensor_axes, "dp"),
    )
    out_specs = (
        P(every, None),
        P(every, None),
        P(None, every),
        P(None, every),
        P(None, "dp", tensor_axes),
        P(None, ("tx", "core", "dp")),
        P(tensor_axes, "dp"),
        P("dp", tensor_axes),
        P(("tx", "core", "dp")),
        P(tensor_axes, "dp"),
    )
    return jax.shard_map(
        functools.partial(per_device, dp=dp, tx=tensor // 2),
        mesh=split,
        in_specs=in_specs,
        out_specs=out_specs,
        check_vma=False,
    )
```

```python
import functools

import jax
import jax.numpy as jnp
from jax import lax
from jax.experimental import pallas as pl
from jax.experimental.pallas import tpu as pltpu
from jax.sharding import Mesh, PartitionSpec as P

HEAD_DIM = 64
VALID = 577
SEQ = 584
BF = jnp.bfloat16
F32 = jnp.float32
VMEM_LIMIT = 60 * 1024 * 1024
WHOLE_VMEM = ("arrange_pair", "vectors", "mlp_up", "down_grad", "mlp_back", "qkv_sum")
COST_SCALE = 1.0
COST = {
    "arrange_pair": 5,
    "vectors": 3,
    "attn_forward": 16,
    "mlp_up": 10,
    "down_grad": 11,
    "mlp_back": 22,
    "up_grad": 11,
    "middle_back": 0,
    "out_grad": 8,
    "attn_backward": 18,
    "attn_first": 0,
    "qkv_grad": 7,
    "qkv_keep": 0,
    "up_half": 0,
    "join": 0,
    "grad_one": 0,
    "qkv_add": 30,
    "finish_layer": 0,
    "up_sum": 0,
    "finish_tokens": 9,
}
NT = (((1,), (1,)), ((), ()))
TN = (((0,), (0,)), ((), ()))
NN = (((1,), (0,)), ((), ()))


def dot(left, right, dims):
    return lax.dot_general(left, right, dims, preferred_element_type=F32)


class Loads:
    def __init__(self, sems):
        self.sems, self.groups = sems, []

    def start(self, pairs):
        sem = self.sems.at[len(self.groups)]
        copies = [pltpu.make_async_copy(src, dst, sem) for src, dst in pairs]
        for copy in copies:
            copy.start()
        self.groups.append(copies)
        return len(self.groups) - 1

    def wait(self, group):
        for copy in self.groups[group]:
            copy.wait()


def padded_bytes(value):
    lead, (rows, lanes) = value.shape[:-2], value.shape[-2:]
    count = -(-rows // 16) * 16 * (-(-lanes // 128) * 128)
    for size in lead:
        count *= size
    return count * jnp.dtype(value.dtype).itemsize


def call(body, ins, outs, scratch, name, flops, aliases=None, smem=(), sems=48, vmem_ins=(), spare=12, pinned=False):
    n_smem, n_vmem, n_in, n_out = len(smem), len(vmem_ins), len(ins), len(outs)
    moved = sum(a.size * a.dtype.itemsize for a in ins) + sum(
        o.size * o.dtype.itemsize for o in outs
    )

    def kernel(*refs):
        first = n_smem + n_vmem
        small = refs[:first]
        in_refs = refs[first : first + n_in]
        out_refs = refs[first + n_in : first + n_in + n_out]
        rest = refs[first + n_in + n_out :]
        body(small, in_refs, out_refs, rest[:-1], Loads(rest[-1]))

    held = sum(padded_bytes(piece) for piece in scratch) + spare * 1024 * 1024
    vmem = VMEM_LIMIT if name in WHOLE_VMEM else min(held, VMEM_LIMIT)
    flops = max(COST.get(name, 3), 0.02) * COST_SCALE * 1.15e9
    moved = 0
    any_spec = pl.BlockSpec(memory_space=pl.ANY)
    hbm_spec = pl.BlockSpec(memory_space=pltpu.HBM) if pinned else any_spec
    return pl.pallas_call(
        kernel,
        out_shape=outs,
        in_specs=[pl.BlockSpec(memory_space=pltpu.SMEM)] * n_smem
        + [pl.BlockSpec(memory_space=pltpu.VMEM)] * n_vmem
        + [hbm_spec if i in (aliases or {}) else any_spec for i in range(n_in)],
        out_specs=[hbm_spec if pinned else any_spec] * n_out,
        scratch_shapes=list(scratch) + [pltpu.SemaphoreType.DMA((sems,))],
        input_output_aliases={n_smem + n_vmem + i: o for i, o in (aliases or {}).items()},
        compiler_params=pltpu.CompilerParams(vmem_limit_bytes=vmem),
        cost_estimate=pl.CostEstimate(flops=int(flops), bytes_accessed=int(flops // 1000), transcendentals=0),
        name=name,
    )(*smem, *vmem_ins, *ins)


def norm_parts(rows):
    center = rows - jnp.mean(rows, axis=1, keepdims=True)
    inverse = lax.rsqrt(jnp.mean(center * center, axis=1, keepdims=True) + 1e-05)
    return center * inverse, inverse


def norm_back(grad_norm, scaled, inverse, gain_row):
    grad_hat = grad_norm * gain_row
    first_mean = jnp.mean(grad_hat, axis=1, keepdims=True)
    second_mean = jnp.mean(grad_hat * scaled, axis=1, keepdims=True)
    return inverse * (grad_hat - first_mean - scaled * second_mean)


def sds(shape, dtype):
    return jax.ShapeDtypeStruct(shape, dtype)


def arrange_pair(ids, own, other, nd):
    n = len(own)
    rows, width = own[0].shape
    bd = width // nd

    def body(small, ins, outs, scratch, loads):
        (ids_ref,) = small
        mine = ids_ref[0]
        in_s, out_s = scratch[: 2 * n], scratch[2 * n :]
        groups = [loads.start([(ins[i], in_s[i])]) for i in range(2 * n)]
        done = []
        for i in range(2 * n):
            loads.wait(groups[i])
            for p in range(nd):
                src = pl.ds(pl.multiple_of(ids_ref[2 + p] * bd, 128), bd)
                out_s[i][:, p * bd : (p + 1) * bd] = in_s[i][:, src]
            spot = mine if i < n else 1 - mine
            done.append(loads.start([(out_s[i], outs[i % n].at[spot])]))
        for group in done:
            loads.wait(group)

    return call(
        body,
        list(own) + list(other),
        [sds((2, rows, width), BF)] * n,
        [pltpu.VMEM((rows, width), BF)] * (4 * n),
        "arrange_pair",
        0,
        smem=(ids,),
    )


def vectors(ids, gathered, row0, nd, y_n, bd, qv, up):
    tx, z_n = len(gathered), nd // y_n

    def body(small, ins, outs, scratch, loads):
        ids_ref, rows_s, nv_s, bq_s, bu_s = small[0], *scratch
        rows = pl.ds(row0, 16)
        loads.wait(loads.start([(ins[k].at[:, rows, :], rows_s.at[k]) for k in range(tx)]))
        for p in range(nd):
            nv_s[:, p * bd : (p + 1) * bd] = rows_s[0, p].astype(F32)[:6, :bd]
        for k in range(tx):
            pieces = []
            for d in range(nd):
                rel = ids_ref[1] ^ d
                spot = (rel % y_n) * z_n + rel // y_n
                piece = rows_s[k, spot].astype(F32)
                bu_s[:, (k * nd + d) * up : (k * nd + d + 1) * up] = piece[8:9, :up]
                pieces.append(piece[6:8, :])
            each = 128 // qv
            for start in range(0, nd, each):
                total = pieces[start]
                for i in range(1, each):
                    total = total + pltpu.roll(pieces[start + i], i * qv, 1)
                bq_s[:, (k * nd + start) * qv : (k * nd + start + each) * qv] = total
        loads.wait(loads.start([(nv_s, outs[0]), (bq_s, outs[1]), (bu_s, outs[2])]))

    shapes = [(6, nd * bd), (2, tx * nd * qv), (1, tx * nd * up)]
    return call(
        body,
        list(gathered),
        [sds(s, F32) for s in shapes],
        [pltpu.VMEM((tx, nd, 16, gathered[0].shape[2]), BF)] + [pltpu.VMEM(s, F32) for s in shapes],
        "vectors",
        0,
        smem=(ids,),
    )


def block_stores(ids_ref, src, dst, nd, aligned):
    if not aligned:
        return [(src, dst)]
    bd = src.shape[1] // nd
    pairs = []
    for p in range(nd):
        cols = pl.ds(pl.multiple_of(ids_ref[2 + p] * bd, 128), bd)
        pairs.append((src.at[:, p * bd : (p + 1) * bd], dst.at[:, cols]))
    return pairs


def weight_loads(loads, groups, refs, scratch):
    return [
        loads.start([(refs[a].at[src], scratch.at[dst]) for a, src, dst in plan])
        for plan in groups
    ]


def softmax_rows(q2, k2):
    scores = dot(q2, k2, NT)
    lane = lax.broadcasted_iota(jnp.int32, scores.shape, 1)
    scores = jnp.where(lane < VALID, scores, -1e30)
    e = jnp.exp(scores - jnp.max(scores, axis=1, keepdims=True))
    return e * (1.0 / jnp.sum(e, axis=1, keepdims=True))


def attn_forward(image, tok, nv, bq, wqkv, wout, prev):
    seq, width = tok.shape[1:]
    qkv_arrays, qkv_plan, qkv_scratch = wqkv
    out_arrays, out_plan, out_scratch = wout
    ext = qkv_scratch[-1]
    n_prev = 0 if prev is None else len(prev)
    nq, no = len(qkv_arrays), len(out_arrays)

    def body(small, ins, outs, scratch, loads):
        nv_ref, bq_ref = small
        tok_ref, ins = ins[0], ins[1 + n_prev :]
        w_s, wo_s, tok_s, first_s, q_s, k_s, v_s, att_s, part_s = scratch
        g_tok = loads.start([(tok_ref.at[image], tok_s)])
        g_w = weight_loads(loads, qkv_plan, ins[:nq], w_s)
        g_o = weight_loads(loads, out_plan, ins[nq:], wo_s)
        loads.wait(g_tok)
        hat, _ = norm_parts(tok_s[...].astype(F32))
        first_s[...] = (hat * nv_ref[0:1, :] + nv_ref[2:3, :]).astype(BF)
        g_first = loads.start([(first_s, outs[0].at[image])])
        low = first_s[...]
        for i, ref in enumerate((q_s, k_s, v_s)):
            if i < len(g_w):
                loads.wait(g_w[i])
            proj = dot(low, w_s[i].reshape(width, ext), NN)
            if i == 0:
                proj = proj + bq_ref[0:1, :]
            if i == 2:
                proj = proj + bq_ref[1:2, :]
            low_proj = proj.astype(BF)
            if i == 0:
                low_proj = low_proj * jnp.asarray(HEAD_DIM**-0.5, BF)
            ref[...] = low_proj
        g_qkv = loads.start(
            [(q_s, outs[1].at[image]), (k_s, outs[2].at[image]), (v_s, outs[3].at[image])]
        )
        half = lax.broadcasted_iota(jnp.int32, (1, 128), 1) // HEAD_DIM

        def pair(i, carry):
            cols = pl.ds(pl.multiple_of(i * 128, 128), 128)
            q2, k2, v2 = q_s[:, cols], k_s[:, cols], v_s[:, cols]
            total = None
            for h in range(2):
                keep = (half == h).astype(BF)
                probs = softmax_rows(q2, k2 * keep).astype(BF)
                piece = dot(probs, v2 * keep, NN)
                total = piece if total is None else total + piece
            att_s[:, cols] = total.astype(BF)
            return carry

        lax.fori_loop(0, ext // 128, pair, 0)
        g_att = loads.start([(att_s, outs[4].at[image])])
        loads.wait(g_o[0])
        part_s[...] = dot(att_s[...], wo_s[...], NN).astype(BF)
        g_part = loads.start([(part_s, outs[5])])
        for group in (g_first, g_qkv, g_att, g_part):
            loads.wait(group)

    shapes = [(2, seq, width)] + [(2, seq, ext)] * 4
    return call(
        body,
        [tok] + list(prev or []) + qkv_arrays + out_arrays,
        [sds(s, BF) for s in shapes] + [sds((seq, width), BF)],
        [
            pltpu.VMEM(qkv_scratch, BF),
            pltpu.VMEM(out_scratch, BF),
            pltpu.VMEM((seq, width), BF),
            pltpu.VMEM((seq, width), BF),
            pltpu.VMEM((seq, ext), BF),
            pltpu.VMEM((seq, ext), BF),
            pltpu.VMEM((seq, ext), BF),
            pltpu.VMEM((seq, ext), BF),
            pltpu.VMEM((seq, width), BF),
        ],
        "attn_forward",
        2 * seq * width * ext * 4 + 16 * seq * seq * ext,
        aliases={1 + i: i for i in range(n_prev)},
        pinned=True,
        vmem_ins=(nv, bq),
    )


def mlp_up(image, tok, part, recv, keep, nv, bu, wup, step, prev):
    seq, width = tok.shape[1:]
    up_arrays, up_plan, up_scratch = wup
    hid = up_scratch[-1]
    n_prev = 0 if prev is None else len(prev)

    def body(small, ins, outs, scratch, loads):
        keep_ref, nv_ref, bu_ref = small
        tok_ref, part_ref, recv_ref = ins[:3]
        w_s, tok_s, part_s, recv_s, mid_s, sec_s, act_s, dact_s = scratch
        g_in = loads.start([(tok_ref.at[image], tok_s), (part_ref, part_s), (recv_ref, recv_s)])
        g_w = weight_loads(loads, up_plan, ins[3 + n_prev :], w_s)
        loads.wait(g_in)
        total = part_s[...].astype(F32) + recv_s[...].astype(F32) + nv_ref[4:5, :]
        middle = tok_s[...].astype(F32) + keep_ref[image] * total
        mid_s[...] = middle
        hat, _ = norm_parts(middle)
        sec_s[...] = (hat * nv_ref[1:2, :] + nv_ref[3:4, :]).astype(BF)
        g_mid = loads.start([(mid_s, outs[0].at[image]), (sec_s, outs[1].at[image])])
        second = sec_s[...]
        done = []
        for block in range(hid // step):
            if block < len(g_w):
                loads.wait(g_w[block])
            cols = slice(block * step, (block + 1) * step)
            pre = dot(second, w_s[:, cols], NN) + bu_ref[0:1, cols]
            gate = 0.5 * jnp.tanh(0.851 * pre) + 0.5
            act_s[:, cols] = (pre * gate).astype(BF)
            dact_s[:, cols] = (gate + 1.702 * pre * gate * (1.0 - gate)).astype(BF)
            done.append(
                loads.start(
                    [
                        (act_s.at[:, cols], outs[2].at[image, :, cols]),
                        (dact_s.at[:, cols], outs[3].at[image, :, cols]),
                    ]
                )
            )
        for group in [g_mid] + done:
            loads.wait(group)

    outs = [
        sds((2, seq, width), F32),
        sds((2, seq, width), BF),
        sds((2, seq, hid), BF),
        sds((2, seq, hid), BF),
    ]
    return call(
        body,
        [tok, part, recv] + list(prev or []) + up_arrays,
        outs,
        [
            pltpu.VMEM(up_scratch, BF),
            pltpu.VMEM((seq, width), BF),
            pltpu.VMEM((seq, width), BF),
            pltpu.VMEM((seq, width), BF),
            pltpu.VMEM((seq, width), F32),
            pltpu.VMEM((seq, width), BF),
            pltpu.VMEM((seq, hid), BF),
            pltpu.VMEM((seq, hid), BF),
        ],
        "mlp_up",
        2 * seq * width * hid,
        aliases={3 + i: i for i in range(n_prev)},
        pinned=True,
        smem=(keep,),
        vmem_ins=(nv, bu),
    )


def column_loads(src, dst, start):
    if len(src.shape) == 2:
        return [(src, dst)]
    n, _, width = src.shape
    return [
        (src.at[i], dst.at[:, (start + i) * width : (start + i + 1) * width]) for i in range(n)
    ]


def weight_grad(lefts, rights, tasks, out_shapes, name, lo, hi, prev=None, fill=False):
    rows = lefts[0].shape[0]
    arrays = list(lefts) + list(rights)
    joined = all(len(a.shape) == 3 for a in rights)
    if joined:
        total = sum(a.shape[0] for a in rights) // 3
        wide = [a.shape[-1] for a in lefts] + [3 * total * rights[0].shape[-1]]
    else:
        wide = [a.shape[-1] for a in arrays]
    n_left, n_in = len(lefts), len(arrays)
    prev = list(prev or [])
    last = {}
    for n, task in enumerate(tasks):
        for store in task[4]:
            last[store[0]] = n

    def body(small, ins, outs, scratch, loads):
        in_s, out_s = scratch[: len(wide)], scratch[len(wide) :]
        order = []
        for l_index, _, r_index, _, _ in tasks:
            for i in (l_index, n_left + r_index):
                if i not in order:
                    order.append(i)
        groups = {}
        for i in order:
            pairs = [(ins[i], in_s[i])]
            if joined and i == n_left:
                pairs, start = [], 0
                for j, stack in enumerate(rights):
                    count = stack.shape[0] // 3
                    for kind in range(3):
                        part = ins[n_left + j].at[kind * count : (kind + 1) * count]
                        pairs += column_loads(part, in_s[i], kind * total + start)
                    start += count
            groups[i] = loads.start(pairs)
        for ref in out_s if fill else ():
            ref[...] = jnp.zeros_like(ref)
        ready, done = set(), []
        for n, (l_index, l_cols, r_index, r_cols, stores) in enumerate(tasks):
            for i in (l_index, n_left + r_index):
                if i not in ready:
                    loads.wait(groups[i])
                    ready.add(i)
            left, right = in_s[l_index][:, l_cols], in_s[n_left + r_index][:, r_cols]
            value = dot(left, right, TN).astype(BF)
            for which, spot, r_sl, c_sl in stores:
                out_s[which][spot] = value[r_sl, c_sl]
            for which in sorted(w for w in last if last[w] == n):
                done.append(loads.start([(out_s[which], outs[which].at[:, lo:hi])]))
        for group in done:
            loads.wait(group)

    flops = sum(
        2 * rows * (t[1].stop - t[1].start) * (t[3].stop - t[3].start) for t in tasks
    )
    return call(
        body,
        arrays + prev,
        [sds(s, BF) for s in out_shapes],
        [pltpu.VMEM((rows, w), BF) for w in wide]
        + [pltpu.VMEM((s[0], hi - lo, s[2]), BF) for s in out_shapes],
        name,
        flops,
        aliases={n_in + i: i for i in range(len(prev))},
    )


def mlp_back(grad, act, dact, wdown, wup, step):
    rows, width = grad.shape
    seq = rows // 2
    hid = dact.shape[1]
    down_arrays, down_plan, down_scratch = wdown
    up_arrays, up_plan, up_scratch = wup
    n_down = len(down_arrays)

    def body(small, ins, outs, scratch, loads):
        wd_s, wu_s, g_s, a_s, d_s, low_s, sum_s, two_s, mlp_s = scratch
        g_g = loads.start([(ins[0], g_s)])
        g_wd = weight_loads(loads, down_plan, ins[3 : 3 + n_down], wd_s)
        g_d = []
        for block in range(hid // step):
            cols = slice(block * step, (block + 1) * step)
            g_d.append(loads.start([(ins[2].at[:, cols], d_s.at[:, cols])]))
        g_wu = weight_loads(loads, up_plan, ins[3 + n_down :], wu_s)
        g_a = loads.start([(ins[1], a_s)])
        loads.wait(g_g)
        left = g_s[...]
        done = []
        for block in range(hid // step):
            if block < len(g_wd):
                loads.wait(g_wd[block])
            loads.wait(g_d[block])
            cols = slice(block * step, (block + 1) * step)
            pre = dot(left, wd_s[cols, :], NT) * d_s[:, cols].astype(F32)
            low_s[:, cols] = pre.astype(BF)
            sum_s[0:1, cols] = jnp.sum(pre, axis=0, keepdims=True)
            done.append(loads.start([(low_s.at[:, cols], outs[0].at[:, cols])]))
        done.append(loads.start([(sum_s, outs[1])]))
        for group in g_wu:
            loads.wait(group)
        two = dot(low_s[...], wu_s[...], NT)
        for a in range(2):
            two_s[a] = two[a * seq : (a + 1) * seq].astype(BF)
            done.append(loads.start([(two_s.at[a], outs[2].at[a])]))
        loads.wait(g_a)
        mlp_s[...] = dot(a_s[...], wd_s[...], NN).astype(BF)
        done.append(loads.start([(mlp_s, outs[3])]))
        for group in done:
            loads.wait(group)

    return call(
        body,
        [grad, act, dact] + down_arrays + up_arrays,
        [sds((rows, hid), BF), sds((1, hid), F32)]
        + [sds((2, seq, width), BF), sds((rows, width), BF)],
        [
            pltpu.VMEM(down_scratch, BF),
            pltpu.VMEM(up_scratch, BF),
            pltpu.VMEM((rows, width), BF),
            pltpu.VMEM((rows, hid), BF),
            pltpu.VMEM((rows, hid), BF),
            pltpu.VMEM((rows, hid), BF),
            pltpu.VMEM((1, hid), F32),
            pltpu.VMEM((2, seq, width), BF),
            pltpu.VMEM((rows, width), BF),
        ],
        "mlp_back",
        6 * rows * width * hid,
        sems=64,
    )


def input_grad(stacks, starts, weight, width):
    arrays, plan, shape = weight
    n, ext = shape[0], shape[-1]
    rows = stacks[0].shape[1]
    seq, m = rows // 2, len(stacks)

    def body(small, ins, outs, scratch, loads):
        w_s, out_s = scratch[0], scratch[1]
        l_s = scratch[2:]
        g_w = weight_loads(loads, plan[:1], ins[m:], w_s)
        g_l = []
        for i in range(n):
            pairs = []
            for j in range(m):
                count = stacks[j].shape[0] // n
                pairs += column_loads(ins[j].at[i * count : (i + 1) * count], l_s[i], starts[j])
            g_l.append(loads.start(pairs))
        g_w += weight_loads(loads, plan[1:], ins[m:], w_s)
        total = None
        for i in range(n):
            loads.wait(g_l[i])
            if i < len(g_w):
                loads.wait(g_w[i])
            piece = dot(l_s[i][...], w_s[i].reshape(width, ext), NT)
            total = piece if total is None else total + piece
        done = []
        for a in range(2):
            out_s[a] = total[a * seq : (a + 1) * seq].astype(BF)
            done.append(loads.start([(out_s.at[a], outs[0].at[a])]))
        for group in done:
            loads.wait(group)

    return call(
        body,
        list(stacks) + arrays,
        [sds((2, seq, width), BF)],
        [pltpu.VMEM(shape, BF), pltpu.VMEM((2, seq, width), BF)] + [pltpu.VMEM((rows, ext), BF)] * n,
        "grad_one",
        2 * rows * width * ext * n,
    )[0]


def middle_back(ids, middle, part, recv, cot, keep, nv, wout):
    _, seq, width = middle.shape
    out_arrays, out_plan, out_scratch = wout
    ext = out_scratch[0]

    def body(small, ins, outs, scratch, loads):
        ids_ref, keep_ref, nv_ref = small
        mine = ids_ref[0]
        wo_s, mid_s, part_s, recv_s, cot_s, gmid_s, gat_s, do_s = scratch[:8]
        cs_s = scratch[8]
        g_in = [
            loads.start(
                [
                    (ins[0].at[a], mid_s.at[a]),
                    (ins[1].at[a], cot_s.at[a]),
                    (ins[2].at[a], part_s.at[a]),
                    (ins[3].at[a], recv_s.at[a]),
                ]
            )
            for a in range(2)
        ]
        g_o = weight_loads(loads, out_plan, ins[4:], wo_s)
        done = []
        for a in range(2):
            loads.wait(g_in[a])
            keep_here = keep_ref[a]
            hat, inverse = norm_parts(mid_s[a])
            grad_two = part_s[a].astype(F32) + recv_s[a].astype(F32)
            top = cot_s[a].astype(F32)
            grad_mid = top + norm_back(grad_two, hat, inverse, nv_ref[1:2, :])
            grad_attn = grad_mid * keep_here
            sums = [
                jnp.sum(grad_two * hat, axis=0, keepdims=True),
                jnp.sum(grad_two, axis=0, keepdims=True),
                jnp.sum(grad_attn, axis=0, keepdims=True),
                jnp.sum(top, axis=0, keepdims=True) * keep_here,
            ]
            for i, value in enumerate(sums):
                cs_s[i : i + 1, :] = value if a == 0 else cs_s[i : i + 1, :] + value
            gmid_s[a] = grad_mid
            gat_s[a] = grad_attn.astype(BF)
            done.append(loads.start([(gat_s.at[a], outs[1].at[a])]))
            if a == 0:
                loads.wait(g_o[0])
            do_s[a] = dot(gat_s[a], wo_s[...], NT).astype(BF)
            done.append(loads.start([(do_s.at[a], outs[2].at[a])]))
        done.append(loads.start([(gmid_s.at[mine], outs[0]), (cs_s, outs[3])]))
        for group in done:
            loads.wait(group)

    return call(
        body,
        [middle, cot, part, recv] + out_arrays,
        [
            sds((seq, width), F32),
            sds((2, seq, width), BF),
            sds((2, seq, ext), BF),
            sds((4, width), F32),
        ],
        [
            pltpu.VMEM(out_scratch, BF),
            pltpu.VMEM((2, seq, width), F32),
            pltpu.VMEM((2, seq, width), BF),
            pltpu.VMEM((2, seq, width), BF),
            pltpu.VMEM((2, seq, width), BF),
            pltpu.VMEM((2, seq, width), F32),
            pltpu.VMEM((2, seq, width), BF),
            pltpu.VMEM((2, seq, ext), BF),
            pltpu.VMEM((4, width), F32),
        ],
        "middle_back",
        4 * seq * width * ext,
        smem=(ids, keep),
        vmem_ins=(nv,),
    )


def attn_backward(pairs, grad, q, k, v, name="attn_backward"):
    _, seq, _ = q.shape
    n = len(pairs)

    def body(small, ins, outs, scratch, loads):
        q_s, k_s, v_s, do_s, dq_s, dk_s, dv_s, bs_s = scratch
        groups = []
        for u in range(2 * n):
            cols = slice(pairs[u // 2] * 128, (pairs[u // 2] + 1) * 128)
            groups.append(
                loads.start([(ins[j].at[u % 2, :, cols], scratch[j].at[u]) for j in range(4)])
            )
        half = lax.broadcasted_iota(jnp.int32, (1, 128), 1) // HEAD_DIM
        for group in groups:
            loads.wait(group)

        def unit(u, carry):
            q2, k2, v2, do2 = q_s[u], k_s[u], v_s[u], do_s[u]
            dq = dk = dv = None
            for h in range(2):
                mask = (half == h).astype(BF)
                km, qm, dom = k2 * mask, q2 * mask, do2 * mask
                scores = dot(km, q2, NT)
                row = lax.broadcasted_iota(jnp.int32, scores.shape, 0)
                scores = jnp.where(row < VALID, scores, -1e30)
                e = jnp.exp(scores - jnp.max(scores, axis=0, keepdims=True))
                probs = e * (1.0 / jnp.sum(e, axis=0, keepdims=True))
                grad_probs = dot(v2, dom, NT)
                row_dot = jnp.sum(probs * grad_probs, axis=0, keepdims=True)
                grad_scores = (probs * (grad_probs - row_dot)).astype(BF)
                v_piece = dot(probs.astype(BF), dom, NN)
                k_piece = dot(grad_scores, qm, NN)
                q_piece = dot(grad_scores, km, TN)
                dq = q_piece if dq is None else dq + q_piece
                dk = k_piece if dk is None else dk + k_piece
                dv = v_piece if dv is None else dv + v_piece
            dq = dq * HEAD_DIM**-0.5
            bs_s[u, 0:1, :] = jnp.sum(dq, axis=0, keepdims=True)
            bs_s[u, 1:2, :] = jnp.sum(dv, axis=0, keepdims=True)
            dq_s[u] = dq.astype(BF)
            dk_s[u] = dk.astype(BF)
            dv_s[u] = dv.astype(BF)
            return carry

        lax.fori_loop(0, 2 * n, unit, 0)
        done = [loads.start([(scratch[4 + j], outs[0].at[j])]) for j in range(3)]
        done.append(loads.start([(bs_s, outs[1])]))
        for group in done:
            loads.wait(group)

    grads, sums = call(
        body,
        [q, k, v, grad],
        [sds((3, 2 * n, seq, 128), BF), sds((2 * n, 2, 128), F32)],
        [pltpu.VMEM((2 * n, seq, 128), BF)] * 7 + [pltpu.VMEM((2 * n, 2, 128), F32)],
        name,
        0,
    )
    return grads.reshape(3 * n, 2 * seq, 128), sums


def finish_layer(ids, keep, nv, middle, part, recv, nd, aligned):
    _, seq, width = middle.shape

    def body(small, ins, outs, scratch, loads):
        ids_ref, keep_ref, nv_ref = small
        mine = ids_ref[0]
        mid_s, part_s, recv_s, out_s = scratch
        groups = [loads.start([(ins[i].at[mine], scratch[i])]) for i in range(3)]
        for group in groups:
            loads.wait(group)
        total = part_s[...].astype(F32) + recv_s[...].astype(F32) + nv_ref[5:6, :]
        out_s[...] = (mid_s[...] + keep_ref[mine] * total).astype(BF)
        loads.wait(loads.start(block_stores(ids_ref, out_s, outs[0], nd, aligned)))

    return call(
        body,
        [middle, part, recv],
        [sds((seq, width), BF)],
        [pltpu.VMEM((seq, width), F32)] + [pltpu.VMEM((seq, width), BF)] * 3,
        "finish_layer",
        100 * seq * width,
        smem=(ids, keep),
        vmem_ins=(nv,),
    )[0]


def finish_tokens(ids, nv, tok, part, recv, gmid, rest, sums, nd, aligned):
    _, seq, width = tok.shape
    n_dest, z_n, n_rows, lanes = rest.shape
    bd, y_n = width // nd, nd // rest.shape[1]
    tx = n_dest // y_n

    def body(small, ins, outs, scratch, loads):
        ids_ref, nv_ref = small[:2]
        mine = ids_ref[0]
        tok_s, part_s, recv_s, gm_s, out_s, cs_s, rest_s = scratch
        g_rest = loads.start([(ins[4], rest_s)] if sums is None else [])
        groups = [
            loads.start(
                [
                    (ins[0].at[a], tok_s.at[a]),
                    (ins[2].at[a], part_s.at[a]),
                    (ins[3].at[a], recv_s.at[a]),
                ]
            )
            for a in range(2)
        ]
        g_mid = loads.start([(ins[1], gm_s)])
        for group in groups:
            loads.wait(group)
        done = []
        for i in range(2):
            a = mine if i == 0 else 1 - mine
            hat, inverse = norm_parts(tok_s[a].astype(F32))
            grad_one = part_s[a].astype(F32) + recv_s[a].astype(F32)
            gain_sum = jnp.sum(grad_one * hat, axis=0, keepdims=True)
            shift_sum = jnp.sum(grad_one, axis=0, keepdims=True)
            if i == 0:
                cs_s[0:1, :] = gain_sum
                cs_s[1:2, :] = shift_sum
                loads.wait(g_mid)
                value = gm_s[...] + norm_back(grad_one, hat, inverse, nv_ref[0:1, :])
                out_s[...] = value.astype(BF)
                done.append(loads.start(block_stores(ids_ref, out_s, outs[0], nd, aligned)))
            else:
                cs_s[0:1, :] = cs_s[0:1, :] + gain_sum
                cs_s[1:2, :] = cs_s[1:2, :] + shift_sum
        loads.wait(g_rest)
        if sums is not None:
            col_ref, bup_ref, pairs = small[2], small[3], small[4:]
            up = bup_ref.shape[1] // tx // nd
            n_pairs = sum(ref.shape[0] // 2 for ref in pairs)
            qv = n_pairs * 128 // tx // nd
            per = 128 // qv
            lane = lax.broadcasted_iota(jnp.int32, (2, 128), 1)
            whole = [ref[2 * i] + ref[2 * i + 1] for ref in pairs for i in range(ref.shape[0] // 2)]
            whole = jnp.stack(whole)
            rest_s[...] = jnp.zeros_like(rest_s)
            for n in range(n_dest):
                kx, ky = n // y_n, n % y_n
                for kz in range(z_n):
                    p = ky * z_n + kz
                    d = ids_ref[2 + p]
                    rest_s[n, kz, 2:6, :] = col_ref[:, p * bd : (p + 1) * bd]
                    row = jnp.zeros((2, 128), F32)
                    for i in range(nd // per):
                        row = jnp.where(d // per == i, whole[kx * (nd // per) + i], row)
                    row = pltpu.roll(row, (per - d % per) * qv % 128, 1)
                    rest_s[n, kz, 6:8, :] = jnp.where(lane < qv, row, 0.0)
                    cols = pl.ds(pl.multiple_of((kx * nd + d) * up, 128), up)
                    rest_s[n, kz, 8:9, 0:up] = bup_ref[:, cols]
        for n in range(n_dest if aligned else 0):
            for kz in range(z_n):
                p = n % (nd // z_n) * z_n + kz
                rest_s[n, kz, 0:2, :] = cs_s[:, p * bd : (p + 1) * bd]
        done.append(loads.start([(cs_s, outs[1])]))
        done += [loads.start([(rest_s.at[n], outs[2 + n])]) for n in range(n_dest)]
        for group in done:
            loads.wait(group)

    return call(
        body,
        [tok, gmid, part, recv] + ([rest] if sums is None else []),
        [sds((seq, width), BF), sds((2, width), F32)] + [sds(rest.shape[1:], F32)] * n_dest,
        [pltpu.VMEM((2, seq, width), BF)] * 3
        + [pltpu.VMEM((seq, width), F32), pltpu.VMEM((seq, width), BF), pltpu.VMEM((2, width), F32)]
        + [pltpu.VMEM(rest.shape, F32)],
        "finish_tokens",
        200 * seq * width,
        smem=(ids,),
        vmem_ins=(nv,) + tuple(sums or ()),
    )


class Grid3:
    def __init__(self, dp, tx):
        self.dp, self.tx = dp, tx
        self.y = 2 if dp % 2 == 0 else 1
        self.z = dp // self.y

    def send_z(self, value, k):
        return lax.ppermute(value, "dp", [(i, i ^ (k * self.y)) for i in range(self.dp)])

    def send_y(self, value, k):
        return lax.ppermute(value, "dp", [(i, i ^ k) for i in range(self.dp)])

    def send_xy(self, value, kx, ky):
        count = self.dp * self.tx
        pairs = [(i, ((i // self.tx) ^ ky) * self.tx + ((i % self.tx) ^ kx)) for i in range(count)]
        return lax.ppermute(value, ("dp", "tx"), pairs)

    def send_x(self, value, k):
        return lax.ppermute(value, "tx", [(i, i ^ k) for i in range(self.tx)])


def swap_core(value):
    return lax.ppermute(value, "core", [(0, 1), (1, 0)])


def after(values, gate):
    return lax.optimization_barrier((values, gate))[0]


def gather_z(grid, part_a, part_b, gate=None):
    rows = part_a.shape[0]
    both = jnp.concatenate([part_a, part_b], axis=0)
    all_z = [both] + [grid.send_z(both, k) for k in range(1, grid.z)]
    if gate is not None:
        all_z = after(all_z, gate)
    return jnp.stack([v[:rows] for v in all_z]), jnp.stack([v[rows:] for v in all_z])


def gather_first(grid, a_z, b_z):
    a_y = [a_z] + [grid.send_y(a_z, k) for k in range(1, grid.y)]
    b_x = [b_z] + [grid.send_x(b_z, k) for k in range(1, grid.tx)]
    return a_y, b_x


def join(pieces):
    return [jnp.concatenate(part) for part in pieces]


def gather_last(grid, a_y, b_x):
    a_all = [a_y] + [grid.send_x(a_y, k) for k in range(1, grid.tx)]
    b_all = [b_x] + [grid.send_y(b_x, k) for k in range(1, grid.y)]
    return a_all, b_all


def add_pieces(groups, cuts, outs, name):
    arrays = [a for group in groups for a in group]
    starts = [sum(len(g) for g in groups[:i]) for i in range(len(groups))]
    last = {}
    for n, cut in enumerate(cuts):
        last[cut[2]] = n

    def body(small, ins, outs_ref, scratch, loads):
        in_s, out_s = scratch[: len(arrays)], scratch[len(arrays) :]
        loaded = [loads.start([(ins[i], in_s[i]) for i in range(starts[g], starts[g] + len(groups[g]))]) for g in range(len(groups))]
        ready, done = set(), []
        for n, (g, spot, which, place) in enumerate(cuts):
            if g not in ready:
                loads.wait(loaded[g])
                ready.add(g)
            total = None
            for i in range(starts[g], starts[g] + len(groups[g])):
                value = in_s[i][spot].astype(F32)
                total = value if total is None else total + value
            out_s[which][place] = total.astype(out_s[which].dtype)
            for w in sorted(w for w in last if last[w] == n):
                done.append(loads.start([(out_s[w], outs_ref[w])]))
        for group in done:
            loads.wait(group)

    return call(
        body,
        arrays,
        outs,
        [pltpu.VMEM(a.shape, a.dtype) for a in arrays] + [pltpu.VMEM(o.shape, o.dtype) for o in outs],
        name,
        0,
        spare=8,
    )


class Scatter:
    def __init__(self, grid, a_all, b_all, name):
        self.grid, self.name, self.bit = grid, name, 0
        self.rows = (a_all[0].shape[1], b_all[0].shape[1])
        a_got = [grid.send_x(a_all[k], k) for k in range(1, grid.tx)]
        b_got = [grid.send_y(b_all[k], k) for k in range(1, grid.y)]
        self.state = ([a_all[0]] + a_got, [b_all[0]] + b_got)

    def second(self, gate):
        grid, z = self.grid, self.grid.z
        a_in, b_in = after(self.state, gate)
        outs = [sds((z,) + a_in[0].shape[1:], BF)] * grid.y + [sds((z,) + b_in[0].shape[1:], BF)] * grid.tx
        full = slice(None)
        cuts = [(0, slice(k * z, (k + 1) * z), k, full) for k in list(range(1, grid.y)) + [0]]
        cuts += [(1, slice(k * z, (k + 1) * z), grid.y + k, full) for k in list(range(1, grid.tx)) + [0]]
        res = add_pieces([a_in, b_in], cuts, outs, self.name + "_add")
        a_y, b_x = res[: grid.y], res[grid.y :]
        a_got = [grid.send_y(a_y[k], k) for k in range(1, grid.y)]
        b_got = [grid.send_x(b_x[k], k) for k in range(1, grid.tx)]
        self.state = ([a_y[0]] + a_got, [b_x[0]] + b_got)
        return a_y, b_x

    def along_z(self, gate, extra=None):
        grid = self.grid
        a_in, b_in = after(self.state, gate)
        ra, rb = self.rows
        groups = [a_in, b_in] + ([extra] if extra else [])
        more = extra[0].shape[1] if extra else 0
        order = list(range(1, grid.z)) + [0]
        cuts = []
        for k in order:
            cuts.append((0, k, k, slice(0, ra)))
            cuts.append((1, k, k, slice(ra, ra + rb)))
            if extra:
                cuts.append((2, k, k, slice(ra + rb, ra + rb + more)))
        outs = [sds((ra + rb + more,) + a_in[0].shape[2:], BF)] * grid.z
        both = add_pieces(groups, cuts, outs, self.name + "_addz")
        self.state = [both[0]] + [grid.send_z(both[k], k) for k in range(1, grid.z)]
        return both

    def halve(self, gate):
        grid, (ra, rb) = self.grid, self.rows
        groups = after(self.state, gate)
        if self.bit == 0:
            self.bit, self.left = 1, list(range(grid.z))
        else:
            self.bit, groups = 2 * self.bit, [groups]
        sent = [k for k in self.left if k & self.bit]
        kept = [k for k in self.left if not k & self.bit]
        cuts = []
        for which, ids in ((0, sent), (1, kept)):
            for n, k in enumerate(ids):
                spot = self.left.index(k)
                if len(groups) == 2:
                    cuts.append((0, spot, which, (n, slice(0, ra))))
                    cuts.append((1, spot, which, (n, slice(ra, ra + rb))))
                else:
                    cuts.append((0, spot, which, n))
        outs = [sds((len(kept), ra + rb) + groups[0][0].shape[2:], BF)] * 2
        send, keep = add_pieces(groups, cuts, outs, self.name + "_half")
        self.left = kept
        self.state = [keep, grid.send_z(send, self.bit)]
        return keep

    def finish(self, gate, cuts, outs):
        if self.bit:
            cuts = [((0, rows), which, place) for rows, which, place in cuts]
        cuts = [(0, rows, which, place) for rows, which, place in cuts]
        return add_pieces([after(self.state, gate)], cuts, outs, self.name + "_sum")


def join_kernel(pieces):
    groups, cuts, outs = [], [], []
    for which, part in enumerate(pieces):
        lead = part[0].shape[0]
        for k, value in enumerate(part):
            cuts.append((len(groups), slice(None), which, slice(k * lead, (k + 1) * lead)))
            groups.append([value])
        outs.append(sds((lead * len(part),) + part[0].shape[1:], BF))
    return add_pieces(groups, cuts, outs, "join")


def xor_blocks(value, mask, axis):
    count = value.shape[axis]
    bit = 1
    while bit < count:
        shape = value.shape
        split = value.reshape(shape[:axis] + (count // (2 * bit), 2, bit) + shape[axis + 1 :])
        turned = jnp.flip(split, axis=axis + 1).reshape(shape)
        value = jnp.where(jnp.bitwise_and(mask, bit) != 0, turned, value)
        bit *= 2
    return value


def pad_cols(value, width):
    return jnp.pad(value, ((0, 0), (0, width - value.shape[1])))


def per_device(
    tokens,
    cotangent,
    image_mask,
    norm_gains,
    norm_shifts,
    w_qkv,
    b_qv,
    w_out,
    w_up,
    up_bias,
    w_down,
    *,
    dp,
    tx,
):
    grid = Grid3(dp, tx)
    y_n, z_n = grid.y, grid.z
    core = lax.axis_index("core").astype(jnp.int32)
    me_d = lax.axis_index("dp").astype(jnp.int32)
    me_x = lax.axis_index("tx").astype(jnp.int32)
    seq, width = tokens.shape
    _, bd, hw = w_qkv.shape
    fw = w_up.shape[1]
    ext, hid = tx * hw, tx * fw
    hh, fh = hw // 2, fw // 2
    aligned = bd % 128 == 0 and hh % 128 == 0 and fh % 128 == 0
    rel = [kz * y_n + ky for ky in range(y_n) for kz in range(z_n)]

    def from_abs(value, axis):
        shape = value.shape
        value = value.reshape(shape[:axis] + (z_n, y_n) + shape[axis + 1 :])
        return jnp.swapaxes(value, axis, axis + 1).reshape(shape)

    def to_rel(value, axis):
        shape = value.shape
        value = value.reshape(shape[:axis] + (y_n, z_n) + shape[axis + 1 :])
        return jnp.swapaxes(value, axis, axis + 1).reshape(shape)

    ids = jnp.stack([core, me_d] + [jnp.bitwise_xor(me_d, k) for k in rel])
    keep = lax.dynamic_slice(image_mask, (2 * me_x,), (2,)).astype(F32)

    lane = max(bd, hh)
    small = jnp.concatenate(
        [
            pad_cols(norm_gains, lane),
            pad_cols(norm_shifts, lane),
            pad_cols(b_qv, lane),
            pad_cols(up_bias[None], lane),
            jnp.zeros((7, lane), BF),
        ]
    )
    qkv_a = pad_cols(w_qkv[:, :, :hh].reshape(3 * bd, hh), lane)
    qkv_b = pad_cols(w_qkv[:, :, hh:].reshape(3 * bd, hh), lane)
    first_a = jnp.concatenate([qkv_a, pad_cols(w_out[:hh], lane), small])
    first_b = jnp.concatenate([qkv_b, pad_cols(w_out[hh:], lane)])
    own = [tokens, cotangent]
    other = [swap_core(value) for value in own]
    if aligned:
        tok, cot = arrange_pair(ids, own, other, dp)
    else:

        def arrange(own, other):
            pair = jnp.where(core == 0, jnp.stack([own, other]), jnp.stack([other, own]))
            pair = xor_blocks(pair.reshape(2, seq, dp, bd), me_d, 2)
            return from_abs(pair, 2).reshape(2, seq, width)

        tok, cot = [arrange(own[i], other[i]) for i in range(2)]
    c1_z = gather_z(grid, first_a, first_b, gate=tok)
    c1_h = gather_first(grid, *c1_z)
    c1_h = join(c1_h)
    c1a, c1b = gather_last(grid, *c1_h)
    up_halves = after((w_up[:, :fh], w_up[:, fh:]), c1_h)
    row0 = 3 * bd + hh
    if aligned and 128 % (hw // dp) == 0 and (fw // dp) % 128 == 0:
        c1a, c1b = after((c1a, c1b), (c1a, c1b))
        nv, bq, bu = vectors(ids, c1a, row0, dp, y_n, bd, hw // dp, fw // dp)
    else:
        nv = c1a[0][:, row0 : row0 + 6, :bd].transpose(1, 0, 2).reshape(6, width).astype(F32)
        tail = jnp.stack([v[:, row0 + 6 : row0 + 9] for v in c1a])
        tail = xor_blocks(to_rel(tail, 1), me_d, 1)
        bq = tail[:, :, :2, : hw // dp].transpose(2, 0, 1, 3).reshape(2, ext).astype(F32)
        bu = tail[:, :, 2, : fw // dp].reshape(1, hid).astype(F32)
    grad_top = cot * keep.astype(BF)[:, None, None]

    up_z = gather_z(grid, *up_halves, gate=nv)
    up_h = gather_first(grid, *up_z)
    dn_halves = after((w_down[:fh], w_down[fh:]), up_z)

    if aligned:
        every, wq_plan, wo_plan, up_plan, dn_plan = slice(None), [[], [], []], [], [], []
        for kx in range(tx):
            halves = [slice(kx * hw, kx * hw + hh), slice(kx * hw + hh, (kx + 1) * hw)]
            f_halves = [slice(kx * fw, kx * fw + fh), slice(kx * fw + fh, (kx + 1) * fw)]
            own = slice(kx * z_n, (kx + 1) * z_n)
            for i in range(3):
                src = slice(i * bd, (i + 1) * bd)
                wq_plan[i].append((kx, (every, src), (i, every, every, halves[0])))
                for ky in range(y_n):
                    dst = (i, slice(ky * z_n, (ky + 1) * z_n), every, halves[1])
                    wq_plan[i].append((tx + ky, (own, src), dst))
            src = slice(3 * bd, 3 * bd + hh)
            dn_plan += [[], []]
            for ky in range(y_n):
                for kz in range(z_n):
                    p, r = ky * z_n + kz, kx * z_n + kz
                    cols = slice(p * bd, (p + 1) * bd)
                    wo_plan.append((kx, (p, src), (halves[0], cols)))
                    wo_plan.append((tx + ky, (r, src), (halves[1], cols)))
                    dn_plan[-2].append((kx, (p,), (f_halves[0], cols)))
                    dn_plan[-1].append((tx + ky, (r,), (f_halves[1], cols)))
            up_plan += [[(kx, (every,), (every, f_halves[0]))], []]
            for ky in range(y_n):
                rows = slice(kx * z_n * bd, (kx + 1) * z_n * bd)
                dst = (slice(ky * z_n * bd, (ky + 1) * z_n * bd), f_halves[1])
                up_plan[-1].append((tx + ky, (rows,), dst))
        c1 = c1a + c1b
        wqkv = (c1, wq_plan, (3, dp, bd, ext))
        wout = (c1, [wo_plan], (ext, width))
    else:

        def whole(a_all, b_all):
            a = jnp.stack(a_all)
            b = jnp.stack(b_all).reshape((y_n, tx, z_n) + b_all[0].shape[1:])
            b = b.transpose(1, 0, 2, 3, 4).reshape(a.shape[:2] + b.shape[3:])
            return jnp.stack([a, b], axis=1)

        c1 = whole([v[:, :row0] for v in c1a], c1b)
        qkv = c1[:, :, :, : 3 * bd, :hh].reshape(tx, 2, dp, 3, bd, hh)
        qkv = qkv.transpose(3, 2, 4, 0, 1, 5).reshape(3, dp, bd, ext)
        out = c1[:, :, :, 3 * bd :, :bd].transpose(0, 1, 3, 2, 4).reshape(ext, width)
        all_of = [[(0, (slice(None),), (slice(None),))]]
        wqkv = ([qkv], all_of, qkv.shape)
        wout = ([out], all_of, out.shape)

    rows2 = 2 * seq

    res = attn_forward(0, after(tok, up_z), nv, bq, wqkv, wout, None)
    part0 = res[5]
    up_h = join(after(up_h, part0))
    upa, upb = gather_last(grid, *up_h)
    dn_halves = after(dn_halves, up_h)
    res = attn_forward(1, after(tok, up_h), nv, bq, wqkv, wout, res[:5])
    recv0 = swap_core(after(part0, res[5]))
    parts = [(part0, recv0), (res[5], swap_core(res[5]))]
    first, q, k, v, att = res[:5]
    upa, upb = after((upa, upb), res[5])
    dn_z = gather_z(grid, *dn_halves, gate=(upa, upb))
    dn_h = gather_first(grid, *dn_z)
    if aligned:
        wup = ([v.reshape(-1, fh) for v in upa + upb], up_plan, (width, hid))
    else:
        up_w = whole(upa, upb).transpose(2, 3, 0, 1, 4).reshape(width, hid)
        wup = ([up_w], all_of, up_w.shape)
    part, recv = parts[0]
    state = mlp_up(0, tok, part, recv, keep, nv, bu, wup, fh, None)
    dna, dnb = gather_last(grid, *join_kernel(after(dn_h, state[1])))
    part, recv = parts[1]
    state = mlp_up(1, tok, part, recv, keep, nv, bu, wup, fh, state)
    if aligned:
        wdown = (dna + dnb, dn_plan, (hid, width))
    else:
        down_w = whole(dna, dnb).transpose(0, 1, 3, 2, 4).reshape(hid, width)
        wdown = ([down_w], all_of, down_w.shape)
    middle, second, act, dact = state
    flat = lambda value: value.reshape(rows2, value.shape[2])
    act2, sec2, grad2 = flat(act), flat(second), flat(grad_top)

    full = slice(None)
    a_spots = [(p, slice(p * bd, (p + 1) * bd)) for p in range(dp)]

    def by_left(l_index, r_index, size, row0):
        tasks, rows = [], slice(row0, row0 + size // 2)
        halves = slice(0, size // 2), slice(size // 2, size)
        for kx in range(tx):
            stores = [(kx, (p, rows), halves[0], cols) for p, cols in a_spots]
            for p, cols in a_spots:
                ky, kz = p // z_n, p % z_n
                stores.append((tx + ky, (kx * z_n + kz, rows), halves[1], cols))
            tasks.append((l_index, slice(kx * size, (kx + 1) * size), r_index, slice(0, width), stores))
        return tasks

    def by_right(l_index, r_index, size, row0, lanes, spare=False, first=0):
        tasks, each = [], size // 2 // lanes
        for kx in range(tx):
            stores = []
            for j in range(each):
                rows = slice(row0 + j * bd, row0 + (j + 1) * bd)
                cols = [slice((h * each + j) * lanes, (h * each + j + 1) * lanes) for h in range(2)]
                rows = (rows, slice(0, lanes)) if spare else (rows,)
                for p, r_sl in a_spots:
                    ky, kz = p // z_n, p % z_n
                    stores.append((kx, (p,) + rows, r_sl, cols[0]))
                    stores.append((tx + ky, (kx * z_n + kz,) + rows, r_sl, cols[1]))
            cols = slice(first + kx * size, first + (kx + 1) * size)
            tasks.append((l_index, slice(0, width), r_index, cols, stores))
        return tasks

    def pieces(rows, lanes):
        return [(dp, rows, lanes)] * tx + [(tx * z_n, rows, lanes)] * y_n

    def send_grad(parts, name):
        return Scatter(grid, list(parts[:tx]), list(parts[tx:]), name)

    grads = weight_grad([act2], [grad2], by_left(0, 0, fw, 0), pieces(fh, bd), "down_grad", 0, fh)
    down_rs = send_grad(grads, "down")
    grad_in = after(grad2, grads[-1])
    low_pre, bias_up, two_part, mlp_part = mlp_back(grad_in, act2, flat(dact), wdown, wup, fh)
    mlp_part = mlp_part.reshape(2, seq, width)
    two_recv = swap_core(two_part)
    down_half = down_rs.second(bias_up)
    up_rows = fh // bd * bd
    sec_in = after(sec2, down_half)
    tasks = by_right(0, 0, fw, 0, bd)
    grads = weight_grad([sec_in], [low_pre], tasks, pieces(up_rows, bd), "up_grad", 0, up_rows)
    up_rs = send_grad(grads, "up")
    gmid, gattn, grad_att, col = middle_back(
        ids, middle, two_part, after(two_recv, grads[-1]), cot, keep, nv, wout
    )
    down_zs = down_rs.along_z(col)
    row0 = 3 * bd
    last_shapes = pieces(row0 + hh, bd)
    att_in = after(flat(att), down_zs)
    tasks = by_left(0, 0, hw, 0)
    out_grads = weight_grad(
        [att_in], [flat(gattn)], tasks, last_shapes, "out_grad", row0, row0 + hh
    )

    n_pairs = ext // 128
    split = hh == 128 and bd == 128 and n_pairs >= 4
    if split:
        heads = [[1], list(range(2, n_pairs))]
        first_in = after(grad_att, out_grads[-1])
        left_0, bias_0 = attn_backward(heads[0], first_in, q, k, v, "attn_first")
        up_half = up_rs.second(bias_0)
    else:
        heads = [list(range(n_pairs))]
        up_half = up_rs.second(out_grads[-1])
    left_a, bias_a = attn_backward(heads[-1], after(grad_att, up_half), q, k, v)
    first_in = flat(first)
    gate = bias_a
    if not split:
        grad_down = down_rs.finish(bias_a, [(full, 0, full)], [sds((fw, bd), F32)])[0]
        mlp_recv = swap_core(after(mlp_part, bias_a))
        gate = up_rs.halve(grad_down) if z_n > 1 else grad_down
    if split:
        stores, count = [], n_pairs - 1
        for i in range(3):
            rows = slice(i * bd, (i + 1) * bd)
            for n, pair in enumerate(range(1, n_pairs)):
                kx, cols = pair // 2, slice((i * count + n) * 128, (i * count + n + 1) * 128)
                for p, r_sl in a_spots:
                    ky, kz = p // z_n, p % z_n
                    spot = (kx - 1, (p, rows))
                    if pair % 2:
                        spot = (tx - 1 + ky, (kx * z_n + kz, rows))
                    stores.append(spot + (r_sl, cols))
        tasks = [(0, slice(0, width), 0, slice(0, 384 * count), stores)]
        sent = weight_grad(
            [first_in], [left_0, left_a], tasks, last_shapes[1:], "qkv_grad", 0, row0, out_grads[1:]
        )
        leaving = (sent[: tx - 1], sent[tx:])
        grad_down = down_rs.finish(sent[-1], [(full, 0, full)], [sds((fw, bd), F32)])[0]
        mlp_recv = swap_core(after(mlp_part, bias_a))
        gate = up_rs.halve((grad_down, leaving)) if z_n > 1 else grad_down
        left_b, bias_b = attn_backward([0], after(grad_att, (leaving, gate)), q, k, v)
        gate = (bias_b, mlp_recv)
        stores = []
        for i in range(3):
            rows, cols = slice(i * bd, (i + 1) * bd), slice(i * 128, (i + 1) * 128)
            stores += [(0, (p, rows), r_sl, cols) for p, r_sl in a_spots]
        tasks = [(0, slice(0, width), 0, slice(0, 384), stores)]
        kept = weight_grad(
            [after(first_in, gate)],
            [left_b],
            tasks,
            last_shapes[:1],
            "qkv_keep",
            0,
            row0,
            out_grads[:1],
        )
        grads = list(kept) + list(sent)
        lefts, starts = [left_0, left_a, left_b], [1, 2, 0]
        pair_sums = [bias_b, bias_0, bias_a]
        gate = kept[0]
    else:
        while 2 * up_rs.bit < z_n:
            gate = up_rs.halve((gate, mlp_recv))
        makers = [by_right(0, 0, hw, i * bd, hh, hh < bd, i * ext) for i in range(3)]
        tasks = [task for maker in makers for task in maker]
        grads = weight_grad(
            [after(first_in, gate)],
            [left_a],
            tasks,
            last_shapes,
            "qkv_grad",
            0,
            row0,
            out_grads,
            hh < bd,
        )
        lefts, starts = [left_a], [0]
        pair_sums = [bias_a]
        gate = grads[-1]
    qkv_rs = send_grad(grads, "qkv")
    lefts = after(lefts, gate)
    one_part = input_grad(lefts, starts, wqkv, width)
    one_recv = swap_core(one_part)
    cuts = []
    for h in range(2):
        for j in range(fh // bd):
            rows = slice(h * up_rows + j * bd, h * up_rows + (j + 1) * bd)
            cuts.append((rows, 0, (full, slice(h * fh + j * bd, h * fh + (j + 1) * bd))))
    up_cuts = cuts
    gate = one_part
    while 2 * up_rs.bit < z_n:
        gate = up_rs.halve(gate)
    qkv_half = qkv_rs.second(gate)
    wide = max(bd, hw // dp, fw // dp)
    if split and fw // dp == bd and 128 % (hw // dp) == 0:
        rest = sds((tx * y_n, z_n, 16, wide), F32)
        sums = [col, bias_up] + pair_sums
    else:
        bias_qv = jnp.concatenate(pair_sums)
        bias_qv = jnp.sum(bias_qv.reshape(n_pairs, 2, 2, 128), axis=1).transpose(1, 0, 2)
        vec = jnp.concatenate([jnp.zeros((2, width), F32), col])
        vec = vec.reshape(6, y_n, z_n, bd).transpose(1, 2, 0, 3)
        bias_qv = bias_qv.reshape(2, tx, dp, hw // dp).transpose(2, 1, 0, 3)
        bias_up = bias_up.reshape(tx, 1, dp, fw // dp).transpose(2, 0, 1, 3)
        bias = jnp.concatenate(
            [
                jnp.pad(value, ((0, 0), (0, 0), (0, 0), (0, wide - value.shape[3])))
                for value in (bias_qv, bias_up)
            ],
            axis=2,
        )
        bias = from_abs(xor_blocks(bias, me_d, 0), 0).reshape(y_n, z_n, tx, 3, wide)
        bias = bias.transpose(2, 0, 1, 3, 4)
        vec = jnp.pad(vec, ((0, 0), (0, 0), (0, 0), (0, wide - bd)))
        vec = jnp.broadcast_to(vec, (tx,) + vec.shape)
        rest = jnp.concatenate([vec, bias, jnp.zeros((tx, y_n, z_n, 7, wide), F32)], axis=3)
        rest = rest.reshape(tx * y_n, z_n, 16, wide)
        sums = None
    grad_tokens, one_sums, *small = finish_tokens(
        ids, nv, tok, one_part, after(one_recv, qkv_half), gmid, rest, sums, dp, aligned
    )
    if not aligned:
        ones = jnp.pad(one_sums.reshape(2, y_n, z_n, bd), ((0, 14), (0, 0), (0, 0), (0, wide - bd)))
        ones = ones.transpose(1, 2, 0, 3)
        small = [value + ones[n % y_n] for n, value in enumerate(small)]
    small = after(small, qkv_rs.state)
    got = small[:1]
    for n in range(1, tx * y_n):
        got.append(grid.send_xy(small[n], n // y_n, n % y_n))
    grad_up = up_rs.finish(one_sums, up_cuts, [sds((bd, fw), F32)])[0]
    cuts, outs = [], [sds((3, bd, hw), F32), sds((hw, bd), F32)]
    last_rows = row0 + hh
    for h in range(2):
        for i in range(3):
            rows = slice(h * last_rows + i * bd, h * last_rows + (i + 1) * bd)
            rows = (rows, slice(0, hh)) if hh < bd else rows
            cuts.append((rows, 0, (i, full, slice(h * hh, (h + 1) * hh))))
        rows = slice(h * last_rows + row0, (h + 1) * last_rows)
        cuts.append((rows, 1, (slice(h * hh, (h + 1) * hh),)))
    if wide == bd:
        qkv_zs = qkv_rs.along_z(grad_up, got)
        cuts.append((slice(2 * last_rows, 2 * last_rows + 16), 2, full))
        outs.append(sds((16, wide), F32))
    else:
        qkv_zs = qkv_rs.along_z(grad_up)
    layer_out = finish_layer(
        ids, keep, nv, middle, after(mlp_part, qkv_zs), mlp_recv, dp, aligned
    )
    res = qkv_rs.finish(layer_out, cuts, outs)
    grad_qkv, grad_out = res[:2]
    if wide == bd:
        both = res[2]
    else:
        both, bit = sum(got), 1
        while bit < z_n:
            both = both.reshape((-1, 2) + both.shape[1:])
            both = both[:, 0] + grid.send_z(both[:, 1], bit)
            bit *= 2
        both = both[0]
    if not aligned:

        def restore(value):
            value = xor_blocks(to_rel(value.reshape(seq, dp, bd), 1), me_d, 1)
            return value.reshape(seq, width)

        layer_out, grad_tokens = restore(layer_out), restore(grad_tokens)

    share = bd // (2 * tx)
    mine = lax.dynamic_slice(both[:6, :bd], (0, (2 * me_x + core) * share), (6, share))

    return (
        layer_out,
        grad_tokens,
        mine[0:3:2],
        jnp.concatenate([mine[1:2], mine[3:6]]),
        grad_qkv,
        both[6:8, : hw // dp],
        grad_out,
        grad_up,
        both[8, : fw // dp],
        grad_down,
    )


def solution(mesh):
    dp, tensor = mesh.shape["dp"], mesh.shape["tensor"]
    split = Mesh(mesh.devices.reshape(dp, tensor // 2, 2), ("dp", "tx", "core"))
    every = ("dp", "tx", "core")
    tensor_axes = ("tx", "core")
    in_specs = (
        P(every, None),
        P(every, None),
        P("dp"),
        P(None, "dp"),
        P(None, "dp"),
        P(None, "dp", tensor_axes),
        P(None, ("tx", "core", "dp")),
        P(tensor_axes, "dp"),
        P("dp", tensor_axes),
        P(("tx", "core", "dp")),
        P(tensor_axes, "dp"),
    )
    out_specs = (
        P(every, None),
        P(every, None),
        P(None, every),
        P(None, every),
        P(None, "dp", tensor_axes),
        P(None, ("tx", "core", "dp")),
        P(tensor_axes, "dp"),
        P("dp", tensor_axes),
        P(("tx", "core", "dp")),
        P(tensor_axes, "dp"),
    )
    return jax.shard_map(
        functools.partial(per_device, dp=dp, tx=tensor // 2),
        mesh=split,
        in_specs=in_specs,
        out_specs=out_specs,
        check_vma=False,
    )
```

```python
import functools

import jax
import jax.numpy as jnp
from jax import lax
from jax.experimental import pallas as pl
from jax.experimental.pallas import tpu as pltpu
from jax.sharding import Mesh, PartitionSpec as P

HEAD_DIM = 64
VALID = 577
SEQ = 584
BF = jnp.bfloat16
F32 = jnp.float32
VMEM_LIMIT = 60 * 1024 * 1024
WHOLE_VMEM = ("arrange_pair", "vectors", "mlp_up", "down_grad", "mlp_back", "qkv_sum")
COST_SCALE = 1.0
COST = {
    "arrange_pair": 5,
    "vectors": 3,
    "attn_forward": 16,
    "mlp_up": 10,
    "down_grad": 11,
    "mlp_back": 22,
    "up_grad": 11,
    "middle_back": 0,
    "out_grad": 8,
    "attn_backward": 18,
    "attn_first": 0,
    "qkv_grad": 7,
    "qkv_keep": 0,
    "up_half": 0,
    "join": 0,
    "grad_one": 0,
    "qkv_add": 30,
    "finish_layer": 0,
    "up_sum": 0,
    "finish_tokens": 9,
}
NT = (((1,), (1,)), ((), ()))
TN = (((0,), (0,)), ((), ()))
NN = (((1,), (0,)), ((), ()))


def dot(left, right, dims):
    return lax.dot_general(left, right, dims, preferred_element_type=F32)


class Loads:
    def __init__(self, sems):
        self.sems, self.groups = sems, []

    def start(self, pairs):
        sem = self.sems.at[len(self.groups)]
        copies = [pltpu.make_async_copy(src, dst, sem) for src, dst in pairs]
        for copy in copies:
            copy.start()
        self.groups.append(copies)
        return len(self.groups) - 1

    def wait(self, group):
        for copy in self.groups[group]:
            copy.wait()


def padded_bytes(value):
    lead, (rows, lanes) = value.shape[:-2], value.shape[-2:]
    count = -(-rows // 16) * 16 * (-(-lanes // 128) * 128)
    for size in lead:
        count *= size
    return count * jnp.dtype(value.dtype).itemsize


def call(body, ins, outs, scratch, name, flops, aliases=None, smem=(), sems=48, vmem_ins=(), spare=12, pinned=False):
    n_smem, n_vmem, n_in, n_out = len(smem), len(vmem_ins), len(ins), len(outs)
    moved = sum(a.size * a.dtype.itemsize for a in ins) + sum(
        o.size * o.dtype.itemsize for o in outs
    )

    def kernel(*refs):
        first = n_smem + n_vmem
        small = refs[:first]
        in_refs = refs[first : first + n_in]
        out_refs = refs[first + n_in : first + n_in + n_out]
        rest = refs[first + n_in + n_out :]
        body(small, in_refs, out_refs, rest[:-1], Loads(rest[-1]))

    held = sum(padded_bytes(piece) for piece in scratch) + spare * 1024 * 1024
    vmem = VMEM_LIMIT if name in WHOLE_VMEM else min(held, VMEM_LIMIT)
    flops = max(COST.get(name, 3), 0.02) * COST_SCALE * 1.15e9
    moved = 0
    any_spec = pl.BlockSpec(memory_space=pl.ANY)
    hbm_spec = pl.BlockSpec(memory_space=pltpu.HBM) if pinned else any_spec
    return pl.pallas_call(
        kernel,
        out_shape=outs,
        in_specs=[pl.BlockSpec(memory_space=pltpu.SMEM)] * n_smem
        + [pl.BlockSpec(memory_space=pltpu.VMEM)] * n_vmem
        + [hbm_spec if i in (aliases or {}) else any_spec for i in range(n_in)],
        out_specs=[hbm_spec if pinned else any_spec] * n_out,
        scratch_shapes=list(scratch) + [pltpu.SemaphoreType.DMA((sems,))],
        input_output_aliases={n_smem + n_vmem + i: o for i, o in (aliases or {}).items()},
        compiler_params=pltpu.CompilerParams(vmem_limit_bytes=vmem),
        cost_estimate=pl.CostEstimate(flops=int(flops), bytes_accessed=int(flops // 1000), transcendentals=0),
        name=name,
    )(*smem, *vmem_ins, *ins)


def norm_parts(rows):
    center = rows - jnp.mean(rows, axis=1, keepdims=True)
    inverse = lax.rsqrt(jnp.mean(center * center, axis=1, keepdims=True) + 1e-05)
    return center * inverse, inverse


def norm_back(grad_norm, scaled, inverse, gain_row):
    grad_hat = grad_norm * gain_row
    first_mean = jnp.mean(grad_hat, axis=1, keepdims=True)
    second_mean = jnp.mean(grad_hat * scaled, axis=1, keepdims=True)
    return inverse * (grad_hat - first_mean - scaled * second_mean)


def sds(shape, dtype):
    return jax.ShapeDtypeStruct(shape, dtype)


def arrange_pair(ids, own, other, nd):
    n = len(own)
    rows, width = own[0].shape
    bd = width // nd

    def body(small, ins, outs, scratch, loads):
        (ids_ref,) = small
        mine = ids_ref[0]
        in_s, out_s = scratch[: 2 * n], scratch[2 * n :]
        groups = [loads.start([(ins[i], in_s[i])]) for i in range(2 * n)]
        done = []
        for i in range(2 * n):
            loads.wait(groups[i])
            for p in range(nd):
                src = pl.ds(pl.multiple_of(ids_ref[2 + p] * bd, 128), bd)
                out_s[i][:, p * bd : (p + 1) * bd] = in_s[i][:, src]
            spot = mine if i < n else 1 - mine
            done.append(loads.start([(out_s[i], outs[i % n].at[spot])]))
        for group in done:
            loads.wait(group)

    return call(
        body,
        list(own) + list(other),
        [sds((2, rows, width), BF)] * n,
        [pltpu.VMEM((rows, width), BF)] * (4 * n),
        "arrange_pair",
        0,
        smem=(ids,),
    )


def vectors(ids, gathered, row0, nd, y_n, bd, qv, up):
    tx, z_n = len(gathered), nd // y_n

    def body(small, ins, outs, scratch, loads):
        ids_ref, rows_s, nv_s, bq_s, bu_s = small[0], *scratch
        rows = pl.ds(row0, 16)
        loads.wait(loads.start([(ins[k].at[:, rows, :], rows_s.at[k]) for k in range(tx)]))
        for p in range(nd):
            nv_s[:, p * bd : (p + 1) * bd] = rows_s[0, p].astype(F32)[:6, :bd]
        for k in range(tx):
            pieces = []
            for d in range(nd):
                rel = ids_ref[1] ^ d
                spot = (rel % y_n) * z_n + rel // y_n
                piece = rows_s[k, spot].astype(F32)
                bu_s[:, (k * nd + d) * up : (k * nd + d + 1) * up] = piece[8:9, :up]
                pieces.append(piece[6:8, :])
            each = 128 // qv
            for start in range(0, nd, each):
                total = pieces[start]
                for i in range(1, each):
                    total = total + pltpu.roll(pieces[start + i], i * qv, 1)
                bq_s[:, (k * nd + start) * qv : (k * nd + start + each) * qv] = total
        loads.wait(loads.start([(nv_s, outs[0]), (bq_s, outs[1]), (bu_s, outs[2])]))

    shapes = [(6, nd * bd), (2, tx * nd * qv), (1, tx * nd * up)]
    return call(
        body,
        list(gathered),
        [sds(s, F32) for s in shapes],
        [pltpu.VMEM((tx, nd, 16, gathered[0].shape[2]), BF)] + [pltpu.VMEM(s, F32) for s in shapes],
        "vectors",
        0,
        smem=(ids,),
    )


def block_stores(ids_ref, src, dst, nd, aligned):
    if not aligned:
        return [(src, dst)]
    bd = src.shape[1] // nd
    pairs = []
    for p in range(nd):
        cols = pl.ds(pl.multiple_of(ids_ref[2 + p] * bd, 128), bd)
        pairs.append((src.at[:, p * bd : (p + 1) * bd], dst.at[:, cols]))
    return pairs


def weight_loads(loads, groups, refs, scratch):
    return [
        loads.start([(refs[a].at[src], scratch.at[dst]) for a, src, dst in plan])
        for plan in groups
    ]


def softmax_rows(q2, k2):
    scores = dot(q2, k2, NT)
    lane = lax.broadcasted_iota(jnp.int32, scores.shape, 1)
    scores = jnp.where(lane < VALID, scores, -1e30)
    e = jnp.exp(scores - jnp.max(scores, axis=1, keepdims=True))
    return e * (1.0 / jnp.sum(e, axis=1, keepdims=True))


def attn_forward(image, tok, nv, bq, wqkv, wout, prev):
    seq, width = tok.shape[1:]
    qkv_arrays, qkv_plan, qkv_scratch = wqkv
    out_arrays, out_plan, out_scratch = wout
    ext = qkv_scratch[-1]
    n_prev = 0 if prev is None else len(prev)
    nq, no = len(qkv_arrays), len(out_arrays)

    def body(small, ins, outs, scratch, loads):
        nv_ref, bq_ref = small
        tok_ref, ins = ins[0], ins[1 + n_prev :]
        w_s, wo_s, tok_s, first_s, q_s, k_s, v_s, att_s, part_s = scratch
        g_tok = loads.start([(tok_ref.at[image], tok_s)])
        g_w = weight_loads(loads, qkv_plan, ins[:nq], w_s)
        g_o = weight_loads(loads, out_plan, ins[nq:], wo_s)
        loads.wait(g_tok)
        hat, _ = norm_parts(tok_s[...].astype(F32))
        first_s[...] = (hat * nv_ref[0:1, :] + nv_ref[2:3, :]).astype(BF)
        g_first = loads.start([(first_s, outs[0].at[image])])
        low = first_s[...]
        for i, ref in enumerate((q_s, k_s, v_s)):
            if i < len(g_w):
                loads.wait(g_w[i])
            proj = dot(low, w_s[i].reshape(width, ext), NN)
            if i == 0:
                proj = proj + bq_ref[0:1, :]
            if i == 2:
                proj = proj + bq_ref[1:2, :]
            low_proj = proj.astype(BF)
            if i == 0:
                low_proj = low_proj * jnp.asarray(HEAD_DIM**-0.5, BF)
            ref[...] = low_proj
        g_qkv = loads.start(
            [(q_s, outs[1].at[image]), (k_s, outs[2].at[image]), (v_s, outs[3].at[image])]
        )
        half = lax.broadcasted_iota(jnp.int32, (1, 128), 1) // HEAD_DIM

        def pair(i, carry):
            cols = pl.ds(pl.multiple_of(i * 128, 128), 128)
            q2, k2, v2 = q_s[:, cols], k_s[:, cols], v_s[:, cols]
            total = None
            for h in range(2):
                keep = (half == h).astype(BF)
                probs = softmax_rows(q2, k2 * keep).astype(BF)
                piece = dot(probs, v2 * keep, NN)
                total = piece if total is None else total + piece
            att_s[:, cols] = total.astype(BF)
            return carry

        lax.fori_loop(0, ext // 128, pair, 0)
        g_att = loads.start([(att_s, outs[4].at[image])])
        loads.wait(g_o[0])
        part_s[...] = dot(att_s[...], wo_s[...], NN).astype(BF)
        g_part = loads.start([(part_s, outs[5])])
        for group in (g_first, g_qkv, g_att, g_part):
            loads.wait(group)

    shapes = [(2, seq, width)] + [(2, seq, ext)] * 4
    return call(
        body,
        [tok] + list(prev or []) + qkv_arrays + out_arrays,
        [sds(s, BF) for s in shapes] + [sds((seq, width), BF)],
        [
            pltpu.VMEM(qkv_scratch, BF),
            pltpu.VMEM(out_scratch, BF),
            pltpu.VMEM((seq, width), BF),
            pltpu.VMEM((seq, width), BF),
            pltpu.VMEM((seq, ext), BF),
            pltpu.VMEM((seq, ext), BF),
            pltpu.VMEM((seq, ext), BF),
            pltpu.VMEM((seq, ext), BF),
            pltpu.VMEM((seq, width), BF),
        ],
        "attn_forward",
        2 * seq * width * ext * 4 + 16 * seq * seq * ext,
        aliases={1 + i: i for i in range(n_prev)},
        pinned=True,
        vmem_ins=(nv, bq),
    )


def mlp_up(image, tok, part, recv, keep, nv, bu, wup, step, prev):
    seq, width = tok.shape[1:]
    up_arrays, up_plan, up_scratch = wup
    hid = up_scratch[-1]
    n_prev = 0 if prev is None else len(prev)

    def body(small, ins, outs, scratch, loads):
        keep_ref, nv_ref, bu_ref = small
        tok_ref, part_ref, recv_ref = ins[:3]
        w_s, tok_s, part_s, recv_s, mid_s, sec_s, act_s, dact_s = scratch
        g_in = loads.start([(tok_ref.at[image], tok_s), (part_ref, part_s), (recv_ref, recv_s)])
        g_w = weight_loads(loads, up_plan, ins[3 + n_prev :], w_s)
        loads.wait(g_in)
        total = part_s[...].astype(F32) + recv_s[...].astype(F32) + nv_ref[4:5, :]
        middle = tok_s[...].astype(F32) + keep_ref[image] * total
        mid_s[...] = middle
        hat, _ = norm_parts(middle)
        sec_s[...] = (hat * nv_ref[1:2, :] + nv_ref[3:4, :]).astype(BF)
        g_mid = loads.start([(mid_s, outs[0].at[image]), (sec_s, outs[1].at[image])])
        second = sec_s[...]
        done = []
        for block in range(hid // step):
            if block < len(g_w):
                loads.wait(g_w[block])
            cols = slice(block * step, (block + 1) * step)
            pre = dot(second, w_s[:, cols], NN) + bu_ref[0:1, cols]
            gate = 0.5 * jnp.tanh(0.851 * pre) + 0.5
            act_s[:, cols] = (pre * gate).astype(BF)
            dact_s[:, cols] = (gate + 1.702 * pre * gate * (1.0 - gate)).astype(BF)
            done.append(
                loads.start(
                    [
                        (act_s.at[:, cols], outs[2].at[image, :, cols]),
                        (dact_s.at[:, cols], outs[3].at[image, :, cols]),
                    ]
                )
            )
        for group in [g_mid] + done:
            loads.wait(group)

    outs = [
        sds((2, seq, width), F32),
        sds((2, seq, width), BF),
        sds((2, seq, hid), BF),
        sds((2, seq, hid), BF),
    ]
    return call(
        body,
        [tok, part, recv] + list(prev or []) + up_arrays,
        outs,
        [
            pltpu.VMEM(up_scratch, BF),
            pltpu.VMEM((seq, width), BF),
            pltpu.VMEM((seq, width), BF),
            pltpu.VMEM((seq, width), BF),
            pltpu.VMEM((seq, width), F32),
            pltpu.VMEM((seq, width), BF),
            pltpu.VMEM((seq, hid), BF),
            pltpu.VMEM((seq, hid), BF),
        ],
        "mlp_up",
        2 * seq * width * hid,
        aliases={3 + i: i for i in range(n_prev)},
        pinned=True,
        smem=(keep,),
        vmem_ins=(nv, bu),
    )


def column_loads(src, dst, start):
    if len(src.shape) == 2:
        return [(src, dst)]
    n, _, width = src.shape
    return [
        (src.at[i], dst.at[:, (start + i) * width : (start + i + 1) * width]) for i in range(n)
    ]


def weight_grad(lefts, rights, tasks, out_shapes, name, lo, hi, prev=None, fill=False):
    rows = lefts[0].shape[0]
    arrays = list(lefts) + list(rights)
    joined = all(len(a.shape) == 3 for a in rights)
    if joined:
        total = sum(a.shape[0] for a in rights) // 3
        wide = [a.shape[-1] for a in lefts] + [3 * total * rights[0].shape[-1]]
    else:
        wide = [a.shape[-1] for a in arrays]
    n_left, n_in = len(lefts), len(arrays)
    prev = list(prev or [])
    last = {}
    for n, task in enumerate(tasks):
        for store in task[4]:
            last[store[0]] = n

    def body(small, ins, outs, scratch, loads):
        in_s, out_s = scratch[: len(wide)], scratch[len(wide) :]
        order = []
        for l_index, _, r_index, _, _ in tasks:
            for i in (l_index, n_left + r_index):
                if i not in order:
                    order.append(i)
        groups = {}
        for i in order:
            pairs = [(ins[i], in_s[i])]
            if joined and i == n_left:
                pairs, start = [], 0
                for j, stack in enumerate(rights):
                    count = stack.shape[0] // 3
                    for kind in range(3):
                        part = ins[n_left + j].at[kind * count : (kind + 1) * count]
                        pairs += column_loads(part, in_s[i], kind * total + start)
                    start += count
            groups[i] = loads.start(pairs)
        for ref in out_s if fill else ():
            ref[...] = jnp.zeros_like(ref)
        ready, done = set(), []
        for n, (l_index, l_cols, r_index, r_cols, stores) in enumerate(tasks):
            for i in (l_index, n_left + r_index):
                if i not in ready:
                    loads.wait(groups[i])
                    ready.add(i)
            left, right = in_s[l_index][:, l_cols], in_s[n_left + r_index][:, r_cols]
            value = dot(left, right, TN).astype(BF)
            for which, spot, r_sl, c_sl in stores:
                out_s[which][spot] = value[r_sl, c_sl]
            for which in sorted(w for w in last if last[w] == n):
                done.append(loads.start([(out_s[which], outs[which].at[:, lo:hi])]))
        for group in done:
            loads.wait(group)

    flops = sum(
        2 * rows * (t[1].stop - t[1].start) * (t[3].stop - t[3].start) for t in tasks
    )
    return call(
        body,
        arrays + prev,
        [sds(s, BF) for s in out_shapes],
        [pltpu.VMEM((rows, w), BF) for w in wide]
        + [pltpu.VMEM((s[0], hi - lo, s[2]), BF) for s in out_shapes],
        name,
        flops,
        aliases={n_in + i: i for i in range(len(prev))},
    )


def mlp_back(grad, act, dact, wdown, wup, step):
    rows, width = grad.shape
    seq = rows // 2
    hid = dact.shape[1]
    down_arrays, down_plan, down_scratch = wdown
    up_arrays, up_plan, up_scratch = wup
    n_down = len(down_arrays)

    def body(small, ins, outs, scratch, loads):
        wd_s, wu_s, g_s, a_s, d_s, low_s, sum_s, two_s, mlp_s = scratch
        g_g = loads.start([(ins[0], g_s)])
        g_wd = weight_loads(loads, down_plan, ins[3 : 3 + n_down], wd_s)
        g_d = []
        for block in range(hid // step):
            cols = slice(block * step, (block + 1) * step)
            g_d.append(loads.start([(ins[2].at[:, cols], d_s.at[:, cols])]))
        g_wu = weight_loads(loads, up_plan, ins[3 + n_down :], wu_s)
        g_a = loads.start([(ins[1], a_s)])
        loads.wait(g_g)
        left = g_s[...]
        done = []
        for block in range(hid // step):
            if block < len(g_wd):
                loads.wait(g_wd[block])
            loads.wait(g_d[block])
            cols = slice(block * step, (block + 1) * step)
            pre = dot(left, wd_s[cols, :], NT) * d_s[:, cols].astype(F32)
            low_s[:, cols] = pre.astype(BF)
            sum_s[0:1, cols] = jnp.sum(pre, axis=0, keepdims=True)
            done.append(loads.start([(low_s.at[:, cols], outs[0].at[:, cols])]))
        done.append(loads.start([(sum_s, outs[1])]))
        for group in g_wu:
            loads.wait(group)
        two = dot(low_s[...], wu_s[...], NT)
        for a in range(2):
            two_s[a] = two[a * seq : (a + 1) * seq].astype(BF)
            done.append(loads.start([(two_s.at[a], outs[2].at[a])]))
        loads.wait(g_a)
        mlp_s[...] = dot(a_s[...], wd_s[...], NN).astype(BF)
        done.append(loads.start([(mlp_s, outs[3])]))
        for group in done:
            loads.wait(group)

    return call(
        body,
        [grad, act, dact] + down_arrays + up_arrays,
        [sds((rows, hid), BF), sds((1, hid), F32)]
        + [sds((2, seq, width), BF), sds((rows, width), BF)],
        [
            pltpu.VMEM(down_scratch, BF),
            pltpu.VMEM(up_scratch, BF),
            pltpu.VMEM((rows, width), BF),
            pltpu.VMEM((rows, hid), BF),
            pltpu.VMEM((rows, hid), BF),
            pltpu.VMEM((rows, hid), BF),
            pltpu.VMEM((1, hid), F32),
            pltpu.VMEM((2, seq, width), BF),
            pltpu.VMEM((rows, width), BF),
        ],
        "mlp_back",
        6 * rows * width * hid,
        sems=64,
    )


def input_grad(stacks, starts, weight, width):
    arrays, plan, shape = weight
    n, ext = shape[0], shape[-1]
    rows = stacks[0].shape[1]
    seq, m = rows // 2, len(stacks)

    def body(small, ins, outs, scratch, loads):
        w_s, out_s = scratch[0], scratch[1]
        l_s = scratch[2:]
        g_w = weight_loads(loads, plan[:1], ins[m:], w_s)
        g_l = []
        for i in range(n):
            pairs = []
            for j in range(m):
                count = stacks[j].shape[0] // n
                pairs += column_loads(ins[j].at[i * count : (i + 1) * count], l_s[i], starts[j])
            g_l.append(loads.start(pairs))
        g_w += weight_loads(loads, plan[1:], ins[m:], w_s)
        total = None
        for i in range(n):
            loads.wait(g_l[i])
            if i < len(g_w):
                loads.wait(g_w[i])
            piece = dot(l_s[i][...], w_s[i].reshape(width, ext), NT)
            total = piece if total is None else total + piece
        done = []
        for a in range(2):
            out_s[a] = total[a * seq : (a + 1) * seq].astype(BF)
            done.append(loads.start([(out_s.at[a], outs[0].at[a])]))
        for group in done:
            loads.wait(group)

    return call(
        body,
        list(stacks) + arrays,
        [sds((2, seq, width), BF)],
        [pltpu.VMEM(shape, BF), pltpu.VMEM((2, seq, width), BF)] + [pltpu.VMEM((rows, ext), BF)] * n,
        "grad_one",
        2 * rows * width * ext * n,
    )[0]


def middle_back(ids, middle, part, recv, cot, keep, nv, wout):
    _, seq, width = middle.shape
    out_arrays, out_plan, out_scratch = wout
    ext = out_scratch[0]

    def body(small, ins, outs, scratch, loads):
        ids_ref, keep_ref, nv_ref = small
        mine = ids_ref[0]
        wo_s, mid_s, part_s, recv_s, cot_s, gmid_s, gat_s, do_s = scratch[:8]
        cs_s = scratch[8]
        g_in = [
            loads.start(
                [
                    (ins[0].at[a], mid_s.at[a]),
                    (ins[1].at[a], cot_s.at[a]),
                    (ins[2].at[a], part_s.at[a]),
                    (ins[3].at[a], recv_s.at[a]),
                ]
            )
            for a in range(2)
        ]
        g_o = weight_loads(loads, out_plan, ins[4:], wo_s)
        done = []
        for a in range(2):
            loads.wait(g_in[a])
            keep_here = keep_ref[a]
            hat, inverse = norm_parts(mid_s[a])
            grad_two = part_s[a].astype(F32) + recv_s[a].astype(F32)
            top = cot_s[a].astype(F32)
            grad_mid = top + norm_back(grad_two, hat, inverse, nv_ref[1:2, :])
            grad_attn = grad_mid * keep_here
            sums = [
                jnp.sum(grad_two * hat, axis=0, keepdims=True),
                jnp.sum(grad_two, axis=0, keepdims=True),
                jnp.sum(grad_attn, axis=0, keepdims=True),
                jnp.sum(top, axis=0, keepdims=True) * keep_here,
            ]
            for i, value in enumerate(sums):
                cs_s[i : i + 1, :] = value if a == 0 else cs_s[i : i + 1, :] + value
            gmid_s[a] = grad_mid
            gat_s[a] = grad_attn.astype(BF)
            done.append(loads.start([(gat_s.at[a], outs[1].at[a])]))
            if a == 0:
                loads.wait(g_o[0])
            do_s[a] = dot(gat_s[a], wo_s[...], NT).astype(BF)
            done.append(loads.start([(do_s.at[a], outs[2].at[a])]))
        done.append(loads.start([(gmid_s.at[mine], outs[0]), (cs_s, outs[3])]))
        for group in done:
            loads.wait(group)

    return call(
        body,
        [middle, cot, part, recv] + out_arrays,
        [
            sds((seq, width), F32),
            sds((2, seq, width), BF),
            sds((2, seq, ext), BF),
            sds((4, width), F32),
        ],
        [
            pltpu.VMEM(out_scratch, BF),
            pltpu.VMEM((2, seq, width), F32),
            pltpu.VMEM((2, seq, width), BF),
            pltpu.VMEM((2, seq, width), BF),
            pltpu.VMEM((2, seq, width), BF),
            pltpu.VMEM((2, seq, width), F32),
            pltpu.VMEM((2, seq, width), BF),
            pltpu.VMEM((2, seq, ext), BF),
            pltpu.VMEM((4, width), F32),
        ],
        "middle_back",
        4 * seq * width * ext,
        smem=(ids, keep),
        vmem_ins=(nv,),
    )


def attn_backward(pairs, grad, q, k, v, name="attn_backward"):
    _, seq, _ = q.shape
    n = len(pairs)

    def body(small, ins, outs, scratch, loads):
        q_s, k_s, v_s, do_s, dq_s, dk_s, dv_s, bs_s = scratch
        groups = []
        for u in range(2 * n):
            cols = slice(pairs[u // 2] * 128, (pairs[u // 2] + 1) * 128)
            groups.append(
                loads.start([(ins[j].at[u % 2, :, cols], scratch[j].at[u]) for j in range(4)])
            )
        half = lax.broadcasted_iota(jnp.int32, (1, 128), 1) // HEAD_DIM
        for group in groups:
            loads.wait(group)

        def unit(u, carry):
            q2, k2, v2, do2 = q_s[u], k_s[u], v_s[u], do_s[u]
            dq = dk = dv = None
            for h in range(2):
                mask = (half == h).astype(BF)
                km, qm, dom = k2 * mask, q2 * mask, do2 * mask
                scores = dot(km, q2, NT)
                row = lax.broadcasted_iota(jnp.int32, scores.shape, 0)
                scores = jnp.where(row < VALID, scores, -1e30)
                e = jnp.exp(scores - jnp.max(scores, axis=0, keepdims=True))
                probs = e * (1.0 / jnp.sum(e, axis=0, keepdims=True))
                grad_probs = dot(v2, dom, NT)
                row_dot = jnp.sum(probs * grad_probs, axis=0, keepdims=True)
                grad_scores = (probs * (grad_probs - row_dot)).astype(BF)
                v_piece = dot(probs.astype(BF), dom, NN)
                k_piece = dot(grad_scores, qm, NN)
                q_piece = dot(grad_scores, km, TN)
                dq = q_piece if dq is None else dq + q_piece
                dk = k_piece if dk is None else dk + k_piece
                dv = v_piece if dv is None else dv + v_piece
            dq = dq * HEAD_DIM**-0.5
            bs_s[u, 0:1, :] = jnp.sum(dq, axis=0, keepdims=True)
            bs_s[u, 1:2, :] = jnp.sum(dv, axis=0, keepdims=True)
            dq_s[u] = dq.astype(BF)
            dk_s[u] = dk.astype(BF)
            dv_s[u] = dv.astype(BF)
            return carry

        lax.fori_loop(0, 2 * n, unit, 0)
        done = [loads.start([(scratch[4 + j], outs[0].at[j])]) for j in range(3)]
        done.append(loads.start([(bs_s, outs[1])]))
        for group in done:
            loads.wait(group)

    grads, sums = call(
        body,
        [q, k, v, grad],
        [sds((3, 2 * n, seq, 128), BF), sds((2 * n, 2, 128), F32)],
        [pltpu.VMEM((2 * n, seq, 128), BF)] * 7 + [pltpu.VMEM((2 * n, 2, 128), F32)],
        name,
        0,
    )
    return grads.reshape(3 * n, 2 * seq, 128), sums


def finish_layer(ids, keep, nv, middle, part, recv, nd, aligned):
    _, seq, width = middle.shape

    def body(small, ins, outs, scratch, loads):
        ids_ref, keep_ref, nv_ref = small
        mine = ids_ref[0]
        mid_s, part_s, recv_s, out_s = scratch
        groups = [loads.start([(ins[i].at[mine], scratch[i])]) for i in range(3)]
        for group in groups:
            loads.wait(group)
        total = part_s[...].astype(F32) + recv_s[...].astype(F32) + nv_ref[5:6, :]
        out_s[...] = (mid_s[...] + keep_ref[mine] * total).astype(BF)
        loads.wait(loads.start(block_stores(ids_ref, out_s, outs[0], nd, aligned)))

    return call(
        body,
        [middle, part, recv],
        [sds((seq, width), BF)],
        [pltpu.VMEM((seq, width), F32)] + [pltpu.VMEM((seq, width), BF)] * 3,
        "finish_layer",
        100 * seq * width,
        smem=(ids, keep),
        vmem_ins=(nv,),
    )[0]


def finish_tokens(ids, nv, tok, part, recv, gmid, rest, sums, nd, aligned):
    _, seq, width = tok.shape
    n_dest, z_n, n_rows, lanes = rest.shape
    bd, y_n = width // nd, nd // rest.shape[1]
    tx = n_dest // y_n

    def body(small, ins, outs, scratch, loads):
        ids_ref, nv_ref = small[:2]
        mine = ids_ref[0]
        tok_s, part_s, recv_s, gm_s, out_s, cs_s, rest_s = scratch
        g_rest = loads.start([(ins[4], rest_s)] if sums is None else [])
        groups = [
            loads.start(
                [
                    (ins[0].at[a], tok_s.at[a]),
                    (ins[2].at[a], part_s.at[a]),
                    (ins[3].at[a], recv_s.at[a]),
                ]
            )
            for a in range(2)
        ]
        g_mid = loads.start([(ins[1], gm_s)])
        for group in groups:
            loads.wait(group)
        done = []
        for i in range(2):
            a = mine if i == 0 else 1 - mine
            hat, inverse = norm_parts(tok_s[a].astype(F32))
            grad_one = part_s[a].astype(F32) + recv_s[a].astype(F32)
            gain_sum = jnp.sum(grad_one * hat, axis=0, keepdims=True)
            shift_sum = jnp.sum(grad_one, axis=0, keepdims=True)
            if i == 0:
                cs_s[0:1, :] = gain_sum
                cs_s[1:2, :] = shift_sum
                loads.wait(g_mid)
                value = gm_s[...] + norm_back(grad_one, hat, inverse, nv_ref[0:1, :])
                out_s[...] = value.astype(BF)
                done.append(loads.start(block_stores(ids_ref, out_s, outs[0], nd, aligned)))
            else:
                cs_s[0:1, :] = cs_s[0:1, :] + gain_sum
                cs_s[1:2, :] = cs_s[1:2, :] + shift_sum
        loads.wait(g_rest)
        if sums is not None:
            col_ref, bup_ref, pairs = small[2], small[3], small[4:]
            up = bup_ref.shape[1] // tx // nd
            n_pairs = sum(ref.shape[0] // 2 for ref in pairs)
            qv = n_pairs * 128 // tx // nd
            per = 128 // qv
            lane = lax.broadcasted_iota(jnp.int32, (2, 128), 1)
            whole = [ref[2 * i] + ref[2 * i + 1] for ref in pairs for i in range(ref.shape[0] // 2)]
            whole = jnp.stack(whole)
            rest_s[...] = jnp.zeros_like(rest_s)
            for n in range(n_dest):
                kx, ky = n // y_n, n % y_n
                for kz in range(z_n):
                    p = ky * z_n + kz
                    d = ids_ref[2 + p]
                    rest_s[n, kz, 2:6, :] = col_ref[:, p * bd : (p + 1) * bd]
                    row = jnp.zeros((2, 128), F32)
                    for i in range(nd // per):
                        row = jnp.where(d // per == i, whole[kx * (nd // per) + i], row)
                    row = pltpu.roll(row, (per - d % per) * qv % 128, 1)
                    rest_s[n, kz, 6:8, :] = jnp.where(lane < qv, row, 0.0)
                    cols = pl.ds(pl.multiple_of((kx * nd + d) * up, 128), up)
                    rest_s[n, kz, 8:9, 0:up] = bup_ref[:, cols]
        for n in range(n_dest if aligned else 0):
            for kz in range(z_n):
                p = n % (nd // z_n) * z_n + kz
                rest_s[n, kz, 0:2, :] = cs_s[:, p * bd : (p + 1) * bd]
        done.append(loads.start([(cs_s, outs[1])]))
        done += [loads.start([(rest_s.at[n], outs[2 + n])]) for n in range(n_dest)]
        for group in done:
            loads.wait(group)

    return call(
        body,
        [tok, gmid, part, recv] + ([rest] if sums is None else []),
        [sds((seq, width), BF), sds((2, width), F32)] + [sds(rest.shape[1:], F32)] * n_dest,
        [pltpu.VMEM((2, seq, width), BF)] * 3
        + [pltpu.VMEM((seq, width), F32), pltpu.VMEM((seq, width), BF), pltpu.VMEM((2, width), F32)]
        + [pltpu.VMEM(rest.shape, F32)],
        "finish_tokens",
        200 * seq * width,
        smem=(ids,),
        vmem_ins=(nv,) + tuple(sums or ()),
    )


class Grid3:
    def __init__(self, dp, tx):
        self.dp, self.tx = dp, tx
        self.y = 2 if dp % 2 == 0 else 1
        self.z = dp // self.y

    def send_z(self, value, k):
        return lax.ppermute(value, "dp", [(i, i ^ (k * self.y)) for i in range(self.dp)])

    def send_y(self, value, k):
        return lax.ppermute(value, "dp", [(i, i ^ k) for i in range(self.dp)])

    def send_xy(self, value, kx, ky):
        count = self.dp * self.tx
        pairs = [(i, ((i // self.tx) ^ ky) * self.tx + ((i % self.tx) ^ kx)) for i in range(count)]
        return lax.ppermute(value, ("dp", "tx"), pairs)

    def send_x(self, value, k):
        return lax.ppermute(value, "tx", [(i, i ^ k) for i in range(self.tx)])


def swap_core(value):
    return lax.ppermute(value, "core", [(0, 1), (1, 0)])


def after(values, gate):
    return lax.optimization_barrier((values, gate))[0]


def gather_z(grid, part_a, part_b, gate=None):
    rows = part_a.shape[0]
    both = jnp.concatenate([part_a, part_b], axis=0)
    all_z = [both] + [grid.send_z(both, k) for k in range(1, grid.z)]
    if gate is not None:
        all_z = after(all_z, gate)
    return jnp.stack([v[:rows] for v in all_z]), jnp.stack([v[rows:] for v in all_z])


def gather_first(grid, a_z, b_z):
    a_y = [a_z] + [grid.send_y(a_z, k) for k in range(1, grid.y)]
    b_x = [b_z] + [grid.send_x(b_z, k) for k in range(1, grid.tx)]
    return a_y, b_x


def join(pieces):
    return [jnp.concatenate(part) for part in pieces]


def gather_last(grid, a_y, b_x):
    a_all = [a_y] + [grid.send_x(a_y, k) for k in range(1, grid.tx)]
    b_all = [b_x] + [grid.send_y(b_x, k) for k in range(1, grid.y)]
    return a_all, b_all


def add_pieces(groups, cuts, outs, name, smem=(), more=(), fill=None):
    arrays = [a for group in groups for a in group]
    starts = [sum(len(g) for g in groups[:i]) for i in range(len(groups))]
    last = {}
    for n, cut in enumerate(cuts):
        last[cut[2]] = n

    def body(small, ins, outs_ref, scratch, loads):
        in_s, out_s = scratch[: len(arrays)], scratch[len(arrays) :]
        more_s = out_s[len(outs) :]
        loaded = [loads.start([(ins[i], in_s[i]) for i in range(starts[g], starts[g] + len(groups[g]))]) for g in range(len(groups))]
        ready, done = set(), []
        for n, (g, spot, which, place) in enumerate(cuts):
            if g not in ready:
                loads.wait(loaded[g])
                ready.add(g)
            total = None
            for i in range(starts[g], starts[g] + len(groups[g])):
                value = in_s[i][spot].astype(F32)
                total = value if total is None else total + value
            out_s[which][place] = total.astype(out_s[which].dtype)
            for w in sorted(w for w in last if last[w] == n):
                done.append(loads.start([(out_s[w], outs_ref[w])]))
        if fill is not None:
            fill(small, out_s, more_s)
            done.append(loads.start(list(zip(more_s, outs_ref[len(outs) :]))))
        for group in done:
            loads.wait(group)

    return call(
        body,
        arrays,
        list(outs) + list(more),
        [pltpu.VMEM(a.shape, a.dtype) for a in list(arrays) + list(outs) + list(more)],
        name,
        0,
        smem=smem,
        spare=8,
    )


class Scatter:
    def __init__(self, grid, a_all, b_all, name):
        self.grid, self.name, self.bit = grid, name, 0
        self.rows = (a_all[0].shape[1], b_all[0].shape[1])
        a_got = [grid.send_x(a_all[k], k) for k in range(1, grid.tx)]
        b_got = [grid.send_y(b_all[k], k) for k in range(1, grid.y)]
        self.state = ([a_all[0]] + a_got, [b_all[0]] + b_got)

    def second(self, gate):
        grid, z = self.grid, self.grid.z
        a_in, b_in = after(self.state, gate)
        outs = [sds((z,) + a_in[0].shape[1:], BF)] * grid.y + [sds((z,) + b_in[0].shape[1:], BF)] * grid.tx
        full = slice(None)
        cuts = [(0, slice(k * z, (k + 1) * z), k, full) for k in list(range(1, grid.y)) + [0]]
        cuts += [(1, slice(k * z, (k + 1) * z), grid.y + k, full) for k in list(range(1, grid.tx)) + [0]]
        res = add_pieces([a_in, b_in], cuts, outs, self.name + "_add")
        a_y, b_x = res[: grid.y], res[grid.y :]
        a_got = [grid.send_y(a_y[k], k) for k in range(1, grid.y)]
        b_got = [grid.send_x(b_x[k], k) for k in range(1, grid.tx)]
        self.state = ([a_y[0]] + a_got, [b_x[0]] + b_got)
        return a_y, b_x

    def along_z(self, gate, extra=None):
        grid = self.grid
        a_in, b_in = after(self.state, gate)
        ra, rb = self.rows
        groups = [a_in, b_in] + ([extra] if extra else [])
        more = extra[0].shape[1] if extra else 0
        order = list(range(1, grid.z)) + [0]
        cuts = []
        for k in order:
            cuts.append((0, k, k, slice(0, ra)))
            cuts.append((1, k, k, slice(ra, ra + rb)))
            if extra:
                cuts.append((2, k, k, slice(ra + rb, ra + rb + more)))
        outs = [sds((ra + rb + more,) + a_in[0].shape[2:], BF)] * grid.z
        both = add_pieces(groups, cuts, outs, self.name + "_addz")
        self.state = [both[0]] + [grid.send_z(both[k], k) for k in range(1, grid.z)]
        return both

    def halve(self, gate):
        grid, (ra, rb) = self.grid, self.rows
        groups = after(self.state, gate)
        if self.bit == 0:
            self.bit, self.left = 1, list(range(grid.z))
        else:
            self.bit, groups = 2 * self.bit, [groups]
        sent = [k for k in self.left if k & self.bit]
        kept = [k for k in self.left if not k & self.bit]
        cuts = []
        for which, ids in ((0, sent), (1, kept)):
            for n, k in enumerate(ids):
                spot = self.left.index(k)
                if len(groups) == 2:
                    cuts.append((0, spot, which, (n, slice(0, ra))))
                    cuts.append((1, spot, which, (n, slice(ra, ra + rb))))
                else:
                    cuts.append((0, spot, which, n))
        outs = [sds((len(kept), ra + rb) + groups[0][0].shape[2:], BF)] * 2
        send, keep = add_pieces(groups, cuts, outs, self.name + "_half")
        self.left = kept
        self.state = [keep, grid.send_z(send, self.bit)]
        return keep, send

    def finish(self, gate, cuts, outs, **extra):
        if self.bit:
            cuts = [((0, rows), which, place) for rows, which, place in cuts]
        cuts = [(0, rows, which, place) for rows, which, place in cuts]
        return add_pieces([after(self.state, gate)], cuts, outs, self.name + "_sum", **extra)


def join_kernel(pieces):
    groups, cuts, outs = [], [], []
    for which, part in enumerate(pieces):
        lead = part[0].shape[0]
        for k, value in enumerate(part):
            cuts.append((len(groups), slice(None), which, slice(k * lead, (k + 1) * lead)))
            groups.append([value])
        outs.append(sds((lead * len(part),) + part[0].shape[1:], BF))
    return add_pieces(groups, cuts, outs, "join")


def xor_blocks(value, mask, axis):
    count = value.shape[axis]
    bit = 1
    while bit < count:
        shape = value.shape
        split = value.reshape(shape[:axis] + (count // (2 * bit), 2, bit) + shape[axis + 1 :])
        turned = jnp.flip(split, axis=axis + 1).reshape(shape)
        value = jnp.where(jnp.bitwise_and(mask, bit) != 0, turned, value)
        bit *= 2
    return value


def pad_cols(value, width):
    return jnp.pad(value, ((0, 0), (0, width - value.shape[1])))


def per_device(
    tokens,
    cotangent,
    image_mask,
    norm_gains,
    norm_shifts,
    w_qkv,
    b_qv,
    w_out,
    w_up,
    up_bias,
    w_down,
    *,
    dp,
    tx,
):
    grid = Grid3(dp, tx)
    y_n, z_n = grid.y, grid.z
    core = lax.axis_index("core").astype(jnp.int32)
    me_d = lax.axis_index("dp").astype(jnp.int32)
    me_x = lax.axis_index("tx").astype(jnp.int32)
    seq, width = tokens.shape
    _, bd, hw = w_qkv.shape
    fw = w_up.shape[1]
    ext, hid = tx * hw, tx * fw
    hh, fh = hw // 2, fw // 2
    aligned = bd % 128 == 0 and hh % 128 == 0 and fh % 128 == 0
    rel = [kz * y_n + ky for ky in range(y_n) for kz in range(z_n)]

    def from_abs(value, axis):
        shape = value.shape
        value = value.reshape(shape[:axis] + (z_n, y_n) + shape[axis + 1 :])
        return jnp.swapaxes(value, axis, axis + 1).reshape(shape)

    def to_rel(value, axis):
        shape = value.shape
        value = value.reshape(shape[:axis] + (y_n, z_n) + shape[axis + 1 :])
        return jnp.swapaxes(value, axis, axis + 1).reshape(shape)

    ids = jnp.stack([core, me_d] + [jnp.bitwise_xor(me_d, k) for k in rel])
    keep = lax.dynamic_slice(image_mask, (2 * me_x,), (2,)).astype(F32)

    lane = max(bd, hh)
    small = jnp.concatenate(
        [
            pad_cols(norm_gains, lane),
            pad_cols(norm_shifts, lane),
            pad_cols(b_qv, lane),
            pad_cols(up_bias[None], lane),
            jnp.zeros((7, lane), BF),
        ]
    )
    qkv_a = pad_cols(w_qkv[:, :, :hh].reshape(3 * bd, hh), lane)
    qkv_b = pad_cols(w_qkv[:, :, hh:].reshape(3 * bd, hh), lane)
    first_a = jnp.concatenate([qkv_a, pad_cols(w_out[:hh], lane), small])
    first_b = jnp.concatenate([qkv_b, pad_cols(w_out[hh:], lane)])
    own = [tokens, cotangent]
    other = [swap_core(value) for value in own]
    if aligned:
        tok, cot = arrange_pair(ids, own, other, dp)
    else:

        def arrange(own, other):
            pair = jnp.where(core == 0, jnp.stack([own, other]), jnp.stack([other, own]))
            pair = xor_blocks(pair.reshape(2, seq, dp, bd), me_d, 2)
            return from_abs(pair, 2).reshape(2, seq, width)

        tok, cot = [arrange(own[i], other[i]) for i in range(2)]
    c1_z = gather_z(grid, first_a, first_b, gate=tok)
    c1_h = gather_first(grid, *c1_z)
    c1_h = join(c1_h)
    c1a, c1b = gather_last(grid, *c1_h)
    up_halves = after((w_up[:, :fh], w_up[:, fh:]), c1_h)
    row0 = 3 * bd + hh
    if aligned and 128 % (hw // dp) == 0 and (fw // dp) % 128 == 0:
        c1a, c1b = after((c1a, c1b), (c1a, c1b))
        nv, bq, bu = vectors(ids, c1a, row0, dp, y_n, bd, hw // dp, fw // dp)
    else:
        nv = c1a[0][:, row0 : row0 + 6, :bd].transpose(1, 0, 2).reshape(6, width).astype(F32)
        tail = jnp.stack([v[:, row0 + 6 : row0 + 9] for v in c1a])
        tail = xor_blocks(to_rel(tail, 1), me_d, 1)
        bq = tail[:, :, :2, : hw // dp].transpose(2, 0, 1, 3).reshape(2, ext).astype(F32)
        bu = tail[:, :, 2, : fw // dp].reshape(1, hid).astype(F32)
    grad_top = cot * keep.astype(BF)[:, None, None]

    up_z = gather_z(grid, *up_halves, gate=nv)
    up_h = gather_first(grid, *up_z)
    dn_halves = after((w_down[:fh], w_down[fh:]), up_z)

    if aligned:
        every, wq_plan, wo_plan, up_plan, dn_plan = slice(None), [[], [], []], [], [], []
        for kx in range(tx):
            halves = [slice(kx * hw, kx * hw + hh), slice(kx * hw + hh, (kx + 1) * hw)]
            f_halves = [slice(kx * fw, kx * fw + fh), slice(kx * fw + fh, (kx + 1) * fw)]
            own = slice(kx * z_n, (kx + 1) * z_n)
            for i in range(3):
                src = slice(i * bd, (i + 1) * bd)
                wq_plan[i].append((kx, (every, src), (i, every, every, halves[0])))
                for ky in range(y_n):
                    dst = (i, slice(ky * z_n, (ky + 1) * z_n), every, halves[1])
                    wq_plan[i].append((tx + ky, (own, src), dst))
            src = slice(3 * bd, 3 * bd + hh)
            dn_plan += [[], []]
            for ky in range(y_n):
                for kz in range(z_n):
                    p, r = ky * z_n + kz, kx * z_n + kz
                    cols = slice(p * bd, (p + 1) * bd)
                    wo_plan.append((kx, (p, src), (halves[0], cols)))
                    wo_plan.append((tx + ky, (r, src), (halves[1], cols)))
                    dn_plan[-2].append((kx, (p,), (f_halves[0], cols)))
                    dn_plan[-1].append((tx + ky, (r,), (f_halves[1], cols)))
            up_plan += [[(kx, (every,), (every, f_halves[0]))], []]
            for ky in range(y_n):
                rows = slice(kx * z_n * bd, (kx + 1) * z_n * bd)
                dst = (slice(ky * z_n * bd, (ky + 1) * z_n * bd), f_halves[1])
                up_plan[-1].append((tx + ky, (rows,), dst))
        c1 = c1a + c1b
        wqkv = (c1, wq_plan, (3, dp, bd, ext))
        wout = (c1, [wo_plan], (ext, width))
    else:

        def whole(a_all, b_all):
            a = jnp.stack(a_all)
            b = jnp.stack(b_all).reshape((y_n, tx, z_n) + b_all[0].shape[1:])
            b = b.transpose(1, 0, 2, 3, 4).reshape(a.shape[:2] + b.shape[3:])
            return jnp.stack([a, b], axis=1)

        c1 = whole([v[:, :row0] for v in c1a], c1b)
        qkv = c1[:, :, :, : 3 * bd, :hh].reshape(tx, 2, dp, 3, bd, hh)
        qkv = qkv.transpose(3, 2, 4, 0, 1, 5).reshape(3, dp, bd, ext)
        out = c1[:, :, :, 3 * bd :, :bd].transpose(0, 1, 3, 2, 4).reshape(ext, width)
        all_of = [[(0, (slice(None),), (slice(None),))]]
        wqkv = ([qkv], all_of, qkv.shape)
        wout = ([out], all_of, out.shape)

    rows2 = 2 * seq

    res = attn_forward(0, after(tok, up_z), nv, bq, wqkv, wout, None)
    part0 = res[5]
    up_h = join(after(up_h, part0))
    upa, upb = gather_last(grid, *up_h)
    dn_halves = after(dn_halves, up_h)
    res = attn_forward(1, after(tok, up_h), nv, bq, wqkv, wout, res[:5])
    recv0 = swap_core(after(part0, res[5]))
    parts = [(part0, recv0), (res[5], swap_core(res[5]))]
    first, q, k, v, att = res[:5]
    upa, upb = after((upa, upb), res[5])
    dn_z = gather_z(grid, *dn_halves, gate=(upa, upb))
    dn_h = gather_first(grid, *dn_z)
    if aligned:
        wup = ([v.reshape(-1, fh) for v in upa + upb], up_plan, (width, hid))
    else:
        up_w = whole(upa, upb).transpose(2, 3, 0, 1, 4).reshape(width, hid)
        wup = ([up_w], all_of, up_w.shape)
    part, recv = parts[0]
    state = mlp_up(0, tok, part, recv, keep, nv, bu, wup, fh, None)
    dna, dnb = gather_last(grid, *join_kernel(after(dn_h, state[1])))
    part, recv = parts[1]
    state = mlp_up(1, tok, part, recv, keep, nv, bu, wup, fh, state)
    if aligned:
        wdown = (dna + dnb, dn_plan, (hid, width))
    else:
        down_w = whole(dna, dnb).transpose(0, 1, 3, 2, 4).reshape(hid, width)
        wdown = ([down_w], all_of, down_w.shape)
    middle, second, act, dact = state
    flat = lambda value: value.reshape(rows2, value.shape[2])
    act2, sec2, grad2 = flat(act), flat(second), flat(grad_top)

    full = slice(None)
    a_spots = [(p, slice(p * bd, (p + 1) * bd)) for p in range(dp)]

    def by_left(l_index, r_index, size, row0):
        tasks, rows = [], slice(row0, row0 + size // 2)
        halves = slice(0, size // 2), slice(size // 2, size)
        for kx in range(tx):
            stores = [(kx, (p, rows), halves[0], cols) for p, cols in a_spots]
            for p, cols in a_spots:
                ky, kz = p // z_n, p % z_n
                stores.append((tx + ky, (kx * z_n + kz, rows), halves[1], cols))
            tasks.append((l_index, slice(kx * size, (kx + 1) * size), r_index, slice(0, width), stores))
        return tasks

    def by_right(l_index, r_index, size, row0, lanes, spare=False, first=0):
        tasks, each = [], size // 2 // lanes
        for kx in range(tx):
            stores = []
            for j in range(each):
                rows = slice(row0 + j * bd, row0 + (j + 1) * bd)
                cols = [slice((h * each + j) * lanes, (h * each + j + 1) * lanes) for h in range(2)]
                rows = (rows, slice(0, lanes)) if spare else (rows,)
                for p, r_sl in a_spots:
                    ky, kz = p // z_n, p % z_n
                    stores.append((kx, (p,) + rows, r_sl, cols[0]))
                    stores.append((tx + ky, (kx * z_n + kz,) + rows, r_sl, cols[1]))
            cols = slice(first + kx * size, first + (kx + 1) * size)
            tasks.append((l_index, slice(0, width), r_index, cols, stores))
        return tasks

    def pieces(rows, lanes):
        return [(dp, rows, lanes)] * tx + [(tx * z_n, rows, lanes)] * y_n

    def send_grad(parts, name):
        return Scatter(grid, list(parts[:tx]), list(parts[tx:]), name)

    grads = weight_grad([act2], [grad2], by_left(0, 0, fw, 0), pieces(fh, bd), "down_grad", 0, fh)
    down_rs = send_grad(grads, "down")
    grad_in = after(grad2, grads[-1])
    low_pre, bias_up, two_part, mlp_part = mlp_back(grad_in, act2, flat(dact), wdown, wup, fh)
    mlp_part = mlp_part.reshape(2, seq, width)
    two_recv = swap_core(two_part)
    down_half = down_rs.second(bias_up)
    up_rows = fh // bd * bd
    sec_in = after(sec2, down_half)
    tasks = by_right(0, 0, fw, 0, bd)
    grads = weight_grad([sec_in], [low_pre], tasks, pieces(up_rows, bd), "up_grad", 0, up_rows)
    up_rs = send_grad(grads, "up")
    gmid, gattn, grad_att, col = middle_back(
        ids, middle, two_part, after(two_recv, grads[-1]), cot, keep, nv, wout
    )
    down_zs = down_rs.along_z(col)
    row0 = 3 * bd
    last_shapes = pieces(row0 + hh, bd)
    att_in = after(flat(att), down_zs)
    tasks = by_left(0, 0, hw, 0)
    out_grads = weight_grad(
        [att_in], [flat(gattn)], tasks, last_shapes, "out_grad", row0, row0 + hh
    )

    n_pairs = ext // 128
    split = hh == 128 and bd == 128 and n_pairs >= 4
    if split:
        heads = [[1], list(range(2, n_pairs))]
        first_in = after(grad_att, out_grads[-1])
        left_0, bias_0 = attn_backward(heads[0], first_in, q, k, v, "attn_first")
        up_half = up_rs.second(bias_0)
    else:
        heads = [list(range(n_pairs))]
        up_half = up_rs.second(out_grads[-1])
    left_a, bias_a = attn_backward(heads[-1], after(grad_att, up_half), q, k, v)
    first_in = flat(first)
    gate = bias_a
    if not split:
        grad_down = down_rs.finish(bias_a, [(full, 0, full)], [sds((fw, bd), F32)])[0]
        mlp_recv = swap_core(after(mlp_part, bias_a))
        gate = up_rs.halve(grad_down) if z_n > 1 else grad_down
    if split:
        stores, count = [], n_pairs - 1
        for i in range(3):
            rows = slice(i * bd, (i + 1) * bd)
            for n, pair in enumerate(range(1, n_pairs)):
                kx, cols = pair // 2, slice((i * count + n) * 128, (i * count + n + 1) * 128)
                for p, r_sl in a_spots:
                    ky, kz = p // z_n, p % z_n
                    spot = (kx - 1, (p, rows))
                    if pair % 2:
                        spot = (tx - 1 + ky, (kx * z_n + kz, rows))
                    stores.append(spot + (r_sl, cols))
        tasks = [(0, slice(0, width), 0, slice(0, 384 * count), stores)]
        sent = weight_grad(
            [first_in], [left_0, left_a], tasks, last_shapes[1:], "qkv_grad", 0, row0, out_grads[1:]
        )
        leaving = (sent[: tx - 1], sent[tx:])
        grad_down = down_rs.finish(sent[-1], [(full, 0, full)], [sds((fw, bd), F32)])[0]
        mlp_recv = swap_core(after(mlp_part, bias_a))
        gate = up_rs.halve((grad_down, leaving)) if z_n > 1 else grad_down
        left_b, bias_b = attn_backward([0], after(grad_att, (leaving, gate)), q, k, v)
        gate = (bias_b, mlp_recv)
        stores = []
        for i in range(3):
            rows, cols = slice(i * bd, (i + 1) * bd), slice(i * 128, (i + 1) * 128)
            stores += [(0, (p, rows), r_sl, cols) for p, r_sl in a_spots]
        tasks = [(0, slice(0, width), 0, slice(0, 384), stores)]
        kept = weight_grad(
            [after(first_in, gate)],
            [left_b],
            tasks,
            last_shapes[:1],
            "qkv_keep",
            0,
            row0,
            out_grads[:1],
        )
        grads = list(kept) + list(sent)
        lefts, starts = [left_0, left_a, left_b], [1, 2, 0]
        pair_sums = [bias_b, bias_0, bias_a]
        gate = kept[0]
    else:
        while 2 * up_rs.bit < z_n:
            gate = up_rs.halve((gate, mlp_recv))
        makers = [by_right(0, 0, hw, i * bd, hh, hh < bd, i * ext) for i in range(3)]
        tasks = [task for maker in makers for task in maker]
        grads = weight_grad(
            [after(first_in, gate)],
            [left_a],
            tasks,
            last_shapes,
            "qkv_grad",
            0,
            row0,
            out_grads,
            hh < bd,
        )
        lefts, starts = [left_a], [0]
        pair_sums = [bias_a]
        gate = grads[-1]
    qkv_rs = send_grad(grads, "qkv")
    lefts = after(lefts, gate)
    one_part = input_grad(lefts, starts, wqkv, width)
    one_recv = swap_core(one_part)
    cuts = []
    for h in range(2):
        for j in range(fh // bd):
            rows = slice(h * up_rows + j * bd, h * up_rows + (j + 1) * bd)
            cuts.append((rows, 0, (full, slice(h * fh + j * bd, h * fh + (j + 1) * bd))))
    up_cuts = cuts
    gate = one_part
    while 2 * up_rs.bit < z_n:
        gate = up_rs.halve(gate)
    qkv_half = qkv_rs.second(gate)
    wide = max(bd, hw // dp, fw // dp)
    if split and fw // dp == bd and 128 % (hw // dp) == 0:
        rest = sds((tx * y_n, z_n, 16, wide), F32)
        sums = [col, bias_up] + pair_sums
    else:
        bias_qv = jnp.concatenate(pair_sums)
        bias_qv = jnp.sum(bias_qv.reshape(n_pairs, 2, 2, 128), axis=1).transpose(1, 0, 2)
        vec = jnp.concatenate([jnp.zeros((2, width), F32), col])
        vec = vec.reshape(6, y_n, z_n, bd).transpose(1, 2, 0, 3)
        bias_qv = bias_qv.reshape(2, tx, dp, hw // dp).transpose(2, 1, 0, 3)
        bias_up = bias_up.reshape(tx, 1, dp, fw // dp).transpose(2, 0, 1, 3)
        bias = jnp.concatenate(
            [
                jnp.pad(value, ((0, 0), (0, 0), (0, 0), (0, wide - value.shape[3])))
                for value in (bias_qv, bias_up)
            ],
            axis=2,
        )
        bias = from_abs(xor_blocks(bias, me_d, 0), 0).reshape(y_n, z_n, tx, 3, wide)
        bias = bias.transpose(2, 0, 1, 3, 4)
        vec = jnp.pad(vec, ((0, 0), (0, 0), (0, 0), (0, wide - bd)))
        vec = jnp.broadcast_to(vec, (tx,) + vec.shape)
        rest = jnp.concatenate([vec, bias, jnp.zeros((tx, y_n, z_n, 7, wide), F32)], axis=3)
        rest = rest.reshape(tx * y_n, z_n, 16, wide)
        sums = None
    grad_tokens, one_sums, *small = finish_tokens(
        ids, nv, tok, one_part, after(one_recv, qkv_half), gmid, rest, sums, dp, aligned
    )
    if not aligned:
        ones = jnp.pad(one_sums.reshape(2, y_n, z_n, bd), ((0, 14), (0, 0), (0, 0), (0, wide - bd)))
        ones = ones.transpose(1, 2, 0, 3)
        small = [value + ones[n % y_n] for n, value in enumerate(small)]
    grad_up = up_rs.finish(small[0], up_cuts, [sds((bd, fw), F32)])[0]
    small = after(small, grad_up)
    got = small[:1]
    for n in range(1, tx * y_n):
        got.append(grid.send_xy(small[n], n // y_n, n % y_n))
    cuts, outs = [], [sds((3, bd, hw), F32), sds((hw, bd), F32)]
    last_rows = row0 + hh
    for h in range(2):
        for i in range(3):
            rows = slice(h * last_rows + i * bd, h * last_rows + (i + 1) * bd)
            rows = (rows, slice(0, hh)) if hh < bd else rows
            cuts.append((rows, 0, (i, full, slice(h * hh, (h + 1) * hh))))
        rows = slice(h * last_rows + row0, (h + 1) * last_rows)
        cuts.append((rows, 1, (slice(h * hh, (h + 1) * hh),)))
    if wide == bd:
        qkv_zs = qkv_rs.along_z(grad_up, got)
        cuts.append((slice(2 * last_rows, 2 * last_rows + 16), 2, full))
        outs.append(sds((16, wide), F32))
    else:
        qkv_zs = qkv_rs.along_z(grad_up)
    layer_out = finish_layer(
        ids, keep, nv, middle, after(mlp_part, qkv_zs), mlp_recv, dp, aligned
    )
    share, own = bd // (2 * tx), None
    if wide == bd == 128 and fw // dp == bd:
        qv = hw // dp

        def fill(small, out_s, more_s):
            rows = out_s[2][...]
            turned = pltpu.roll(rows, (128 - small[0][0]) % 128, 1)
            more_s[0][0:1, :] = turned[0:1, :share]
            more_s[0][1:2, :] = turned[2:3, :share]
            more_s[1][0:1, :] = turned[1:2, :share]
            more_s[1][1:4, :] = turned[3:6, :share]
            more_s[2][...] = rows[6:8, :qv]
            more_s[3][...] = rows[8:9, :]

        shapes = [(2, share), (4, share), (2, qv), (1, bd)]
        place = ((2 * me_x + core) * share)[None]
        more = [sds(shape, F32) for shape in shapes]
        res = qkv_rs.finish(layer_out, cuts, outs, smem=(place,), more=more, fill=fill)
        own = res[3:]
    else:
        res = qkv_rs.finish(layer_out, cuts, outs)
    grad_qkv, grad_out = res[:2]
    if wide == bd:
        both = res[2]
    else:
        both, bit = sum(got), 1
        while bit < z_n:
            both = both.reshape((-1, 2) + both.shape[1:])
            both = both[:, 0] + grid.send_z(both[:, 1], bit)
            bit *= 2
        both = both[0]
    if not aligned:

        def restore(value):
            value = xor_blocks(to_rel(value.reshape(seq, dp, bd), 1), me_d, 1)
            return value.reshape(seq, width)

        layer_out, grad_tokens = restore(layer_out), restore(grad_tokens)

    if own is None:
        mine = lax.dynamic_slice(both[:6, :bd], (0, (2 * me_x + core) * share), (6, share))
        own = [
            mine[0:3:2],
            jnp.concatenate([mine[1:2], mine[3:6]]),
            both[6:8, : hw // dp],
            both[8:9, : fw // dp],
        ]
    return (
        layer_out,
        grad_tokens,
        own[0],
        own[1],
        grad_qkv,
        own[2],
        grad_out,
        grad_up,
        own[3].reshape(fw // dp),
        grad_down,
    )


def solution(mesh):
    dp, tensor = mesh.shape["dp"], mesh.shape["tensor"]
    split = Mesh(mesh.devices.reshape(dp, tensor // 2, 2), ("dp", "tx", "core"))
    every = ("dp", "tx", "core")
    tensor_axes = ("tx", "core")
    in_specs = (
        P(every, None),
        P(every, None),
        P("dp"),
        P(None, "dp"),
        P(None, "dp"),
        P(None, "dp", tensor_axes),
        P(None, ("tx", "core", "dp")),
        P(tensor_axes, "dp"),
        P("dp", tensor_axes),
        P(("tx", "core", "dp")),
        P(tensor_axes, "dp"),
    )
    out_specs = (
        P(every, None),
        P(every, None),
        P(None, every),
        P(None, every),
        P(None, "dp", tensor_axes),
        P(None, ("tx", "core", "dp")),
        P(tensor_axes, "dp"),
        P("dp", tensor_axes),
        P(("tx", "core", "dp")),
        P(tensor_axes, "dp"),
    )
    return jax.shard_map(
        functools.partial(per_device, dp=dp, tx=tensor // 2),
        mesh=split,
        in_specs=in_specs,
        out_specs=out_specs,
        check_vma=False,
    )
```

```python
import functools

import jax
import jax.numpy as jnp
from jax import lax
from jax.experimental import pallas as pl
from jax.experimental.pallas import tpu as pltpu
from jax.sharding import Mesh, PartitionSpec as P

HEAD_DIM = 64
VALID = 577
SEQ = 584
BF = jnp.bfloat16
F32 = jnp.float32
VMEM_LIMIT = 60 * 1024 * 1024
WHOLE_VMEM = ("arrange_pair", "vectors", "mlp_up", "down_grad", "mlp_back", "qkv_sum")
COST_SCALE = 1.0
COST = {
    "arrange_pair": 5,
    "vectors": 3,
    "attn_forward": 16,
    "mlp_up": 10,
    "down_grad": 11,
    "mlp_back": 22,
    "up_grad": 11,
    "middle_back": 0,
    "out_grad": 8,
    "attn_backward": 18,
    "attn_first": 0,
    "qkv_grad": 7,
    "qkv_keep": 0,
    "up_half": 0,
    "join": 0,
    "grad_one": 0,
    "qkv_add": 30,
    "finish_layer": 0,
    "up_sum": 0,
    "finish_tokens": 9,
}
NT = (((1,), (1,)), ((), ()))
TN = (((0,), (0,)), ((), ()))
NN = (((1,), (0,)), ((), ()))


def dot(left, right, dims):
    return lax.dot_general(left, right, dims, preferred_element_type=F32)


class Loads:
    def __init__(self, sems):
        self.sems, self.groups = sems, []

    def start(self, pairs):
        sem = self.sems.at[len(self.groups)]
        copies = [pltpu.make_async_copy(src, dst, sem) for src, dst in pairs]
        for copy in copies:
            copy.start()
        self.groups.append(copies)
        return len(self.groups) - 1

    def wait(self, group):
        for copy in self.groups[group]:
            copy.wait()


def padded_bytes(value):
    lead, (rows, lanes) = value.shape[:-2], value.shape[-2:]
    count = -(-rows // 16) * 16 * (-(-lanes // 128) * 128)
    for size in lead:
        count *= size
    return count * jnp.dtype(value.dtype).itemsize


def call(body, ins, outs, scratch, name, flops, aliases=None, smem=(), sems=48, vmem_ins=(), spare=12, pinned=False):
    n_smem, n_vmem, n_in, n_out = len(smem), len(vmem_ins), len(ins), len(outs)
    moved = sum(a.size * a.dtype.itemsize for a in ins) + sum(
        o.size * o.dtype.itemsize for o in outs
    )

    def kernel(*refs):
        first = n_smem + n_vmem
        small = refs[:first]
        in_refs = refs[first : first + n_in]
        out_refs = refs[first + n_in : first + n_in + n_out]
        rest = refs[first + n_in + n_out :]
        body(small, in_refs, out_refs, rest[:-1], Loads(rest[-1]))

    held = sum(padded_bytes(piece) for piece in scratch) + spare * 1024 * 1024
    vmem = VMEM_LIMIT if name in WHOLE_VMEM else min(held, VMEM_LIMIT)
    flops = max(COST.get(name, 3), 0.02) * COST_SCALE * 1.15e9
    moved = 0
    any_spec = pl.BlockSpec(memory_space=pl.ANY)
    hbm_spec = pl.BlockSpec(memory_space=pltpu.HBM) if pinned else any_spec
    return pl.pallas_call(
        kernel,
        out_shape=outs,
        in_specs=[pl.BlockSpec(memory_space=pltpu.SMEM)] * n_smem
        + [pl.BlockSpec(memory_space=pltpu.VMEM)] * n_vmem
        + [hbm_spec if i in (aliases or {}) else any_spec for i in range(n_in)],
        out_specs=[hbm_spec if pinned else any_spec] * n_out,
        scratch_shapes=list(scratch) + [pltpu.SemaphoreType.DMA((sems,))],
        input_output_aliases={n_smem + n_vmem + i: o for i, o in (aliases or {}).items()},
        compiler_params=pltpu.CompilerParams(vmem_limit_bytes=vmem),
        cost_estimate=pl.CostEstimate(flops=int(flops), bytes_accessed=int(flops // 1000), transcendentals=0),
        name=name,
    )(*smem, *vmem_ins, *ins)


def norm_parts(rows):
    center = rows - jnp.mean(rows, axis=1, keepdims=True)
    inverse = lax.rsqrt(jnp.mean(center * center, axis=1, keepdims=True) + 1e-05)
    return center * inverse, inverse


def norm_back(grad_norm, scaled, inverse, gain_row):
    grad_hat = grad_norm * gain_row
    first_mean = jnp.mean(grad_hat, axis=1, keepdims=True)
    second_mean = jnp.mean(grad_hat * scaled, axis=1, keepdims=True)
    return inverse * (grad_hat - first_mean - scaled * second_mean)


def sds(shape, dtype):
    return jax.ShapeDtypeStruct(shape, dtype)


def arrange_pair(ids, keep, own, other, nd):
    n = len(own)
    rows, width = own[0].shape
    bd = width // nd

    def body(small, ins, outs, scratch, loads):
        ids_ref, keep_ref = small
        mine = ids_ref[0]
        in_s, out_s, kept_s = scratch[: 2 * n], scratch[2 * n : 4 * n], scratch[4 * n :]
        groups = [loads.start([(ins[i], in_s[i])]) for i in range(2 * n)]
        done = []
        for i in range(2 * n):
            loads.wait(groups[i])
            for p in range(nd):
                src = pl.ds(pl.multiple_of(ids_ref[2 + p] * bd, 128), bd)
                out_s[i][:, p * bd : (p + 1) * bd] = in_s[i][:, src]
            spot = mine if i < n else 1 - mine
            done.append(loads.start([(out_s[i], outs[i % n].at[spot])]))
            if i % n == n - 1:
                kept = kept_s[i // n]
                kept[...] = (out_s[i][...].astype(F32) * keep_ref[spot]).astype(BF)
                done.append(loads.start([(kept, outs[n].at[spot])]))
        for group in done:
            loads.wait(group)

    return call(
        body,
        list(own) + list(other),
        [sds((2, rows, width), BF)] * (n + 1),
        [pltpu.VMEM((rows, width), BF)] * (4 * n + 2),
        "arrange_pair",
        0,
        smem=(ids, keep),
    )


def vectors(ids, gathered, row0, nd, y_n, bd, qv, up):
    tx, z_n = len(gathered), nd // y_n

    def body(small, ins, outs, scratch, loads):
        ids_ref, rows_s, nv_s, bq_s, bu_s = small[0], *scratch
        rows = pl.ds(row0, 16)
        loads.wait(loads.start([(ins[k].at[:, rows, :], rows_s.at[k]) for k in range(tx)]))
        for p in range(nd):
            nv_s[:, p * bd : (p + 1) * bd] = rows_s[0, p].astype(F32)[:6, :bd]
        for k in range(tx):
            pieces = []
            for d in range(nd):
                rel = ids_ref[1] ^ d
                spot = (rel % y_n) * z_n + rel // y_n
                piece = rows_s[k, spot].astype(F32)
                bu_s[:, (k * nd + d) * up : (k * nd + d + 1) * up] = piece[8:9, :up]
                pieces.append(piece[6:8, :])
            each = 128 // qv
            for start in range(0, nd, each):
                total = pieces[start]
                for i in range(1, each):
                    total = total + pltpu.roll(pieces[start + i], i * qv, 1)
                bq_s[:, (k * nd + start) * qv : (k * nd + start + each) * qv] = total
        loads.wait(loads.start([(nv_s, outs[0]), (bq_s, outs[1]), (bu_s, outs[2])]))

    shapes = [(6, nd * bd), (2, tx * nd * qv), (1, tx * nd * up)]
    return call(
        body,
        list(gathered),
        [sds(s, F32) for s in shapes],
        [pltpu.VMEM((tx, nd, 16, gathered[0].shape[2]), BF)] + [pltpu.VMEM(s, F32) for s in shapes],
        "vectors",
        0,
        smem=(ids,),
    )


def block_stores(ids_ref, src, dst, nd, aligned):
    if not aligned:
        return [(src, dst)]
    bd = src.shape[1] // nd
    pairs = []
    for p in range(nd):
        cols = pl.ds(pl.multiple_of(ids_ref[2 + p] * bd, 128), bd)
        pairs.append((src.at[:, p * bd : (p + 1) * bd], dst.at[:, cols]))
    return pairs


def weight_loads(loads, groups, refs, scratch):
    return [
        loads.start([(refs[a].at[src], scratch.at[dst]) for a, src, dst in plan])
        for plan in groups
    ]


def softmax_rows(q2, k2):
    scores = dot(q2, k2, NT)
    lane = lax.broadcasted_iota(jnp.int32, scores.shape, 1)
    scores = jnp.where(lane < VALID, scores, -1e30)
    e = jnp.exp(scores - jnp.max(scores, axis=1, keepdims=True))
    return e * (1.0 / jnp.sum(e, axis=1, keepdims=True))


def attn_forward(image, tok, nv, bq, wqkv, wout, prev):
    seq, width = tok.shape[1:]
    qkv_arrays, qkv_plan, qkv_scratch = wqkv
    out_arrays, out_plan, out_scratch = wout
    ext = qkv_scratch[-1]
    n_prev = 0 if prev is None else len(prev)
    nq, no = len(qkv_arrays), len(out_arrays)

    def body(small, ins, outs, scratch, loads):
        nv_ref, bq_ref = small
        tok_ref, ins = ins[0], ins[1 + n_prev :]
        w_s, wo_s, tok_s, first_s, q_s, k_s, v_s, att_s, part_s = scratch
        g_tok = loads.start([(tok_ref.at[image], tok_s)])
        g_w = weight_loads(loads, qkv_plan, ins[:nq], w_s)
        g_o = weight_loads(loads, out_plan, ins[nq:], wo_s)
        loads.wait(g_tok)
        hat, _ = norm_parts(tok_s[...].astype(F32))
        first_s[...] = (hat * nv_ref[0:1, :] + nv_ref[2:3, :]).astype(BF)
        g_first = loads.start([(first_s, outs[0].at[image])])
        low = first_s[...]
        for i, ref in enumerate((q_s, k_s, v_s)):
            if i < len(g_w):
                loads.wait(g_w[i])
            proj = dot(low, w_s[i].reshape(width, ext), NN)
            if i == 0:
                proj = proj + bq_ref[0:1, :]
            if i == 2:
                proj = proj + bq_ref[1:2, :]
            low_proj = proj.astype(BF)
            if i == 0:
                low_proj = low_proj * jnp.asarray(HEAD_DIM**-0.5, BF)
            ref[...] = low_proj
        g_qkv = loads.start(
            [(q_s, outs[1].at[image]), (k_s, outs[2].at[image]), (v_s, outs[3].at[image])]
        )
        half = lax.broadcasted_iota(jnp.int32, (1, 128), 1) // HEAD_DIM

        def pair(i, carry):
            cols = pl.ds(pl.multiple_of(i * 128, 128), 128)
            q2, k2, v2 = q_s[:, cols], k_s[:, cols], v_s[:, cols]
            total = None
            for h in range(2):
                keep = (half == h).astype(BF)
                probs = softmax_rows(q2, k2 * keep).astype(BF)
                piece = dot(probs, v2 * keep, NN)
                total = piece if total is None else total + piece
            att_s[:, cols] = total.astype(BF)
            return carry

        lax.fori_loop(0, ext // 128, pair, 0)
        g_att = loads.start([(att_s, outs[4].at[image])])
        loads.wait(g_o[0])
        part_s[...] = dot(att_s[...], wo_s[...], NN).astype(BF)
        g_part = loads.start([(part_s, outs[5])])
        for group in (g_first, g_qkv, g_att, g_part):
            loads.wait(group)

    shapes = [(2, seq, width)] + [(2, seq, ext)] * 4
    return call(
        body,
        [tok] + list(prev or []) + qkv_arrays + out_arrays,
        [sds(s, BF) for s in shapes] + [sds((seq, width), BF)],
        [
            pltpu.VMEM(qkv_scratch, BF),
            pltpu.VMEM(out_scratch, BF),
            pltpu.VMEM((seq, width), BF),
            pltpu.VMEM((seq, width), BF),
            pltpu.VMEM((seq, ext), BF),
            pltpu.VMEM((seq, ext), BF),
            pltpu.VMEM((seq, ext), BF),
            pltpu.VMEM((seq, ext), BF),
            pltpu.VMEM((seq, width), BF),
        ],
        "attn_forward",
        2 * seq * width * ext * 4 + 16 * seq * seq * ext,
        aliases={1 + i: i for i in range(n_prev)},
        pinned=True,
        vmem_ins=(nv, bq),
    )


def mlp_up(image, tok, part, recv, keep, nv, bu, wup, step, prev):
    seq, width = tok.shape[1:]
    up_arrays, up_plan, up_scratch = wup
    hid = up_scratch[-1]
    n_prev = 0 if prev is None else len(prev)

    def body(small, ins, outs, scratch, loads):
        keep_ref, nv_ref, bu_ref = small
        tok_ref, part_ref, recv_ref = ins[:3]
        w_s, tok_s, part_s, recv_s, mid_s, sec_s, act_s, dact_s = scratch
        g_in = loads.start([(tok_ref.at[image], tok_s), (part_ref, part_s), (recv_ref, recv_s)])
        g_w = weight_loads(loads, up_plan, ins[3 + n_prev :], w_s)
        loads.wait(g_in)
        total = part_s[...].astype(F32) + recv_s[...].astype(F32) + nv_ref[4:5, :]
        middle = tok_s[...].astype(F32) + keep_ref[image] * total
        mid_s[...] = middle
        hat, _ = norm_parts(middle)
        sec_s[...] = (hat * nv_ref[1:2, :] + nv_ref[3:4, :]).astype(BF)
        g_mid = loads.start([(mid_s, outs[0].at[image]), (sec_s, outs[1].at[image])])
        second = sec_s[...]
        done = []
        for block in range(hid // step):
            if block < len(g_w):
                loads.wait(g_w[block])
            cols = slice(block * step, (block + 1) * step)
            pre = dot(second, w_s[:, cols], NN) + bu_ref[0:1, cols]
            gate = 0.5 * jnp.tanh(0.851 * pre) + 0.5
            act_s[:, cols] = (pre * gate).astype(BF)
            dact_s[:, cols] = (gate + 1.702 * pre * gate * (1.0 - gate)).astype(BF)
            done.append(
                loads.start(
                    [
                        (act_s.at[:, cols], outs[2].at[image, :, cols]),
                        (dact_s.at[:, cols], outs[3].at[image, :, cols]),
                    ]
                )
            )
        for group in [g_mid] + done:
            loads.wait(group)

    outs = [
        sds((2, seq, width), F32),
        sds((2, seq, width), BF),
        sds((2, seq, hid), BF),
        sds((2, seq, hid), BF),
    ]
    return call(
        body,
        [tok, part, recv] + list(prev or []) + up_arrays,
        outs,
        [
            pltpu.VMEM(up_scratch, BF),
            pltpu.VMEM((seq, width), BF),
            pltpu.VMEM((seq, width), BF),
            pltpu.VMEM((seq, width), BF),
            pltpu.VMEM((seq, width), F32),
            pltpu.VMEM((seq, width), BF),
            pltpu.VMEM((seq, hid), BF),
            pltpu.VMEM((seq, hid), BF),
        ],
        "mlp_up",
        2 * seq * width * hid,
        aliases={3 + i: i for i in range(n_prev)},
        pinned=True,
        smem=(keep,),
        vmem_ins=(nv, bu),
    )


def column_loads(src, dst, start):
    if len(src.shape) == 2:
        return [(src, dst)]
    n, _, width = src.shape
    return [
        (src.at[i], dst.at[:, (start + i) * width : (start + i + 1) * width]) for i in range(n)
    ]


def weight_grad(lefts, rights, tasks, out_shapes, name, lo, hi, prev=None, fill=False):
    rows = lefts[0].shape[0]
    arrays = list(lefts) + list(rights)
    joined = all(len(a.shape) == 3 for a in rights)
    if joined:
        total = sum(a.shape[0] for a in rights) // 3
        wide = [a.shape[-1] for a in lefts] + [3 * total * rights[0].shape[-1]]
    else:
        wide = [a.shape[-1] for a in arrays]
    n_left, n_in = len(lefts), len(arrays)
    prev = list(prev or [])
    last = {}
    for n, task in enumerate(tasks):
        for store in task[4]:
            last[store[0]] = n

    def body(small, ins, outs, scratch, loads):
        in_s, out_s = scratch[: len(wide)], scratch[len(wide) :]
        order = []
        for l_index, _, r_index, _, _ in tasks:
            for i in (l_index, n_left + r_index):
                if i not in order:
                    order.append(i)
        groups = {}
        for i in order:
            pairs = [(ins[i], in_s[i])]
            if joined and i == n_left:
                pairs, start = [], 0
                for j, stack in enumerate(rights):
                    count = stack.shape[0] // 3
                    for kind in range(3):
                        part = ins[n_left + j].at[kind * count : (kind + 1) * count]
                        pairs += column_loads(part, in_s[i], kind * total + start)
                    start += count
            groups[i] = loads.start(pairs)
        for ref in out_s if fill else ():
            ref[...] = jnp.zeros_like(ref)
        ready, done = set(), []
        for n, (l_index, l_cols, r_index, r_cols, stores) in enumerate(tasks):
            for i in (l_index, n_left + r_index):
                if i not in ready:
                    loads.wait(groups[i])
                    ready.add(i)
            left, right = in_s[l_index][:, l_cols], in_s[n_left + r_index][:, r_cols]
            value = dot(left, right, TN).astype(BF)
            for which, spot, r_sl, c_sl in stores:
                out_s[which][spot] = value[r_sl, c_sl]
            for which in sorted(w for w in last if last[w] == n):
                done.append(loads.start([(out_s[which], outs[which].at[:, lo:hi])]))
        for group in done:
            loads.wait(group)

    flops = sum(
        2 * rows * (t[1].stop - t[1].start) * (t[3].stop - t[3].start) for t in tasks
    )
    return call(
        body,
        arrays + prev,
        [sds(s, BF) for s in out_shapes],
        [pltpu.VMEM((rows, w), BF) for w in wide]
        + [pltpu.VMEM((s[0], hi - lo, s[2]), BF) for s in out_shapes],
        name,
        flops,
        aliases={n_in + i: i for i in range(len(prev))},
    )


def mlp_back(grad, act, dact, wdown, wup, step):
    rows, width = grad.shape
    seq = rows // 2
    hid = dact.shape[1]
    down_arrays, down_plan, down_scratch = wdown
    up_arrays, up_plan, up_scratch = wup
    n_down = len(down_arrays)

    def body(small, ins, outs, scratch, loads):
        wd_s, wu_s, g_s, a_s, d_s, low_s, sum_s, two_s, mlp_s = scratch
        g_g = loads.start([(ins[0], g_s)])
        g_wd = weight_loads(loads, down_plan, ins[3 : 3 + n_down], wd_s)
        g_d = []
        for block in range(hid // step):
            cols = slice(block * step, (block + 1) * step)
            g_d.append(loads.start([(ins[2].at[:, cols], d_s.at[:, cols])]))
        g_wu = weight_loads(loads, up_plan, ins[3 + n_down :], wu_s)
        g_a = loads.start([(ins[1], a_s)])
        loads.wait(g_g)
        left = g_s[...]
        done = []
        for block in range(hid // step):
            if block < len(g_wd):
                loads.wait(g_wd[block])
            loads.wait(g_d[block])
            cols = slice(block * step, (block + 1) * step)
            pre = dot(left, wd_s[cols, :], NT) * d_s[:, cols].astype(F32)
            low_s[:, cols] = pre.astype(BF)
            sum_s[0:1, cols] = jnp.sum(pre, axis=0, keepdims=True)
            done.append(loads.start([(low_s.at[:, cols], outs[0].at[:, cols])]))
        done.append(loads.start([(sum_s, outs[1])]))
        for group in g_wu:
            loads.wait(group)
        two = dot(low_s[...], wu_s[...], NT)
        for a in range(2):
            two_s[a] = two[a * seq : (a + 1) * seq].astype(BF)
            done.append(loads.start([(two_s.at[a], outs[2].at[a])]))
        loads.wait(g_a)
        mlp_s[...] = dot(a_s[...], wd_s[...], NN).astype(BF)
        done.append(loads.start([(mlp_s, outs[3])]))
        for group in done:
            loads.wait(group)

    return call(
        body,
        [grad, act, dact] + down_arrays + up_arrays,
        [sds((rows, hid), BF), sds((1, hid), F32)]
        + [sds((2, seq, width), BF), sds((rows, width), BF)],
        [
            pltpu.VMEM(down_scratch, BF),
            pltpu.VMEM(up_scratch, BF),
            pltpu.VMEM((rows, width), BF),
            pltpu.VMEM((rows, hid), BF),
            pltpu.VMEM((rows, hid), BF),
            pltpu.VMEM((rows, hid), BF),
            pltpu.VMEM((1, hid), F32),
            pltpu.VMEM((2, seq, width), BF),
            pltpu.VMEM((rows, width), BF),
        ],
        "mlp_back",
        6 * rows * width * hid,
        sems=64,
    )


def input_grad(stacks, starts, weight, width):
    arrays, plan, shape = weight
    n, ext = shape[0], shape[-1]
    rows = stacks[0].shape[1]
    seq, m = rows // 2, len(stacks)

    def body(small, ins, outs, scratch, loads):
        w_s, out_s = scratch[0], scratch[1]
        l_s = scratch[2:]
        g_w = weight_loads(loads, plan[:1], ins[m:], w_s)
        g_l = []
        for i in range(n):
            pairs = []
            for j in range(m):
                count = stacks[j].shape[0] // n
                pairs += column_loads(ins[j].at[i * count : (i + 1) * count], l_s[i], starts[j])
            g_l.append(loads.start(pairs))
        g_w += weight_loads(loads, plan[1:], ins[m:], w_s)
        total = None
        for i in range(n):
            loads.wait(g_l[i])
            if i < len(g_w):
                loads.wait(g_w[i])
            piece = dot(l_s[i][...], w_s[i].reshape(width, ext), NT)
            total = piece if total is None else total + piece
        done = []
        for a in range(2):
            out_s[a] = total[a * seq : (a + 1) * seq].astype(BF)
            done.append(loads.start([(out_s.at[a], outs[0].at[a])]))
        for group in done:
            loads.wait(group)

    return call(
        body,
        list(stacks) + arrays,
        [sds((2, seq, width), BF)],
        [pltpu.VMEM(shape, BF), pltpu.VMEM((2, seq, width), BF)] + [pltpu.VMEM((rows, ext), BF)] * n,
        "grad_one",
        2 * rows * width * ext * n,
    )[0]


def middle_back(ids, middle, part, recv, cot, keep, nv, wout):
    _, seq, width = middle.shape
    out_arrays, out_plan, out_scratch = wout
    ext = out_scratch[0]

    def body(small, ins, outs, scratch, loads):
        ids_ref, keep_ref, nv_ref = small
        mine = ids_ref[0]
        wo_s, mid_s, part_s, recv_s, cot_s, gmid_s, gat_s, do_s = scratch[:8]
        cs_s = scratch[8]
        g_in = [
            loads.start(
                [
                    (ins[0].at[a], mid_s.at[a]),
                    (ins[1].at[a], cot_s.at[a]),
                    (ins[2].at[a], part_s.at[a]),
                    (ins[3].at[a], recv_s.at[a]),
                ]
            )
            for a in range(2)
        ]
        g_o = weight_loads(loads, out_plan, ins[4:], wo_s)
        done = []
        for a in range(2):
            loads.wait(g_in[a])
            keep_here = keep_ref[a]
            hat, inverse = norm_parts(mid_s[a])
            grad_two = part_s[a].astype(F32) + recv_s[a].astype(F32)
            top = cot_s[a].astype(F32)
            grad_mid = top + norm_back(grad_two, hat, inverse, nv_ref[1:2, :])
            grad_attn = grad_mid * keep_here
            sums = [
                jnp.sum(grad_two * hat, axis=0, keepdims=True),
                jnp.sum(grad_two, axis=0, keepdims=True),
                jnp.sum(grad_attn, axis=0, keepdims=True),
                jnp.sum(top, axis=0, keepdims=True) * keep_here,
            ]
            for i, value in enumerate(sums):
                cs_s[i : i + 1, :] = value if a == 0 else cs_s[i : i + 1, :] + value
            gmid_s[a] = grad_mid
            gat_s[a] = grad_attn.astype(BF)
            done.append(loads.start([(gat_s.at[a], outs[1].at[a])]))
            if a == 0:
                loads.wait(g_o[0])
            do_s[a] = dot(gat_s[a], wo_s[...], NT).astype(BF)
            done.append(loads.start([(do_s.at[a], outs[2].at[a])]))
        done.append(loads.start([(gmid_s.at[mine], outs[0]), (cs_s, outs[3])]))
        for group in done:
            loads.wait(group)

    return call(
        body,
        [middle, cot, part, recv] + out_arrays,
        [
            sds((seq, width), F32),
            sds((2, seq, width), BF),
            sds((2, seq, ext), BF),
            sds((4, width), F32),
        ],
        [
            pltpu.VMEM(out_scratch, BF),
            pltpu.VMEM((2, seq, width), F32),
            pltpu.VMEM((2, seq, width), BF),
            pltpu.VMEM((2, seq, width), BF),
            pltpu.VMEM((2, seq, width), BF),
            pltpu.VMEM((2, seq, width), F32),
            pltpu.VMEM((2, seq, width), BF),
            pltpu.VMEM((2, seq, ext), BF),
            pltpu.VMEM((4, width), F32),
        ],
        "middle_back",
        4 * seq * width * ext,
        smem=(ids, keep),
        vmem_ins=(nv,),
    )


def attn_backward(pairs, grad, q, k, v, name="attn_backward"):
    _, seq, _ = q.shape
    n = len(pairs)

    def body(small, ins, outs, scratch, loads):
        q_s, k_s, v_s, do_s, dq_s, dk_s, dv_s, bs_s = scratch
        groups = []
        for u in range(2 * n):
            cols = slice(pairs[u // 2] * 128, (pairs[u // 2] + 1) * 128)
            groups.append(
                loads.start([(ins[j].at[u % 2, :, cols], scratch[j].at[u]) for j in range(4)])
            )
        half = lax.broadcasted_iota(jnp.int32, (1, 128), 1) // HEAD_DIM
        for group in groups:
            loads.wait(group)

        def unit(u, carry):
            q2, k2, v2, do2 = q_s[u], k_s[u], v_s[u], do_s[u]
            dq = dk = dv = None
            for h in range(2):
                mask = (half == h).astype(BF)
                km, qm, dom = k2 * mask, q2 * mask, do2 * mask
                scores = dot(km, q2, NT)
                row = lax.broadcasted_iota(jnp.int32, scores.shape, 0)
                scores = jnp.where(row < VALID, scores, -1e30)
                e = jnp.exp(scores - jnp.max(scores, axis=0, keepdims=True))
                probs = e * (1.0 / jnp.sum(e, axis=0, keepdims=True))
                grad_probs = dot(v2, dom, NT)
                row_dot = jnp.sum(probs * grad_probs, axis=0, keepdims=True)
                grad_scores = (probs * (grad_probs - row_dot)).astype(BF)
                v_piece = dot(probs.astype(BF), dom, NN)
                k_piece = dot(grad_scores, qm, NN)
                q_piece = dot(grad_scores, km, TN)
                dq = q_piece if dq is None else dq + q_piece
                dk = k_piece if dk is None else dk + k_piece
                dv = v_piece if dv is None else dv + v_piece
            dq = dq * HEAD_DIM**-0.5
            bs_s[u, 0:1, :] = jnp.sum(dq, axis=0, keepdims=True)
            bs_s[u, 1:2, :] = jnp.sum(dv, axis=0, keepdims=True)
            dq_s[u] = dq.astype(BF)
            dk_s[u] = dk.astype(BF)
            dv_s[u] = dv.astype(BF)
            return carry

        lax.fori_loop(0, 2 * n, unit, 0)
        done = [loads.start([(scratch[4 + j], outs[0].at[j])]) for j in range(3)]
        done.append(loads.start([(bs_s, outs[1])]))
        for group in done:
            loads.wait(group)

    grads, sums = call(
        body,
        [q, k, v, grad],
        [sds((3, 2 * n, seq, 128), BF), sds((2 * n, 2, 128), F32)],
        [pltpu.VMEM((2 * n, seq, 128), BF)] * 7 + [pltpu.VMEM((2 * n, 2, 128), F32)],
        name,
        0,
    )
    return grads.reshape(3 * n, 2 * seq, 128), sums


def finish_layer(ids, keep, nv, middle, part, recv, nd, aligned):
    _, seq, width = middle.shape

    def body(small, ins, outs, scratch, loads):
        ids_ref, keep_ref, nv_ref = small
        mine = ids_ref[0]
        mid_s, part_s, recv_s, out_s = scratch
        groups = [loads.start([(ins[i].at[mine], scratch[i])]) for i in range(3)]
        for group in groups:
            loads.wait(group)
        total = part_s[...].astype(F32) + recv_s[...].astype(F32) + nv_ref[5:6, :]
        out_s[...] = (mid_s[...] + keep_ref[mine] * total).astype(BF)
        loads.wait(loads.start(block_stores(ids_ref, out_s, outs[0], nd, aligned)))

    return call(
        body,
        [middle, part, recv],
        [sds((seq, width), BF)],
        [pltpu.VMEM((seq, width), F32)] + [pltpu.VMEM((seq, width), BF)] * 3,
        "finish_layer",
        100 * seq * width,
        smem=(ids, keep),
        vmem_ins=(nv,),
    )[0]


def finish_tokens(ids, nv, tok, part, recv, gmid, rest, sums, nd, aligned):
    _, seq, width = tok.shape
    n_dest, z_n, n_rows, lanes = rest.shape
    bd, y_n = width // nd, nd // rest.shape[1]
    tx = n_dest // y_n

    def body(small, ins, outs, scratch, loads):
        ids_ref, nv_ref = small[:2]
        mine = ids_ref[0]
        tok_s, part_s, recv_s, gm_s, out_s, cs_s, rest_s = scratch
        g_rest = loads.start([(ins[4], rest_s)] if sums is None else [])
        groups = [
            loads.start(
                [
                    (ins[0].at[a], tok_s.at[a]),
                    (ins[2].at[a], part_s.at[a]),
                    (ins[3].at[a], recv_s.at[a]),
                ]
            )
            for a in range(2)
        ]
        g_mid = loads.start([(ins[1], gm_s)])
        for group in groups:
            loads.wait(group)
        done = []
        for i in range(2):
            a = mine if i == 0 else 1 - mine
            hat, inverse = norm_parts(tok_s[a].astype(F32))
            grad_one = part_s[a].astype(F32) + recv_s[a].astype(F32)
            gain_sum = jnp.sum(grad_one * hat, axis=0, keepdims=True)
            shift_sum = jnp.sum(grad_one, axis=0, keepdims=True)
            if i == 0:
                cs_s[0:1, :] = gain_sum
                cs_s[1:2, :] = shift_sum
                loads.wait(g_mid)
                value = gm_s[...] + norm_back(grad_one, hat, inverse, nv_ref[0:1, :])
                out_s[...] = value.astype(BF)
                done.append(loads.start(block_stores(ids_ref, out_s, outs[0], nd, aligned)))
            else:
                cs_s[0:1, :] = cs_s[0:1, :] + gain_sum
                cs_s[1:2, :] = cs_s[1:2, :] + shift_sum
        loads.wait(g_rest)
        if sums is not None:
            col_ref, bup_ref, pairs = small[2], small[3], small[4:]
            up = bup_ref.shape[1] // tx // nd
            n_pairs = sum(ref.shape[0] // 2 for ref in pairs)
            qv = n_pairs * 128 // tx // nd
            per = 128 // qv
            lane = lax.broadcasted_iota(jnp.int32, (2, 128), 1)
            whole = [ref[2 * i] + ref[2 * i + 1] for ref in pairs for i in range(ref.shape[0] // 2)]
            whole = jnp.stack(whole)
            rest_s[...] = jnp.zeros_like(rest_s)
            for n in range(n_dest):
                kx, ky = n // y_n, n % y_n
                for kz in range(z_n):
                    p = ky * z_n + kz
                    d = ids_ref[2 + p]
                    rest_s[n, kz, 2:6, :] = col_ref[:, p * bd : (p + 1) * bd]
                    row = jnp.zeros((2, 128), F32)
                    for i in range(nd // per):
                        row = jnp.where(d // per == i, whole[kx * (nd // per) + i], row)
                    row = pltpu.roll(row, (per - d % per) * qv % 128, 1)
                    rest_s[n, kz, 6:8, :] = jnp.where(lane < qv, row, 0.0)
                    cols = pl.ds(pl.multiple_of((kx * nd + d) * up, 128), up)
                    rest_s[n, kz, 8:9, 0:up] = bup_ref[:, cols]
        for n in range(n_dest if aligned else 0):
            for kz in range(z_n):
                p = n % (nd // z_n) * z_n + kz
                rest_s[n, kz, 0:2, :] = cs_s[:, p * bd : (p + 1) * bd]
        done.append(loads.start([(cs_s, outs[1])]))
        done += [loads.start([(rest_s.at[n], outs[2 + n])]) for n in range(n_dest)]
        for group in done:
            loads.wait(group)

    return call(
        body,
        [tok, gmid, part, recv] + ([rest] if sums is None else []),
        [sds((seq, width), BF), sds((2, width), F32)] + [sds(rest.shape[1:], F32)] * n_dest,
        [pltpu.VMEM((2, seq, width), BF)] * 3
        + [pltpu.VMEM((seq, width), F32), pltpu.VMEM((seq, width), BF), pltpu.VMEM((2, width), F32)]
        + [pltpu.VMEM(rest.shape, F32)],
        "finish_tokens",
        200 * seq * width,
        smem=(ids,),
        vmem_ins=(nv,) + tuple(sums or ()),
    )


class Grid3:
    def __init__(self, dp, tx):
        self.dp, self.tx = dp, tx
        self.y = 2 if dp % 2 == 0 else 1
        self.z = dp // self.y

    def send_z(self, value, k):
        return lax.ppermute(value, "dp", [(i, i ^ (k * self.y)) for i in range(self.dp)])

    def send_y(self, value, k):
        return lax.ppermute(value, "dp", [(i, i ^ k) for i in range(self.dp)])

    def send_xy(self, value, kx, ky):
        count = self.dp * self.tx
        pairs = [(i, ((i // self.tx) ^ ky) * self.tx + ((i % self.tx) ^ kx)) for i in range(count)]
        return lax.ppermute(value, ("dp", "tx"), pairs)

    def send_x(self, value, k):
        return lax.ppermute(value, "tx", [(i, i ^ k) for i in range(self.tx)])


def swap_core(value):
    return lax.ppermute(value, "core", [(0, 1), (1, 0)])


def after(values, gate):
    return lax.optimization_barrier((values, gate))[0]


def gather_z(grid, part_a, part_b, gate=None):
    rows = part_a.shape[0]
    both = jnp.concatenate([part_a, part_b], axis=0)
    all_z = [both] + [grid.send_z(both, k) for k in range(1, grid.z)]
    if gate is not None:
        all_z = after(all_z, gate)
    return jnp.stack([v[:rows] for v in all_z]), jnp.stack([v[rows:] for v in all_z])


def gather_first(grid, a_z, b_z):
    a_y = [a_z] + [grid.send_y(a_z, k) for k in range(1, grid.y)]
    b_x = [b_z] + [grid.send_x(b_z, k) for k in range(1, grid.tx)]
    return a_y, b_x


def join(pieces):
    return [jnp.concatenate(part) for part in pieces]


def gather_last(grid, a_y, b_x):
    a_all = [a_y] + [grid.send_x(a_y, k) for k in range(1, grid.tx)]
    b_all = [b_x] + [grid.send_y(b_x, k) for k in range(1, grid.y)]
    return a_all, b_all


def add_pieces(groups, cuts, outs, name, smem=(), more=(), fill=None):
    arrays = [a for group in groups for a in group]
    starts = [sum(len(g) for g in groups[:i]) for i in range(len(groups))]
    last = {}
    for n, cut in enumerate(cuts):
        last[cut[2]] = n

    def body(small, ins, outs_ref, scratch, loads):
        in_s, out_s = scratch[: len(arrays)], scratch[len(arrays) :]
        more_s = out_s[len(outs) :]
        loaded = [loads.start([(ins[i], in_s[i]) for i in range(starts[g], starts[g] + len(groups[g]))]) for g in range(len(groups))]
        ready, done = set(), []
        for n, (g, spot, which, place) in enumerate(cuts):
            if g not in ready:
                loads.wait(loaded[g])
                ready.add(g)
            total = None
            for i in range(starts[g], starts[g] + len(groups[g])):
                value = in_s[i][spot].astype(F32)
                total = value if total is None else total + value
            out_s[which][place] = total.astype(out_s[which].dtype)
            for w in sorted(w for w in last if last[w] == n):
                done.append(loads.start([(out_s[w], outs_ref[w])]))
        if fill is not None:
            fill(small, out_s, more_s)
            done.append(loads.start(list(zip(more_s, outs_ref[len(outs) :]))))
        for group in done:
            loads.wait(group)

    return call(
        body,
        arrays,
        list(outs) + list(more),
        [pltpu.VMEM(a.shape, a.dtype) for a in list(arrays) + list(outs) + list(more)],
        name,
        0,
        smem=smem,
        spare=8,
    )


class Scatter:
    def __init__(self, grid, a_all, b_all, name):
        self.grid, self.name, self.bit = grid, name, 0
        self.rows = (a_all[0].shape[1], b_all[0].shape[1])
        a_got = [grid.send_x(a_all[k], k) for k in range(1, grid.tx)]
        b_got = [grid.send_y(b_all[k], k) for k in range(1, grid.y)]
        self.state = ([a_all[0]] + a_got, [b_all[0]] + b_got)

    def second(self, gate):
        grid, z = self.grid, self.grid.z
        a_in, b_in = after(self.state, gate)
        outs = [sds((z,) + a_in[0].shape[1:], BF)] * grid.y + [sds((z,) + b_in[0].shape[1:], BF)] * grid.tx
        full = slice(None)
        cuts = [(0, slice(k * z, (k + 1) * z), k, full) for k in list(range(1, grid.y)) + [0]]
        cuts += [(1, slice(k * z, (k + 1) * z), grid.y + k, full) for k in list(range(1, grid.tx)) + [0]]
        res = add_pieces([a_in, b_in], cuts, outs, self.name + "_add")
        a_y, b_x = res[: grid.y], res[grid.y :]
        a_got = [grid.send_y(a_y[k], k) for k in range(1, grid.y)]
        b_got = [grid.send_x(b_x[k], k) for k in range(1, grid.tx)]
        self.state = ([a_y[0]] + a_got, [b_x[0]] + b_got)
        return a_y, b_x

    def along_z(self, gate, extra=None):
        grid = self.grid
        a_in, b_in = after(self.state, gate)
        ra, rb = self.rows
        groups = [a_in, b_in] + ([extra] if extra else [])
        more = extra[0].shape[1] if extra else 0
        order = list(range(1, grid.z)) + [0]
        cuts = []
        for k in order:
            cuts.append((0, k, k, slice(0, ra)))
            cuts.append((1, k, k, slice(ra, ra + rb)))
            if extra:
                cuts.append((2, k, k, slice(ra + rb, ra + rb + more)))
        outs = [sds((ra + rb + more,) + a_in[0].shape[2:], BF)] * grid.z
        both = add_pieces(groups, cuts, outs, self.name + "_addz")
        self.state = [both[0]] + [grid.send_z(both[k], k) for k in range(1, grid.z)]
        return both

    def halve(self, gate):
        grid, (ra, rb) = self.grid, self.rows
        groups = after(self.state, gate)
        if self.bit == 0:
            self.bit, self.left = 1, list(range(grid.z))
        else:
            self.bit, groups = 2 * self.bit, [groups]
        sent = [k for k in self.left if k & self.bit]
        kept = [k for k in self.left if not k & self.bit]
        cuts = []
        for which, ids in ((0, sent), (1, kept)):
            for n, k in enumerate(ids):
                spot = self.left.index(k)
                if len(groups) == 2:
                    cuts.append((0, spot, which, (n, slice(0, ra))))
                    cuts.append((1, spot, which, (n, slice(ra, ra + rb))))
                else:
                    cuts.append((0, spot, which, n))
        outs = [sds((len(kept), ra + rb) + groups[0][0].shape[2:], BF)] * 2
        send, keep = add_pieces(groups, cuts, outs, self.name + "_half")
        self.left = kept
        self.state = [keep, grid.send_z(send, self.bit)]
        return keep, send

    def finish(self, gate, cuts, outs, **extra):
        if self.bit:
            cuts = [((0, rows), which, place) for rows, which, place in cuts]
        cuts = [(0, rows, which, place) for rows, which, place in cuts]
        return add_pieces([after(self.state, gate)], cuts, outs, self.name + "_sum", **extra)


def join_kernel(pieces):
    groups, cuts, outs = [], [], []
    for which, part in enumerate(pieces):
        lead = part[0].shape[0]
        for k, value in enumerate(part):
            cuts.append((len(groups), slice(None), which, slice(k * lead, (k + 1) * lead)))
            groups.append([value])
        outs.append(sds((lead * len(part),) + part[0].shape[1:], BF))
    return add_pieces(groups, cuts, outs, "join")


def xor_blocks(value, mask, axis):
    count = value.shape[axis]
    bit = 1
    while bit < count:
        shape = value.shape
        split = value.reshape(shape[:axis] + (count // (2 * bit), 2, bit) + shape[axis + 1 :])
        turned = jnp.flip(split, axis=axis + 1).reshape(shape)
        value = jnp.where(jnp.bitwise_and(mask, bit) != 0, turned, value)
        bit *= 2
    return value


def pad_cols(value, width):
    return jnp.pad(value, ((0, 0), (0, width - value.shape[1])))


def per_device(
    tokens,
    cotangent,
    image_mask,
    norm_gains,
    norm_shifts,
    w_qkv,
    b_qv,
    w_out,
    w_up,
    up_bias,
    w_down,
    *,
    dp,
    tx,
):
    grid = Grid3(dp, tx)
    y_n, z_n = grid.y, grid.z
    core = lax.axis_index("core").astype(jnp.int32)
    me_d = lax.axis_index("dp").astype(jnp.int32)
    me_x = lax.axis_index("tx").astype(jnp.int32)
    seq, width = tokens.shape
    _, bd, hw = w_qkv.shape
    fw = w_up.shape[1]
    ext, hid = tx * hw, tx * fw
    hh, fh = hw // 2, fw // 2
    aligned = bd % 128 == 0 and hh % 128 == 0 and fh % 128 == 0
    rel = [kz * y_n + ky for ky in range(y_n) for kz in range(z_n)]

    def from_abs(value, axis):
        shape = value.shape
        value = value.reshape(shape[:axis] + (z_n, y_n) + shape[axis + 1 :])
        return jnp.swapaxes(value, axis, axis + 1).reshape(shape)

    def to_rel(value, axis):
        shape = value.shape
        value = value.reshape(shape[:axis] + (y_n, z_n) + shape[axis + 1 :])
        return jnp.swapaxes(value, axis, axis + 1).reshape(shape)

    ids = jnp.stack([core, me_d] + [jnp.bitwise_xor(me_d, k) for k in rel])
    keep = lax.dynamic_slice(image_mask, (2 * me_x,), (2,)).astype(F32)

    lane = max(bd, hh)
    small = jnp.concatenate(
        [
            pad_cols(norm_gains, lane),
            pad_cols(norm_shifts, lane),
            pad_cols(b_qv, lane),
            pad_cols(up_bias[None], lane),
            jnp.zeros((7, lane), BF),
        ]
    )
    qkv_a = pad_cols(w_qkv[:, :, :hh].reshape(3 * bd, hh), lane)
    qkv_b = pad_cols(w_qkv[:, :, hh:].reshape(3 * bd, hh), lane)
    first_a = jnp.concatenate([qkv_a, pad_cols(w_out[:hh], lane), small])
    first_b = jnp.concatenate([qkv_b, pad_cols(w_out[hh:], lane)])
    own = [tokens, cotangent]
    other = [swap_core(value) for value in own]
    if aligned:
        tok, cot, grad_top = arrange_pair(ids, keep, own, other, dp)
    else:

        def arrange(own, other):
            pair = jnp.where(core == 0, jnp.stack([own, other]), jnp.stack([other, own]))
            pair = xor_blocks(pair.reshape(2, seq, dp, bd), me_d, 2)
            return from_abs(pair, 2).reshape(2, seq, width)

        tok, cot = [arrange(own[i], other[i]) for i in range(2)]
        grad_top = cot * keep.astype(BF)[:, None, None]
    c1_z = gather_z(grid, first_a, first_b, gate=tok)
    c1_h = gather_first(grid, *c1_z)
    c1_h = join(c1_h)
    c1a, c1b = gather_last(grid, *c1_h)
    up_halves = after((w_up[:, :fh], w_up[:, fh:]), c1_h)
    row0 = 3 * bd + hh
    if aligned and 128 % (hw // dp) == 0 and (fw // dp) % 128 == 0:
        c1a, c1b = after((c1a, c1b), (c1a, c1b))
        nv, bq, bu = vectors(ids, c1a, row0, dp, y_n, bd, hw // dp, fw // dp)
    else:
        nv = c1a[0][:, row0 : row0 + 6, :bd].transpose(1, 0, 2).reshape(6, width).astype(F32)
        tail = jnp.stack([v[:, row0 + 6 : row0 + 9] for v in c1a])
        tail = xor_blocks(to_rel(tail, 1), me_d, 1)
        bq = tail[:, :, :2, : hw // dp].transpose(2, 0, 1, 3).reshape(2, ext).astype(F32)
        bu = tail[:, :, 2, : fw // dp].reshape(1, hid).astype(F32)

    up_z = gather_z(grid, *up_halves, gate=nv)
    up_h = gather_first(grid, *up_z)
    dn_halves = after((w_down[:fh], w_down[fh:]), up_z)

    if aligned:
        every, wq_plan, wo_plan, up_plan, dn_plan = slice(None), [[], [], []], [], [], []
        for kx in range(tx):
            halves = [slice(kx * hw, kx * hw + hh), slice(kx * hw + hh, (kx + 1) * hw)]
            f_halves = [slice(kx * fw, kx * fw + fh), slice(kx * fw + fh, (kx + 1) * fw)]
            own = slice(kx * z_n, (kx + 1) * z_n)
            for i in range(3):
                src = slice(i * bd, (i + 1) * bd)
                wq_plan[i].append((kx, (every, src), (i, every, every, halves[0])))
                for ky in range(y_n):
                    dst = (i, slice(ky * z_n, (ky + 1) * z_n), every, halves[1])
                    wq_plan[i].append((tx + ky, (own, src), dst))
            src = slice(3 * bd, 3 * bd + hh)
            dn_plan += [[], []]
            for ky in range(y_n):
                for kz in range(z_n):
                    p, r = ky * z_n + kz, kx * z_n + kz
                    cols = slice(p * bd, (p + 1) * bd)
                    wo_plan.append((kx, (p, src), (halves[0], cols)))
                    wo_plan.append((tx + ky, (r, src), (halves[1], cols)))
                    dn_plan[-2].append((kx, (p,), (f_halves[0], cols)))
                    dn_plan[-1].append((tx + ky, (r,), (f_halves[1], cols)))
            up_plan += [[(kx, (every,), (every, f_halves[0]))], []]
            for ky in range(y_n):
                rows = slice(kx * z_n * bd, (kx + 1) * z_n * bd)
                dst = (slice(ky * z_n * bd, (ky + 1) * z_n * bd), f_halves[1])
                up_plan[-1].append((tx + ky, (rows,), dst))
        c1 = c1a + c1b
        wqkv = (c1, wq_plan, (3, dp, bd, ext))
        wout = (c1, [wo_plan], (ext, width))
    else:

        def whole(a_all, b_all):
            a = jnp.stack(a_all)
            b = jnp.stack(b_all).reshape((y_n, tx, z_n) + b_all[0].shape[1:])
            b = b.transpose(1, 0, 2, 3, 4).reshape(a.shape[:2] + b.shape[3:])
            return jnp.stack([a, b], axis=1)

        c1 = whole([v[:, :row0] for v in c1a], c1b)
        qkv = c1[:, :, :, : 3 * bd, :hh].reshape(tx, 2, dp, 3, bd, hh)
        qkv = qkv.transpose(3, 2, 4, 0, 1, 5).reshape(3, dp, bd, ext)
        out = c1[:, :, :, 3 * bd :, :bd].transpose(0, 1, 3, 2, 4).reshape(ext, width)
        all_of = [[(0, (slice(None),), (slice(None),))]]
        wqkv = ([qkv], all_of, qkv.shape)
        wout = ([out], all_of, out.shape)

    rows2 = 2 * seq

    res = attn_forward(0, after(tok, up_z), nv, bq, wqkv, wout, None)
    part0 = res[5]
    up_h = join(after(up_h, part0))
    upa, upb = gather_last(grid, *up_h)
    dn_halves = after(dn_halves, up_h)
    res = attn_forward(1, after(tok, up_h), nv, bq, wqkv, wout, res[:5])
    recv0 = swap_core(after(part0, res[5]))
    parts = [(part0, recv0), (res[5], swap_core(res[5]))]
    first, q, k, v, att = res[:5]
    upa, upb = after((upa, upb), res[5])
    dn_z = gather_z(grid, *dn_halves, gate=(upa, upb))
    dn_h = gather_first(grid, *dn_z)
    if aligned:
        wup = ([v.reshape(-1, fh) for v in upa + upb], up_plan, (width, hid))
    else:
        up_w = whole(upa, upb).transpose(2, 3, 0, 1, 4).reshape(width, hid)
        wup = ([up_w], all_of, up_w.shape)
    part, recv = parts[0]
    state = mlp_up(0, tok, part, recv, keep, nv, bu, wup, fh, None)
    dna, dnb = gather_last(grid, *join_kernel(after(dn_h, state[1])))
    part, recv = parts[1]
    state = mlp_up(1, tok, part, recv, keep, nv, bu, wup, fh, state)
    if aligned:
        wdown = (dna + dnb, dn_plan, (hid, width))
    else:
        down_w = whole(dna, dnb).transpose(0, 1, 3, 2, 4).reshape(hid, width)
        wdown = ([down_w], all_of, down_w.shape)
    middle, second, act, dact = state
    flat = lambda value: value.reshape(rows2, value.shape[2])
    act2, sec2, grad2 = flat(act), flat(second), flat(grad_top)

    full = slice(None)
    a_spots = [(p, slice(p * bd, (p + 1) * bd)) for p in range(dp)]

    def by_left(l_index, r_index, size, row0):
        tasks, rows = [], slice(row0, row0 + size // 2)
        halves = slice(0, size // 2), slice(size // 2, size)
        for kx in range(tx):
            stores = [(kx, (p, rows), halves[0], cols) for p, cols in a_spots]
            for p, cols in a_spots:
                ky, kz = p // z_n, p % z_n
                stores.append((tx + ky, (kx * z_n + kz, rows), halves[1], cols))
            tasks.append((l_index, slice(kx * size, (kx + 1) * size), r_index, slice(0, width), stores))
        return tasks

    def by_right(l_index, r_index, size, row0, lanes, spare=False, first=0):
        tasks, each = [], size // 2 // lanes
        for kx in range(tx):
            stores = []
            for j in range(each):
                rows = slice(row0 + j * bd, row0 + (j + 1) * bd)
                cols = [slice((h * each + j) * lanes, (h * each + j + 1) * lanes) for h in range(2)]
                rows = (rows, slice(0, lanes)) if spare else (rows,)
                for p, r_sl in a_spots:
                    ky, kz = p // z_n, p % z_n
                    stores.append((kx, (p,) + rows, r_sl, cols[0]))
                    stores.append((tx + ky, (kx * z_n + kz,) + rows, r_sl, cols[1]))
            cols = slice(first + kx * size, first + (kx + 1) * size)
            tasks.append((l_index, slice(0, width), r_index, cols, stores))
        return tasks

    def pieces(rows, lanes):
        return [(dp, rows, lanes)] * tx + [(tx * z_n, rows, lanes)] * y_n

    def send_grad(parts, name):
        return Scatter(grid, list(parts[:tx]), list(parts[tx:]), name)

    grads = weight_grad([act2], [grad2], by_left(0, 0, fw, 0), pieces(fh, bd), "down_grad", 0, fh)
    down_rs = send_grad(grads, "down")
    grad_in = after(grad2, grads[-1])
    low_pre, bias_up, two_part, mlp_part = mlp_back(grad_in, act2, flat(dact), wdown, wup, fh)
    mlp_part = mlp_part.reshape(2, seq, width)
    two_recv = swap_core(two_part)
    down_half = down_rs.second(bias_up)
    up_rows = fh // bd * bd
    sec_in = after(sec2, down_half)
    tasks = by_right(0, 0, fw, 0, bd)
    grads = weight_grad([sec_in], [low_pre], tasks, pieces(up_rows, bd), "up_grad", 0, up_rows)
    up_rs = send_grad(grads, "up")
    gmid, gattn, grad_att, col = middle_back(
        ids, middle, two_part, after(two_recv, grads[-1]), cot, keep, nv, wout
    )
    down_zs = down_rs.along_z(col)
    row0 = 3 * bd
    last_shapes = pieces(row0 + hh, bd)
    att_in = after(flat(att), down_zs)
    tasks = by_left(0, 0, hw, 0)
    out_grads = weight_grad(
        [att_in], [flat(gattn)], tasks, last_shapes, "out_grad", row0, row0 + hh
    )

    n_pairs = ext // 128
    split = hh == 128 and bd == 128 and n_pairs >= 4
    if split:
        heads = [[1], list(range(2, n_pairs))]
        first_in = after(grad_att, out_grads[-1])
        left_0, bias_0 = attn_backward(heads[0], first_in, q, k, v, "attn_first")
        up_half = up_rs.second(bias_0)
    else:
        heads = [list(range(n_pairs))]
        up_half = up_rs.second(out_grads[-1])
    left_a, bias_a = attn_backward(heads[-1], after(grad_att, up_half), q, k, v)
    first_in = flat(first)
    gate = bias_a
    if not split:
        grad_down = down_rs.finish(bias_a, [(full, 0, full)], [sds((fw, bd), F32)])[0]
        mlp_recv = swap_core(after(mlp_part, bias_a))
        gate = up_rs.halve(grad_down) if z_n > 1 else grad_down
    if split:
        stores, count = [], n_pairs - 1
        for i in range(3):
            rows = slice(i * bd, (i + 1) * bd)
            for n, pair in enumerate(range(1, n_pairs)):
                kx, cols = pair // 2, slice((i * count + n) * 128, (i * count + n + 1) * 128)
                for p, r_sl in a_spots:
                    ky, kz = p // z_n, p % z_n
                    spot = (kx - 1, (p, rows))
                    if pair % 2:
                        spot = (tx - 1 + ky, (kx * z_n + kz, rows))
                    stores.append(spot + (r_sl, cols))
        tasks = [(0, slice(0, width), 0, slice(0, 384 * count), stores)]
        sent = weight_grad(
            [first_in], [left_0, left_a], tasks, last_shapes[1:], "qkv_grad", 0, row0, out_grads[1:]
        )
        leaving = (sent[: tx - 1], sent[tx:])
        grad_down = down_rs.finish(sent[-1], [(full, 0, full)], [sds((fw, bd), F32)])[0]
        mlp_recv = swap_core(after(mlp_part, bias_a))
        gate = up_rs.halve((grad_down, leaving)) if z_n > 1 else grad_down
        left_b, bias_b = attn_backward([0], after(grad_att, (leaving, gate)), q, k, v)
        gate = (bias_b, mlp_recv)
        stores = []
        for i in range(3):
            rows, cols = slice(i * bd, (i + 1) * bd), slice(i * 128, (i + 1) * 128)
            stores += [(0, (p, rows), r_sl, cols) for p, r_sl in a_spots]
        tasks = [(0, slice(0, width), 0, slice(0, 384), stores)]
        kept = weight_grad(
            [after(first_in, gate)],
            [left_b],
            tasks,
            last_shapes[:1],
            "qkv_keep",
            0,
            row0,
            out_grads[:1],
        )
        grads = list(kept) + list(sent)
        lefts, starts = [left_0, left_a, left_b], [1, 2, 0]
        pair_sums = [bias_b, bias_0, bias_a]
        gate = kept[0]
    else:
        while 2 * up_rs.bit < z_n:
            gate = up_rs.halve((gate, mlp_recv))
        makers = [by_right(0, 0, hw, i * bd, hh, hh < bd, i * ext) for i in range(3)]
        tasks = [task for maker in makers for task in maker]
        grads = weight_grad(
            [after(first_in, gate)],
            [left_a],
            tasks,
            last_shapes,
            "qkv_grad",
            0,
            row0,
            out_grads,
            hh < bd,
        )
        lefts, starts = [left_a], [0]
        pair_sums = [bias_a]
        gate = grads[-1]
    qkv_rs = send_grad(grads, "qkv")
    lefts = after(lefts, gate)
    one_part = input_grad(lefts, starts, wqkv, width)
    one_recv = swap_core(one_part)
    cuts = []
    for h in range(2):
        for j in range(fh // bd):
            rows = slice(h * up_rows + j * bd, h * up_rows + (j + 1) * bd)
            cuts.append((rows, 0, (full, slice(h * fh + j * bd, h * fh + (j + 1) * bd))))
    up_cuts = cuts
    gate = one_part
    while 2 * up_rs.bit < z_n:
        gate = up_rs.halve(gate)
    qkv_half = qkv_rs.second(gate)
    wide = max(bd, hw // dp, fw // dp)
    if split and fw // dp == bd and 128 % (hw // dp) == 0:
        rest = sds((tx * y_n, z_n, 16, wide), F32)
        sums = [col, bias_up] + pair_sums
    else:
        bias_qv = jnp.concatenate(pair_sums)
        bias_qv = jnp.sum(bias_qv.reshape(n_pairs, 2, 2, 128), axis=1).transpose(1, 0, 2)
        vec = jnp.concatenate([jnp.zeros((2, width), F32), col])
        vec = vec.reshape(6, y_n, z_n, bd).transpose(1, 2, 0, 3)
        bias_qv = bias_qv.reshape(2, tx, dp, hw // dp).transpose(2, 1, 0, 3)
        bias_up = bias_up.reshape(tx, 1, dp, fw // dp).transpose(2, 0, 1, 3)
        bias = jnp.concatenate(
            [
                jnp.pad(value, ((0, 0), (0, 0), (0, 0), (0, wide - value.shape[3])))
                for value in (bias_qv, bias_up)
            ],
            axis=2,
        )
        bias = from_abs(xor_blocks(bias, me_d, 0), 0).reshape(y_n, z_n, tx, 3, wide)
        bias = bias.transpose(2, 0, 1, 3, 4)
        vec = jnp.pad(vec, ((0, 0), (0, 0), (0, 0), (0, wide - bd)))
        vec = jnp.broadcast_to(vec, (tx,) + vec.shape)
        rest = jnp.concatenate([vec, bias, jnp.zeros((tx, y_n, z_n, 7, wide), F32)], axis=3)
        rest = rest.reshape(tx * y_n, z_n, 16, wide)
        sums = None
    grad_tokens, one_sums, *small = finish_tokens(
        ids, nv, tok, one_part, after(one_recv, qkv_half), gmid, rest, sums, dp, aligned
    )
    if not aligned:
        ones = jnp.pad(one_sums.reshape(2, y_n, z_n, bd), ((0, 14), (0, 0), (0, 0), (0, wide - bd)))
        ones = ones.transpose(1, 2, 0, 3)
        small = [value + ones[n % y_n] for n, value in enumerate(small)]
    grad_up = up_rs.finish(small[0], up_cuts, [sds((bd, fw), F32)])[0]
    small = after(small, grad_up)
    got = small[:1]
    for n in range(1, tx * y_n):
        got.append(grid.send_xy(small[n], n // y_n, n % y_n))
    cuts, outs = [], [sds((3, bd, hw), F32), sds((hw, bd), F32)]
    last_rows = row0 + hh
    for h in range(2):
        for i in range(3):
            rows = slice(h * last_rows + i * bd, h * last_rows + (i + 1) * bd)
            rows = (rows, slice(0, hh)) if hh < bd else rows
            cuts.append((rows, 0, (i, full, slice(h * hh, (h + 1) * hh))))
        rows = slice(h * last_rows + row0, (h + 1) * last_rows)
        cuts.append((rows, 1, (slice(h * hh, (h + 1) * hh),)))
    if wide == bd:
        qkv_zs = qkv_rs.along_z(grad_up, got)
        cuts.append((slice(2 * last_rows, 2 * last_rows + 16), 2, full))
        outs.append(sds((16, wide), F32))
    else:
        qkv_zs = qkv_rs.along_z(grad_up)
    layer_out = finish_layer(
        ids, keep, nv, middle, after(mlp_part, qkv_zs), mlp_recv, dp, aligned
    )
    share, own = bd // (2 * tx), None
    if wide == bd == 128 and fw // dp == bd:
        qv = hw // dp

        def fill(small, out_s, more_s):
            rows = out_s[2][...]
            turned = pltpu.roll(rows, (128 - small[0][0]) % 128, 1)
            more_s[0][0:1, :] = turned[0:1, :share]
            more_s[0][1:2, :] = turned[2:3, :share]
            more_s[1][0:1, :] = turned[1:2, :share]
            more_s[1][1:4, :] = turned[3:6, :share]
            more_s[2][...] = rows[6:8, :qv]
            more_s[3][...] = rows[8:9, :]

        shapes = [(2, share), (4, share), (2, qv), (1, bd)]
        place = ((2 * me_x + core) * share)[None]
        more = [sds(shape, F32) for shape in shapes]
        res = qkv_rs.finish(layer_out, cuts, outs, smem=(place,), more=more, fill=fill)
        own = res[3:]
    else:
        res = qkv_rs.finish(layer_out, cuts, outs)
    grad_qkv, grad_out = res[:2]
    if wide == bd:
        both = res[2]
    else:
        both, bit = sum(got), 1
        while bit < z_n:
            both = both.reshape((-1, 2) + both.shape[1:])
            both = both[:, 0] + grid.send_z(both[:, 1], bit)
            bit *= 2
        both = both[0]
    if not aligned:

        def restore(value):
            value = xor_blocks(to_rel(value.reshape(seq, dp, bd), 1), me_d, 1)
            return value.reshape(seq, width)

        layer_out, grad_tokens = restore(layer_out), restore(grad_tokens)

    if own is None:
        mine = lax.dynamic_slice(both[:6, :bd], (0, (2 * me_x + core) * share), (6, share))
        own = [
            mine[0:3:2],
            jnp.concatenate([mine[1:2], mine[3:6]]),
            both[6:8, : hw // dp],
            both[8:9, : fw // dp],
        ]
    return (
        layer_out,
        grad_tokens,
        own[0],
        own[1],
        grad_qkv,
        own[2],
        grad_out,
        grad_up,
        own[3].reshape(fw // dp),
        grad_down,
    )


def solution(mesh):
    dp, tensor = mesh.shape["dp"], mesh.shape["tensor"]
    split = Mesh(mesh.devices.reshape(dp, tensor // 2, 2), ("dp", "tx", "core"))
    every = ("dp", "tx", "core")
    tensor_axes = ("tx", "core")
    in_specs = (
        P(every, None),
        P(every, None),
        P("dp"),
        P(None, "dp"),
        P(None, "dp"),
        P(None, "dp", tensor_axes),
        P(None, ("tx", "core", "dp")),
        P(tensor_axes, "dp"),
        P("dp", tensor_axes),
        P(("tx", "core", "dp")),
        P(tensor_axes, "dp"),
    )
    out_specs = (
        P(every, None),
        P(every, None),
        P(None, every),
        P(None, every),
        P(None, "dp", tensor_axes),
        P(None, ("tx", "core", "dp")),
        P(tensor_axes, "dp"),
        P("dp", tensor_axes),
        P(("tx", "core", "dp")),
        P(tensor_axes, "dp"),
    )
    return jax.shard_map(
        functools.partial(per_device, dp=dp, tx=tensor // 2),
        mesh=split,
        in_specs=in_specs,
        out_specs=out_specs,
        check_vma=False,
    )
```
